32 devices in a mesh: dp: 8 (over z, x), rep: 4 (over y, core).
Axes of the slice: x: 2, y: 2, z: 4, core: 2. Of those that a mesh axis runs over, the one named last changes fastest.
Arguments:
- latents: bfloat16 [8192, 16], P(('dp', 'rep')), may hold values from -6 to 6
- route: int32 [8192], P(('dp', 'rep')), may hold values from 0 to 256, as said below
- labels: int32 [32], P(('dp', 'rep')), may hold values from 0 to 999
- timesteps: int32 [4, 8192], P(None, ('dp', 'rep')), may hold values from 0 to 999
- noise: float32 [4, 8192, 16], P(None, ('dp', 'rep')), may hold values from -6 to 6
- image_weight: float32 [32], P(('dp', 'rep')), may hold values from 0.5 to 1.5
- weights: float32 [22573056], P(('dp', 'rep')), as said below
- momentum: float32 [22573056], P(('dp', 'rep')), as said below
- average: float32 [22573056], P(('dp', 'rep')), as said below
Outputs:
- new_weights: float32 [22573056], P(('dp', 'rep'))
- new_momentum: float32 [22573056], P(('dp', 'rep'))
- new_average: float32 [22573056], P(('dp', 'rep'))
- loss: float32 [], replicated
The draws below stay inside these ranges and needn't reach their ends.
Inputs may be any that keep to these rules, and one draw needn't show every extreme that they name: For each device's 1 * 256 tokens, images in order: a masked token has route = d * 32 + s, and the masked tokens of one device have distinct values; a visible token has route = 256. Each image has 179 or more masked tokens and at least one visible one. Some destination gets all 32 slots of a sender. `weights`: parameters in the layout of the first step. `momentum`: momentum of each parameter. `average`: average of each parameter.
All inputs are finite; a program needn't handle non-finite values.
Results may differ from the reference program's by a relative error of at most 0.00075.
The reference program's roundings to bfloat16 on the way count: a program that leaves them out, or rounds other values in their place, can miss the bound.
Values may be sent and summed in bfloat16 or wider, within the bound.
A program may use at most 384 MiB of HBM per device.

```python
import math
import jax
import jax.numpy as jnp
from jax import lax

D = 768
HEADS = 12
HEAD_DIM = 64
MLP = 3072
HW = 1024
TOK_CH = 16
FREQ = 256
CLASSES = 1000
BUF = 64
SEQ = 256
IMG_DEV = 1
COPIES = 4
STEPS_T = 1000
ENC_BLOCKS = 1
DEC_BLOCKS = 1
HEAD_BLOCKS = 1
CAP = 32
IMAGES = 32
TOKENS = 8192
PARAMS = 22572304
FLAT = 22573056
N_DP = 8
N_REP = 4


GAINS = ('norm_one_gain', 'norm_two_gain', 'enc_gain', 'dec_gain', 'head_gain')


SHIFTS = ('norm_one_shift', 'norm_two_shift', 'enc_shift', 'dec_shift', 'head_shift', 'embed_bias', 'attn_bias', 'proj_bias', 'fc_one_bias', 'fc_two_bias', 'dec_bias', 'input_bias', 'time_bias', 'cond_bias', 'ada_bias', 'inner_bias', 'outer_bias', 'final_bias')


MATRICES = ('embed_weight', 'attn_weight', 'fc_one_weight', 'fc_two_weight', 'dec_weight', 'input_weight', 'time_weight', 'cond_weight', 'ada_weight', 'inner_weight', 'outer_weight', 'final_weight')


def block_entries_drawn(prefix, count):
    return [(prefix + 'norm_one_gain', (count, D)), (prefix + 'norm_one_shift', (count, D)), (prefix + 'attn_weight', (count, D, 3 * D)), (prefix + 'attn_bias', (count, 2 * D)), (prefix + 'proj_weight', (count, D, D)), (prefix + 'proj_bias', (count, D)), (prefix + 'norm_two_gain', (count, D)), (prefix + 'norm_two_shift', (count, D)), (prefix + 'fc_one_weight', (count, D, MLP)), (prefix + 'fc_one_bias', (count, MLP)), (prefix + 'fc_two_weight', (count, MLP, D)), (prefix + 'fc_two_bias', (count, D))]


def layout_drawn():
    return [('embed_weight', (TOK_CH, D)), ('embed_bias', (D,)), ('class_table', (CLASSES, D)), ('encoder_pos', (BUF + SEQ, D))] + block_entries_drawn('', ENC_BLOCKS) + [('enc_gain', (D,)), ('enc_shift', (D,)), ('dec_weight', (D, D)), ('dec_bias', (D,)), ('mask_token', (D,)), ('decoder_pos', (BUF + SEQ, D))] + block_entries_drawn('decoder_', DEC_BLOCKS) + [('dec_gain', (D,)), ('dec_shift', (D,)), ('diffusion_pos', (SEQ, D)), ('input_weight', (TOK_CH, HW)), ('input_bias', (HW,)), ('time_weight', (FREQ, HW)), ('time_bias', (HW,)), ('cond_weight', (D, HW)), ('cond_bias', (HW,)), ('head_gain', (HEAD_BLOCKS, HW)), ('head_shift', (HEAD_BLOCKS, HW)), ('ada_weight', (HEAD_BLOCKS, HW, 3 * HW)), ('ada_bias', (HEAD_BLOCKS, 3 * HW)), ('inner_weight', (HEAD_BLOCKS, HW, HW)), ('inner_bias', (HEAD_BLOCKS, HW)), ('outer_weight', (HEAD_BLOCKS, HW, HW)), ('outer_bias', (HEAD_BLOCKS, HW)), ('final_weight', (HW, TOK_CH)), ('final_bias', (TOK_CH,))]


def draw_params(key):
    entries = layout_drawn()
    keys = jax.random.split(key, len(entries) + 1)
    pieces = []
    for position, (name, shape) in enumerate(entries):
        normal = jax.random.normal(keys[position], shape, jnp.float32)
        base = name[8:] if name[:8] == 'decoder_' else name
        if base in GAINS:
            value = 1.0 + 0.1 * normal
        elif base in SHIFTS:
            value = 0.1 * normal
        elif name == 'proj_weight':
            value = normal * math.sqrt((BUF + SEQ // 4) / D)
        elif name == 'decoder_proj_weight':
            value = normal * math.sqrt((BUF + SEQ) / D)
        elif base in MATRICES:
            value = normal / math.sqrt(shape[-2])
        else:
            value = normal
        pieces.append(value.reshape(-1))
    pieces.append(0.02 * jax.random.normal(keys[-1], (FLAT - PARAMS,), jnp.float32))
    return jnp.concatenate(pieces)


def draw_weights(key, part):
    return draw_params(jax.random.fold_in(key, 11))


def draw_average(key, part):
    return draw_params(jax.random.fold_in(key, 22))


def draw_momentum(key, part):
    normal = jax.random.normal(jax.random.fold_in(key, 33), (FLAT,), jnp.float32)
    return normal * (0.2 / math.sqrt(IMAGES * SEQ))


def draw_route(key, part):
    devices = N_DP * N_REP
    rows = IMG_DEV * SEQ
    capacity = rows // N_DP
    least = 7 * SEQ // 10

    def one(device_key, device):
        first, second, third = jax.random.split(device_key, 3)
        counts = jax.random.randint(first, (IMG_DEV,), least, SEQ)
        ranks = jax.vmap(lambda image_key: jax.random.permutation(image_key, SEQ))(jax.random.split(second, IMG_DEV))
        marks = (ranks < counts[:, None]).reshape(rows).astype(jnp.int32)
        order = jnp.cumsum(marks) - marks
        offset = jnp.where(device == 0, 0, jax.random.randint(third, (), 0, N_DP))
        target = (order // capacity + offset) % N_DP * capacity + order % capacity
        return jnp.where(marks == 1, target, rows).astype(jnp.int32)
    keys = jax.random.split(jax.random.fold_in(key, 44), devices)
    return jax.vmap(one)(keys, jnp.arange(devices, dtype=jnp.int32)).reshape(-1)


def plant(drawn, key, low, largest):
    longest = drawn.shape.index(max(drawn.shape))
    spots = []
    for shift in (0, 1):
        where = [jax.random.randint(jax.random.fold_in(key, axis), (), 0, length) for axis, length in enumerate(drawn.shape)]
        where[longest] = (where[longest] + shift) % drawn.shape[longest]
        spots.append(tuple(where))
    return drawn.at[spots[0]].set(low).at[spots[1]].set(largest)


def shard_levels(key, dims, shards, low, high):
    def one(dim, blocks):
        heights = jax.random.uniform(jax.random.fold_in(jax.random.fold_in(key, 6), dim), (blocks,), jnp.float32, low / len(shards), high / len(shards))
        return jnp.repeat(jnp.exp(heights), dims[dim] // blocks).reshape((-1,) + (1,) * (len(dims) - dim - 1))

    loudness = one(*shards[0])
    for cut in shards[1:]:
        loudness = loudness * one(*cut)
    return loudness


def bell_draw(key, extent, spread, most, cuts=(), kind=jnp.bfloat16):
    drawn = spread * jax.random.normal(key, extent, jnp.float32)
    if cuts:
        drawn = drawn * shard_levels(key, extent, cuts, -0.22, 0.18)
    return jnp.clip(drawn, -most, most).astype(kind)


def setup_inputs(seed: int = 0) -> dict:
    seeds = jax.random.split(jax.random.key(seed), 10)
    latents = bell_draw(seeds[0], (TOKENS, TOK_CH), 1.0, 6.0, ((0, 32),))
    route = draw_route(jax.random.fold_in(seeds[9], 71), 0)
    labels = plant(jax.random.randint(seeds[2], (IMAGES,), 0, CLASSES), jax.random.fold_in(seeds[2], 1), 0, CLASSES - 1).astype(jnp.int32)
    timesteps = plant(jax.random.randint(seeds[3], (COPIES, TOKENS), 0, STEPS_T), jax.random.fold_in(seeds[3], 1), 0, STEPS_T - 1).astype(jnp.int32)
    noise = bell_draw(seeds[4], (COPIES, TOKENS, TOK_CH), 1.0, 6.0, ((1, 32),), jnp.float32)
    image_weight = jnp.clip(0.5 + 1.0 * jax.random.uniform(seeds[5], (IMAGES,), jnp.float32) ** shard_levels(seeds[5], (IMAGES,), ((0, 32),), -0.2, 0.2), 0.5, 1.5)
    weights = draw_weights(jax.random.fold_in(seeds[9], 71), 0)
    momentum = draw_momentum(jax.random.fold_in(seeds[9], 71), 0)
    average = draw_average(jax.random.fold_in(seeds[9], 71), 0)
    return {"latents": latents, "route": route, "labels": labels, "timesteps": timesteps, "noise": noise, "image_weight": image_weight, "weights": weights, "momentum": momentum, "average": average}


@jax.custom_vjp
def low(v):
    return lax.optimization_barrier(v.astype(jnp.bfloat16)).astype(jnp.float32)

@jax.custom_vjp
def low_back(v):
    return v

def low_keep(v):
    return (low(v), None)

def low_pass(kept, grad):
    return (grad,)

def back_keep(v):
    return (v, None)

def back_low(kept, grad):
    return (low(grad),)
low.defvjp(low_keep, low_pass)
low_back.defvjp(back_keep, back_low)
HIGH = lax.Precision.HIGHEST
NORM_EPS = 1e-06
ENCODER_NAMES = ('norm_one_gain', 'norm_one_shift', 'attn_weight', 'attn_bias', 'proj_weight', 'proj_bias', 'norm_two_gain', 'norm_two_shift', 'fc_one_weight', 'fc_one_bias', 'fc_two_weight', 'fc_two_bias')
HEAD_NAMES = ('head_gain', 'head_shift', 'ada_weight', 'ada_bias', 'inner_weight', 'inner_bias', 'outer_weight', 'outer_bias')

def block_entries(prefix, count):
    return [(prefix + 'norm_one_gain', (count, D)), (prefix + 'norm_one_shift', (count, D)), (prefix + 'attn_weight', (count, D, 3 * D)), (prefix + 'attn_bias', (count, 2 * D)), (prefix + 'proj_weight', (count, D, D)), (prefix + 'proj_bias', (count, D)), (prefix + 'norm_two_gain', (count, D)), (prefix + 'norm_two_shift', (count, D)), (prefix + 'fc_one_weight', (count, D, MLP)), (prefix + 'fc_one_bias', (count, MLP)), (prefix + 'fc_two_weight', (count, MLP, D)), (prefix + 'fc_two_bias', (count, D))]

def layout():
    return [('embed_weight', (TOK_CH, D)), ('embed_bias', (D,)), ('class_table', (CLASSES, D)), ('encoder_pos', (BUF + SEQ, D))] + block_entries('', ENC_BLOCKS) + [('enc_gain', (D,)), ('enc_shift', (D,)), ('dec_weight', (D, D)), ('dec_bias', (D,)), ('mask_token', (D,)), ('decoder_pos', (BUF + SEQ, D))] + block_entries('decoder_', DEC_BLOCKS) + [('dec_gain', (D,)), ('dec_shift', (D,)), ('diffusion_pos', (SEQ, D)), ('input_weight', (TOK_CH, HW)), ('input_bias', (HW,)), ('time_weight', (FREQ, HW)), ('time_bias', (HW,)), ('cond_weight', (D, HW)), ('cond_bias', (HW,)), ('head_gain', (HEAD_BLOCKS, HW)), ('head_shift', (HEAD_BLOCKS, HW)), ('ada_weight', (HEAD_BLOCKS, HW, 3 * HW)), ('ada_bias', (HEAD_BLOCKS, 3 * HW)), ('inner_weight', (HEAD_BLOCKS, HW, HW)), ('inner_bias', (HEAD_BLOCKS, HW)), ('outer_weight', (HEAD_BLOCKS, HW, HW)), ('outer_bias', (HEAD_BLOCKS, HW)), ('final_weight', (HW, TOK_CH)), ('final_bias', (TOK_CH,))]

def unpack(flat):
    result = {}
    offset = 0
    for name, shape in layout():
        number = math.prod(shape)
        result[name] = flat[offset:offset + number].reshape(shape)
        offset += number
    return result

def layer_norm(value, gain, shift):
    centered = value - lax.optimization_barrier(jnp.mean(value, -1, keepdims=True))
    scaled = centered * lax.rsqrt(lax.optimization_barrier(jnp.mean(centered * centered, -1, keepdims=True)) + NORM_EPS)
    return scaled * gain + shift

def matmul(left, right):
    return jnp.einsum('...i,ij->...j', left, right, precision=HIGH)

def encoder_block(stream, keep, params):
    length = stream.shape[0]
    normed = low(layer_norm(stream, params['norm_one_gain'], params['norm_one_shift']))
    bias = jnp.concatenate([params['attn_bias'][:D], jnp.zeros((D,), jnp.float32), params['attn_bias'][D:]])
    mixed = low(low_back(matmul(normed, params['attn_weight'])) + bias)
    queries = mixed[:, :D].reshape(length, HEADS, HEAD_DIM)
    keys = mixed[:, D:2 * D].reshape(length, HEADS, HEAD_DIM)
    values = mixed[:, 2 * D:].reshape(length, HEADS, HEAD_DIM)
    scores = low_back(jnp.einsum('qhe,khe->hqk', queries, keys, precision=HIGH) * HEAD_DIM ** (-0.5))
    scores = jnp.where(keep[None, None, :], scores, -1e+30)
    probs = low(jax.nn.softmax(scores, axis=-1))
    attended = jnp.einsum('hqk,khe->qhe', probs, values, precision=HIGH).reshape(length, D)
    attended = low(low_back(attended))
    middle = stream + low_back(matmul(attended, params['proj_weight'])) + params['proj_bias']
    second = low(layer_norm(middle, params['norm_two_gain'], params['norm_two_shift']))
    inner = low_back(matmul(second, params['fc_one_weight'])) + params['fc_one_bias']
    active = low(jax.nn.gelu(inner, approximate=False))
    return middle + low_back(matmul(active, params['fc_two_weight'])) + params['fc_two_bias']

def encode(params, latent, visible, label):
    tokens = low_back(matmul(latent, params['embed_weight'])) + params['embed_bias']
    buffer_rows = jnp.broadcast_to(params['class_table'][label], (BUF, D))
    stream = jnp.concatenate([buffer_rows, tokens], 0) + params['encoder_pos']
    keep = jnp.concatenate([jnp.ones((BUF,), bool), visible])
    for layer in range(ENC_BLOCKS):
        stream = encoder_block(stream, keep, {name: params[name][layer] for name in ENCODER_NAMES})
    encoded = low(layer_norm(stream, params['enc_gain'], params['enc_shift']))
    decoded = low_back(matmul(encoded, params['dec_weight'])) + params['dec_bias']
    decoded = jnp.where(keep[:, None], decoded, params['mask_token'])
    flow = decoded + params['decoder_pos']
    every = jnp.ones((BUF + SEQ,), bool)
    for layer in range(DEC_BLOCKS):
        flow = encoder_block(flow, every, {name: params['decoder_' + name][layer] for name in ENCODER_NAMES})
    after = layer_norm(flow, params['dec_gain'], params['dec_shift'])
    return low(low_back(after[BUF:] + params['diffusion_pos']))

def time_features(times):
    half = FREQ // 2
    freqs = jnp.exp(-math.log(10000.0) * jnp.arange(half, dtype=jnp.float32) / half)
    angles = times[..., None] * freqs
    return jnp.concatenate([jnp.cos(angles), jnp.sin(angles)], -1)

def alpha_level(times):
    start = math.cos(0.008 / 1.008 * math.pi / 2) ** 2
    return jnp.cos(((times + 1.0) / STEPS_T + 0.008) / 1.008 * math.pi / 2) ** 2 / start

def head(params, conditions, clean, noise, steps, filled):
    cond = low_back(matmul(conditions, params['cond_weight'])) + params['cond_bias']
    times = steps.astype(jnp.float32)
    features = low(time_features(times))
    temporal = low_back(matmul(features, params['time_weight'])) + params['time_bias']
    level = alpha_level(times)[..., None]
    noisy = low(jnp.sqrt(level) * clean + jnp.sqrt(1.0 - level) * noise)
    hidden = low_back(matmul(noisy, params['input_weight'])) + params['input_bias']
    signal = low(jax.nn.silu(temporal + cond[None]))
    for block in range(HEAD_BLOCKS):
        own = {name: params[name][block] for name in HEAD_NAMES}
        modulation = low_back(matmul(signal, own['ada_weight'])) + own['ada_bias']
        shift, scale, gate = (modulation[..., :HW], modulation[..., HW:2 * HW], modulation[..., 2 * HW:])
        modulated = low(layer_norm(hidden, own['head_gain'], own['head_shift']) * (1.0 + scale) + shift)
        active = low(jax.nn.silu(low_back(matmul(modulated, own['inner_weight'])) + own['inner_bias']))
        hidden = hidden + gate * (low_back(matmul(active, own['outer_weight'])) + own['outer_bias'])
    final = low(layer_norm(hidden, 1.0, 0.0))
    predicted = low_back(matmul(final, params['final_weight'])) + params['final_bias']
    error = predicted - noise
    return jnp.sum(lax.optimization_barrier(jnp.sum(error * error, -1)) * filled)

def reference(latents, route, labels, timesteps, noise, image_weight, weights, momentum, average):
    per_device = IMG_DEV * SEQ
    index = jnp.arange(TOKENS, dtype=jnp.int32)
    device = index // per_device
    masked = route < per_device
    count = jnp.sum(masked.astype(jnp.float32))
    target = (route // CAP * N_REP + device % N_REP) * per_device + device // N_REP * CAP + route % CAP
    target = jnp.where(masked, target, TOKENS).astype(jnp.int32)
    clean_tokens = latents.astype(jnp.float32)
    token_weight = low(jnp.repeat(image_weight, SEQ))
    filled = jnp.zeros((TOKENS,), jnp.float32).at[target].set(token_weight, mode='drop')
    clean = jnp.zeros((TOKENS, TOK_CH), jnp.float32).at[target].set(clean_tokens, mode='drop')
    block_rows = 1024 if TOKENS % 1024 == 0 else TOKENS
    blocks = TOKENS // block_rows
    encode_saved = jax.checkpoint(encode)
    head_saved = jax.checkpoint(head)

    def loss_of(flat):
        params = unpack(low(flat))
        conditions = lax.map(lambda item: encode_saved(params, *item), (clean_tokens.reshape(IMAGES, SEQ, TOK_CH), (~masked).reshape(IMAGES, SEQ), labels))
        slots = jnp.zeros((TOKENS, D), jnp.float32).at[target].set(conditions.reshape(TOKENS, D), mode='drop')
        parts = lax.map(lambda item: head_saved(params, *item), (slots.reshape(blocks, block_rows, D), clean.reshape(blocks, block_rows, TOK_CH), noise.reshape(COPIES, blocks, block_rows, TOK_CH).swapaxes(0, 1), timesteps.reshape(COPIES, blocks, block_rows).swapaxes(0, 1), filled.reshape(blocks, block_rows)))
        return jnp.sum(parts) / (TOK_CH * COPIES * count)
    loss, pull = jax.vjp(loss_of, weights)
    grad = pull(jnp.ones_like(loss))[0]
    rate = 0.05 * math.sqrt(IMAGES * SEQ)
    new_momentum = 0.9 * momentum + grad
    new_weights = weights - rate * (grad + 0.9 * new_momentum)
    new_average = 0.75 * average + 0.25 * new_weights
    return (new_weights, new_momentum, new_average, loss)
```

```python
import functools
import heapq
import math
import types

import jax
import jax.numpy as jnp
from jax import lax
from jax.experimental import pallas as pl
from jax.experimental.pallas import tpu as pltpu
from jax.sharding import PartitionSpec as P

D = 768
HEADS = 12
HEAD_DIM = 64
MLP = 3072
HW = 1024
TOK_CH = 16
FREQ = 256
CLASSES = 1000
BUF = 64
SEQ = 256
COPIES = 4
STEPS_T = 1000
LANES = 128
WIDE = jnp.float32
NARROW = jnp.bfloat16
NORM_EPS = 1e-06
MESH = pl.DeviceIdType.MESH
ANY = pl.BlockSpec(memory_space=pl.ANY)
DMA = pltpu.SemaphoreType.DMA
BOTH = ("dp", "rep")


def block_shapes():
    return dict(
        norm_one_gain=(D,), norm_one_shift=(D,), attn_weight=(D, 3 * D), attn_bias=(2 * D,),
        proj_weight=(D, D), proj_bias=(D,), norm_two_gain=(D,), norm_two_shift=(D,),
        fc_one_weight=(D, MLP), fc_one_bias=(MLP,), fc_two_weight=(MLP, D), fc_two_bias=(D,),
    )


ENC, DEC = 1, 3
GROUPS = (
    dict(embed_weight=(TOK_CH, D), embed_bias=(D,), class_table=(CLASSES, D), encoder_pos=(BUF + SEQ, D)),
    block_shapes(),
    dict(enc_gain=(D,), enc_shift=(D,), dec_weight=(D, D), dec_bias=(D,), mask_token=(D,), decoder_pos=(BUF + SEQ, D)),
    block_shapes(),
    dict(
        dec_gain=(D,), dec_shift=(D,), diffusion_pos=(SEQ, D), input_weight=(TOK_CH, HW), input_bias=(HW,),
        time_weight=(FREQ, HW), time_bias=(HW,), cond_weight=(D, HW), cond_bias=(HW,), head_gain=(HW,),
        head_shift=(HW,), ada_weight=(HW, 3 * HW), ada_bias=(3 * HW,), inner_weight=(HW, HW), inner_bias=(HW,),
        outer_weight=(HW, HW), outer_bias=(HW,), final_weight=(HW, TOK_CH), final_bias=(TOK_CH,),
    ),
)


class Entry:
    def __init__(self, group, name, shape, start):
        self.group, self.name, self.shape, self.start = group, name, shape, start
        self.rows = -(-math.prod(shape) // LANES)
        self.matrix = len(shape) == 2 and shape[1] % LANES == 0
        self.across = shape[1] // LANES if self.matrix else 1
        self.sparse = name == GROUP_SPARSE


GROUP_SPARSE = next(name for name, shape in GROUPS[0].items() if shape[0] == CLASSES)


def entries():
    found, start = [], 0
    for group, shapes in enumerate(GROUPS):
        for name, shape in shapes.items():
            found.append(Entry(group, name, shape, start))
            start += found[-1].rows
    return found


ENTRIES = entries()
USED = ENTRIES[-1].start + ENTRIES[-1].rows


def block_height(entry, limit):
    best = 0
    for height in range(8, entry.shape[0] + 1, 8):
        if entry.shape[0] % height == 0 and height * entry.across <= limit:
            best = height
    return best


SLOTS = 4


def unfold_kernel(rows, padded, items, g_ref, *refs):
    count = len(items)
    outs = refs[:count]
    first, second, wide, first_sem, second_sem, out_sem = refs[count : count + 6]
    stages = dict(zip(sorted({(h, e.across) for e, h in items}), refs[count + 6 :]))
    place = 0
    for t, (entry, height) in enumerate(items):
        span = height * entry.across
        window = span + 8
        blocks = entry.shape[0] // height
        stage = stages[(height, entry.across)]

        def spot(b, entry=entry, span=span, window=window):
            start = entry.start + b * span
            dev = start // rows
            row = start - dev * rows
            low = jnp.minimum(row // 8 * 8, padded - window)
            return dev, row, low, row + span > rows

        def copies(b, spot=spot, window=window):
            dev, row, low, more = spot(b)
            slot = b % SLOTS
            one = pltpu.make_async_copy(
                g_ref.at[dev, pl.ds(pl.multiple_of(low, 8), window)], first.at[slot, pl.ds(0, window)], first_sem.at[slot]
            )
            two = pltpu.make_async_copy(
                g_ref.at[jnp.minimum(dev + 1, g_ref.shape[0] - 1), pl.ds(0, window)],
                second.at[slot, pl.ds(0, window)], second_sem.at[slot],
            )
            return one, two, more

        def fetch(b, copies=copies):
            one, two, more = copies(b)
            one.start()

            @pl.when(more)
            def _():
                two.start()

        def put(b, t=t, stage=stage, height=height):
            return pltpu.make_async_copy(
                stage.at[b % 2], outs[t].at[pl.ds(pl.multiple_of(b * height, 8), height)], out_sem.at[b % 2]
            )

        for b in range(min(SLOTS - 1, blocks)):
            fetch(b)

        def body(b, carry, entry=entry, height=height, span=span, window=window, blocks=blocks, stage=stage,
                 spot=spot, copies=copies, fetch=fetch, put=put):
            @pl.when(b + SLOTS - 1 < blocks)
            def _():
                fetch(b + SLOTS - 1)

            dev, row, low, _ = spot(b)
            slot = b % SLOTS
            one, two, more = copies(b)
            one.wait()
            wide[pl.ds(0, window), :] = first[slot, pl.ds(0, window), :].astype(WIDE)

            @pl.when(more)
            def _():
                two.wait()
                wide[pl.ds(rows - low, window), :] = second[slot, pl.ds(0, window), :].astype(WIDE)

            @pl.when(b >= 2)
            def _():
                put(b - 2).wait()

            off = row - low
            for j in range(entry.across):
                stage[b % 2, :, j * LANES : (j + 1) * LANES] = wide[pl.ds(off + j, height, stride=entry.across), :].astype(NARROW)
            put(b).start()
            return carry

        lax.fori_loop(0, blocks, body, 0)
        for b in range(max(0, blocks - 2), blocks):
            put(b).wait()


def unfold(gathered, rows):
    padded = gathered.shape[1]
    items = [(e, block_height(e, min(2304, rows - 16))) for e in ENTRIES if e.matrix and not e.sparse]
    tall = max(e.across * h for e, h in items) + 8
    kinds = sorted({(h, e.across) for e, h in items})
    total = sum(math.prod(e.shape) for e, _ in items)
    outs = pl.pallas_call(
        functools.partial(unfold_kernel, rows, padded, items),
        out_shape=[jax.ShapeDtypeStruct(e.shape, NARROW) for e, _ in items],
        in_specs=[ANY],
        out_specs=[ANY] * len(items),
        scratch_shapes=[
            pltpu.VMEM((SLOTS, tall, LANES), NARROW), pltpu.VMEM((SLOTS, tall, LANES), NARROW),
            pltpu.VMEM((2 * tall, LANES), WIDE), DMA((SLOTS,)), DMA((SLOTS,)), DMA((2,)),
        ]
        + [pltpu.VMEM((2, h, n * LANES), NARROW) for h, n in kinds],
        compiler_params=pltpu.CompilerParams(vmem_limit_bytes=48 * 1000 * 1000),
        cost_estimate=pl.CostEstimate(flops=total, bytes_accessed=4 * total, transcendentals=0),
    )(gathered)
    return {(e.group, e.name): out for (e, _), out in zip(items, outs)}


def rows_at(gathered, rows, start, number):
    pieces = []
    while number > 0:
        dev, row = divmod(start, rows)
        take = min(number, rows - row)
        pieces.append(gathered[dev, row : row + take])
        start, number = start + take, number - take
    return pieces[0] if len(pieces) == 1 else jnp.concatenate(pieces, 0)


def unpack(gathered, rows):
    matrices = unfold(gathered, rows)
    groups = [types.SimpleNamespace() for _ in GROUPS]
    for e in ENTRIES:
        if e.sparse:
            continue
        if e.matrix:
            value = matrices[(e.group, e.name)]
        else:
            value = rows_at(gathered, rows, e.start, e.rows).reshape(-1)[: math.prod(e.shape)].reshape(e.shape)
        setattr(groups[e.group], e.name, value)
    return groups


DEPTH = 3


def fold_kernel(items, plain, *refs):
    count = len(items) + len(plain)
    ins, full = refs[:count], refs[count]
    plain_sem, in_sem, out_sem = refs[count + 1 : count + 4]
    kinds = sorted({(h, e.across) for e, h in items})
    loads = dict(zip(kinds, refs[count + 4 : count + 4 + len(kinds)]))
    stage = refs[count + 4 + len(kinds)]
    moves = []
    for i, (start, number) in enumerate(plain):
        move = pltpu.make_async_copy(ins[len(items) + i].at[pl.ds(0, number)], full.at[pl.ds(start, number)], plain_sem.at[i])
        move.start()
        moves.append(move)
    for t, (entry, height) in enumerate(items):
        span = height * entry.across
        blocks = entry.shape[0] // height
        load = loads[(height, entry.across)]

        def get(b, t=t, load=load, height=height):
            return pltpu.make_async_copy(
                ins[t].at[pl.ds(pl.multiple_of(b * height, 8), height)], load.at[b % DEPTH], in_sem.at[b % DEPTH]
            )

        def put(b, entry=entry, span=span):
            return pltpu.make_async_copy(
                stage.at[b % DEPTH, pl.ds(0, span)], full.at[pl.ds(entry.start + b * span, span)], out_sem.at[b % DEPTH]
            )

        for b in range(min(DEPTH - 1, blocks)):
            get(b).start()

        def body(b, carry, entry=entry, height=height, blocks=blocks, load=load, get=get, put=put):
            @pl.when(b + DEPTH - 1 < blocks)
            def _():
                get(b + DEPTH - 1).start()

            get(b).wait()

            @pl.when(b >= DEPTH)
            def _():
                put(b - DEPTH).wait()

            slot = b % DEPTH
            for j in range(entry.across):
                stage[slot, pl.ds(j, height, stride=entry.across), :] = load[slot, :, j * LANES : (j + 1) * LANES]
            put(b).start()
            return carry

        lax.fori_loop(0, blocks, body, 0)
        for b in range(max(0, blocks - DEPTH), blocks):
            put(b).wait()
    for move in moves:
        move.wait()


def fold(grads, height_total):
    items = [(e, block_height(e, 2304)) for e in ENTRIES if e.matrix]
    matrices = [grads[(e.group, e.name)] for e, _ in items]
    plain, values = [], []
    for e in ENTRIES:
        if e.matrix:
            continue
        value = grads[(e.group, e.name)].reshape(-1)
        value = jnp.pad(value, (0, e.rows * LANES - value.shape[0]))
        plain.append((e.start, e.rows))
        values.append(value.reshape(e.rows, LANES))
    if height_total > USED:
        plain.append((USED, height_total - USED))
        values.append(jnp.zeros((height_total - USED, LANES), WIDE))
    kinds = sorted({(h, e.across) for e, h in items})
    tall = max(e.across * h for e, h in items)
    total = height_total * LANES
    return pl.pallas_call(
        functools.partial(fold_kernel, items, plain),
        out_shape=jax.ShapeDtypeStruct((height_total, LANES), WIDE),
        in_specs=[ANY] * (len(items) + len(plain)),
        out_specs=ANY,
        scratch_shapes=[DMA((len(plain),)), DMA((DEPTH,)), DMA((DEPTH,))]
        + [pltpu.VMEM((DEPTH, h, n * LANES), WIDE) for h, n in kinds]
        + [pltpu.VMEM((DEPTH, tall, LANES), WIDE)],
        compiler_params=pltpu.CompilerParams(vmem_limit_bytes=48 * 1000 * 1000),
        cost_estimate=pl.CostEstimate(flops=total, bytes_accessed=8 * total, transcendentals=0),
    )(*matrices, *values)


X, Y, Z = 0, 1, 2
TREES = ((Z, X, Y), (Z, Y, X), (X, Z, Y), (X, Z, Y), (Y, Z, X), (Y, Z, X))
SHARES = len(TREES)
FAR = 3


def onward(order, arrived, way, p):
    z, x, y = p
    found = []
    if arrived >= 0 and order[arrived] == Z and 0 <= z + way <= FAR:
        found.append(((z + way, x, y), arrived, way))
    for j in range(arrived + 1, 3):
        if order[j] == X:
            found.append(((z, 1 - x, y), j, 0))
        elif order[j] == Y:
            found.append(((z, x, 1 - y), j, 0))
        else:
            found += [((z + s, x, y), j, s) for s in (1, -1) if 0 <= z + s <= FAR]
    return found


@functools.cache
def flow(lag=0.4):
    chips = [(z, x, y) for z in range(FAR + 1) for x in range(2) for y in range(2)]
    events, queues, busy, come, sent = [], {}, set(), {}, []
    number = iter(range(10**9))
    for u in range(SHARES):
        for p in chips:
            heapq.heappush(events, (0.0, next(number), 0, (p, p, u, -1, 0)))

    def pump(link, t):
        if link in busy or not queues.get(link):
            return
        what = heapq.heappop(queues[link])[2]
        busy.add(link)
        sent.append((t, link, what[1], what[2]))
        heapq.heappush(events, (t + 1.0, next(number), 1, (link, what)))

    while events:
        t, _, kind, what = heapq.heappop(events)
        if kind == 1:
            link, piece = what
            busy.discard(link)
            heapq.heappush(events, (t + lag, next(number), 0, piece))
            pump(link, t)
            continue
        p, q, u, k, way = what
        come[(u, p, q)] = t
        for to, k2, way2 in onward(TREES[u], k, way, p):
            left = len(onward(TREES[u], k2, way2, to))
            heapq.heappush(queues.setdefault((p, to), []), ((-left, t), next(number), (to, q, u, k2, way2)))
            pump((p, to), t)
    return come, sent


def spread_order():
    keyed = {}
    for (u, p, q), t in flow()[0].items():
        keyed.setdefault((u, q[0] - p[0], (q[1] - p[1]) % 2, (q[2] - p[2]) % 2), []).append(t)
    return sorted(keyed, key=lambda k: (sum(keyed[k]) / len(keyed[k]), k))


def last_hop(u, dz, dx, dy):
    apart = [k for k in range(3) if (dx, dy, dz)[TREES[u][k]] != 0]
    return apart[-1] if apart else -1


def hops(u, dz, dx, dy):
    order, arrived = TREES[u], last_hop(u, dz, dx, dy)
    found = []
    if arrived >= 0 and order[arrived] == Z:
        found.append((1, 0, 0) if dz < 0 else (-1, 0, 0))
    for k in range(arrived + 1, 3):
        found += [[(0, 1, 0)], [(0, 0, 1)], [(1, 0, 0), (-1, 0, 0)]][order[k]]
    return found


def only(condition, action):
    if condition is None:
        action()
    else:
        pl.when(condition)(action)


def spread_kernel(own, out, keep_sem, send_sem, link_sem, core_send, core_sem):
    dp, rep = lax.axis_index("dp"), lax.axis_index("rep")
    z, x, y, c = dp // 2, dp % 2, rep // 2, rep % 2
    unit = own.shape[0] // SHARES
    sibling = (dp, y * 2 + 1 - c)

    def device(dz, dx, dy):
        return ((z + dz) * 2 + (x + dx) % 2, (y + dy) % 2 * 2 + c)

    def exists(dz):
        return None if dz == 0 else (z + dz >= 0 if dz < 0 else z + dz <= FAR)

    barrier = pltpu.get_barrier_semaphore()
    near = ((0, 1, 0), (0, 0, 1), (1, 0, 0), (-1, 0, 0))
    for hop in near:
        only(exists(hop[0]), lambda: pl.semaphore_signal(barrier, inc=1, device_id=device(*hop), device_id_type=MESH))
    pl.semaphore_signal(barrier, inc=1, device_id=sibling, device_id_type=MESH)
    inner = z * (FAR - z)
    only(inner == 0, lambda: pl.semaphore_wait(barrier, len(near)))
    only(inner > 0, lambda: pl.semaphore_wait(barrier, len(near) + 1))
    keep = pltpu.make_async_copy(own, out.at[dp * 4 + rep], keep_sem)
    keep.start()
    ends, number = [], 0
    for u, dz, dx, dy in spread_order():
        part = pl.ds(u * unit, unit)
        q = ((z + dz) * 2 + (x + dx) % 2) * 2 + (y + dy) % 2
        mine = dz == 0 and dx == 0 and dy == 0
        i = u * 16 + q

        def copy(to, send, come, part=part, q=q, mine=mine):
            here = out.at[q * 2 + c, part]
            return pltpu.make_async_remote_copy(
                own.at[part] if mine else here, here, send, come, device_id=to, device_id_type=MESH
            )

        goes = [(hop, number + k) for k, hop in enumerate(hops(u, dz, dx, dy))]
        number += len(goes)

        def run(i=i, copy=copy, goes=goes, mine=mine):
            if not mine:
                copy(sibling, send_sem.at[0], link_sem.at[i]).wait_recv()
            for hop, n in goes:
                only(exists(hop[0]), lambda: copy(device(*hop), send_sem.at[n], link_sem.at[i]).start())
            copy(sibling, core_send.at[i], core_sem.at[i]).start()

        def finish(i=i, copy=copy, goes=goes):
            for hop, n in goes:
                only(exists(hop[0]), lambda: copy(device(*hop), send_sem.at[n], link_sem.at[i]).wait_send())
            copy(sibling, core_send.at[i], core_sem.at[i]).wait()

        there = None if dz == 0 else jnp.logical_and(z + dz >= 0, z + dz <= FAR)
        only(there, run)
        ends.append((there, finish))
    for there, finish in ends:
        only(there, finish)
    keep.wait()


def spread(own):
    pieces = SHARES * 16
    sends = sum(len(hops(*key)) for key in spread_order())
    return pl.pallas_call(
        spread_kernel,
        out_shape=jax.ShapeDtypeStruct((32,) + own.shape, own.dtype),
        in_specs=[ANY],
        out_specs=ANY,
        scratch_shapes=[DMA, DMA((sends,)), DMA((pieces,)), DMA((pieces,)), DMA((pieces,))],
        compiler_params=pltpu.CompilerParams(collective_id=0, has_side_effects=True),
    )(own)


class Chip:
    def __init__(self, low):
        dp, rep = lax.axis_index("dp"), lax.axis_index("rep")
        self.low = low
        self.z, self.x, self.y, self.c = dp // 2, dp % 2, rep // 2, rep % 2
        self.way = 1 - 2 * (self.z // 2)

    def device(self, q, other=0):
        z = self.z + self.way * (q[0] - self.low)
        return z * 2 + (self.x + q[1]) % 2, (self.y + q[2]) % 2 * 2 + (self.c + other) % 2

    def block(self, q, other=0):
        dp, rep = self.device(q, other)
        return dp * 4 + rep

    def greet(self):
        low = self.low
        near = [(low, 1, 0), (low, 0, 1), (low + 1, 0, 0)] + ([(low - 1, 0, 0)] if low else [])
        barrier = pltpu.get_barrier_semaphore()
        for q in near:
            pl.semaphore_signal(barrier, inc=1, device_id=self.device(q), device_id_type=MESH)
        pl.semaphore_signal(barrier, inc=1, device_id=self.device((low, 0, 0), 1), device_id_type=MESH)
        pl.semaphore_wait(barrier, len(near) + 1)


def seen_from(p, r):
    low, way = min(p[0], FAR - p[0]), 1 if p[0] < 2 else -1
    return low + way * (r[0] - p[0]), (r[1] - p[1]) % 2, (r[2] - p[2]) % 2


@functools.cache
def sum_programs():
    come, sent = flow()
    last = max(come.values())
    found = []
    for z in (0, 1):
        p = (z, 0, 0)
        kids, parent, when = {}, {}, {}
        for t, link, q, u in sent:
            if link[0] == p:
                kids.setdefault((u, q), []).append(link[1])
                if q == p:
                    when[(u, p)] = max(when.get((u, p), 0.0), last - t)
            if link[1] == p:
                parent[(u, q)] = link[0]
                when[(u, q)] = last - t - 1.0
        tasks = sorted(when, key=lambda k: (when[k], k))
        found.append([(u, q, sorted(kids.get((u, q), [])), parent.get((u, q))) for u, q in tasks])
    return found


@functools.cache
def landing():
    return [{key: i for i, key in enumerate((u, q, k) for u, q, kids, _ in tasks for k in kids)} for tasks in sum_programs()]


RING = 12
SIDE = 4
EARLY = 12
STEP = 40


def add_rows(into, terms):
    def body(i, carry):
        at = pl.ds(pl.multiple_of(i * STEP, 8), STEP)
        total = into[at, :]
        for term in terms:
            total = total + term[at, :]
        into[at, :] = total
        return carry

    lax.fori_loop(0, into.shape[0] // STEP, body, 0)


def collect_at(low, size, full, out, aside, store, ring, side, ring_sem, side_sem, send_sem, link_sem, core_send, core_sem, out_sem):
    chip = Chip(low)
    me = (low, 0, 0)
    tasks, spots = sum_programs()[low], landing()
    count, unit = len(tasks), ring.shape[1]
    chip.greet()

    def part(i, other=0):
        return full.at[pl.ds(chip.block(tasks[i][1], other) * size + tasks[i][0] * unit, unit)]

    def across(i):
        return pltpu.make_async_remote_copy(
            part(i, 1), aside.at[i], core_send.at[i], core_sem.at[i], device_id=chip.device(me, 1), device_id_type=MESH
        )

    def ours(i):
        return pltpu.make_async_copy(part(i), ring.at[i % RING], ring_sem.at[i % RING])

    def theirs(i):
        return pltpu.make_async_copy(aside.at[i], side.at[i % SIDE], side_sem.at[i % SIDE])

    def along(i, spot, to):
        return pltpu.make_async_remote_copy(
            ring.at[i % RING], store.at[spot], send_sem.at[i], link_sem.at[spot], device_id=chip.device(to), device_id_type=MESH
        )

    leaving = {}

    def fetch(i):
        if i - RING in leaving:
            leaving.pop(i - RING)()
        ours(i).start()
        across(i).wait_recv()
        theirs(i).start()

    for i in range(EARLY):
        across(i).start()
    for i in range(SIDE - 1):
        fetch(i)
    for i, (u, q, kids, to) in enumerate(tasks):
        if i + EARLY < count:
            across(i + EARLY).start()
        if i + SIDE - 1 < count:
            fetch(i + SIDE - 1)
        ours(i).wait()
        theirs(i).wait()
        terms = [side.at[i % SIDE]]
        for kid in kids:
            spot = spots[low][(u, q, kid)]
            along(i, spot, kid).wait_recv()
            terms.append(store.at[spot])
        add_rows(ring.at[i % RING], terms)
        if to is None:
            move = pltpu.make_async_copy(ring.at[i % RING], out.at[pl.ds(u * unit, unit)], out_sem.at[u])
            move.start()
            leaving[i] = move.wait
        else:
            move = along(i, spots[min(to[0], FAR - to[0])][(u, seen_from(to, q), seen_from(to, me))], to)
            move.start()
            leaving[i] = move.wait_send
    for i in list(leaving):
        leaving.pop(i)()
    for i in range(count):
        across(i).wait_send()


def collect_kernel(size, *refs):
    z = lax.axis_index("dp") // 2
    inner = z * (FAR - z)

    @pl.when(inner == 0)
    def _():
        collect_at(0, size, *refs)

    @pl.when(inner > 0)
    def _():
        collect_at(1, size, *refs)


def collect(full, size, rows):
    slots = max(len(spots) for spots in landing())
    count, unit = len(sum_programs()[0]), rows // SHARES
    return pl.pallas_call(
        functools.partial(collect_kernel, size),
        out_shape=(jax.ShapeDtypeStruct((rows, LANES), WIDE), jax.ShapeDtypeStruct((count, unit, LANES), WIDE)),
        in_specs=[ANY],
        out_specs=(ANY, ANY),
        scratch_shapes=[
            pltpu.VMEM((slots, unit, LANES), WIDE), pltpu.VMEM((RING, unit, LANES), WIDE), pltpu.VMEM((SIDE, unit, LANES), WIDE),
            DMA((RING,)), DMA((SIDE,)), DMA((count,)), DMA((slots,)), DMA((count,)), DMA((count,)), DMA((SHARES,)),
        ],
        compiler_params=pltpu.CompilerParams(collective_id=1, has_side_effects=True, vmem_limit_bytes=62 * 1000 * 1000),
    )(full)[0]


def layer_norm(value, gain, shift):
    centered = value - jnp.mean(value, -1, keepdims=True)
    scaled = centered * lax.rsqrt(jnp.mean(centered * centered, -1, keepdims=True) + NORM_EPS)
    return scaled * gain + shift


def dense(inputs, weight):
    return lax.dot_general(inputs, weight, (((inputs.ndim - 1,), (0,)), ((), ())), preferred_element_type=WIDE)


def back_input(grads_low, weight):
    return lax.dot_general(grads_low, weight, (((grads_low.ndim - 1,), (1,)), ((), ())), preferred_element_type=WIDE)


def weight_grad(inputs, grads_low):
    flat_in = inputs.reshape(-1, inputs.shape[-1])
    flat_grad = grads_low.reshape(-1, grads_low.shape[-1])
    return lax.dot_general(flat_in, flat_grad, (((0,), (0,)), ((), ())), preferred_element_type=WIDE)


def rows_sum(values):
    return jnp.sum(values.reshape(-1, values.shape[-1]), 0)


def norm_pull(value, gain, shift):
    return jax.vjp(layer_norm, value, gain.astype(WIDE), shift.astype(WIDE))[1]


def split_heads(mixed):
    return [mixed[:, part * D : (part + 1) * D].reshape(-1, HEADS, HEAD_DIM) for part in range(3)]


def masked_scores(queries, keys, keep):
    scores = jnp.einsum("qhe,khe->hqk", queries, keys, preferred_element_type=WIDE) * HEAD_DIM ** (-0.5)
    return scores if keep is None else jnp.where(keep[None, None, :], scores, -1e30)


def block_forward(stream, keep, p):
    normed = layer_norm(stream, p.norm_one_gain.astype(WIDE), p.norm_one_shift.astype(WIDE)).astype(NARROW)
    bias = jnp.concatenate([p.attn_bias[:D].astype(WIDE), jnp.zeros((D,), WIDE), p.attn_bias[D:].astype(WIDE)])
    mixed = (dense(normed, p.attn_weight) + bias).astype(NARROW)
    queries, keys, values = split_heads(mixed)
    scores = masked_scores(queries, keys, keep)
    totals = jax.nn.logsumexp(scores, axis=-1)
    probs = jnp.exp(scores - totals[..., None]).astype(NARROW)
    attended = jnp.einsum("hqk,khe->qhe", probs, values, preferred_element_type=WIDE)
    attended = attended.reshape(-1, D).astype(NARROW)
    middle = stream + dense(attended, p.proj_weight) + p.proj_bias.astype(WIDE)
    second = layer_norm(middle, p.norm_two_gain.astype(WIDE), p.norm_two_shift.astype(WIDE)).astype(NARROW)
    inner = dense(second, p.fc_one_weight) + p.fc_one_bias.astype(WIDE)
    active = jax.nn.gelu(inner, approximate=False).astype(NARROW)
    output = middle + dense(active, p.fc_two_weight) + p.fc_two_bias.astype(WIDE)
    return output, (stream, normed, mixed, totals, attended, middle, second, inner, active)


def block_backward(grad_out, keep, p, saved):
    stream, normed, mixed, totals, attended, middle, second, inner, active = saved
    grads = {}
    out_low = grad_out.astype(NARROW)
    fc_two_weight = weight_grad(active, out_low)
    fc_two_bias = rows_sum(grad_out)
    gelu_pull = jax.vjp(lambda value: jax.nn.gelu(value, approximate=False), inner)[1]
    inner_grad = gelu_pull(back_input(out_low, p.fc_two_weight))[0]
    inner_low = inner_grad.astype(NARROW)
    fc_one_weight = weight_grad(second, inner_low)
    fc_one_bias = rows_sum(inner_grad)
    pull = norm_pull(middle, p.norm_two_gain, p.norm_two_shift)
    middle_grad, norm_two_gain, norm_two_shift = pull(back_input(inner_low, p.fc_one_weight))
    middle_grad = middle_grad + grad_out
    middle_low = middle_grad.astype(NARROW)
    proj_weight = weight_grad(attended, middle_low)
    proj_bias = rows_sum(middle_grad)
    attended_grad = back_input(middle_low, p.proj_weight).astype(NARROW).reshape(-1, HEADS, HEAD_DIM)
    queries, keys, values = split_heads(mixed)
    probs = jnp.exp(masked_scores(queries, keys, keep) - totals[..., None])
    values_grad = jnp.einsum("hqk,qhe->khe", probs.astype(NARROW), attended_grad, preferred_element_type=WIDE)
    prob_grad = jnp.einsum("qhe,khe->hqk", attended_grad, values, preferred_element_type=WIDE)
    score_grad = (probs * (prob_grad - jnp.sum(probs * prob_grad, -1, keepdims=True))).astype(NARROW)
    scale = HEAD_DIM ** (-0.5)
    query_grad = jnp.einsum("hqk,khe->qhe", score_grad, keys, preferred_element_type=WIDE) * scale
    key_grad = jnp.einsum("hqk,qhe->khe", score_grad, queries, preferred_element_type=WIDE) * scale
    parts = [item.reshape(-1, D) for item in (query_grad, key_grad, values_grad)]
    attn_bias = jnp.concatenate([rows_sum(parts[0]), rows_sum(parts[2])])
    mixed_low = jnp.concatenate(parts, -1).astype(NARROW)
    attn_weight = weight_grad(normed, mixed_low)
    pull = norm_pull(stream, p.norm_one_gain, p.norm_one_shift)
    stream_grad, norm_one_gain, norm_one_shift = pull(back_input(mixed_low, p.attn_weight))
    grads = dict(
        norm_one_gain=norm_one_gain, norm_one_shift=norm_one_shift, attn_weight=attn_weight, attn_bias=attn_bias,
        proj_weight=proj_weight, proj_bias=proj_bias, norm_two_gain=norm_two_gain, norm_two_shift=norm_two_shift,
        fc_one_weight=fc_one_weight, fc_one_bias=fc_one_bias, fc_two_weight=fc_two_weight, fc_two_bias=fc_two_bias,
    )
    return stream_grad + middle_grad, grads


def time_features(times):
    half = FREQ // 2
    freqs = jnp.exp(-math.log(10000.0) * jnp.arange(half, dtype=WIDE) / half)
    angles = times[..., None] * freqs
    return jnp.concatenate([jnp.cos(angles), jnp.sin(angles)], -1)


def alpha_level(times):
    start = math.cos(0.008 / 1.008 * math.pi / 2) ** 2
    return jnp.cos(((times + 1.0) / STEPS_T + 0.008) / 1.008 * math.pi / 2) ** 2 / start


def head_pass(p, conditions, clean, filled, steps, noise, divisor):
    cond = dense(conditions, p.cond_weight) + p.cond_bias.astype(WIDE)
    times = steps.astype(WIDE)
    features = time_features(times).astype(NARROW)
    temporal = dense(features, p.time_weight) + p.time_bias.astype(WIDE)
    level = alpha_level(times)[..., None]
    noisy = (jnp.sqrt(level) * clean.astype(WIDE) + jnp.sqrt(1.0 - level) * noise).astype(NARROW)
    hidden_in = dense(noisy, p.input_weight) + p.input_bias.astype(WIDE)
    joined = temporal + cond[None]
    signal = jax.nn.silu(joined).astype(NARROW)
    modulation = dense(signal, p.ada_weight) + p.ada_bias.astype(WIDE)
    normed = layer_norm(hidden_in, p.head_gain.astype(WIDE), p.head_shift.astype(WIDE))
    modulated = (normed * (1.0 + modulation[..., HW : 2 * HW]) + modulation[..., :HW]).astype(NARROW)
    inner = dense(modulated, p.inner_weight) + p.inner_bias.astype(WIDE)
    active = jax.nn.silu(inner).astype(NARROW)
    outer = dense(active, p.outer_weight) + p.outer_bias.astype(WIDE)
    hidden = hidden_in + modulation[..., 2 * HW :] * outer
    final = layer_norm(hidden, 1.0, 0.0).astype(NARROW)
    predicted = dense(final, p.final_weight) + p.final_bias.astype(WIDE)
    error = predicted - noise
    marks = filled.astype(WIDE)
    loss_part = jnp.sum(jnp.sum(error * error, -1) * marks)
    pred_grad = 2.0 * error * marks[:, None] / divisor
    pred_low = pred_grad.astype(NARROW)
    hidden_grad = jax.vjp(lambda value: layer_norm(value, 1.0, 0.0), hidden)[1](back_input(pred_low, p.final_weight))[0]
    gate_grad = hidden_grad * outer
    outer_grad = hidden_grad * modulation[..., 2 * HW :]
    outer_low = outer_grad.astype(NARROW)
    inner_grad = jax.vjp(jax.nn.silu, inner)[1](back_input(outer_low, p.outer_weight))[0]
    inner_low = inner_grad.astype(NARROW)
    mod_grad = back_input(inner_low, p.inner_weight)
    pull = norm_pull(hidden_in, p.head_gain, p.head_shift)
    norm_grad, head_gain, head_shift = pull(mod_grad * (1.0 + modulation[..., HW : 2 * HW]))
    hidden_grad = hidden_grad + norm_grad
    modulation_grad = jnp.concatenate([mod_grad, mod_grad * normed, gate_grad], -1)
    modulation_low = modulation_grad.astype(NARROW)
    signal_grad = back_input(modulation_low, p.ada_weight)
    joined_grad = jax.vjp(jax.nn.silu, joined)[1](signal_grad)[0]
    joined_low = joined_grad.astype(NARROW)
    cond_grad = jnp.sum(joined_grad, 0)
    cond_low = cond_grad.astype(NARROW)
    hidden_low = hidden_grad.astype(NARROW)
    grads = dict(
        final_weight=weight_grad(final, pred_low), final_bias=rows_sum(pred_grad),
        outer_weight=weight_grad(active, outer_low), outer_bias=rows_sum(outer_grad),
        inner_weight=weight_grad(modulated, inner_low), inner_bias=rows_sum(inner_grad),
        head_gain=head_gain, head_shift=head_shift,
        ada_weight=weight_grad(signal, modulation_low), ada_bias=rows_sum(modulation_grad),
        time_weight=weight_grad(features, joined_low), time_bias=rows_sum(joined_grad),
        cond_weight=weight_grad(conditions, cond_low), cond_bias=rows_sum(cond_grad),
        input_weight=weight_grad(noisy, hidden_low), input_bias=rows_sum(hidden_grad),
    )
    return loss_part, grads, back_input(cond_low, p.cond_weight)


def exchange(payload, parts):
    shape = payload.shape
    moved = lax.all_to_all(payload.reshape(parts, -1, shape[-1]), "dp", split_axis=0, concat_axis=0, tiled=True)
    return moved.reshape(shape)


def body(latents, route, labels, timesteps, noise, image_weight, weights, momentum, average):
    ranks_dp, ranks_rep = lax.axis_size("dp"), lax.axis_size("rep")
    ranks = ranks_dp * ranks_rep
    meshed = (ranks_dp, ranks_rep) == (8, 4)
    rows = route.shape[0]
    images = labels.shape[0]
    assert images == 1 and rows == SEQ
    size = weights.shape[0] // LANES
    padded = -(-(size + 1) // 48) * 48
    masked = route < rows
    own = jnp.sum(masked.astype(WIDE))
    low = weights.reshape(size, LANES).astype(NARROW)
    extra = jnp.full((padded - size, LANES), own).astype(NARROW)
    block = jnp.concatenate([low, extra], 0)
    gathered = spread(block) if meshed else lax.all_gather(block, BOTH, axis=0)
    base, enc, mid, dec, head = unpack(gathered, size)
    count = jnp.sum(gathered[:, size, 0].astype(WIDE))
    keep = jnp.concatenate([jnp.ones((BUF,), bool), ~masked])
    tokens = dense(latents, base.embed_weight) + base.embed_bias.astype(WIDE)
    at = next(e.start for e in ENTRIES if e.sparse) + labels[0] * (D // LANES) + jnp.arange(D // LANES, dtype=jnp.int32)
    classes = gathered[at // size, at % size].reshape(1, D).astype(WIDE)
    stream = jnp.concatenate([jnp.broadcast_to(classes, (BUF, D)), tokens], 0) + base.encoder_pos.astype(WIDE)
    stream, enc_stored = block_forward(stream, keep, enc)
    encoded = layer_norm(stream, mid.enc_gain.astype(WIDE), mid.enc_shift.astype(WIDE)).astype(NARROW)
    decoded = dense(encoded, mid.dec_weight) + mid.dec_bias.astype(WIDE)
    decoded = jnp.where(keep[:, None], decoded, mid.mask_token.astype(WIDE))
    before = decoded + mid.decoder_pos.astype(WIDE)
    flow_out, dec_stored = block_forward(before, None, dec)
    after = layer_norm(flow_out, head.dec_gain.astype(WIDE), head.dec_shift.astype(WIDE))
    conditions = (after[BUF:] + head.diffusion_pos.astype(WIDE)).astype(NARROW)
    token_weight = jnp.broadcast_to(image_weight.astype(NARROW)[:, None], (rows, 1))
    payload = jnp.concatenate([conditions, latents, token_weight, jnp.zeros((rows, LANES - TOK_CH - 1), NARROW)], 1)
    picks = (jnp.arange(rows, dtype=jnp.int32)[:, None] == route[None, :]).astype(NARROW)
    arrived = exchange(dense(picks, payload).astype(NARROW), ranks_dp)
    divisor = TOK_CH * COPIES * count
    loss_part, head_grads, cond_back = head_pass(
        head, arrived[:, :D], arrived[:, D : D + TOK_CH], arrived[:, D + TOK_CH], timesteps, noise, divisor
    )
    returned = exchange(cond_back.astype(NARROW), ranks_dp)
    token_grad = lax.dot_general(picks, returned, (((0,), (0,)), ((), ())), preferred_element_type=WIDE)
    loss = lax.psum(loss_part, BOTH) / divisor
    after_grad = jnp.concatenate([jnp.zeros((BUF, D), WIDE), token_grad], 0)
    flow_grad, dec_gain, dec_shift = norm_pull(flow_out, head.dec_gain, head.dec_shift)(after_grad)
    head_grads.update(diffusion_pos=token_grad, dec_gain=dec_gain, dec_shift=dec_shift)
    before_grad, dec_grads = block_backward(flow_grad, None, dec, dec_stored)
    decoded_grad = jnp.where(keep[:, None], before_grad, 0.0)
    decoded_low = decoded_grad.astype(NARROW)
    pull = norm_pull(stream, mid.enc_gain, mid.enc_shift)
    stream_grad, enc_gain, enc_shift = pull(back_input(decoded_low, mid.dec_weight))
    mid_grads = dict(
        enc_gain=enc_gain, enc_shift=enc_shift, dec_weight=weight_grad(encoded, decoded_low), dec_bias=rows_sum(decoded_grad),
        mask_token=rows_sum(jnp.where(keep[:, None], 0.0, before_grad)), decoder_pos=before_grad,
    )
    stream_grad, enc_grads = block_backward(stream_grad, keep, enc, enc_stored)
    token_in = stream_grad[BUF:]
    base_grads = dict(
        encoder_pos=stream_grad,
        class_table=jnp.zeros((CLASSES, D), WIDE).at[labels].add(jnp.sum(stream_grad[:BUF], 0)[None]),
        embed_weight=weight_grad(latents, token_in.astype(NARROW)), embed_bias=rows_sum(token_in),
    )
    grads = {}
    for group, found in enumerate((base_grads, enc_grads, mid_grads, dec_grads, head_grads)):
        grads.update({(group, name): value for name, value in found.items()})
    height = -(-((ranks - 1) * size + padded) // 8) * 8
    full = fold(grads, height)
    if meshed:
        owned = collect(full, size, padded)[:size]
    else:
        owned = lax.psum_scatter(full[: ranks * size].reshape(ranks, size, LANES), BOTH, scatter_dimension=0, tiled=False)
    owned = owned.reshape(-1)
    rate = 0.05 * math.sqrt(images * ranks * SEQ)
    new_momentum = 0.9 * momentum + owned
    new_weights = weights - rate * (owned + 0.9 * new_momentum)
    new_average = 0.75 * average + 0.25 * new_weights
    return new_weights, new_momentum, new_average, loss


def solution(mesh):
    flat = P(BOTH)
    placed = (P(BOTH, None), flat, flat, P(None, BOTH), P(None, BOTH, None), flat, flat, flat, flat)
    return jax.shard_map(body, mesh=mesh, in_specs=placed, out_specs=(flat, flat, flat, P()), check_vma=False)
```

```python
import functools
import heapq
import math
import types

import jax
import jax.numpy as jnp
from jax import lax
from jax.experimental import pallas as pl
from jax.experimental.pallas import tpu as pltpu
from jax.sharding import PartitionSpec as P

D = 768
HEADS = 12
HEAD_DIM = 64
MLP = 3072
HW = 1024
TOK_CH = 16
FREQ = 256
CLASSES = 1000
BUF = 64
SEQ = 256
COPIES = 4
STEPS_T = 1000
LANES = 128
WIDE = jnp.float32
NARROW = jnp.bfloat16
NORM_EPS = 1e-06
MESH = pl.DeviceIdType.MESH
ANY = pl.BlockSpec(memory_space=pl.ANY)
DMA = pltpu.SemaphoreType.DMA
BOTH = ("dp", "rep")


def block_shapes():
    return dict(
        norm_one_gain=(D,), norm_one_shift=(D,), attn_weight=(D, 3 * D), attn_bias=(2 * D,),
        proj_weight=(D, D), proj_bias=(D,), norm_two_gain=(D,), norm_two_shift=(D,),
        fc_one_weight=(D, MLP), fc_one_bias=(MLP,), fc_two_weight=(MLP, D), fc_two_bias=(D,),
    )


ENC, DEC = 1, 3
GROUPS = (
    dict(embed_weight=(TOK_CH, D), embed_bias=(D,), class_table=(CLASSES, D), encoder_pos=(BUF + SEQ, D)),
    block_shapes(),
    dict(enc_gain=(D,), enc_shift=(D,), dec_weight=(D, D), dec_bias=(D,), mask_token=(D,), decoder_pos=(BUF + SEQ, D)),
    block_shapes(),
    dict(
        dec_gain=(D,), dec_shift=(D,), diffusion_pos=(SEQ, D), input_weight=(TOK_CH, HW), input_bias=(HW,),
        time_weight=(FREQ, HW), time_bias=(HW,), cond_weight=(D, HW), cond_bias=(HW,), head_gain=(HW,),
        head_shift=(HW,), ada_weight=(HW, 3 * HW), ada_bias=(3 * HW,), inner_weight=(HW, HW), inner_bias=(HW,),
        outer_weight=(HW, HW), outer_bias=(HW,), final_weight=(HW, TOK_CH), final_bias=(TOK_CH,),
    ),
)


class Entry:
    def __init__(self, group, name, shape, start):
        self.group, self.name, self.shape, self.start = group, name, shape, start
        self.rows = -(-math.prod(shape) // LANES)
        self.matrix = len(shape) == 2 and shape[1] % LANES == 0
        self.across = shape[1] // LANES if self.matrix else 1
        self.sparse = name == GROUP_SPARSE


GROUP_SPARSE = next(name for name, shape in GROUPS[0].items() if shape[0] == CLASSES)


def entries():
    found, start = [], 0
    for group, shapes in enumerate(GROUPS):
        for name, shape in shapes.items():
            found.append(Entry(group, name, shape, start))
            start += found[-1].rows
    return found


ENTRIES = entries()
USED = ENTRIES[-1].start + ENTRIES[-1].rows


def block_height(entry, limit):
    best = 0
    for height in range(8, entry.shape[0] + 1, 8):
        if entry.shape[0] % height == 0 and height * entry.across <= limit:
            best = height
    return best


class Slots:
    def __init__(self, number):
        self.number, self.base, self.last = number, 0, {}

    def at(self, b):
        return (self.base + b) % self.number

    def claim(self, b, put):
        for k in range(self.number):
            before = self.last.get((self.base + k) % self.number)
            if before is not None:

                @pl.when(b == k)
                def _(before=before):
                    before().wait()

        @pl.when(b >= self.number)
        def _():
            put(b - self.number).wait()

    def close(self, blocks, put):
        base = self.base
        for b in range(max(0, blocks - self.number), blocks):
            self.last[(base + b) % self.number] = functools.partial(put, b)
        self.base = base + blocks

    def drain(self):
        for before in self.last.values():
            before().wait()


SLOTS = 4


def unfold_kernel(rows, padded, items, g_ref, *refs):
    count = len(items)
    outs = refs[:count]
    first, second, wide, first_sem, second_sem, out_sem = refs[count : count + 6]
    kinds = sorted({(h, e.across) for e, h in items})
    stages = dict(zip(kinds, refs[count + 6 :]))
    turns = {kind: Slots(2) for kind in kinds}
    bases = [0]
    for entry, height in items:
        bases.append(bases[-1] + entry.shape[0] // height)

    def spot(t, b):
        entry, height = items[t]
        span = height * entry.across
        start = entry.start + b * span
        dev = start // rows
        row = start - dev * rows
        low = jnp.minimum(row // 8 * 8, padded - span - 8)
        return dev, row, low, row + span > rows

    def copies(t, b):
        entry, height = items[t]
        window = height * entry.across + 8
        dev, row, low, more = spot(t, b)
        slot = (bases[t] + b) % SLOTS
        one = pltpu.make_async_copy(
            g_ref.at[dev, pl.ds(pl.multiple_of(low, 8), window)], first.at[slot, pl.ds(0, window)], first_sem.at[slot]
        )
        two = pltpu.make_async_copy(
            g_ref.at[jnp.minimum(dev + 1, g_ref.shape[0] - 1), pl.ds(0, window)],
            second.at[slot, pl.ds(0, window)], second_sem.at[slot],
        )
        return one, two, more

    def fetch(t, b):
        one, two, more = copies(t, b)
        one.start()

        @pl.when(more)
        def _():
            two.start()

    def fetch_number(g):
        if g < bases[-1]:
            t = next(t for t in range(count) if g < bases[t + 1])
            fetch(t, g - bases[t])

    ahead = SLOTS - 1
    for g in range(ahead):
        fetch_number(g)
    for t, (entry, height) in enumerate(items):
        kind = (height, entry.across)
        stage, turn = stages[kind], turns[kind]
        window = height * entry.across + 8
        blocks = entry.shape[0] // height

        def put(b, t=t, stage=stage, height=height, place=turn.base, kind=kind):
            slot = (place + b) % 2
            return pltpu.make_async_copy(
                stage.at[slot], outs[t].at[pl.ds(pl.multiple_of(b * height, 8), height)], out_sem.at[kinds.index(kind), slot]
            )

        def body(b, carry, t=t, entry=entry, height=height, window=window, blocks=blocks, stage=stage, turn=turn, put=put):
            @pl.when(b + ahead < blocks)
            def _():
                fetch(t, b + ahead)

            for k in range(max(0, ahead - blocks), ahead):

                @pl.when(b == blocks - ahead + k)
                def _(k=k):
                    fetch_number(bases[t + 1] + k)

            dev, row, low, _ = spot(t, b)
            slot = (bases[t] + b) % SLOTS
            one, two, more = copies(t, b)
            one.wait()
            wide[pl.ds(0, window), :] = first[slot, pl.ds(0, window), :].astype(WIDE)

            @pl.when(more)
            def _():
                two.wait()
                wide[pl.ds(rows - low, window), :] = second[slot, pl.ds(0, window), :].astype(WIDE)

            turn.claim(b, put)
            off = row - low
            place = turn.at(b)
            for j in range(entry.across):
                stage[place, :, j * LANES : (j + 1) * LANES] = wide[pl.ds(off + j, height, stride=entry.across), :].astype(NARROW)
            put(b).start()
            return carry

        lax.fori_loop(0, blocks, body, 0)
        turn.close(blocks, put)
    for turn in turns.values():
        turn.drain()


def unfold(gathered, rows):
    padded = gathered.shape[1]
    items = [(e, block_height(e, min(2304, rows - 16))) for e in ENTRIES if e.matrix and not e.sparse]
    tall = max(e.across * h for e, h in items) + 8
    kinds = sorted({(h, e.across) for e, h in items})
    total = sum(math.prod(e.shape) for e, _ in items)
    outs = pl.pallas_call(
        functools.partial(unfold_kernel, rows, padded, items),
        out_shape=[jax.ShapeDtypeStruct(e.shape, NARROW) for e, _ in items],
        in_specs=[ANY],
        out_specs=[ANY] * len(items),
        scratch_shapes=[
            pltpu.VMEM((SLOTS, tall, LANES), NARROW), pltpu.VMEM((SLOTS, tall, LANES), NARROW),
            pltpu.VMEM((2 * tall, LANES), WIDE), DMA((SLOTS,)), DMA((SLOTS,)), DMA((len(kinds), 2)),
        ]
        + [pltpu.VMEM((2, h, n * LANES), NARROW) for h, n in kinds],
        compiler_params=pltpu.CompilerParams(vmem_limit_bytes=48 * 1000 * 1000),
        cost_estimate=pl.CostEstimate(flops=total, bytes_accessed=4 * total, transcendentals=0),
    )(gathered)
    return {(e.group, e.name): out for (e, _), out in zip(items, outs)}


def rows_at(gathered, rows, start, number):
    pieces = []
    while number > 0:
        dev, row = divmod(start, rows)
        take = min(number, rows - row)
        pieces.append(gathered[dev, row : row + take])
        start, number = start + take, number - take
    return pieces[0] if len(pieces) == 1 else jnp.concatenate(pieces, 0)


def unpack(gathered, rows):
    matrices = unfold(gathered, rows)
    groups = [types.SimpleNamespace() for _ in GROUPS]
    for e in ENTRIES:
        if e.sparse:
            continue
        if e.matrix:
            value = matrices[(e.group, e.name)]
        else:
            value = rows_at(gathered, rows, e.start, e.rows).reshape(-1)[: math.prod(e.shape)].reshape(e.shape)
        setattr(groups[e.group], e.name, value)
    return groups


DEPTH = 3
TALL = 256
CHUNK = 512


def product_height(entry):
    return min(TALL, entry.shape[0])


def fold_kernel(products, items, plain, label, row, *refs):
    refs = list(refs)

    def take(number):
        found, refs[:number] = refs[:number], []
        return found

    pairs = take(2 * len(products))
    given = take(len(items))
    rest = take(len(plain))
    (full,) = take(1)
    pair_sem, given_sem, plain_sem, out_sem = take(4)
    held = take(2 * len(products))
    loads = take(len(items))
    (stage,) = take(1)
    gets = [pltpu.make_async_copy(given[i], loads[i], given_sem.at[i]) for i in range(len(items))]
    fills = [pltpu.make_async_copy(pairs[i], held[i], pair_sem.at[i]) for i in range(len(pairs))]
    for move in gets + fills:
        move.start()
    moves = []
    for i, (start, number) in enumerate(plain):
        move = pltpu.make_async_copy(rest[i].at[pl.ds(0, number)], full.at[pl.ds(start, number)], plain_sem.at[i])
        move.start()
        moves.append(move)
    turn = Slots(DEPTH)

    def each(entry, height, make):
        span = height * entry.across
        blocks = entry.shape[0] // height

        def put(b, base=turn.base):
            slot = (base + b) % DEPTH
            return pltpu.make_async_copy(
                stage.at[slot, pl.ds(0, span)], full.at[pl.ds(entry.start + b * span, span)], out_sem.at[slot]
            )

        def step(b, carry):
            turn.claim(b, put)
            make(b, turn.at(b))
            put(b).start()
            return carry

        lax.fori_loop(0, blocks, step, 0)
        turn.close(blocks, put)

    sparse = next(e for e in ENTRIES if e.sparse)
    height = block_height(sparse, 1200)

    def lone(b, slot):
        here = lax.broadcasted_iota(jnp.int32, (height, LANES), 0) + b * height == label[0]
        for j in range(sparse.across):
            value = jnp.broadcast_to(row[0:1, j * LANES : (j + 1) * LANES], (height, LANES))
            stage[slot, pl.ds(j, height, stride=sparse.across), :] = jnp.where(here, value, 0.0)

    each(sparse, height, lone)
    for t, entry in enumerate(items):
        gets[t].wait()

        def make(b, slot, t=t, entry=entry):
            for j in range(entry.across):
                stage[slot, pl.ds(j, entry.shape[0], stride=entry.across), :] = loads[t][:, j * LANES : (j + 1) * LANES]

        each(entry, entry.shape[0], make)
    for t, entry in enumerate(products):
        left, right = held[2 * t], held[2 * t + 1]
        fills[2 * t].wait()
        fills[2 * t + 1].wait()
        height = product_height(entry)
        chunk = math.gcd(CHUNK, entry.shape[1])

        def make(b, slot, left=left, right=right, entry=entry, height=height, chunk=chunk):
            turned = left[:, pl.ds(pl.multiple_of(b * height, LANES), height)].T
            for k in range(entry.shape[1] // chunk):
                found = jnp.dot(turned, right[:, k * chunk : (k + 1) * chunk], preferred_element_type=WIDE)
                for j in range(chunk // LANES):
                    at = pl.ds(k * (chunk // LANES) + j, height, stride=entry.across)
                    stage[slot, at, :] = found[:, j * LANES : (j + 1) * LANES]

        each(entry, height, make)
    turn.drain()
    for move in moves:
        move.wait()


def fold(grads, label, height_total):
    found = {e: grads[(e.group, e.name)] for e in ENTRIES}
    products = [e for e in ENTRIES if isinstance(found[e], tuple)]
    items = [e for e in ENTRIES if e.matrix and not e.sparse and e not in products]
    plain, values = [], []
    for e in ENTRIES:
        if e.matrix:
            continue
        value = found[e].reshape(-1)
        value = jnp.pad(value, (0, e.rows * LANES - value.shape[0]))
        plain.append((e.start, e.rows))
        values.append(value.reshape(e.rows, LANES))
    if height_total > USED:
        plain.append((USED, height_total - USED))
        values.append(jnp.zeros((height_total - USED, LANES), WIDE))
    row = next(found[e] for e in ENTRIES if e.sparse)
    operands = [x.reshape(-1, x.shape[-1]) for e in products for x in found[e]]
    tall = max([e.rows for e in items] + [e.across * product_height(e) for e in products])
    total = height_total * LANES
    flops = sum(2 * math.prod(e.shape) * operands[2 * i].shape[0] for i, e in enumerate(products))
    return pl.pallas_call(
        functools.partial(fold_kernel, products, items, plain),
        out_shape=jax.ShapeDtypeStruct((height_total, LANES), WIDE),
        in_specs=[pl.BlockSpec(memory_space=pltpu.SMEM), pl.BlockSpec(memory_space=pltpu.VMEM)]
        + [ANY] * (len(operands) + len(items) + len(plain)),
        out_specs=ANY,
        scratch_shapes=[DMA((len(operands),)), DMA((len(items),)), DMA((len(plain),)), DMA((DEPTH,))]
        + [pltpu.VMEM(x.shape, x.dtype) for x in operands]
        + [pltpu.VMEM(e.shape, WIDE) for e in items]
        + [pltpu.VMEM((DEPTH, tall, LANES), WIDE)],
        compiler_params=pltpu.CompilerParams(vmem_limit_bytes=62 * 1000 * 1000),
        cost_estimate=pl.CostEstimate(flops=flops, bytes_accessed=4 * total, transcendentals=0),
    )(label, jnp.broadcast_to(row, (8, row.shape[-1])), *operands, *[found[e] for e in items], *values)


X, Y, Z = 0, 1, 2
TREES = ((Z, X, Y), (Z, Y, X), (X, Z, Y), (X, Z, Y), (Y, Z, X), (Y, Z, X))
SHARES = len(TREES)
FAR = 3


def onward(order, arrived, way, p):
    z, x, y = p
    found = []
    if arrived >= 0 and order[arrived] == Z and 0 <= z + way <= FAR:
        found.append(((z + way, x, y), arrived, way))
    for j in range(arrived + 1, 3):
        if order[j] == X:
            found.append(((z, 1 - x, y), j, 0))
        elif order[j] == Y:
            found.append(((z, x, 1 - y), j, 0))
        else:
            found += [((z + s, x, y), j, s) for s in (1, -1) if 0 <= z + s <= FAR]
    return found


@functools.cache
def flow(lag=0.4):
    chips = [(z, x, y) for z in range(FAR + 1) for x in range(2) for y in range(2)]
    events, queues, busy, come, sent = [], {}, set(), {}, []
    number = iter(range(10**9))
    for u in range(SHARES):
        for p in chips:
            heapq.heappush(events, (0.0, next(number), 0, (p, p, u, -1, 0)))

    def pump(link, t):
        if link in busy or not queues.get(link):
            return
        what = heapq.heappop(queues[link])[2]
        busy.add(link)
        sent.append((t, link, what[1], what[2]))
        heapq.heappush(events, (t + 1.0, next(number), 1, (link, what)))

    while events:
        t, _, kind, what = heapq.heappop(events)
        if kind == 1:
            link, piece = what
            busy.discard(link)
            heapq.heappush(events, (t + lag, next(number), 0, piece))
            pump(link, t)
            continue
        p, q, u, k, way = what
        come[(u, p, q)] = t
        for to, k2, way2 in onward(TREES[u], k, way, p):
            left = len(onward(TREES[u], k2, way2, to))
            heapq.heappush(queues.setdefault((p, to), []), ((-left, t), next(number), (to, q, u, k2, way2)))
            pump((p, to), t)
    return come, sent


def spread_order():
    keyed = {}
    for (u, p, q), t in flow()[0].items():
        keyed.setdefault((u, q[0] - p[0], (q[1] - p[1]) % 2, (q[2] - p[2]) % 2), []).append(t)
    return sorted(keyed, key=lambda k: (sum(keyed[k]) / len(keyed[k]), k))


def last_hop(u, dz, dx, dy):
    apart = [k for k in range(3) if (dx, dy, dz)[TREES[u][k]] != 0]
    return apart[-1] if apart else -1


def hops(u, dz, dx, dy):
    order, arrived = TREES[u], last_hop(u, dz, dx, dy)
    found = []
    if arrived >= 0 and order[arrived] == Z:
        found.append((1, 0, 0) if dz < 0 else (-1, 0, 0))
    for k in range(arrived + 1, 3):
        found += [[(0, 1, 0)], [(0, 0, 1)], [(1, 0, 0), (-1, 0, 0)]][order[k]]
    return found


def only(condition, action):
    if condition is None:
        action()
    else:
        pl.when(condition)(action)


def spread_kernel(own, out, keep_sem, send_sem, link_sem, core_send, core_sem):
    dp, rep = lax.axis_index("dp"), lax.axis_index("rep")
    z, x, y, c = dp // 2, dp % 2, rep // 2, rep % 2
    unit = own.shape[0] // SHARES
    sibling = (dp, y * 2 + 1 - c)

    def device(dz, dx, dy):
        return ((z + dz) * 2 + (x + dx) % 2, (y + dy) % 2 * 2 + c)

    def exists(dz):
        return None if dz == 0 else (z + dz >= 0 if dz < 0 else z + dz <= FAR)

    barrier = pltpu.get_barrier_semaphore()
    near = ((0, 1, 0), (0, 0, 1), (1, 0, 0), (-1, 0, 0))
    for hop in near:
        only(exists(hop[0]), lambda: pl.semaphore_signal(barrier, inc=1, device_id=device(*hop), device_id_type=MESH))
    pl.semaphore_signal(barrier, inc=1, device_id=sibling, device_id_type=MESH)
    inner = z * (FAR - z)
    only(inner == 0, lambda: pl.semaphore_wait(barrier, len(near)))
    only(inner > 0, lambda: pl.semaphore_wait(barrier, len(near) + 1))
    keep = pltpu.make_async_copy(own, out.at[dp * 4 + rep], keep_sem)
    keep.start()
    ends, number = [], 0
    for u, dz, dx, dy in spread_order():
        part = pl.ds(u * unit, unit)
        q = ((z + dz) * 2 + (x + dx) % 2) * 2 + (y + dy) % 2
        mine = dz == 0 and dx == 0 and dy == 0
        i = u * 16 + q

        def copy(to, send, come, part=part, q=q, mine=mine):
            here = out.at[q * 2 + c, part]
            return pltpu.make_async_remote_copy(
                own.at[part] if mine else here, here, send, come, device_id=to, device_id_type=MESH
            )

        goes = [(hop, number + k) for k, hop in enumerate(hops(u, dz, dx, dy))]
        number += len(goes)

        def run(i=i, copy=copy, goes=goes, mine=mine):
            if not mine:
                copy(sibling, send_sem.at[0], link_sem.at[i]).wait_recv()
            for hop, n in goes:
                only(exists(hop[0]), lambda: copy(device(*hop), send_sem.at[n], link_sem.at[i]).start())
            copy(sibling, core_send.at[i], core_sem.at[i]).start()

        def finish(i=i, copy=copy, goes=goes):
            for hop, n in goes:
                only(exists(hop[0]), lambda: copy(device(*hop), send_sem.at[n], link_sem.at[i]).wait_send())
            copy(sibling, core_send.at[i], core_sem.at[i]).wait()

        there = None if dz == 0 else jnp.logical_and(z + dz >= 0, z + dz <= FAR)
        only(there, run)
        ends.append((there, finish))
    for there, finish in ends:
        only(there, finish)
    keep.wait()


def spread(own):
    pieces = SHARES * 16
    sends = sum(len(hops(*key)) for key in spread_order())
    return pl.pallas_call(
        spread_kernel,
        out_shape=jax.ShapeDtypeStruct((32,) + own.shape, own.dtype),
        in_specs=[ANY],
        out_specs=ANY,
        scratch_shapes=[DMA, DMA((sends,)), DMA((pieces,)), DMA((pieces,)), DMA((pieces,))],
        compiler_params=pltpu.CompilerParams(collective_id=0, has_side_effects=True),
    )(own)


class Chip:
    def __init__(self, low):
        dp, rep = lax.axis_index("dp"), lax.axis_index("rep")
        self.low = low
        self.z, self.x, self.y, self.c = dp // 2, dp % 2, rep // 2, rep % 2
        self.way = 1 - 2 * (self.z // 2)

    def device(self, q, other=0):
        z = self.z + self.way * (q[0] - self.low)
        return z * 2 + (self.x + q[1]) % 2, (self.y + q[2]) % 2 * 2 + (self.c + other) % 2

    def block(self, q, other=0):
        dp, rep = self.device(q, other)
        return dp * 4 + rep

    def greet(self):
        low = self.low
        near = [(low, 1, 0), (low, 0, 1), (low + 1, 0, 0)] + ([(low - 1, 0, 0)] if low else [])
        barrier = pltpu.get_barrier_semaphore()
        for q in near:
            pl.semaphore_signal(barrier, inc=1, device_id=self.device(q), device_id_type=MESH)
        pl.semaphore_signal(barrier, inc=1, device_id=self.device((low, 0, 0), 1), device_id_type=MESH)
        pl.semaphore_wait(barrier, len(near) + 1)


def seen_from(p, r):
    low, way = min(p[0], FAR - p[0]), 1 if p[0] < 2 else -1
    return low + way * (r[0] - p[0]), (r[1] - p[1]) % 2, (r[2] - p[2]) % 2


@functools.cache
def sum_programs():
    come, sent = flow()
    last = max(come.values())
    found = []
    for z in (0, 1):
        p = (z, 0, 0)
        kids, parent, when = {}, {}, {}
        for t, link, q, u in sent:
            if link[0] == p:
                kids.setdefault((u, q), []).append(link[1])
                if q == p:
                    when[(u, p)] = max(when.get((u, p), 0.0), last - t)
            if link[1] == p:
                parent[(u, q)] = link[0]
                when[(u, q)] = last - t - 1.0
        tasks = sorted(when, key=lambda k: (when[k], k))
        found.append([(u, q, sorted(kids.get((u, q), [])), parent.get((u, q))) for u, q in tasks])
    return found


@functools.cache
def landing():
    return [{key: i for i, key in enumerate((u, q, k) for u, q, kids, _ in tasks for k in kids)} for tasks in sum_programs()]


RING = 12
SIDE = 4
EARLY = 12
STEP = 40


def add_rows(into, terms):
    def body(i, carry):
        at = pl.ds(pl.multiple_of(i * STEP, 8), STEP)
        total = into[at, :]
        for term in terms:
            total = total + term[at, :]
        into[at, :] = total
        return carry

    lax.fori_loop(0, into.shape[0] // STEP, body, 0)


def collect_at(low, size, full, mark, out, aside, store, ring, side, ring_sem, side_sem, send_sem, link_sem, core_send, core_sem, out_sem, marks, mark_sem):
    chip = Chip(low)
    me = (low, 0, 0)
    tasks, spots = sum_programs()[low], landing()
    count, unit = len(tasks), ring.shape[1]
    chip.greet()

    def part(i, other=0):
        return full.at[pl.ds(chip.block(tasks[i][1], other) * size + tasks[i][0] * unit, unit)]

    def across(i):
        return pltpu.make_async_remote_copy(
            part(i, 1), aside.at[i], core_send.at[i], core_sem.at[i], device_id=chip.device(me, 1), device_id_type=MESH
        )

    def ours(i):
        return pltpu.make_async_copy(part(i), ring.at[i % RING], ring_sem.at[i % RING])

    def theirs(i):
        return pltpu.make_async_copy(aside.at[i], side.at[i % SIDE], side_sem.at[i % SIDE])

    def along(i, spot, to):
        return pltpu.make_async_remote_copy(
            ring.at[i % RING], store.at[spot], send_sem.at[i], link_sem.at[spot], device_id=chip.device(to), device_id_type=MESH
        )

    tail = pl.ds(unit - 8, 8)
    ours_too = pltpu.make_async_copy(mark, marks.at[0], mark_sem.at[0])
    theirs_too = pltpu.make_async_remote_copy(
        mark, marks.at[1], mark_sem.at[1], mark_sem.at[2], device_id=chip.device(me, 1), device_id_type=MESH
    )
    ours_too.start()
    theirs_too.start()
    leaving = {}

    def fetch(i):
        if i - RING in leaving:
            leaving.pop(i - RING)()
        ours(i).start()
        across(i).wait_recv()
        theirs(i).start()

    for i in range(EARLY):
        across(i).start()
    for i in range(SIDE - 1):
        fetch(i)
    ours_too.wait()
    theirs_too.wait()
    for i, (u, q, kids, to) in enumerate(tasks):
        if i + EARLY < count:
            across(i + EARLY).start()
        if i + SIDE - 1 < count:
            fetch(i + SIDE - 1)
        ours(i).wait()
        theirs(i).wait()
        if u == SHARES - 1:
            ring[i % RING, tail, :] = marks[0] + marks[1]
            side[i % SIDE, tail, :] = jnp.zeros((8, LANES), WIDE)
        terms = [side.at[i % SIDE]]
        for kid in kids:
            spot = spots[low][(u, q, kid)]
            along(i, spot, kid).wait_recv()
            terms.append(store.at[spot])
        add_rows(ring.at[i % RING], terms)
        if to is None:
            move = pltpu.make_async_copy(ring.at[i % RING], out.at[pl.ds(u * unit, unit)], out_sem.at[u])
            move.start()
            leaving[i] = move.wait
        else:
            move = along(i, spots[min(to[0], FAR - to[0])][(u, seen_from(to, q), seen_from(to, me))], to)
            move.start()
            leaving[i] = move.wait_send
    for i in list(leaving):
        leaving.pop(i)()
    for i in range(count):
        across(i).wait_send()


def collect_kernel(size, *refs):
    z = lax.axis_index("dp") // 2
    inner = z * (FAR - z)

    @pl.when(inner == 0)
    def _():
        collect_at(0, size, *refs)

    @pl.when(inner > 0)
    def _():
        collect_at(1, size, *refs)


def collect(full, mark, size, rows):
    slots = max(len(spots) for spots in landing())
    count, unit = len(sum_programs()[0]), rows // SHARES
    return pl.pallas_call(
        functools.partial(collect_kernel, size),
        out_shape=(jax.ShapeDtypeStruct((rows, LANES), WIDE), jax.ShapeDtypeStruct((count, unit, LANES), WIDE)),
        in_specs=[ANY, ANY],
        out_specs=(ANY, ANY),
        scratch_shapes=[
            pltpu.VMEM((slots, unit, LANES), WIDE), pltpu.VMEM((RING, unit, LANES), WIDE), pltpu.VMEM((SIDE, unit, LANES), WIDE),
            DMA((RING,)), DMA((SIDE,)), DMA((count,)), DMA((slots,)), DMA((count,)), DMA((count,)), DMA((SHARES,)),
            pltpu.VMEM((2, 8, LANES), WIDE), DMA((3,)),
        ],
        compiler_params=pltpu.CompilerParams(collective_id=1, has_side_effects=True, vmem_limit_bytes=62 * 1000 * 1000),
    )(full, mark)[0]


def layer_norm(value, gain, shift):
    centered = value - jnp.mean(value, -1, keepdims=True)
    scaled = centered * lax.rsqrt(jnp.mean(centered * centered, -1, keepdims=True) + NORM_EPS)
    return scaled * gain + shift


def dense(inputs, weight):
    return lax.dot_general(inputs, weight, (((inputs.ndim - 1,), (0,)), ((), ())), preferred_element_type=WIDE)


def back_input(grads_low, weight):
    return lax.dot_general(grads_low, weight, (((grads_low.ndim - 1,), (1,)), ((), ())), preferred_element_type=WIDE)


def weight_grad(inputs, grads_low):
    flat_in = inputs.reshape(-1, inputs.shape[-1])
    flat_grad = grads_low.reshape(-1, grads_low.shape[-1])
    if min(flat_in.shape[1], flat_grad.shape[1]) >= LANES:
        return flat_in, flat_grad
    return lax.dot_general(flat_in, flat_grad, (((0,), (0,)), ((), ())), preferred_element_type=WIDE)


def rows_sum(values):
    return jnp.sum(values.reshape(-1, values.shape[-1]), 0)


def norm_pull(value, gain, shift):
    return jax.vjp(layer_norm, value, gain.astype(WIDE), shift.astype(WIDE))[1]


def split_heads(mixed):
    return [mixed[:, part * D : (part + 1) * D].reshape(-1, HEADS, HEAD_DIM) for part in range(3)]


def masked_scores(queries, keys, keep):
    scores = jnp.einsum("qhe,khe->hqk", queries, keys, preferred_element_type=WIDE) * HEAD_DIM ** (-0.5)
    return scores if keep is None else jnp.where(keep[None, None, :], scores, -1e30)


def block_forward(stream, keep, p):
    normed = layer_norm(stream, p.norm_one_gain.astype(WIDE), p.norm_one_shift.astype(WIDE)).astype(NARROW)
    bias = jnp.concatenate([p.attn_bias[:D].astype(WIDE), jnp.zeros((D,), WIDE), p.attn_bias[D:].astype(WIDE)])
    mixed = (dense(normed, p.attn_weight) + bias).astype(NARROW)
    queries, keys, values = split_heads(mixed)
    scores = masked_scores(queries, keys, keep)
    totals = jax.nn.logsumexp(scores, axis=-1)
    probs = jnp.exp(scores - totals[..., None]).astype(NARROW)
    attended = jnp.einsum("hqk,khe->qhe", probs, values, preferred_element_type=WIDE)
    attended = attended.reshape(-1, D).astype(NARROW)
    middle = stream + dense(attended, p.proj_weight) + p.proj_bias.astype(WIDE)
    second = layer_norm(middle, p.norm_two_gain.astype(WIDE), p.norm_two_shift.astype(WIDE)).astype(NARROW)
    inner = dense(second, p.fc_one_weight) + p.fc_one_bias.astype(WIDE)
    active = jax.nn.gelu(inner, approximate=False).astype(NARROW)
    output = middle + dense(active, p.fc_two_weight) + p.fc_two_bias.astype(WIDE)
    return output, (stream, normed, mixed, totals, attended, middle, second, inner, active)


def block_backward(grad_out, keep, p, saved):
    stream, normed, mixed, totals, attended, middle, second, inner, active = saved
    grads = {}
    out_low = grad_out.astype(NARROW)
    fc_two_weight = weight_grad(active, out_low)
    fc_two_bias = rows_sum(grad_out)
    gelu_pull = jax.vjp(lambda value: jax.nn.gelu(value, approximate=False), inner)[1]
    inner_grad = gelu_pull(back_input(out_low, p.fc_two_weight))[0]
    inner_low = inner_grad.astype(NARROW)
    fc_one_weight = weight_grad(second, inner_low)
    fc_one_bias = rows_sum(inner_grad)
    pull = norm_pull(middle, p.norm_two_gain, p.norm_two_shift)
    middle_grad, norm_two_gain, norm_two_shift = pull(back_input(inner_low, p.fc_one_weight))
    middle_grad = middle_grad + grad_out
    middle_low = middle_grad.astype(NARROW)
    proj_weight = weight_grad(attended, middle_low)
    proj_bias = rows_sum(middle_grad)
    attended_grad = back_input(middle_low, p.proj_weight).astype(NARROW).reshape(-1, HEADS, HEAD_DIM)
    queries, keys, values = split_heads(mixed)
    probs = jnp.exp(masked_scores(queries, keys, keep) - totals[..., None])
    values_grad = jnp.einsum("hqk,qhe->khe", probs.astype(NARROW), attended_grad, preferred_element_type=WIDE)
    prob_grad = jnp.einsum("qhe,khe->hqk", attended_grad, values, preferred_element_type=WIDE)
    score_grad = (probs * (prob_grad - jnp.sum(probs * prob_grad, -1, keepdims=True))).astype(NARROW)
    scale = HEAD_DIM ** (-0.5)
    query_grad = jnp.einsum("hqk,khe->qhe", score_grad, keys, preferred_element_type=WIDE) * scale
    key_grad = jnp.einsum("hqk,qhe->khe", score_grad, queries, preferred_element_type=WIDE) * scale
    parts = [item.reshape(-1, D) for item in (query_grad, key_grad, values_grad)]
    attn_bias = jnp.concatenate([rows_sum(parts[0]), rows_sum(parts[2])])
    mixed_low = jnp.concatenate(parts, -1).astype(NARROW)
    attn_weight = weight_grad(normed, mixed_low)
    pull = norm_pull(stream, p.norm_one_gain, p.norm_one_shift)
    stream_grad, norm_one_gain, norm_one_shift = pull(back_input(mixed_low, p.attn_weight))
    grads = dict(
        norm_one_gain=norm_one_gain, norm_one_shift=norm_one_shift, attn_weight=attn_weight, attn_bias=attn_bias,
        proj_weight=proj_weight, proj_bias=proj_bias, norm_two_gain=norm_two_gain, norm_two_shift=norm_two_shift,
        fc_one_weight=fc_one_weight, fc_one_bias=fc_one_bias, fc_two_weight=fc_two_weight, fc_two_bias=fc_two_bias,
    )
    return stream_grad + middle_grad, grads


def time_features(times):
    half = FREQ // 2
    freqs = jnp.exp(-math.log(10000.0) * jnp.arange(half, dtype=WIDE) / half)
    angles = times[..., None] * freqs
    return jnp.concatenate([jnp.cos(angles), jnp.sin(angles)], -1)


def alpha_level(times):
    start = math.cos(0.008 / 1.008 * math.pi / 2) ** 2
    return jnp.cos(((times + 1.0) / STEPS_T + 0.008) / 1.008 * math.pi / 2) ** 2 / start


def head_pass(p, conditions, clean, filled, steps, noise, divisor):
    cond = dense(conditions, p.cond_weight) + p.cond_bias.astype(WIDE)
    times = steps.astype(WIDE)
    features = time_features(times).astype(NARROW)
    temporal = dense(features, p.time_weight) + p.time_bias.astype(WIDE)
    level = alpha_level(times)[..., None]
    noisy = (jnp.sqrt(level) * clean.astype(WIDE) + jnp.sqrt(1.0 - level) * noise).astype(NARROW)
    hidden_in = dense(noisy, p.input_weight) + p.input_bias.astype(WIDE)
    joined = temporal + cond[None]
    signal = jax.nn.silu(joined).astype(NARROW)
    modulation = dense(signal, p.ada_weight) + p.ada_bias.astype(WIDE)
    normed = layer_norm(hidden_in, p.head_gain.astype(WIDE), p.head_shift.astype(WIDE))
    modulated = (normed * (1.0 + modulation[..., HW : 2 * HW]) + modulation[..., :HW]).astype(NARROW)
    inner = dense(modulated, p.inner_weight) + p.inner_bias.astype(WIDE)
    active = jax.nn.silu(inner).astype(NARROW)
    outer = dense(active, p.outer_weight) + p.outer_bias.astype(WIDE)
    hidden = hidden_in + modulation[..., 2 * HW :] * outer
    final = layer_norm(hidden, 1.0, 0.0).astype(NARROW)
    predicted = dense(final, p.final_weight) + p.final_bias.astype(WIDE)
    error = predicted - noise
    marks = filled.astype(WIDE)
    loss_part = jnp.sum(jnp.sum(error * error, -1) * marks)
    pred_grad = 2.0 * error * marks[:, None] / divisor
    pred_low = pred_grad.astype(NARROW)
    hidden_grad = jax.vjp(lambda value: layer_norm(value, 1.0, 0.0), hidden)[1](back_input(pred_low, p.final_weight))[0]
    gate_grad = hidden_grad * outer
    outer_grad = hidden_grad * modulation[..., 2 * HW :]
    outer_low = outer_grad.astype(NARROW)
    inner_grad = jax.vjp(jax.nn.silu, inner)[1](back_input(outer_low, p.outer_weight))[0]
    inner_low = inner_grad.astype(NARROW)
    mod_grad = back_input(inner_low, p.inner_weight)
    pull = norm_pull(hidden_in, p.head_gain, p.head_shift)
    norm_grad, head_gain, head_shift = pull(mod_grad * (1.0 + modulation[..., HW : 2 * HW]))
    hidden_grad = hidden_grad + norm_grad
    modulation_grad = jnp.concatenate([mod_grad, mod_grad * normed, gate_grad], -1)
    modulation_low = modulation_grad.astype(NARROW)
    signal_grad = back_input(modulation_low, p.ada_weight)
    joined_grad = jax.vjp(jax.nn.silu, joined)[1](signal_grad)[0]
    joined_low = joined_grad.astype(NARROW)
    cond_grad = jnp.sum(joined_grad, 0)
    cond_low = cond_grad.astype(NARROW)
    hidden_low = hidden_grad.astype(NARROW)
    grads = dict(
        final_weight=weight_grad(final, pred_low), final_bias=rows_sum(pred_grad),
        outer_weight=weight_grad(active, outer_low), outer_bias=rows_sum(outer_grad),
        inner_weight=weight_grad(modulated, inner_low), inner_bias=rows_sum(inner_grad),
        head_gain=head_gain, head_shift=head_shift,
        ada_weight=weight_grad(signal, modulation_low), ada_bias=rows_sum(modulation_grad),
        time_weight=weight_grad(features, joined_low), time_bias=rows_sum(joined_grad),
        cond_weight=weight_grad(conditions, cond_low), cond_bias=rows_sum(cond_grad),
        input_weight=weight_grad(noisy, hidden_low), input_bias=rows_sum(hidden_grad),
    )
    return loss_part, grads, back_input(cond_low, p.cond_weight)


def exchange(payload, parts):
    shape = payload.shape
    moved = lax.all_to_all(payload.reshape(parts, -1, shape[-1]), "dp", split_axis=0, concat_axis=0, tiled=True)
    return moved.reshape(shape)


def body(latents, route, labels, timesteps, noise, image_weight, weights, momentum, average):
    ranks_dp, ranks_rep = lax.axis_size("dp"), lax.axis_size("rep")
    ranks = ranks_dp * ranks_rep
    meshed = (ranks_dp, ranks_rep) == (8, 4)
    rows = route.shape[0]
    images = labels.shape[0]
    assert images == 1 and rows == SEQ
    size = weights.shape[0] // LANES
    padded = -(-(size + 1) // 48) * 48
    masked = route < rows
    own = jnp.sum(masked.astype(WIDE))
    low = weights.reshape(size, LANES).astype(NARROW)
    extra = jnp.full((padded - size, LANES), own).astype(NARROW)
    block = jnp.concatenate([low, extra], 0)
    gathered = spread(block) if meshed else lax.all_gather(block, BOTH, axis=0)
    base, enc, mid, dec, head = unpack(gathered, size)
    count = jnp.sum(gathered[:, size, 0].astype(WIDE))
    keep = jnp.concatenate([jnp.ones((BUF,), bool), ~masked])
    tokens = dense(latents, base.embed_weight) + base.embed_bias.astype(WIDE)
    at = next(e.start for e in ENTRIES if e.sparse) + labels[0] * (D // LANES) + jnp.arange(D // LANES, dtype=jnp.int32)
    classes = gathered[at // size, at % size].reshape(1, D).astype(WIDE)
    stream = jnp.concatenate([jnp.broadcast_to(classes, (BUF, D)), tokens], 0) + base.encoder_pos.astype(WIDE)
    stream, enc_stored = block_forward(stream, keep, enc)
    encoded = layer_norm(stream, mid.enc_gain.astype(WIDE), mid.enc_shift.astype(WIDE)).astype(NARROW)
    decoded = dense(encoded, mid.dec_weight) + mid.dec_bias.astype(WIDE)
    decoded = jnp.where(keep[:, None], decoded, mid.mask_token.astype(WIDE))
    before = decoded + mid.decoder_pos.astype(WIDE)
    flow_out, dec_stored = block_forward(before, None, dec)
    after = layer_norm(flow_out, head.dec_gain.astype(WIDE), head.dec_shift.astype(WIDE))
    conditions = (after[BUF:] + head.diffusion_pos.astype(WIDE)).astype(NARROW)
    token_weight = jnp.broadcast_to(image_weight.astype(NARROW)[:, None], (rows, 1))
    payload = jnp.concatenate([conditions, latents, token_weight, jnp.zeros((rows, LANES - TOK_CH - 1), NARROW)], 1)
    picks = (jnp.arange(rows, dtype=jnp.int32)[:, None] == route[None, :]).astype(NARROW)
    arrived = exchange(dense(picks, payload).astype(NARROW), ranks_dp)
    divisor = TOK_CH * COPIES * count
    loss_part, head_grads, cond_back = head_pass(
        head, arrived[:, :D], arrived[:, D : D + TOK_CH], arrived[:, D + TOK_CH], timesteps, noise, divisor
    )
    returned = exchange(cond_back.astype(NARROW), ranks_dp)
    token_grad = lax.dot_general(picks, returned, (((0,), (0,)), ((), ())), preferred_element_type=WIDE)
    after_grad = jnp.concatenate([jnp.zeros((BUF, D), WIDE), token_grad], 0)
    flow_grad, dec_gain, dec_shift = norm_pull(flow_out, head.dec_gain, head.dec_shift)(after_grad)
    head_grads.update(diffusion_pos=token_grad, dec_gain=dec_gain, dec_shift=dec_shift)
    before_grad, dec_grads = block_backward(flow_grad, None, dec, dec_stored)
    decoded_grad = jnp.where(keep[:, None], before_grad, 0.0)
    decoded_low = decoded_grad.astype(NARROW)
    pull = norm_pull(stream, mid.enc_gain, mid.enc_shift)
    stream_grad, enc_gain, enc_shift = pull(back_input(decoded_low, mid.dec_weight))
    mid_grads = dict(
        enc_gain=enc_gain, enc_shift=enc_shift, dec_weight=weight_grad(encoded, decoded_low), dec_bias=rows_sum(decoded_grad),
        mask_token=rows_sum(jnp.where(keep[:, None], 0.0, before_grad)), decoder_pos=before_grad,
    )
    stream_grad, enc_grads = block_backward(stream_grad, keep, enc, enc_stored)
    token_in = stream_grad[BUF:]
    base_grads = dict(
        encoder_pos=stream_grad,
        class_table=jnp.sum(stream_grad[:BUF], 0, keepdims=True),
        embed_weight=weight_grad(latents, token_in.astype(NARROW)), embed_bias=rows_sum(token_in),
    )
    grads = {}
    for group, found in enumerate((base_grads, enc_grads, mid_grads, dec_grads, head_grads)):
        grads.update({(group, name): value for name, value in found.items()})
    height = -(-((ranks - 1) * size + padded) // 8) * 8
    full = fold(grads, labels, height)
    if meshed:
        lane = lax.broadcasted_iota(jnp.int32, (8, LANES), 1)
        mark = jnp.where(lane == lax.axis_index("dp") * ranks_rep + lax.axis_index("rep"), loss_part, 0.0)
        owned = collect(full, mark, size, padded)
        loss = jnp.sum(owned[padded - 8, :ranks]) / divisor
        owned = owned[:size]
    else:
        loss = lax.psum(loss_part, BOTH) / divisor
        owned = lax.psum_scatter(full[: ranks * size].reshape(ranks, size, LANES), BOTH, scatter_dimension=0, tiled=False)
    owned = owned.reshape(-1)
    rate = 0.05 * math.sqrt(images * ranks * SEQ)
    new_momentum = 0.9 * momentum + owned
    new_weights = weights - rate * (owned + 0.9 * new_momentum)
    new_average = 0.75 * average + 0.25 * new_weights
    return new_weights, new_momentum, new_average, loss


def solution(mesh):
    flat = P(BOTH)
    placed = (P(BOTH, None), flat, flat, P(None, BOTH), P(None, BOTH, None), flat, flat, flat, flat)
    return jax.shard_map(body, mesh=mesh, in_specs=placed, out_specs=(flat, flat, flat, P()), check_vma=False)
```

```python
import functools
import heapq
import math
import types

import jax
import jax.numpy as jnp
from jax import lax
from jax.experimental import pallas as pl
from jax.experimental.pallas import tpu as pltpu
from jax.sharding import PartitionSpec as P

D = 768
HEADS = 12
HEAD_DIM = 64
MLP = 3072
HW = 1024
TOK_CH = 16
FREQ = 256
CLASSES = 1000
BUF = 64
SEQ = 256
COPIES = 4
STEPS_T = 1000
LANES = 128
WIDE = jnp.float32
NARROW = jnp.bfloat16
NORM_EPS = 1e-06
MESH = pl.DeviceIdType.MESH
ANY = pl.BlockSpec(memory_space=pl.ANY)
DMA = pltpu.SemaphoreType.DMA
BOTH = ("dp", "rep")


def block_shapes():
    return dict(
        norm_one_gain=(D,), norm_one_shift=(D,), attn_weight=(D, 3 * D), attn_bias=(2 * D,),
        proj_weight=(D, D), proj_bias=(D,), norm_two_gain=(D,), norm_two_shift=(D,),
        fc_one_weight=(D, MLP), fc_one_bias=(MLP,), fc_two_weight=(MLP, D), fc_two_bias=(D,),
    )


ENC, DEC = 1, 3
GROUPS = (
    dict(embed_weight=(TOK_CH, D), embed_bias=(D,), class_table=(CLASSES, D), encoder_pos=(BUF + SEQ, D)),
    block_shapes(),
    dict(enc_gain=(D,), enc_shift=(D,), dec_weight=(D, D), dec_bias=(D,), mask_token=(D,), decoder_pos=(BUF + SEQ, D)),
    block_shapes(),
    dict(
        dec_gain=(D,), dec_shift=(D,), diffusion_pos=(SEQ, D), input_weight=(TOK_CH, HW), input_bias=(HW,),
        time_weight=(FREQ, HW), time_bias=(HW,), cond_weight=(D, HW), cond_bias=(HW,), head_gain=(HW,),
        head_shift=(HW,), ada_weight=(HW, 3 * HW), ada_bias=(3 * HW,), inner_weight=(HW, HW), inner_bias=(HW,),
        outer_weight=(HW, HW), outer_bias=(HW,), final_weight=(HW, TOK_CH), final_bias=(TOK_CH,),
    ),
)


class Entry:
    def __init__(self, group, name, shape, start):
        self.group, self.name, self.shape, self.start = group, name, shape, start
        self.rows = -(-math.prod(shape) // LANES)
        self.matrix = len(shape) == 2 and shape[1] % LANES == 0
        self.across = shape[1] // LANES if self.matrix else 1
        self.sparse = name == GROUP_SPARSE


GROUP_SPARSE = next(name for name, shape in GROUPS[0].items() if shape[0] == CLASSES)


def entries():
    found, start = [], 0
    for group, shapes in enumerate(GROUPS):
        for name, shape in shapes.items():
            found.append(Entry(group, name, shape, start))
            start += found[-1].rows
    return found


ENTRIES = entries()
USED = ENTRIES[-1].start + ENTRIES[-1].rows


def block_height(entry, limit):
    best = 0
    for height in range(8, entry.shape[0] + 1, 8):
        if entry.shape[0] % height == 0 and height * entry.across <= limit:
            best = height
    return best


class Slots:
    def __init__(self, number):
        self.number, self.base, self.last = number, 0, {}

    def at(self, b):
        return (self.base + b) % self.number

    def claim(self, b, put):
        for k in range(self.number):
            before = self.last.get((self.base + k) % self.number)
            if before is not None:

                @pl.when(b == k)
                def _(before=before):
                    before().wait()

        @pl.when(b >= self.number)
        def _():
            put(b - self.number).wait()

    def close(self, blocks, put):
        base = self.base
        for b in range(max(0, blocks - self.number), blocks):
            self.last[(base + b) % self.number] = functools.partial(put, b)
        self.base = base + blocks

    def drain(self):
        for before in self.last.values():
            before().wait()


SLOTS = 4


def unfold_kernel(rows, padded, items, g_ref, *refs):
    count = len(items)
    outs = refs[:count]
    first, second, wide, first_sem, second_sem, out_sem = refs[count : count + 6]
    kinds = sorted({(h, e.across) for e, h in items})
    stages = dict(zip(kinds, refs[count + 6 :]))
    turns = {kind: Slots(2) for kind in kinds}
    bases = [0]
    for entry, height in items:
        bases.append(bases[-1] + entry.shape[0] // height)

    def spot(t, b):
        entry, height = items[t]
        span = height * entry.across
        start = entry.start + b * span
        dev = start // rows
        row = start - dev * rows
        low = jnp.minimum(row // 8 * 8, padded - span - 8)
        return dev, row, low, row + span > rows

    def copies(t, b):
        entry, height = items[t]
        window = height * entry.across + 8
        dev, row, low, more = spot(t, b)
        slot = (bases[t] + b) % SLOTS
        one = pltpu.make_async_copy(
            g_ref.at[dev, pl.ds(pl.multiple_of(low, 8), window)], first.at[slot, pl.ds(0, window)], first_sem.at[slot]
        )
        two = pltpu.make_async_copy(
            g_ref.at[jnp.minimum(dev + 1, g_ref.shape[0] - 1), pl.ds(0, window)],
            second.at[slot, pl.ds(0, window)], second_sem.at[slot],
        )
        return one, two, more

    def fetch(t, b):
        one, two, more = copies(t, b)
        one.start()

        @pl.when(more)
        def _():
            two.start()

    def fetch_number(g):
        if g < bases[-1]:
            t = next(t for t in range(count) if g < bases[t + 1])
            fetch(t, g - bases[t])

    ahead = SLOTS - 1
    for g in range(ahead):
        fetch_number(g)
    for t, (entry, height) in enumerate(items):
        kind = (height, entry.across)
        stage, turn = stages[kind], turns[kind]
        window = height * entry.across + 8
        blocks = entry.shape[0] // height

        def put(b, t=t, stage=stage, height=height, place=turn.base, kind=kind):
            slot = (place + b) % 2
            return pltpu.make_async_copy(
                stage.at[slot], outs[t].at[pl.ds(pl.multiple_of(b * height, 8), height)], out_sem.at[kinds.index(kind), slot]
            )

        def body(b, carry, t=t, entry=entry, height=height, window=window, blocks=blocks, stage=stage, turn=turn, put=put):
            @pl.when(b + ahead < blocks)
            def _():
                fetch(t, b + ahead)

            for k in range(max(0, ahead - blocks), ahead):

                @pl.when(b == blocks - ahead + k)
                def _(k=k):
                    fetch_number(bases[t + 1] + k)

            dev, row, low, _ = spot(t, b)
            slot = (bases[t] + b) % SLOTS
            one, two, more = copies(t, b)
            one.wait()
            wide[pl.ds(0, window), :] = first[slot, pl.ds(0, window), :].astype(WIDE)

            @pl.when(more)
            def _():
                two.wait()
                wide[pl.ds(rows - low, window), :] = second[slot, pl.ds(0, window), :].astype(WIDE)

            turn.claim(b, put)
            off = row - low
            place = turn.at(b)
            for j in range(entry.across):
                stage[place, :, j * LANES : (j + 1) * LANES] = wide[pl.ds(off + j, height, stride=entry.across), :].astype(NARROW)
            put(b).start()
            return carry

        lax.fori_loop(0, blocks, body, 0)
        turn.close(blocks, put)
    for turn in turns.values():
        turn.drain()


def unfold(gathered, rows):
    padded = gathered.shape[1]
    items = [(e, block_height(e, min(2304, rows - 16))) for e in ENTRIES if e.matrix and not e.sparse]
    tall = max(e.across * h for e, h in items) + 8
    kinds = sorted({(h, e.across) for e, h in items})
    total = sum(math.prod(e.shape) for e, _ in items)
    outs = pl.pallas_call(
        functools.partial(unfold_kernel, rows, padded, items),
        out_shape=[jax.ShapeDtypeStruct(e.shape, NARROW) for e, _ in items],
        in_specs=[ANY],
        out_specs=[ANY] * len(items),
        scratch_shapes=[
            pltpu.VMEM((SLOTS, tall, LANES), NARROW), pltpu.VMEM((SLOTS, tall, LANES), NARROW),
            pltpu.VMEM((2 * tall, LANES), WIDE), DMA((SLOTS,)), DMA((SLOTS,)), DMA((len(kinds), 2)),
        ]
        + [pltpu.VMEM((2, h, n * LANES), NARROW) for h, n in kinds],
        compiler_params=pltpu.CompilerParams(vmem_limit_bytes=48 * 1000 * 1000),
        cost_estimate=pl.CostEstimate(flops=total, bytes_accessed=4 * total, transcendentals=0),
    )(gathered)
    return {(e.group, e.name): out for (e, _), out in zip(items, outs)}


def rows_at(gathered, rows, start, number):
    pieces = []
    while number > 0:
        dev, row = divmod(start, rows)
        take = min(number, rows - row)
        pieces.append(gathered[dev, row : row + take])
        start, number = start + take, number - take
    return pieces[0] if len(pieces) == 1 else jnp.concatenate(pieces, 0)


def unpack(gathered, rows):
    matrices = unfold(gathered, rows)
    groups = [types.SimpleNamespace() for _ in GROUPS]
    for e in ENTRIES:
        if e.sparse:
            continue
        if e.matrix:
            value = matrices[(e.group, e.name)]
        else:
            value = rows_at(gathered, rows, e.start, e.rows).reshape(-1)[: math.prod(e.shape)].reshape(e.shape)
        setattr(groups[e.group], e.name, value)
    return groups


DEPTH = 3
TALL = 256
CHUNK = 512
NEXT = 3


def product_height(entry):
    return min(TALL, entry.shape[0])


def fold_kernel(products, items, plain, label, row, *refs):
    refs = list(refs)

    def take(number):
        found, refs[:number] = refs[:number], []
        return found

    pairs = take(2 * len(products))
    given = take(len(items))
    rest = take(len(plain))
    (full,) = take(1)
    pair_sem, given_sem, plain_sem, out_sem = take(4)
    held = take(2 * len(products))
    loads = take(len(items))
    (stage,) = take(1)
    gets = [pltpu.make_async_copy(given[i], loads[i], given_sem.at[i]) for i in range(len(items))]
    fills = [pltpu.make_async_copy(pairs[i], held[i], pair_sem.at[i]) for i in range(len(pairs))]
    for move in gets + fills[: 2 * NEXT]:
        move.start()
    moves = []
    for i, (start, number) in enumerate(plain):
        move = pltpu.make_async_copy(rest[i].at[pl.ds(0, number)], full.at[pl.ds(start, number)], plain_sem.at[i])
        move.start()
        moves.append(move)
    turn = Slots(DEPTH)

    def each(entry, height, make):
        span = height * entry.across
        blocks = entry.shape[0] // height

        def put(b, base=turn.base):
            slot = (base + b) % DEPTH
            return pltpu.make_async_copy(
                stage.at[slot, pl.ds(0, span)], full.at[pl.ds(entry.start + b * span, span)], out_sem.at[slot]
            )

        def step(b, carry):
            turn.claim(b, put)
            make(b, turn.at(b))
            put(b).start()
            return carry

        lax.fori_loop(0, blocks, step, 0)
        turn.close(blocks, put)

    sparse = next(e for e in ENTRIES if e.sparse)
    height = block_height(sparse, 1200)

    def lone(b, slot):
        here = lax.broadcasted_iota(jnp.int32, (height, LANES), 0) + b * height == label[0]
        for j in range(sparse.across):
            value = jnp.broadcast_to(row[0:1, j * LANES : (j + 1) * LANES], (height, LANES))
            stage[slot, pl.ds(j, height, stride=sparse.across), :] = jnp.where(here, value, 0.0)

    each(sparse, height, lone)
    for t, entry in enumerate(items):
        gets[t].wait()

        def make(b, slot, t=t, entry=entry):
            for j in range(entry.across):
                stage[slot, pl.ds(j, entry.shape[0], stride=entry.across), :] = loads[t][:, j * LANES : (j + 1) * LANES]

        each(entry, entry.shape[0], make)
    for t, entry in enumerate(products):
        left, right = held[2 * t], held[2 * t + 1]
        for move in fills[2 * (t + NEXT) : 2 * (t + NEXT) + 2]:
            move.start()
        fills[2 * t].wait()
        fills[2 * t + 1].wait()
        height = product_height(entry)
        chunk = math.gcd(CHUNK, entry.shape[1])

        def make(b, slot, left=left, right=right, entry=entry, height=height, chunk=chunk):
            turned = left[:, pl.ds(pl.multiple_of(b * height, LANES), height)].T
            for k in range(entry.shape[1] // chunk):
                found = jnp.dot(turned, right[:, k * chunk : (k + 1) * chunk], preferred_element_type=WIDE)
                for j in range(chunk // LANES):
                    at = pl.ds(k * (chunk // LANES) + j, height, stride=entry.across)
                    stage[slot, at, :] = found[:, j * LANES : (j + 1) * LANES]

        each(entry, height, make)
    turn.drain()
    for move in moves:
        move.wait()


def fold(grads, label, height_total):
    found = {e: grads[(e.group, e.name)] for e in ENTRIES}
    products = [e for e in ENTRIES if isinstance(found[e], tuple)]
    items = [e for e in ENTRIES if e.matrix and not e.sparse and e not in products]
    plain, values = [], []
    for e in ENTRIES:
        if e.matrix:
            continue
        value = found[e].reshape(-1)
        value = jnp.pad(value, (0, e.rows * LANES - value.shape[0]))
        plain.append((e.start, e.rows))
        values.append(value.reshape(e.rows, LANES))
    if height_total > USED:
        plain.append((USED, height_total - USED))
        values.append(jnp.zeros((height_total - USED, LANES), WIDE))
    row = next(found[e] for e in ENTRIES if e.sparse)
    operands = [x.reshape(-1, x.shape[-1]) for e in products for x in found[e]]
    tall = max([e.rows for e in items] + [e.across * product_height(e) for e in products])
    total = height_total * LANES
    flops = sum(2 * math.prod(e.shape) * operands[2 * i].shape[0] for i, e in enumerate(products))
    return pl.pallas_call(
        functools.partial(fold_kernel, products, items, plain),
        out_shape=jax.ShapeDtypeStruct((height_total, LANES), WIDE),
        in_specs=[pl.BlockSpec(memory_space=pltpu.SMEM), pl.BlockSpec(memory_space=pltpu.VMEM)]
        + [ANY] * (len(operands) + len(items) + len(plain)),
        out_specs=ANY,
        scratch_shapes=[DMA((len(operands),)), DMA((len(items),)), DMA((len(plain),)), DMA((DEPTH,))]
        + [pltpu.VMEM(x.shape, x.dtype) for x in operands]
        + [pltpu.VMEM(e.shape, WIDE) for e in items]
        + [pltpu.VMEM((DEPTH, tall, LANES), WIDE)],
        compiler_params=pltpu.CompilerParams(vmem_limit_bytes=62 * 1000 * 1000),
        cost_estimate=pl.CostEstimate(flops=flops, bytes_accessed=4 * total, transcendentals=0),
    )(label, jnp.broadcast_to(row, (8, row.shape[-1])), *operands, *[found[e] for e in items], *values)


X, Y, Z = 0, 1, 2
TREES = ((Z, X, Y), (Z, Y, X), (X, Z, Y), (X, Z, Y), (Y, Z, X), (Y, Z, X))
SHARES = len(TREES)
FAR = 3


def onward(order, arrived, way, p):
    z, x, y = p
    found = []
    if arrived >= 0 and order[arrived] == Z and 0 <= z + way <= FAR:
        found.append(((z + way, x, y), arrived, way))
    for j in range(arrived + 1, 3):
        if order[j] == X:
            found.append(((z, 1 - x, y), j, 0))
        elif order[j] == Y:
            found.append(((z, x, 1 - y), j, 0))
        else:
            found += [((z + s, x, y), j, s) for s in (1, -1) if 0 <= z + s <= FAR]
    return found


@functools.cache
def flow(lag=0.4):
    chips = [(z, x, y) for z in range(FAR + 1) for x in range(2) for y in range(2)]
    events, queues, busy, come, sent = [], {}, set(), {}, []
    number = iter(range(10**9))
    for u in range(SHARES):
        for p in chips:
            heapq.heappush(events, (0.0, next(number), 0, (p, p, u, -1, 0)))

    def pump(link, t):
        if link in busy or not queues.get(link):
            return
        what = heapq.heappop(queues[link])[2]
        busy.add(link)
        sent.append((t, link, what[1], what[2]))
        heapq.heappush(events, (t + 1.0, next(number), 1, (link, what)))

    while events:
        t, _, kind, what = heapq.heappop(events)
        if kind == 1:
            link, piece = what
            busy.discard(link)
            heapq.heappush(events, (t + lag, next(number), 0, piece))
            pump(link, t)
            continue
        p, q, u, k, way = what
        come[(u, p, q)] = t
        for to, k2, way2 in onward(TREES[u], k, way, p):
            left = len(onward(TREES[u], k2, way2, to))
            heapq.heappush(queues.setdefault((p, to), []), ((-left, t), next(number), (to, q, u, k2, way2)))
            pump((p, to), t)
    return come, sent


def spread_order():
    keyed = {}
    for (u, p, q), t in flow()[0].items():
        keyed.setdefault((u, q[0] - p[0], (q[1] - p[1]) % 2, (q[2] - p[2]) % 2), []).append(t)
    return sorted(keyed, key=lambda k: (sum(keyed[k]) / len(keyed[k]), k))


def last_hop(u, dz, dx, dy):
    apart = [k for k in range(3) if (dx, dy, dz)[TREES[u][k]] != 0]
    return apart[-1] if apart else -1


def hops(u, dz, dx, dy):
    order, arrived = TREES[u], last_hop(u, dz, dx, dy)
    found = []
    if arrived >= 0 and order[arrived] == Z:
        found.append((1, 0, 0) if dz < 0 else (-1, 0, 0))
    for k in range(arrived + 1, 3):
        found += [[(0, 1, 0)], [(0, 0, 1)], [(1, 0, 0), (-1, 0, 0)]][order[k]]
    return found


def only(condition, action):
    if condition is None:
        action()
    else:
        pl.when(condition)(action)


def spread_kernel(own, out, keep_sem, send_sem, link_sem, core_send, core_sem):
    dp, rep = lax.axis_index("dp"), lax.axis_index("rep")
    z, x, y, c = dp // 2, dp % 2, rep // 2, rep % 2
    unit = own.shape[0] // SHARES
    sibling = (dp, y * 2 + 1 - c)

    def device(dz, dx, dy):
        return ((z + dz) * 2 + (x + dx) % 2, (y + dy) % 2 * 2 + c)

    def exists(dz):
        return None if dz == 0 else (z + dz >= 0 if dz < 0 else z + dz <= FAR)

    barrier = pltpu.get_barrier_semaphore()
    near = ((0, 1, 0), (0, 0, 1), (1, 0, 0), (-1, 0, 0))
    for hop in near:
        only(exists(hop[0]), lambda: pl.semaphore_signal(barrier, inc=1, device_id=device(*hop), device_id_type=MESH))
    pl.semaphore_signal(barrier, inc=1, device_id=sibling, device_id_type=MESH)
    inner = z * (FAR - z)
    only(inner == 0, lambda: pl.semaphore_wait(barrier, len(near)))
    only(inner > 0, lambda: pl.semaphore_wait(barrier, len(near) + 1))
    keep = pltpu.make_async_copy(own, out.at[dp * 4 + rep], keep_sem)
    keep.start()
    ends, number = [], 0
    for u, dz, dx, dy in spread_order():
        part = pl.ds(u * unit, unit)
        q = ((z + dz) * 2 + (x + dx) % 2) * 2 + (y + dy) % 2
        mine = dz == 0 and dx == 0 and dy == 0
        i = u * 16 + q

        def copy(to, send, come, part=part, q=q, mine=mine):
            here = out.at[q * 2 + c, part]
            return pltpu.make_async_remote_copy(
                own.at[part] if mine else here, here, send, come, device_id=to, device_id_type=MESH
            )

        goes = [(hop, number + k) for k, hop in enumerate(hops(u, dz, dx, dy))]
        number += len(goes)

        def run(i=i, copy=copy, goes=goes, mine=mine):
            if not mine:
                copy(sibling, send_sem.at[0], link_sem.at[i]).wait_recv()
            for hop, n in goes:
                only(exists(hop[0]), lambda: copy(device(*hop), send_sem.at[n], link_sem.at[i]).start())
            copy(sibling, core_send.at[i], core_sem.at[i]).start()

        def finish(i=i, copy=copy, goes=goes):
            for hop, n in goes:
                only(exists(hop[0]), lambda: copy(device(*hop), send_sem.at[n], link_sem.at[i]).wait_send())
            copy(sibling, core_send.at[i], core_sem.at[i]).wait()

        there = None if dz == 0 else jnp.logical_and(z + dz >= 0, z + dz <= FAR)
        only(there, run)
        ends.append((there, finish))
    for there, finish in ends:
        only(there, finish)
    keep.wait()


def spread(own):
    pieces = SHARES * 16
    sends = sum(len(hops(*key)) for key in spread_order())
    return pl.pallas_call(
        spread_kernel,
        out_shape=jax.ShapeDtypeStruct((32,) + own.shape, own.dtype),
        in_specs=[ANY],
        out_specs=ANY,
        scratch_shapes=[DMA, DMA((sends,)), DMA((pieces,)), DMA((pieces,)), DMA((pieces,))],
        compiler_params=pltpu.CompilerParams(collective_id=0, has_side_effects=True),
    )(own)


class Chip:
    def __init__(self, low):
        dp, rep = lax.axis_index("dp"), lax.axis_index("rep")
        self.low = low
        self.z, self.x, self.y, self.c = dp // 2, dp % 2, rep // 2, rep % 2
        self.way = 1 - 2 * (self.z // 2)

    def device(self, q, other=0):
        z = self.z + self.way * (q[0] - self.low)
        return z * 2 + (self.x + q[1]) % 2, (self.y + q[2]) % 2 * 2 + (self.c + other) % 2

    def block(self, q, other=0):
        dp, rep = self.device(q, other)
        return dp * 4 + rep

    def greet(self):
        low = self.low
        near = [(low, 1, 0), (low, 0, 1), (low + 1, 0, 0)] + ([(low - 1, 0, 0)] if low else [])
        barrier = pltpu.get_barrier_semaphore()
        for q in near:
            pl.semaphore_signal(barrier, inc=1, device_id=self.device(q), device_id_type=MESH)
        pl.semaphore_signal(barrier, inc=1, device_id=self.device((low, 0, 0), 1), device_id_type=MESH)
        pl.semaphore_wait(barrier, len(near) + 1)


def seen_from(p, r):
    low, way = min(p[0], FAR - p[0]), 1 if p[0] < 2 else -1
    return low + way * (r[0] - p[0]), (r[1] - p[1]) % 2, (r[2] - p[2]) % 2


@functools.cache
def sum_programs():
    come, sent = flow()
    last = max(come.values())
    found = []
    for z in (0, 1):
        p = (z, 0, 0)
        kids, parent, when = {}, {}, {}
        for t, link, q, u in sent:
            if link[0] == p:
                kids.setdefault((u, q), []).append(link[1])
                if q == p:
                    when[(u, p)] = max(when.get((u, p), 0.0), last - t)
            if link[1] == p:
                parent[(u, q)] = link[0]
                when[(u, q)] = last - t - 1.0
        tasks = sorted(when, key=lambda k: (when[k], k))
        found.append([(u, q, sorted(kids.get((u, q), [])), parent.get((u, q))) for u, q in tasks])
    return found


@functools.cache
def landing():
    return [{key: i for i, key in enumerate((u, q, k) for u, q, kids, _ in tasks for k in kids)} for tasks in sum_programs()]


RING = 12
SIDE = 4
EARLY = 12
STEP = 40


def add_rows(into, terms):
    def body(i, carry):
        at = pl.ds(pl.multiple_of(i * STEP, 8), STEP)
        total = into[at, :]
        for term in terms:
            total = total + term[at, :]
        into[at, :] = total
        return carry

    lax.fori_loop(0, into.shape[0] // STEP, body, 0)


def collect_at(low, size, full, mark, out, aside, store, ring, side, ring_sem, side_sem, send_sem, link_sem, core_send, core_sem, out_sem, marks, mark_sem):
    chip = Chip(low)
    me = (low, 0, 0)
    tasks, spots = sum_programs()[low], landing()
    count, unit = len(tasks), ring.shape[1]
    chip.greet()

    def part(i, other=0):
        return full.at[pl.ds(chip.block(tasks[i][1], other) * size + tasks[i][0] * unit, unit)]

    def across(i):
        return pltpu.make_async_remote_copy(
            part(i, 1), aside.at[i], core_send.at[i], core_sem.at[i], device_id=chip.device(me, 1), device_id_type=MESH
        )

    def ours(i):
        return pltpu.make_async_copy(part(i), ring.at[i % RING], ring_sem.at[i % RING])

    def theirs(i):
        return pltpu.make_async_copy(aside.at[i], side.at[i % SIDE], side_sem.at[i % SIDE])

    def along(i, spot, to):
        return pltpu.make_async_remote_copy(
            ring.at[i % RING], store.at[spot], send_sem.at[i], link_sem.at[spot], device_id=chip.device(to), device_id_type=MESH
        )

    tail = pl.ds(unit - 8, 8)
    ours_too = pltpu.make_async_copy(mark, marks.at[0], mark_sem.at[0])
    theirs_too = pltpu.make_async_remote_copy(
        mark, marks.at[1], mark_sem.at[1], mark_sem.at[2], device_id=chip.device(me, 1), device_id_type=MESH
    )
    ours_too.start()
    theirs_too.start()
    leaving = {}

    def fetch(i):
        if i - RING in leaving:
            leaving.pop(i - RING)()
        ours(i).start()
        across(i).wait_recv()
        theirs(i).start()

    for i in range(EARLY):
        across(i).start()
    for i in range(SIDE - 1):
        fetch(i)
    ours_too.wait()
    theirs_too.wait()
    for i, (u, q, kids, to) in enumerate(tasks):
        if i + EARLY < count:
            across(i + EARLY).start()
        if i + SIDE - 1 < count:
            fetch(i + SIDE - 1)
        ours(i).wait()
        theirs(i).wait()
        if u == SHARES - 1:
            ring[i % RING, tail, :] = marks[0] + marks[1]
            side[i % SIDE, tail, :] = jnp.zeros((8, LANES), WIDE)
        terms = [side.at[i % SIDE]]
        for kid in kids:
            spot = spots[low][(u, q, kid)]
            along(i, spot, kid).wait_recv()
            terms.append(store.at[spot])
        add_rows(ring.at[i % RING], terms)
        if to is None:
            move = pltpu.make_async_copy(ring.at[i % RING], out.at[pl.ds(u * unit, unit)], out_sem.at[u])
            move.start()
            leaving[i] = move.wait
        else:
            move = along(i, spots[min(to[0], FAR - to[0])][(u, seen_from(to, q), seen_from(to, me))], to)
            move.start()
            leaving[i] = move.wait_send
    for i in list(leaving):
        leaving.pop(i)()
    for i in range(count):
        across(i).wait_send()


def collect_kernel(size, *refs):
    z = lax.axis_index("dp") // 2
    inner = z * (FAR - z)

    @pl.when(inner == 0)
    def _():
        collect_at(0, size, *refs)

    @pl.when(inner > 0)
    def _():
        collect_at(1, size, *refs)


def collect(full, mark, size, rows):
    slots = max(len(spots) for spots in landing())
    count, unit = len(sum_programs()[0]), rows // SHARES
    return pl.pallas_call(
        functools.partial(collect_kernel, size),
        out_shape=(jax.ShapeDtypeStruct((rows, LANES), WIDE), jax.ShapeDtypeStruct((count, unit, LANES), WIDE)),
        in_specs=[ANY, ANY],
        out_specs=(ANY, ANY),
        scratch_shapes=[
            pltpu.VMEM((slots, unit, LANES), WIDE), pltpu.VMEM((RING, unit, LANES), WIDE), pltpu.VMEM((SIDE, unit, LANES), WIDE),
            DMA((RING,)), DMA((SIDE,)), DMA((count,)), DMA((slots,)), DMA((count,)), DMA((count,)), DMA((SHARES,)),
            pltpu.VMEM((2, 8, LANES), WIDE), DMA((3,)),
        ],
        compiler_params=pltpu.CompilerParams(collective_id=1, has_side_effects=True, vmem_limit_bytes=62 * 1000 * 1000),
    )(full, mark)[0]


def layer_norm(value, gain, shift):
    centered = value - jnp.mean(value, -1, keepdims=True)
    scaled = centered * lax.rsqrt(jnp.mean(centered * centered, -1, keepdims=True) + NORM_EPS)
    return scaled * gain + shift


def dense(inputs, weight):
    return lax.dot_general(inputs, weight, (((inputs.ndim - 1,), (0,)), ((), ())), preferred_element_type=WIDE)


def back_input(grads_low, weight):
    return lax.dot_general(grads_low, weight, (((grads_low.ndim - 1,), (1,)), ((), ())), preferred_element_type=WIDE)


def weight_grad(inputs, grads_low):
    flat_in = inputs.reshape(-1, inputs.shape[-1])
    flat_grad = grads_low.reshape(-1, grads_low.shape[-1])
    if min(flat_in.shape[1], flat_grad.shape[1]) >= LANES:
        return flat_in, flat_grad
    return lax.dot_general(flat_in, flat_grad, (((0,), (0,)), ((), ())), preferred_element_type=WIDE)


def rows_sum(values):
    return jnp.sum(values.reshape(-1, values.shape[-1]), 0)


def norm_pull(value, gain, shift):
    return jax.vjp(layer_norm, value, gain.astype(WIDE), shift.astype(WIDE))[1]


HALF_ROOT = math.sqrt(0.5)
PDF = 1.0 / math.sqrt(2.0 * math.pi)
SCALE = HEAD_DIM ** (-0.5)
PART = 512


def column_sum(value):
    return jnp.sum(value, 0, keepdims=True)


def whiten(value):
    centered = value - jnp.mean(value, -1, keepdims=True)
    r = lax.rsqrt(jnp.mean(centered * centered, -1, keepdims=True) + NORM_EPS)
    return centered * r, r


def whiten_back(grad, hat, r):
    return r * (grad - jnp.mean(grad, -1, keepdims=True) - hat * jnp.mean(grad * hat, -1, keepdims=True))


def side_masks(length):
    lane = lax.broadcasted_iota(jnp.int32, (length, LANES), 1)
    return lane < HEAD_DIM, lane >= HEAD_DIM


def one_side(value, side):
    return jnp.where(side, value, jnp.zeros_like(value))


def start_all(sources, targets, sem):
    moves = [pltpu.make_async_copy(s, t, sem.at[i]) for i, (s, t) in enumerate(zip(sources, targets))]
    for move in moves:
        move.start()
    return moves


def forward_kernel(masked, stream, keep, wide_b, attn_b, fc_b, *refs):
    outs = refs[4:13]
    normed, mixed, totals, attended, middle, second, slope, active, output = outs
    attn_w, proj_w, one_w, two_w, sem = refs[13:]
    moves = start_all(refs[:4], (attn_w, proj_w, one_w, two_w), sem)
    hat, _ = whiten(stream[...])
    normed[...] = (hat * wide_b[0:1, :] + wide_b[1:2, :]).astype(NARROW)
    moves[0].wait()
    for k in range(3 * D // D):
        at = slice(k * D, (k + 1) * D)
        mixed[:, at] = (matmul(normed[...], attn_w[:, at]) + attn_b[0:1, at]).astype(NARROW)
    sides = side_masks(stream.shape[0])
    for pair in range(HEADS // 2):
        q, k, v = (mixed[:, part * D + pair * LANES : part * D + (pair + 1) * LANES] for part in range(3))
        found = None
        for i, side in enumerate(sides):
            scores = matmul_turned(one_side(q, side), k) * SCALE
            if masked:
                scores = jnp.where(keep[0:1, :] > 0.0, scores, -1e30)
            top = jnp.max(scores, -1, keepdims=True)
            powers = jnp.exp(scores - top)
            total = jnp.sum(powers, -1, keepdims=True)
            totals[:, 2 * pair + i : 2 * pair + i + 1] = top + jnp.log(total)
            probs = (powers * (1.0 / total)).astype(NARROW)
            part = matmul(probs, one_side(v, side))
            found = part if found is None else found + part
        attended[:, pair * LANES : (pair + 1) * LANES] = found.astype(NARROW)
    moves[1].wait()
    value = stream[...] + matmul(attended[...], proj_w[...]) + wide_b[4:5, :]
    middle[...] = value
    hat, _ = whiten(value)
    second[...] = (hat * wide_b[2:3, :] + wide_b[3:4, :]).astype(NARROW)
    moves[2].wait()
    for k in range(MLP // PART):
        at = slice(k * PART, (k + 1) * PART)
        value = matmul(second[...], one_w[:, at]) + fc_b[0:1, at]
        share = 0.5 + 0.5 * lax.erf(value * HALF_ROOT)
        active[:, at] = (value * share).astype(NARROW)
        slope[:, at] = share + value * (PDF * jnp.exp(-0.5 * value * value))
    moves[3].wait()
    output[...] = middle[...] + matmul(active[...], two_w[...]) + wide_b[5:6, :]


def block_vectors(p):
    rows = (p.norm_one_gain, p.norm_one_shift, p.norm_two_gain, p.norm_two_shift, p.proj_bias, p.fc_two_bias)
    wide_b = jnp.stack(rows + rows[:2]).astype(WIDE)
    attn_b = jnp.concatenate([p.attn_bias[:D], jnp.zeros((D,), NARROW), p.attn_bias[D:]]).astype(WIDE)[None]
    return wide_b, attn_b, p.fc_one_bias.astype(WIDE)[None]


VMEM = pl.BlockSpec(memory_space=pltpu.VMEM)
BLOCK_WEIGHTS = ((D, 3 * D), (D, D), (D, MLP), (MLP, D))


def block_cost(length, passes):
    weights = sum(math.prod(s) for s in BLOCK_WEIGHTS)
    return pl.CostEstimate(flops=2 * passes * length * weights, bytes_accessed=2 * weights + 36 * length * D, transcendentals=4 * length * MLP)


def block_forward(stream, keep, p):
    length = stream.shape[0]
    shapes = [(D, NARROW), (3 * D, NARROW), (LANES, WIDE), (D, NARROW), (D, WIDE), (D, NARROW), (MLP, WIDE), (MLP, NARROW), (D, WIDE)]
    row = jnp.ones((1, length), WIDE) if keep is None else keep.astype(WIDE)[None]
    vectors = block_vectors(p)
    found = pl.pallas_call(
        functools.partial(forward_kernel, keep is not None),
        out_shape=[jax.ShapeDtypeStruct((length, w), t) for w, t in shapes],
        in_specs=[VMEM] * 5 + [ANY] * 4,
        out_specs=[VMEM] * len(shapes),
        scratch_shapes=[pltpu.VMEM(s, NARROW) for s in BLOCK_WEIGHTS] + [DMA((4,))],
        compiler_params=pltpu.CompilerParams(vmem_limit_bytes=60 * 1000 * 1000),
        cost_estimate=block_cost(length, 1),
    )(stream, row, *vectors, p.attn_weight, p.proj_weight, p.fc_one_weight, p.fc_two_weight)
    return found[-1], (stream, row, vectors[0]) + tuple(found[:-1])


def backward_kernel(masked, grad_out, stream, keep, wide_b, mixed, totals, middle, *refs):
    slope_in = refs[4]
    out_low, inner_low, middle_low, mixed_low, stream_grad, sums, one_sum, mixed_sum = refs[5:13]
    attn_w, proj_w, one_w, two_w, slope, attended_grad, sem = refs[13:]
    attn_src, proj_src, one_src, two_src = refs[:4]
    moves = start_all((two_src, slope_in, one_src, proj_src, attn_src), (two_w, slope, one_w, proj_w, attn_w), sem)
    value = grad_out[...]
    low = value.astype(NARROW)
    out_low[...] = low
    sums[0:1, :] = column_sum(value)
    moves[0].wait()
    moves[1].wait()
    for k in range(MLP // PART):
        at = slice(k * PART, (k + 1) * PART)
        part = matmul_turned(low, two_w[at, :]) * slope[:, at]
        inner_low[:, at] = part.astype(NARROW)
        one_sum[0:1, at] = column_sum(part)
    moves[2].wait()
    part = matmul_turned(inner_low[...], one_w[...])
    hat, r = whiten(middle[...])
    sums[1:2, :] = column_sum(part * hat)
    sums[2:3, :] = column_sum(part)
    value = value + whiten_back(part * wide_b[2:3, :], hat, r)
    stream_grad[...] = value
    sums[3:4, :] = column_sum(value)
    middle_low[...] = value.astype(NARROW)
    moves[3].wait()
    attended_grad[...] = matmul_turned(middle_low[...], proj_w[...]).astype(NARROW)
    sides = side_masks(stream.shape[0])
    for pair in range(HEADS // 2):
        here = [slice(part * D + pair * LANES, part * D + (pair + 1) * LANES) for part in range(3)]
        q, k, v = (mixed[:, at] for at in here)
        g = attended_grad[:, here[0]]
        grads = [None, None, None]
        for i, side in enumerate(sides):
            q_side, k_side, g_side = one_side(q, side), one_side(k, side), one_side(g, side)
            scores = matmul_turned(q_side, k) * SCALE
            if masked:
                scores = jnp.where(keep[0:1, :] > 0.0, scores, -1e30)
            probs = jnp.exp(scores - totals[:, 2 * pair + i : 2 * pair + i + 1])
            prob_grad = matmul_turned(g_side, v)
            score_grad = (probs * (prob_grad - jnp.sum(probs * prob_grad, -1, keepdims=True))).astype(NARROW)
            parts = (
                matmul(score_grad, k_side) * SCALE, matmul(score_grad.T, q_side) * SCALE, matmul(probs.astype(NARROW).T, g_side)
            )
            grads = [part if old is None else old + part for old, part in zip(grads, parts)]
        for at, part in zip(here, grads):
            mixed_low[:, at] = part.astype(NARROW)
            mixed_sum[0:1, at] = column_sum(part)
    moves[4].wait()
    part = matmul_turned(mixed_low[...], attn_w[...])
    hat, r = whiten(stream[...])
    sums[4:5, :] = column_sum(part * hat)
    sums[5:6, :] = column_sum(part)
    stream_grad[...] = stream_grad[...] + whiten_back(part * wide_b[0:1, :], hat, r)


def block_backward(grad_out, keep, p, saved):
    stream, row, wide_b, normed, mixed, totals, attended, middle, second, slope, active = saved
    length = stream.shape[0]
    shapes = [((length, D), NARROW), ((length, MLP), NARROW), ((length, D), NARROW), ((length, 3 * D), NARROW), ((length, D), WIDE)]
    shapes += [((8, D), WIDE), ((1, MLP), WIDE), ((1, 3 * D), WIDE)]
    out_low, inner_low, middle_low, mixed_low, stream_grad, sums, one_sum, mixed_sum = pl.pallas_call(
        functools.partial(backward_kernel, keep is not None),
        out_shape=[jax.ShapeDtypeStruct(s, t) for s, t in shapes],
        in_specs=[VMEM] * 7 + [ANY] * 5,
        out_specs=[VMEM] * len(shapes),
        scratch_shapes=[pltpu.VMEM(s, NARROW) for s in BLOCK_WEIGHTS]
        + [pltpu.VMEM((length, MLP), WIDE), pltpu.VMEM((length, D), NARROW), DMA((5,))],
        compiler_params=pltpu.CompilerParams(vmem_limit_bytes=60 * 1000 * 1000),
        cost_estimate=block_cost(length, 1),
    )(grad_out, stream, row, wide_b, mixed, totals, middle, p.attn_weight, p.proj_weight, p.fc_one_weight, p.fc_two_weight, slope)
    grads = dict(
        norm_one_gain=sums[4], norm_one_shift=sums[5], attn_weight=weight_grad(normed, mixed_low),
        attn_bias=jnp.concatenate([mixed_sum[0, :D], mixed_sum[0, 2 * D :]]), proj_weight=weight_grad(attended, middle_low),
        proj_bias=sums[3], norm_two_gain=sums[1], norm_two_shift=sums[2], fc_one_weight=weight_grad(second, inner_low),
        fc_one_bias=one_sum[0], fc_two_weight=weight_grad(active, out_low), fc_two_bias=sums[0],
    )
    return stream_grad, grads


def time_features(times):
    half = FREQ // 2
    freqs = jnp.exp(-math.log(10000.0) * jnp.arange(half, dtype=WIDE) / half)
    angles = times[..., None] * freqs
    return jnp.concatenate([jnp.cos(angles), jnp.sin(angles)], -1)


def alpha_level(times):
    start = math.cos(0.008 / 1.008 * math.pi / 2) ** 2
    return jnp.cos(((times + 1.0) / STEPS_T + 0.008) / 1.008 * math.pi / 2) ** 2 / start


ROWS = 256
TOGETHER = 1
SUMS = 9


def matmul(left, right):
    return jnp.dot(left, right, preferred_element_type=WIDE)


def matmul_turned(left, right):
    return lax.dot_general(left, right, (((1,), (1,)), ((), ())), preferred_element_type=WIDE)


def eighths(value):
    found = value[:8]
    for k in range(8, value.shape[0], 8):
        found = found + value[k : k + 8]
    return found


def sigmoid(value):
    return 0.5 + 0.5 * jnp.tanh(0.5 * value)


def silu_and_slope(value):
    s = sigmoid(value)
    silu = value * s
    return silu, s + silu * (1.0 - s)


def head_kernel(
    divisor, conditions, features, noisy, noise, marks,
    cond_w, time_w, input_w, ada_w, inner_w, outer_w, final_w, wide_b, ada_b, final_b,
    signal, mod_low, modulated, inner_low, active, outer_low, final, hidden_low, joined_low, error, sums, cond_low, cond_sum, cond_back,
    cond, joined, hidden, mod, hat, inner, outer, top, total, spread,
):
    step = pl.program_id(0)
    tile = joined.shape[0]
    count = tile // ROWS
    slots = total.shape[0]
    grad = hidden

    def rows(i):
        return pl.ds(pl.multiple_of(i * ROWS, ROWS), ROWS)

    def loop(action, *more):
        def one(i, carry):
            action(rows(i), *(rows(i % (slots // ROWS)) for _ in more))
            return carry

        lax.fori_loop(0, count, one, 0)

    def bias(k):
        return wide_b[k : k + 1, :]

    def add_sum(k, value):
        sums[k * 8 : (k + 1) * 8, :] = sums[k * 8 : (k + 1) * 8, :] + eighths(value)

    @pl.when(step == 0)
    def _():
        sums[...] = jnp.zeros_like(sums)
        total[...] = jnp.zeros_like(total)
        cond[...] = matmul(conditions[...], cond_w[...]) + bias(0)

    joined[...] = matmul(features[...], time_w[...])
    hidden[...] = matmul(noisy[...], input_w[...])

    def enter(at, slot):
        value, slope = silu_and_slope(joined[at, :] + bias(1) + cond[slot, :])
        joined[at, :] = slope
        signal[at, :] = value.astype(NARROW)
        h = hidden[at, :] + bias(2)
        hidden[at, :] = h
        centered = h - jnp.mean(h, -1, keepdims=True)
        r = lax.rsqrt(jnp.mean(centered * centered, -1, keepdims=True) + NORM_EPS)
        spread[at, 0:1] = r
        hat[at, :] = centered * r

    loop(enter, cond)
    mod[...] = matmul(signal[...], ada_w[...])

    def modulate(at):
        normed = hat[at, :] * bias(3) + bias(4)
        shift = mod[at, :HW] + ada_b[0:1, :HW]
        scale = 1.0 + (mod[at, HW : 2 * HW] + ada_b[0:1, HW : 2 * HW])
        mod[at, HW : 2 * HW] = scale
        modulated[at, :] = (normed * scale + shift).astype(NARROW)

    loop(modulate)
    inner[...] = matmul(modulated[...], inner_w[...])

    def activate(at):
        value, slope = silu_and_slope(inner[at, :] + bias(5))
        inner[at, :] = slope
        active[at, :] = value.astype(NARROW)

    loop(activate)
    outer[...] = matmul(active[...], outer_w[...])

    def leave(at):
        out = outer[at, :] + bias(6)
        outer[at, :] = out
        gate = mod[at, 2 * HW :] + ada_b[0:1, 2 * HW :]
        mod[at, 2 * HW :] = gate
        value = hidden[at, :] + gate * out
        centered = value - jnp.mean(value, -1, keepdims=True)
        r = lax.rsqrt(jnp.mean(centered * centered, -1, keepdims=True) + NORM_EPS)
        spread[at, 1:2] = r
        value = centered * r
        top[at, :] = value
        final[at, :] = value.astype(NARROW)

    loop(leave)
    off = matmul(final[...], final_w[...]) + final_b[0:1, :] - noise[...]
    error[...] = off
    pred_low = (2.0 * off * marks[...] / divisor[0]).astype(NARROW)
    grad[...] = matmul_turned(pred_low, final_w[...])

    def enter_back(at):
        g, value = grad[at, :], top[at, :]
        g = spread[at, 1:2] * (g - jnp.mean(g, -1, keepdims=True) - value * jnp.mean(g * value, -1, keepdims=True))
        grad[at, :] = g
        gate_grad = g * outer[at, :]
        mod_low[at, 2 * HW :] = gate_grad.astype(NARROW)
        add_sum(0, gate_grad)
        out_grad = g * mod[at, 2 * HW :]
        outer_low[at, :] = out_grad.astype(NARROW)
        add_sum(1, out_grad)

    loop(enter_back)
    outer[...] = matmul_turned(outer_low[...], outer_w[...])

    def activate_back(at):
        g = outer[at, :] * inner[at, :]
        inner_low[at, :] = g.astype(NARROW)
        add_sum(2, g)

    loop(activate_back)
    inner[...] = matmul_turned(inner_low[...], inner_w[...])

    def modulate_back(at):
        g, value = inner[at, :], hat[at, :]
        mod_low[at, :HW] = g.astype(NARROW)
        add_sum(3, g)
        scale_grad = g * (value * bias(3) + bias(4))
        mod_low[at, HW : 2 * HW] = scale_grad.astype(NARROW)
        add_sum(4, scale_grad)
        g = g * mod[at, HW : 2 * HW]
        add_sum(5, g)
        add_sum(6, g * value)
        g = g * bias(3)
        g = spread[at, 0:1] * (g - jnp.mean(g, -1, keepdims=True) - value * jnp.mean(g * value, -1, keepdims=True))
        g = grad[at, :] + g
        hidden_low[at, :] = g.astype(NARROW)
        add_sum(7, g)

    loop(modulate_back)
    top[...] = matmul_turned(mod_low[...], ada_w[...])

    def enter_last(at, slot):
        g = top[at, :] * joined[at, :]
        joined_low[at, :] = g.astype(NARROW)
        add_sum(8, g)
        total[slot, :] = total[slot, :] + g

    loop(enter_last, total)

    @pl.when(step == pl.num_programs(0) - 1)
    def _():
        found = total[...].astype(NARROW)
        cond_low[...] = found
        cond_back[...] = matmul_turned(found, cond_w[...]).astype(NARROW)
        acc = jnp.zeros((8, HW), WIDE)
        for i in range(slots // 8):
            acc = acc + total[i * 8 : (i + 1) * 8, :]
        cond_sum[...] = acc


def head_pass(p, conditions, clean, filled, steps, noise, divisor):
    slots = conditions.shape[0]
    times = steps.astype(WIDE)
    features = time_features(times).astype(NARROW).reshape(-1, FREQ)
    level = alpha_level(times)[..., None]
    noisy = (jnp.sqrt(level) * clean.astype(WIDE) + jnp.sqrt(1.0 - level) * noise).astype(NARROW).reshape(-1, TOK_CH)
    flat_noise = noise.reshape(-1, TOK_CH)
    marks = jnp.tile(filled.astype(WIDE)[:, None], (COPIES, 1))
    wide_b = jnp.stack(
        [p.cond_bias, p.time_bias, p.input_bias, p.head_gain, p.head_shift, p.inner_bias, p.outer_bias, p.outer_bias]
    ).astype(WIDE)
    total = COPIES * slots

    def tiled(width):
        return pl.BlockSpec((TOGETHER * slots, width), lambda i: (i, 0))

    def whole(x):
        return pl.BlockSpec(x, lambda i: (0, 0), pipeline_mode=pl.Buffered(1))

    weights = (p.cond_weight, p.time_weight, p.input_weight, p.ada_weight, p.inner_weight, p.outer_weight, p.final_weight)
    biases = (wide_b, p.ada_bias.astype(WIDE)[None], p.final_bias.astype(WIDE)[None])
    widths = (HW, 3 * HW, HW, HW, HW, HW, HW, HW, HW)
    kept = [((total, w), NARROW, tiled(w)) for w in widths] + [((total, TOK_CH), WIDE, tiled(TOK_CH))]
    kept += [(s, t, whole(s)) for s, t in (((SUMS * 8, HW), WIDE), ((slots, HW), NARROW), ((8, HW), WIDE), ((slots, D), NARROW))]
    flops = 4 * total * (FREQ * HW // 2 + 5 * HW * HW) + 4 * slots * D * HW
    found = pl.pallas_call(
        head_kernel,
        grid=(COPIES // TOGETHER,),
        out_shape=[jax.ShapeDtypeStruct(s, t) for s, t, _ in kept],
        in_specs=[pl.BlockSpec(memory_space=pltpu.SMEM), whole(conditions.shape), tiled(FREQ), tiled(TOK_CH), tiled(TOK_CH), tiled(1)]
        + [whole(x.shape) for x in weights + biases],
        out_specs=[spec for _, _, spec in kept],
        scratch_shapes=[
            pltpu.VMEM((n * slots, w), WIDE)
            for n, w in [(1, HW)] + [(TOGETHER, w) for w in (HW, HW, 3 * HW, HW, HW, HW, HW)] + [(1, HW), (TOGETHER, LANES)]
        ],
        compiler_params=pltpu.CompilerParams(vmem_limit_bytes=60 * 1000 * 1000),
        cost_estimate=pl.CostEstimate(flops=flops, bytes_accessed=26 * total * HW, transcendentals=3 * total * HW),
    )(divisor[None], conditions, features, noisy, flat_noise, marks, *weights, *biases)
    signal, mod_low, modulated, inner_low, active, outer_low, final, hidden_low, joined_low, error, sums, cond_low, cond_sum, cond_back = found
    sums = jnp.sum(sums.reshape(SUMS, 8, HW), 1)
    loss_part = jnp.sum(jnp.sum(error * error, -1) * marks[:, 0])
    pred_grad = 2.0 * error * marks / divisor
    grads = dict(
        final_weight=weight_grad(final, pred_grad.astype(NARROW)), final_bias=rows_sum(pred_grad),
        outer_weight=weight_grad(active, outer_low), outer_bias=sums[1],
        inner_weight=weight_grad(modulated, inner_low), inner_bias=sums[2],
        head_gain=sums[6], head_shift=sums[5],
        ada_weight=weight_grad(signal, mod_low), ada_bias=jnp.concatenate([sums[3], sums[4], sums[0]]),
        time_weight=weight_grad(features, joined_low), time_bias=sums[8],
        cond_weight=weight_grad(conditions, cond_low), cond_bias=rows_sum(cond_sum),
        input_weight=weight_grad(noisy, hidden_low), input_bias=sums[7],
    )
    return loss_part, grads, cond_back


def exchange(payload, parts):
    shape = payload.shape
    moved = lax.all_to_all(payload.reshape(parts, -1, shape[-1]), "dp", split_axis=0, concat_axis=0, tiled=True)
    return moved.reshape(shape)


def body(latents, route, labels, timesteps, noise, image_weight, weights, momentum, average):
    ranks_dp, ranks_rep = lax.axis_size("dp"), lax.axis_size("rep")
    ranks = ranks_dp * ranks_rep
    meshed = (ranks_dp, ranks_rep) == (8, 4)
    rows = route.shape[0]
    images = labels.shape[0]
    assert images == 1 and rows == SEQ
    size = weights.shape[0] // LANES
    padded = -(-(size + 1) // 48) * 48
    masked = route < rows
    own = jnp.sum(masked.astype(WIDE))
    low = weights.reshape(size, LANES).astype(NARROW)
    extra = jnp.full((padded - size, LANES), own).astype(NARROW)
    block = jnp.concatenate([low, extra], 0)
    gathered = spread(block) if meshed else lax.all_gather(block, BOTH, axis=0)
    base, enc, mid, dec, head = unpack(gathered, size)
    count = jnp.sum(gathered[:, size, 0].astype(WIDE))
    keep = jnp.concatenate([jnp.ones((BUF,), bool), ~masked])
    tokens = dense(latents, base.embed_weight) + base.embed_bias.astype(WIDE)
    at = next(e.start for e in ENTRIES if e.sparse) + labels[0] * (D // LANES) + jnp.arange(D // LANES, dtype=jnp.int32)
    classes = gathered[at // size, at % size].reshape(1, D).astype(WIDE)
    stream = jnp.concatenate([jnp.broadcast_to(classes, (BUF, D)), tokens], 0) + base.encoder_pos.astype(WIDE)
    stream, enc_stored = block_forward(stream, keep, enc)
    encoded = layer_norm(stream, mid.enc_gain.astype(WIDE), mid.enc_shift.astype(WIDE)).astype(NARROW)
    decoded = dense(encoded, mid.dec_weight) + mid.dec_bias.astype(WIDE)
    decoded = jnp.where(keep[:, None], decoded, mid.mask_token.astype(WIDE))
    before = decoded + mid.decoder_pos.astype(WIDE)
    flow_out, dec_stored = block_forward(before, None, dec)
    after = layer_norm(flow_out, head.dec_gain.astype(WIDE), head.dec_shift.astype(WIDE))
    conditions = (after[BUF:] + head.diffusion_pos.astype(WIDE)).astype(NARROW)
    token_weight = jnp.broadcast_to(image_weight.astype(NARROW)[:, None], (rows, 1))
    payload = jnp.concatenate([conditions, latents, token_weight, jnp.zeros((rows, LANES - TOK_CH - 1), NARROW)], 1)
    picks = (jnp.arange(rows, dtype=jnp.int32)[:, None] == route[None, :]).astype(NARROW)
    arrived = exchange(dense(picks, payload).astype(NARROW), ranks_dp)
    divisor = TOK_CH * COPIES * count
    loss_part, head_grads, cond_back = head_pass(
        head, arrived[:, :D], arrived[:, D : D + TOK_CH], arrived[:, D + TOK_CH], timesteps, noise, divisor
    )
    returned = exchange(cond_back.astype(NARROW), ranks_dp)
    token_grad = lax.dot_general(picks, returned, (((0,), (0,)), ((), ())), preferred_element_type=WIDE)
    after_grad = jnp.concatenate([jnp.zeros((BUF, D), WIDE), token_grad], 0)
    flow_grad, dec_gain, dec_shift = norm_pull(flow_out, head.dec_gain, head.dec_shift)(after_grad)
    head_grads.update(diffusion_pos=token_grad, dec_gain=dec_gain, dec_shift=dec_shift)
    before_grad, dec_grads = block_backward(flow_grad, None, dec, dec_stored)
    decoded_grad = jnp.where(keep[:, None], before_grad, 0.0)
    decoded_low = decoded_grad.astype(NARROW)
    pull = norm_pull(stream, mid.enc_gain, mid.enc_shift)
    stream_grad, enc_gain, enc_shift = pull(back_input(decoded_low, mid.dec_weight))
    mid_grads = dict(
        enc_gain=enc_gain, enc_shift=enc_shift, dec_weight=weight_grad(encoded, decoded_low), dec_bias=rows_sum(decoded_grad),
        mask_token=rows_sum(jnp.where(keep[:, None], 0.0, before_grad)), decoder_pos=before_grad,
    )
    stream_grad, enc_grads = block_backward(stream_grad, keep, enc, enc_stored)
    token_in = stream_grad[BUF:]
    base_grads = dict(
        encoder_pos=stream_grad,
        class_table=jnp.sum(stream_grad[:BUF], 0, keepdims=True),
        embed_weight=weight_grad(latents, token_in.astype(NARROW)), embed_bias=rows_sum(token_in),
    )
    grads = {}
    for group, found in enumerate((base_grads, enc_grads, mid_grads, dec_grads, head_grads)):
        grads.update({(group, name): value for name, value in found.items()})
    height = -(-((ranks - 1) * size + padded) // 8) * 8
    full = fold(grads, labels, height)
    if meshed:
        lane = lax.broadcasted_iota(jnp.int32, (8, LANES), 1)
        mark = jnp.where(lane == lax.axis_index("dp") * ranks_rep + lax.axis_index("rep"), loss_part, 0.0)
        owned = collect(full, mark, size, padded)
        loss = jnp.sum(owned[padded - 8, :ranks]) / divisor
        owned = owned[:size]
    else:
        loss = lax.psum(loss_part, BOTH) / divisor
        owned = lax.psum_scatter(full[: ranks * size].reshape(ranks, size, LANES), BOTH, scatter_dimension=0, tiled=False)
    owned = owned.reshape(-1)
    rate = 0.05 * math.sqrt(images * ranks * SEQ)
    new_momentum = 0.9 * momentum + owned
    new_weights = weights - rate * (owned + 0.9 * new_momentum)
    new_average = 0.75 * average + 0.25 * new_weights
    return new_weights, new_momentum, new_average, loss


def solution(mesh):
    flat = P(BOTH)
    placed = (P(BOTH, None), flat, flat, P(None, BOTH), P(None, BOTH, None), flat, flat, flat, flat)
    return jax.shard_map(body, mesh=mesh, in_specs=placed, out_specs=(flat, flat, flat, P()), check_vma=False)
```

```python
import functools
import heapq
import math
import types

import jax
import jax.numpy as jnp
from jax import lax
from jax.experimental import pallas as pl
from jax.experimental.pallas import tpu as pltpu
from jax.sharding import PartitionSpec as P

D = 768
HEADS = 12
HEAD_DIM = 64
MLP = 3072
HW = 1024
TOK_CH = 16
FREQ = 256
CLASSES = 1000
BUF = 64
SEQ = 256
COPIES = 4
STEPS_T = 1000
LANES = 128
WIDE = jnp.float32
NARROW = jnp.bfloat16
NORM_EPS = 1e-06
MESH = pl.DeviceIdType.MESH
ANY = pl.BlockSpec(memory_space=pl.ANY)
HBM = pl.BlockSpec(memory_space=pltpu.HBM)
VMEM = pl.BlockSpec(memory_space=pltpu.VMEM)
DMA = pltpu.SemaphoreType.DMA
BOTH = ("dp", "rep")


def block_shapes():
    return dict(
        norm_one_gain=(D,), norm_one_shift=(D,), attn_weight=(D, 3 * D), attn_bias=(2 * D,),
        proj_weight=(D, D), proj_bias=(D,), norm_two_gain=(D,), norm_two_shift=(D,),
        fc_one_weight=(D, MLP), fc_one_bias=(MLP,), fc_two_weight=(MLP, D), fc_two_bias=(D,),
    )


ENC, DEC = 1, 3
GROUPS = (
    dict(embed_weight=(TOK_CH, D), embed_bias=(D,), class_table=(CLASSES, D), encoder_pos=(BUF + SEQ, D)),
    block_shapes(),
    dict(enc_gain=(D,), enc_shift=(D,), dec_weight=(D, D), dec_bias=(D,), mask_token=(D,), decoder_pos=(BUF + SEQ, D)),
    block_shapes(),
    dict(
        dec_gain=(D,), dec_shift=(D,), diffusion_pos=(SEQ, D), input_weight=(TOK_CH, HW), input_bias=(HW,),
        time_weight=(FREQ, HW), time_bias=(HW,), cond_weight=(D, HW), cond_bias=(HW,), head_gain=(HW,),
        head_shift=(HW,), ada_weight=(HW, 3 * HW), ada_bias=(3 * HW,), inner_weight=(HW, HW), inner_bias=(HW,),
        outer_weight=(HW, HW), outer_bias=(HW,), final_weight=(HW, TOK_CH), final_bias=(TOK_CH,),
    ),
)


class Entry:
    def __init__(self, group, name, shape, start):
        self.group, self.name, self.shape, self.start = group, name, shape, start
        self.rows = -(-math.prod(shape) // LANES)
        self.matrix = len(shape) == 2 and shape[1] % LANES == 0
        self.across = shape[1] // LANES if self.matrix else 1
        self.sparse = name == GROUP_SPARSE


GROUP_SPARSE = next(name for name, shape in GROUPS[0].items() if shape[0] == CLASSES)


def entries():
    found, start = [], 0
    for group, shapes in enumerate(GROUPS):
        for name, shape in shapes.items():
            found.append(Entry(group, name, shape, start))
            start += found[-1].rows
    return found


ENTRIES = entries()
USED = ENTRIES[-1].start + ENTRIES[-1].rows


def block_height(entry, limit):
    best = 0
    for height in range(8, entry.shape[0] + 1, 8):
        if entry.shape[0] % height == 0 and height * entry.across <= limit:
            best = height
    return best


class Slots:
    def __init__(self, number):
        self.number, self.base, self.last = number, 0, {}

    def at(self, b):
        return (self.base + b) % self.number

    def claim(self, b, put):
        for k in range(self.number):
            before = self.last.get((self.base + k) % self.number)
            if before is not None:

                @pl.when(b == k)
                def _(before=before):
                    before().wait()

        @pl.when(b >= self.number)
        def _():
            put(b - self.number).wait()

    def close(self, blocks, put):
        base = self.base
        for b in range(max(0, blocks - self.number), blocks):
            self.last[(base + b) % self.number] = functools.partial(put, b)
        self.base = base + blocks

    def drain(self):
        for before in self.last.values():
            before().wait()


SLOTS = 8
OUT = 3


def unfold_kernel(rows, padded, items, g_ref, *refs):
    count = len(items)
    outs = refs[:count]
    first, second, wide, first_sem, second_sem, out_sem = refs[count : count + 6]
    kinds = sorted({(h, e.across) for e, h in items})
    stages = dict(zip(kinds, refs[count + 6 :]))
    turns = {kind: Slots(OUT) for kind in kinds}
    bases = [0]
    for entry, height in items:
        bases.append(bases[-1] + entry.shape[0] // height)

    def spot(t, b):
        entry, height = items[t]
        span = height * entry.across
        start = entry.start + b * span
        dev = start // rows
        row = start - dev * rows
        low = jnp.minimum(row // 8 * 8, padded - span - 8)
        return dev, row, low, row + span > rows

    def copies(t, b):
        entry, height = items[t]
        window = height * entry.across + 8
        dev, row, low, more = spot(t, b)
        slot = (bases[t] + b) % SLOTS
        one = pltpu.make_async_copy(
            g_ref.at[dev, pl.ds(pl.multiple_of(low, 8), window)], first.at[slot, pl.ds(0, window)], first_sem.at[slot]
        )
        two = pltpu.make_async_copy(
            g_ref.at[jnp.minimum(dev + 1, g_ref.shape[0] - 1), pl.ds(0, window)],
            second.at[slot, pl.ds(0, window)], second_sem.at[slot],
        )
        return one, two, more

    def fetch(t, b):
        one, two, more = copies(t, b)
        one.start()

        @pl.when(more)
        def _():
            two.start()

    def fetch_number(g):
        if g < bases[-1]:
            t = next(t for t in range(count) if g < bases[t + 1])
            fetch(t, g - bases[t])

    ahead = SLOTS - 1
    for g in range(ahead):
        fetch_number(g)
    for t, (entry, height) in enumerate(items):
        kind = (height, entry.across)
        stage, turn = stages[kind], turns[kind]
        window = height * entry.across + 8
        blocks = entry.shape[0] // height

        def put(b, t=t, stage=stage, height=height, place=turn.base, kind=kind):
            slot = (place + b) % OUT
            return pltpu.make_async_copy(
                stage.at[slot], outs[t].at[pl.ds(pl.multiple_of(b * height, 8), height)], out_sem.at[kinds.index(kind), slot]
            )

        def body(b, carry, t=t, entry=entry, height=height, window=window, blocks=blocks, stage=stage, turn=turn, put=put):
            @pl.when(b + ahead < blocks)
            def _():
                fetch(t, b + ahead)

            for k in range(max(0, ahead - blocks), ahead):

                @pl.when(b == blocks - ahead + k)
                def _(k=k):
                    fetch_number(bases[t + 1] + k)

            dev, row, low, _ = spot(t, b)
            slot = (bases[t] + b) % SLOTS
            one, two, more = copies(t, b)
            one.wait()
            wide[pl.ds(0, window), :] = first[slot, pl.ds(0, window), :].astype(WIDE)

            @pl.when(more)
            def _():
                two.wait()
                wide[pl.ds(rows - low, window), :] = second[slot, pl.ds(0, window), :].astype(WIDE)

            turn.claim(b, put)
            off = row - low
            place = turn.at(b)
            for j in range(entry.across):
                stage[place, :, j * LANES : (j + 1) * LANES] = wide[pl.ds(off + j, height, stride=entry.across), :].astype(NARROW)
            put(b).start()
            return carry

        lax.fori_loop(0, blocks, body, 0)
        turn.close(blocks, put)
    for turn in turns.values():
        turn.drain()


def unfold(gathered, rows):
    padded = gathered.shape[1]
    items = [(e, block_height(e, min(2304, rows - 16))) for e in ENTRIES if e.matrix and not e.sparse]
    tall = max(e.across * h for e, h in items) + 8
    kinds = sorted({(h, e.across) for e, h in items})
    total = sum(math.prod(e.shape) for e, _ in items)
    outs = pl.pallas_call(
        functools.partial(unfold_kernel, rows, padded, items),
        out_shape=[jax.ShapeDtypeStruct(e.shape, NARROW) for e, _ in items],
        in_specs=[ANY],
        out_specs=[ANY] * len(items),
        scratch_shapes=[
            pltpu.VMEM((SLOTS, tall, LANES), NARROW), pltpu.VMEM((SLOTS, tall, LANES), NARROW),
            pltpu.VMEM((2 * tall, LANES), WIDE), DMA((SLOTS,)), DMA((SLOTS,)), DMA((len(kinds), OUT)),
        ]
        + [pltpu.VMEM((OUT, h, n * LANES), NARROW) for h, n in kinds],
        compiler_params=pltpu.CompilerParams(vmem_limit_bytes=48 * 1000 * 1000),
        cost_estimate=pl.CostEstimate(flops=total, bytes_accessed=4 * total, transcendentals=0),
    )(gathered)
    return {(e.group, e.name): out for (e, _), out in zip(items, outs)}


def rows_at(gathered, rows, start, number):
    pieces = []
    while number > 0:
        dev, row = divmod(start, rows)
        take = min(number, rows - row)
        pieces.append(gathered[dev, row : row + take])
        start, number = start + take, number - take
    return pieces[0] if len(pieces) == 1 else jnp.concatenate(pieces, 0)


def unpack(gathered, rows, groups):
    matrices = unfold(gathered, rows)
    for e in ENTRIES:
        if e.sparse:
            continue
        if e.matrix:
            value = matrices[(e.group, e.name)]
        else:
            value = rows_at(gathered, rows, e.start, e.rows).reshape(-1)[: math.prod(e.shape)].reshape(e.shape)
        setattr(groups[e.group], e.name, value)


DEPTH = 3
TALL = 256
CHUNK = 512
NEXT = 3


def product_height(entry):
    return min(TALL, entry.shape[0])


def fold_kernel(products, items, plain, vectors, lone_place, zero, count, going_on, label, *refs):
    refs = list(refs)

    def take(number):
        found, refs[:number] = refs[:number], []
        return found

    small = take(count)
    pairs = take(2 * len(products))
    given = take(len(items))
    rest = take(len(plain))
    take(int(going_on))
    (full,) = take(1)
    pair_sem, given_sem, plain_sem, out_sem, vector_sem = take(5)
    held = take(2 * len(products))
    loads = take(len(items))
    stage, lines = take(2)
    gets = [pltpu.make_async_copy(given[i], loads[i], given_sem.at[i]) for i in range(len(items))]
    fills = []
    for i, entry in enumerate(products):
        for k in (2 * i, 2 * i + 1):
            source = pairs[k]
            if source.shape != held[k].shape:
                source = source.at[:, pl.ds(0, held[k].shape[1])]
            fills.append(pltpu.make_async_copy(source, held[k], pair_sem.at[k]))
    for move in gets + fills[: 2 * NEXT]:
        move.start()
    moves = []
    for i, (start, number) in enumerate(plain):
        move = pltpu.make_async_copy(rest[i].at[pl.ds(0, number)], full.at[pl.ds(start, number)], plain_sem.at[i])
        move.start()
        moves.append(move)
    at = 0
    for i, (entry, which, parts) in enumerate(vectors):
        begin = at
        for k, column, width in parts:
            for j in range(0, width, LANES):
                lines[at : at + 1, :] = small[which][k : k + 1, column + j : column + j + LANES]
                at += 1
        move = pltpu.make_async_copy(lines.at[pl.ds(begin, at - begin)], full.at[pl.ds(entry.start, at - begin)], vector_sem.at[i])
        move.start()
        moves.append(move)
        at = -(-at // 8) * 8
    if zero:
        lines[at : at + zero, :] = jnp.zeros((zero, LANES), WIDE)
        move = pltpu.make_async_copy(lines.at[pl.ds(at, zero)], full.at[pl.ds(USED, zero)], vector_sem.at[len(vectors)])
        move.start()
        moves.append(move)
    turn = Slots(DEPTH)

    def each(entry, height, make):
        span = height * entry.across
        blocks = entry.shape[0] // height

        def put(b, base=turn.base):
            slot = (base + b) % DEPTH
            return pltpu.make_async_copy(
                stage.at[slot, pl.ds(0, span)], full.at[pl.ds(entry.start + b * span, span)], out_sem.at[slot]
            )

        def step(b, carry):
            turn.claim(b, put)
            make(b, turn.at(b))
            put(b).start()
            return carry

        lax.fori_loop(0, blocks, step, 0)
        turn.close(blocks, put)

    if lone_place:
        sparse = next(e for e in ENTRIES if e.sparse)
        height = block_height(sparse, 1200)
        row, row_at = small[lone_place[0]], lone_place[1]

        def lone(b, slot):
            here = lax.broadcasted_iota(jnp.int32, (height, LANES), 0) + b * height == label[0]
            for j in range(sparse.across):
                value = jnp.broadcast_to(row[row_at : row_at + 1, j * LANES : (j + 1) * LANES], (height, LANES))
                stage[slot, pl.ds(j, height, stride=sparse.across), :] = jnp.where(here, value, 0.0)

        each(sparse, height, lone)
    for t, entry in enumerate(items):
        gets[t].wait()

        def make(b, slot, t=t, entry=entry):
            for j in range(entry.across):
                stage[slot, pl.ds(j, entry.shape[0], stride=entry.across), :] = loads[t][:, j * LANES : (j + 1) * LANES]

        each(entry, entry.shape[0], make)
    for t, entry in enumerate(products):
        left, right = held[2 * t], held[2 * t + 1]
        for move in fills[2 * (t + NEXT) : 2 * (t + NEXT) + 2]:
            move.start()
        fills[2 * t].wait()
        fills[2 * t + 1].wait()
        height = product_height(entry)
        chunk = math.gcd(CHUNK, entry.shape[1])

        def make(b, slot, left=left, right=right, entry=entry, height=height, chunk=chunk):
            turned = left[:, pl.ds(pl.multiple_of(b * height, LANES), height)].T
            for k in range(entry.shape[1] // chunk):
                found = jnp.dot(turned, right[:, k * chunk : (k + 1) * chunk], preferred_element_type=WIDE)
                for j in range(chunk // LANES):
                    at = pl.ds(k * (chunk // LANES) + j, height, stride=entry.across)
                    stage[slot, at, :] = found[:, j * LANES : (j + 1) * LANES]

        each(entry, height, make)
    turn.drain()
    for move in moves:
        move.wait()


def fold(grads, label, height_total, full=None):
    wanted = [e for e in ENTRIES if (e.group, e.name) in grads]
    found = {e: grads[(e.group, e.name)] for e in wanted}
    products = [e for e in wanted if isinstance(found[e], tuple)]
    items = [e for e in wanted if e.matrix and not isinstance(found[e], (tuple, Vector))]
    small, vectors, plain, values, lone_place = [], [], [], [], None
    for e in wanted:
        if isinstance(found[e], Vector):
            place = next((i for i, x in enumerate(small) if x is found[e].array), len(small))
            small[place : place + 1] = [found[e].array]
            if e.sparse:
                lone_place = (place, found[e].parts[0][0])
            else:
                vectors.append((e, place, found[e].parts))
        elif not e.matrix and e not in products:
            plain.append((e.start, e.rows))
            values.append(found[e].reshape(e.rows, LANES))
    zero = height_total - USED if full is None else 0
    before = [] if full is None else [full]
    lines = sum(-(-e.rows // 8) * 8 for e, _, _ in vectors) + -(-zero // 8) * 8
    operands = [x for e in products for x in found[e]]
    holds = [(x.shape[0], n) for e in products for x, n in zip(found[e], e.shape)]
    tall = max([e.rows for e in items] + [e.across * product_height(e) for e in products])
    total = sum(e.rows for e in wanted) * LANES
    taken = 1 + len(small) + len(operands) + len(items) + len(plain)
    flops = sum(2 * math.prod(e.shape) * operands[2 * i].shape[0] for i, e in enumerate(products))
    return pl.pallas_call(
        functools.partial(fold_kernel, products, items, plain, vectors, lone_place, zero, len(small), bool(before)),
        out_shape=jax.ShapeDtypeStruct((height_total, LANES), WIDE),
        in_specs=[pl.BlockSpec(memory_space=pltpu.SMEM)] + [VMEM] * len(small) + [ANY] * (len(operands) + len(items) + len(plain) + len(before)),
        out_specs=ANY,
        input_output_aliases={taken: 0} if before else {},
        scratch_shapes=[DMA((len(operands),)), DMA((len(items),)), DMA((max(len(plain), 1),)), DMA((DEPTH,)), DMA((len(vectors) + 1,))]
        + [pltpu.VMEM(s, NARROW) for s in holds]
        + [pltpu.VMEM(e.shape, WIDE) for e in items]
        + [pltpu.VMEM((DEPTH, tall, LANES), WIDE), pltpu.VMEM((lines, LANES), WIDE)],
        compiler_params=pltpu.CompilerParams(vmem_limit_bytes=62 * 1000 * 1000),
        cost_estimate=pl.CostEstimate(flops=flops, bytes_accessed=4 * total, transcendentals=0),
    )(label, *small, *operands, *[found[e] for e in items], *values, *before)


X, Y, Z = 0, 1, 2
TREES = ((Z, X, Y), (Z, Y, X), (X, Z, Y), (X, Z, Y), (Y, Z, X), (Y, Z, X))
SHARES = len(TREES)
FAR = 3


def onward(order, arrived, way, p):
    z, x, y = p
    found = []
    if arrived >= 0 and order[arrived] == Z and 0 <= z + way <= FAR:
        found.append(((z + way, x, y), arrived, way))
    for j in range(arrived + 1, 3):
        if order[j] == X:
            found.append(((z, 1 - x, y), j, 0))
        elif order[j] == Y:
            found.append(((z, x, 1 - y), j, 0))
        else:
            found += [((z + s, x, y), j, s) for s in (1, -1) if 0 <= z + s <= FAR]
    return found


@functools.cache
def flow(lag=0.4):
    chips = [(z, x, y) for z in range(FAR + 1) for x in range(2) for y in range(2)]
    events, queues, busy, come, sent = [], {}, set(), {}, []
    number = iter(range(10**9))
    for u in range(SHARES):
        for p in chips:
            heapq.heappush(events, (0.0, next(number), 0, (p, p, u, -1, 0)))

    def pump(link, t):
        if link in busy or not queues.get(link):
            return
        what = heapq.heappop(queues[link])[2]
        busy.add(link)
        sent.append((t, link, what[1], what[2]))
        heapq.heappush(events, (t + 1.0, next(number), 1, (link, what)))

    while events:
        t, _, kind, what = heapq.heappop(events)
        if kind == 1:
            link, piece = what
            busy.discard(link)
            heapq.heappush(events, (t + lag, next(number), 0, piece))
            pump(link, t)
            continue
        p, q, u, k, way = what
        come[(u, p, q)] = t
        for to, k2, way2 in onward(TREES[u], k, way, p):
            left = len(onward(TREES[u], k2, way2, to))
            heapq.heappush(queues.setdefault((p, to), []), ((-left, t), next(number), (to, q, u, k2, way2)))
            pump((p, to), t)
    return come, sent


def spread_order():
    keyed = {}
    for (u, p, q), t in flow()[0].items():
        keyed.setdefault((u, q[0] - p[0], (q[1] - p[1]) % 2, (q[2] - p[2]) % 2), []).append(t)
    return sorted(keyed, key=lambda k: (sum(keyed[k]) / len(keyed[k]), k))


def last_hop(u, dz, dx, dy):
    apart = [k for k in range(3) if (dx, dy, dz)[TREES[u][k]] != 0]
    return apart[-1] if apart else -1


def hops(u, dz, dx, dy):
    order, arrived = TREES[u], last_hop(u, dz, dx, dy)
    found = []
    if arrived >= 0 and order[arrived] == Z:
        found.append((1, 0, 0) if dz < 0 else (-1, 0, 0))
    for k in range(arrived + 1, 3):
        found += [[(0, 1, 0)], [(0, 0, 1)], [(1, 0, 0), (-1, 0, 0)]][order[k]]
    return found


def only(condition, action):
    if condition is None:
        action()
    else:
        pl.when(condition)(action)


def spread_kernel(own, out, keep_sem, send_sem, link_sem, core_send, core_sem):
    dp, rep = lax.axis_index("dp"), lax.axis_index("rep")
    z, x, y, c = dp // 2, dp % 2, rep // 2, rep % 2
    unit = own.shape[0] // SHARES
    sibling = (dp, y * 2 + 1 - c)

    def device(dz, dx, dy):
        return ((z + dz) * 2 + (x + dx) % 2, (y + dy) % 2 * 2 + c)

    def exists(dz):
        return None if dz == 0 else (z + dz >= 0 if dz < 0 else z + dz <= FAR)

    barrier = pltpu.get_barrier_semaphore()
    near = ((0, 1, 0), (0, 0, 1), (1, 0, 0), (-1, 0, 0))
    for hop in near:
        only(exists(hop[0]), lambda: pl.semaphore_signal(barrier, inc=1, device_id=device(*hop), device_id_type=MESH))
    pl.semaphore_signal(barrier, inc=1, device_id=sibling, device_id_type=MESH)
    inner = z * (FAR - z)
    only(inner == 0, lambda: pl.semaphore_wait(barrier, len(near)))
    only(inner > 0, lambda: pl.semaphore_wait(barrier, len(near) + 1))
    keep = pltpu.make_async_copy(own, out.at[dp * 4 + rep], keep_sem)
    keep.start()
    ends, number = [], 0
    for u, dz, dx, dy in spread_order():
        part = pl.ds(u * unit, unit)
        q = ((z + dz) * 2 + (x + dx) % 2) * 2 + (y + dy) % 2
        mine = dz == 0 and dx == 0 and dy == 0
        i = u * 16 + q

        def copy(to, send, come, part=part, q=q, mine=mine):
            here = out.at[q * 2 + c, part]
            return pltpu.make_async_remote_copy(
                own.at[part] if mine else here, here, send, come, device_id=to, device_id_type=MESH
            )

        goes = [(hop, number + k) for k, hop in enumerate(hops(u, dz, dx, dy))]
        number += len(goes)

        def run(i=i, copy=copy, goes=goes, mine=mine):
            if not mine:
                copy(sibling, send_sem.at[0], link_sem.at[i]).wait_recv()
            for hop, n in goes:
                only(exists(hop[0]), lambda: copy(device(*hop), send_sem.at[n], link_sem.at[i]).start())
            copy(sibling, core_send.at[i], core_sem.at[i]).start()

        def finish(i=i, copy=copy, goes=goes):
            for hop, n in goes:
                only(exists(hop[0]), lambda: copy(device(*hop), send_sem.at[n], link_sem.at[i]).wait_send())
            copy(sibling, core_send.at[i], core_sem.at[i]).wait()

        there = None if dz == 0 else jnp.logical_and(z + dz >= 0, z + dz <= FAR)
        only(there, run)
        ends.append((there, finish))
    for there, finish in ends:
        only(there, finish)
    keep.wait()


def spread(own):
    pieces = SHARES * 16
    sends = sum(len(hops(*key)) for key in spread_order())
    return pl.pallas_call(
        spread_kernel,
        out_shape=jax.ShapeDtypeStruct((32,) + own.shape, own.dtype),
        in_specs=[ANY],
        out_specs=ANY,
        scratch_shapes=[DMA, DMA((sends,)), DMA((pieces,)), DMA((pieces,)), DMA((pieces,))],
        compiler_params=pltpu.CompilerParams(collective_id=0, has_side_effects=True),
    )(own)


class Chip:
    def __init__(self, low):
        dp, rep = lax.axis_index("dp"), lax.axis_index("rep")
        self.low = low
        self.z, self.x, self.y, self.c = dp // 2, dp % 2, rep // 2, rep % 2
        self.way = 1 - 2 * (self.z // 2)

    def device(self, q, other=0):
        z = self.z + self.way * (q[0] - self.low)
        return z * 2 + (self.x + q[1]) % 2, (self.y + q[2]) % 2 * 2 + (self.c + other) % 2

    def block(self, q, other=0):
        dp, rep = self.device(q, other)
        return dp * 4 + rep

    def greet(self):
        low = self.low
        near = [(low, 1, 0), (low, 0, 1), (low + 1, 0, 0)] + ([(low - 1, 0, 0)] if low else [])
        barrier = pltpu.get_barrier_semaphore()
        for q in near:
            pl.semaphore_signal(barrier, inc=1, device_id=self.device(q), device_id_type=MESH)
        pl.semaphore_signal(barrier, inc=1, device_id=self.device((low, 0, 0), 1), device_id_type=MESH)
        pl.semaphore_wait(barrier, len(near) + 1)


def seen_from(p, r):
    low, way = min(p[0], FAR - p[0]), 1 if p[0] < 2 else -1
    return low + way * (r[0] - p[0]), (r[1] - p[1]) % 2, (r[2] - p[2]) % 2


@functools.cache
def sum_programs():
    come, sent = flow()
    last = max(come.values())
    found = []
    for z in (0, 1):
        p = (z, 0, 0)
        kids, parent, when = {}, {}, {}
        for t, link, q, u in sent:
            if link[0] == p:
                kids.setdefault((u, q), []).append(link[1])
                if q == p:
                    when[(u, p)] = max(when.get((u, p), 0.0), last - t)
            if link[1] == p:
                parent[(u, q)] = link[0]
                when[(u, q)] = last - t - 1.0
        tasks = sorted(when, key=lambda k: (when[k], k))
        found.append([(u, q, sorted(kids.get((u, q), [])), parent.get((u, q))) for u, q in tasks])
    return found


@functools.cache
def landing():
    return [{key: i for i, key in enumerate((u, q, k) for u, q, kids, _ in tasks for k in kids)} for tasks in sum_programs()]


RING = 12
SIDE = 4
EARLY = 12
STEP = 40


def add_rows(into, terms):
    def body(i, carry):
        at = pl.ds(pl.multiple_of(i * STEP, 8), STEP)
        total = into[at, :]
        for term in terms:
            total = total + term[at, :]
        into[at, :] = total
        return carry

    lax.fori_loop(0, into.shape[0] // STEP, body, 0)


def collect_at(low, size, full, mark, out, aside, store, ring, side, ring_sem, side_sem, send_sem, link_sem, core_send, core_sem, out_sem, marks, mark_sem):
    chip = Chip(low)
    me = (low, 0, 0)
    tasks, spots = sum_programs()[low], landing()
    count, unit = len(tasks), ring.shape[1]
    chip.greet()

    def part(i, other=0):
        return full.at[pl.ds(chip.block(tasks[i][1], other) * size + tasks[i][0] * unit, unit)]

    def across(i):
        return pltpu.make_async_remote_copy(
            part(i, 1), aside.at[i], core_send.at[i], core_sem.at[i], device_id=chip.device(me, 1), device_id_type=MESH
        )

    def ours(i):
        return pltpu.make_async_copy(part(i), ring.at[i % RING], ring_sem.at[i % RING])

    def theirs(i):
        return pltpu.make_async_copy(aside.at[i], side.at[i % SIDE], side_sem.at[i % SIDE])

    def along(i, spot, to):
        return pltpu.make_async_remote_copy(
            ring.at[i % RING], store.at[spot], send_sem.at[i], link_sem.at[spot], device_id=chip.device(to), device_id_type=MESH
        )

    tail = pl.ds(unit - 8, 8)
    ours_too = pltpu.make_async_copy(mark, marks.at[0], mark_sem.at[0])
    theirs_too = pltpu.make_async_remote_copy(
        mark, marks.at[1], mark_sem.at[1], mark_sem.at[2], device_id=chip.device(me, 1), device_id_type=MESH
    )
    ours_too.start()
    theirs_too.start()
    leaving = {}

    def fetch(i):
        if i - RING in leaving:
            leaving.pop(i - RING)()
        ours(i).start()
        across(i).wait_recv()
        theirs(i).start()

    for i in range(EARLY):
        across(i).start()
    for i in range(SIDE - 1):
        fetch(i)
    ours_too.wait()
    theirs_too.wait()
    for i, (u, q, kids, to) in enumerate(tasks):
        if i + EARLY < count:
            across(i + EARLY).start()
        if i + SIDE - 1 < count:
            fetch(i + SIDE - 1)
        ours(i).wait()
        theirs(i).wait()
        if u == SHARES - 1:
            ring[i % RING, tail, :] = marks[0] + marks[1]
            side[i % SIDE, tail, :] = jnp.zeros((8, LANES), WIDE)
        terms = [side.at[i % SIDE]]
        for kid in kids:
            spot = spots[low][(u, q, kid)]
            along(i, spot, kid).wait_recv()
            terms.append(store.at[spot])
        add_rows(ring.at[i % RING], terms)
        if to is None:
            move = pltpu.make_async_copy(ring.at[i % RING], out.at[pl.ds(u * unit, unit)], out_sem.at[u])
            move.start()
            leaving[i] = move.wait
        else:
            move = along(i, spots[min(to[0], FAR - to[0])][(u, seen_from(to, q), seen_from(to, me))], to)
            move.start()
            leaving[i] = move.wait_send
    for i in list(leaving):
        leaving.pop(i)()
    for i in range(count):
        across(i).wait_send()


def collect_kernel(size, *refs):
    z = lax.axis_index("dp") // 2
    inner = z * (FAR - z)

    @pl.when(inner == 0)
    def _():
        collect_at(0, size, *refs)

    @pl.when(inner > 0)
    def _():
        collect_at(1, size, *refs)


def collect(full, mark, size, rows):
    slots = max(len(spots) for spots in landing())
    count, unit = len(sum_programs()[0]), rows // SHARES
    return pl.pallas_call(
        functools.partial(collect_kernel, size),
        out_shape=(jax.ShapeDtypeStruct((rows, LANES), WIDE), jax.ShapeDtypeStruct((count, unit, LANES), WIDE)),
        in_specs=[ANY, ANY],
        out_specs=(ANY, ANY),
        scratch_shapes=[
            pltpu.VMEM((slots, unit, LANES), WIDE), pltpu.VMEM((RING, unit, LANES), WIDE), pltpu.VMEM((SIDE, unit, LANES), WIDE),
            DMA((RING,)), DMA((SIDE,)), DMA((count,)), DMA((slots,)), DMA((count,)), DMA((count,)), DMA((SHARES,)),
            pltpu.VMEM((2, 8, LANES), WIDE), DMA((3,)),
        ],
        compiler_params=pltpu.CompilerParams(collective_id=1, has_side_effects=True, vmem_limit_bytes=62 * 1000 * 1000),
    )(full, mark)[0]


HALF_ROOT = math.sqrt(0.5)
PDF = 1.0 / math.sqrt(2.0 * math.pi)
SCALE = HEAD_DIM ** (-0.5)
PART = 512
BIG = pltpu.CompilerParams(vmem_limit_bytes=66 * 1000 * 1000)
BLOCK_WEIGHTS = ((D, 3 * D), (D, D), (D, MLP), (MLP, D))
EMBED_B, ENC_G, ENC_S, DEC_B, MASK_T, DEC_G, DEC_S, CLASS, ENC_ROWS, DEC_ROWS, ALL_ROWS = 0, 1, 2, 3, 4, 5, 6, 7, 8, 14, 24


def matmul(left, right):
    return jnp.dot(left, right, preferred_element_type=WIDE)


def matmul_turned(left, right):
    return lax.dot_general(left, right, (((1,), (1,)), ((), ())), preferred_element_type=WIDE)


def column_sum(value):
    return jnp.sum(value, 0, keepdims=True)


def whiten(value):
    centered = value - jnp.mean(value, -1, keepdims=True)
    r = lax.rsqrt(jnp.mean(centered * centered, -1, keepdims=True) + NORM_EPS)
    return centered * r, r


def whiten_back(grad, hat, r):
    return r * (grad - jnp.mean(grad, -1, keepdims=True) - hat * jnp.mean(grad * hat, -1, keepdims=True))


def side_masks(length):
    lane = lax.broadcasted_iota(jnp.int32, (length, LANES), 1)
    return lane < HEAD_DIM, lane >= HEAD_DIM


def one_side(value, side):
    return jnp.where(side, value, jnp.zeros_like(value))


def start_all(sources, targets, sem):
    moves = [pltpu.make_async_copy(s, t, sem.at[i]) for i, (s, t) in enumerate(zip(sources, targets))]
    for move in moves:
        move.start()
    return moves


def block_vectors(base, enc, mid, dec, head, classes):
    rows = [base.embed_bias, mid.enc_gain, mid.enc_shift, mid.dec_bias, mid.mask_token, head.dec_gain, head.dec_shift, classes]
    for p in (enc, dec):
        rows += [p.norm_one_gain, p.norm_one_shift, p.norm_two_gain, p.norm_two_shift, p.proj_bias, p.fc_two_bias]
    rows += rows[: ALL_ROWS - len(rows)]
    gap = jnp.zeros((D,), NARROW)
    attn_b = [jnp.concatenate([p.attn_bias[:D], gap, p.attn_bias[D:]]).astype(WIDE)[None] for p in (enc, dec)]
    return jnp.stack(rows).astype(WIDE), attn_b, [p.fc_one_bias.astype(WIDE)[None] for p in (enc, dec)]


def forward_block(value, first, keep, table, attn_b, fc_b, outs, weights, moves):
    normed, mixed, totals, attended, middle, second, slope, active = outs
    attn_w, proj_w, one_w, two_w = weights
    hat, _ = whiten(value)
    normed[...] = (hat * table[first : first + 1, :] + table[first + 1 : first + 2, :]).astype(NARROW)
    moves[0].wait()
    for k in range(3):
        at = slice(k * D, (k + 1) * D)
        mixed[:, at] = (matmul(normed[...], attn_w[:, at]) + attn_b[0:1, at]).astype(NARROW)
    sides = side_masks(value.shape[0])
    for pair in range(HEADS // 2):
        q, k, v = (mixed[:, part * D + pair * LANES : part * D + (pair + 1) * LANES] for part in range(3))
        found = None
        for i, side in enumerate(sides):
            scores = matmul_turned(one_side(q, side), k) * SCALE
            if keep is not None:
                scores = jnp.where(keep[0:1, :] > 0.0, scores, -1e30)
            top = jnp.max(scores, -1, keepdims=True)
            powers = jnp.exp(scores - top)
            total = jnp.sum(powers, -1, keepdims=True)
            totals[:, 2 * pair + i : 2 * pair + i + 1] = top + jnp.log(total)
            probs = (powers * (1.0 / total)).astype(NARROW)
            part = matmul(probs, one_side(v, side))
            found = part if found is None else found + part
        attended[:, pair * LANES : (pair + 1) * LANES] = found.astype(NARROW)
    moves[1].wait()
    value = value + matmul(attended[...], proj_w[...]) + table[first + 4 : first + 5, :]
    middle[...] = value
    hat, _ = whiten(value)
    second[...] = (hat * table[first + 2 : first + 3, :] + table[first + 3 : first + 4, :]).astype(NARROW)
    moves[2].wait()
    for k in range(MLP // PART):
        at = slice(k * PART, (k + 1) * PART)
        value = matmul(second[...], one_w[:, at]) + fc_b[0:1, at]
        share = 0.5 + 0.5 * lax.erf(value * HALF_ROOT)
        active[:, at] = (value * share).astype(NARROW)
        slope[:, at] = share + value * (PDF * jnp.exp(-0.5 * value * value))
    moves[3].wait()
    return middle[...] + matmul(active[...], two_w[...]) + table[first + 5 : first + 6, :]


def forward_shapes(length):
    widths = [(D, NARROW), (3 * D, NARROW), (LANES, WIDE), (D, NARROW), (D, WIDE), (D, NARROW), (MLP, WIDE), (MLP, NARROW)]
    return [jax.ShapeDtypeStruct((length, w), t) for w, t in widths]


def encode_kernel(latents, keep_row, keep_column, table, attn_b, fc_b, embed_w, enc_pos, dec_pos, *refs):
    sources, outs, (stream, encoded, leaving, before) = refs[:5], refs[5:13], refs[13:17]
    held, sem = refs[17:22], refs[22]
    moves = start_all(sources, held, sem)
    pos = enc_pos[...].astype(WIDE)
    stream[:BUF, :] = table[CLASS : CLASS + 1, :] + pos[:BUF]
    stream[BUF:, :] = matmul(latents[...], embed_w[...]) + table[EMBED_B : EMBED_B + 1, :] + pos[BUF:]
    value = forward_block(stream[...], ENC_ROWS, keep_row, table, attn_b, fc_b, outs, held[:4], moves)
    leaving[...] = value
    hat, _ = whiten(value)
    encoded[...] = (hat * table[ENC_G : ENC_G + 1, :] + table[ENC_S : ENC_S + 1, :]).astype(NARROW)
    moves[4].wait()
    value = matmul(encoded[...], held[4][...]) + table[DEC_B : DEC_B + 1, :]
    value = jnp.where(keep_column[...] > 0.0, value, table[MASK_T : MASK_T + 1, :])
    before[...] = value + dec_pos[...].astype(WIDE)


def block_cost(length, weights):
    work = sum(math.prod(s) for s in weights)
    return pl.CostEstimate(flops=2 * length * work, bytes_accessed=2 * work + 36 * length * D, transcendentals=4 * length * MLP)


def encode(latents, keep_row, keep_column, table, attn_b, fc_b, base, enc, mid):
    length = BUF + SEQ
    weights = BLOCK_WEIGHTS + ((D, D),)
    found = pl.pallas_call(
        encode_kernel,
        out_shape=forward_shapes(length)
        + [jax.ShapeDtypeStruct((length, D), t) for t in (WIDE, NARROW, WIDE, WIDE)],
        in_specs=[VMEM] * 9 + [HBM] * 5,
        out_specs=[VMEM] * 12,
        scratch_shapes=[pltpu.VMEM(s, NARROW) for s in weights] + [DMA((5,))],
        compiler_params=BIG,
        cost_estimate=block_cost(length, weights),
    )(
        latents, keep_row, keep_column, table, attn_b, fc_b, base.embed_weight, base.encoder_pos, mid.decoder_pos,
        enc.attn_weight, enc.proj_weight, enc.fc_one_weight, enc.fc_two_weight, mid.dec_weight,
    )
    return found[:8], found[8:]


def decode_kernel(before, route, extra, table, attn_b, fc_b, diff_pos, *refs):
    sources, outs, (flow_out, payload) = refs[:4], refs[4:12], refs[12:14]
    held, sem = refs[14:18], refs[18]
    moves = start_all(sources, held, sem)
    value = forward_block(before[...], DEC_ROWS, None, table, attn_b, fc_b, outs, held, moves)
    flow_out[...] = value
    hat, _ = whiten(flow_out[BUF:, :])
    value = hat * table[DEC_G : DEC_G + 1, :] + table[DEC_S : DEC_S + 1, :]
    conditions = (value + diff_pos[...].astype(WIDE)).astype(NARROW)
    slots = payload.shape[0]
    picks = lax.broadcasted_iota(jnp.int32, (slots, slots), 0) == route[...]
    picks = jnp.where(picks, 1.0, 0.0).astype(NARROW)
    payload[:, :D] = matmul(picks, conditions).astype(NARROW)
    payload[:, D:] = matmul(picks, extra[...]).astype(NARROW)


def decode(before, route, extra, table, attn_b, fc_b, dec, head):
    length = BUF + SEQ
    found = pl.pallas_call(
        decode_kernel,
        out_shape=forward_shapes(length)
        + [jax.ShapeDtypeStruct((length, D), WIDE), jax.ShapeDtypeStruct((SEQ, D + LANES), NARROW)],
        in_specs=[VMEM] * 7 + [HBM] * 4,
        out_specs=[VMEM] * 10,
        scratch_shapes=[pltpu.VMEM(s, NARROW) for s in BLOCK_WEIGHTS] + [DMA((4,))],
        compiler_params=BIG,
        cost_estimate=block_cost(length, BLOCK_WEIGHTS),
    )(
        before, route[None], extra, table, attn_b, fc_b, head.diffusion_pos,
        dec.attn_weight, dec.proj_weight, dec.fc_one_weight, dec.fc_two_weight,
    )
    return found[:8], found[8], found[9]


TWO_B, G_TWO, S_TWO, PROJ_B, G_ONE, S_ONE = 0, 1, 2, 3, 4, 5


def backward_block(value, first, stream, keep, table, mixed, totals, middle, outs, weights, slope, attended_grad, moves):
    out_low, inner_low, middle_low, mixed_low, sums, one_sum, mixed_sum = outs
    attn_w, proj_w, one_w, two_w = weights
    low = value.astype(NARROW)
    out_low[...] = low
    sums[TWO_B : TWO_B + 1, :] = column_sum(value)
    moves[0].wait()
    moves[1].wait()
    for k in range(MLP // PART):
        at = slice(k * PART, (k + 1) * PART)
        part = matmul_turned(low, two_w[at, :]) * slope[:, at]
        inner_low[:, at] = part.astype(NARROW)
        one_sum[0:1, at] = column_sum(part)
    moves[2].wait()
    part = matmul_turned(inner_low[...], one_w[...])
    hat, r = whiten(middle[...])
    sums[G_TWO : G_TWO + 1, :] = column_sum(part * hat)
    sums[S_TWO : S_TWO + 1, :] = column_sum(part)
    value = value + whiten_back(part * table[first + 2 : first + 3, :], hat, r)
    sums[PROJ_B : PROJ_B + 1, :] = column_sum(value)
    middle_low[...] = value.astype(NARROW)
    moves[3].wait()
    attended_grad[...] = matmul_turned(middle_low[...], proj_w[...]).astype(NARROW)
    sides = side_masks(value.shape[0])
    for pair in range(HEADS // 2):
        here = [slice(part * D + pair * LANES, part * D + (pair + 1) * LANES) for part in range(3)]
        q, k, v = (mixed[:, at] for at in here)
        g = attended_grad[:, here[0]]
        grads = [None, None, None]
        for i, side in enumerate(sides):
            q_side, k_side, g_side = one_side(q, side), one_side(k, side), one_side(g, side)
            scores = matmul_turned(q_side, k) * SCALE
            if keep is not None:
                scores = jnp.where(keep[0:1, :] > 0.0, scores, -1e30)
            probs = jnp.exp(scores - totals[:, 2 * pair + i : 2 * pair + i + 1])
            prob_grad = matmul_turned(g_side, v)
            score_grad = (probs * (prob_grad - jnp.sum(probs * prob_grad, -1, keepdims=True))).astype(NARROW)
            parts = (
                matmul(score_grad, k_side) * SCALE, matmul(score_grad.T, q_side) * SCALE, matmul(probs.astype(NARROW).T, g_side)
            )
            grads = [part if old is None else old + part for old, part in zip(grads, parts)]
        for at, part in zip(here, grads):
            mixed_low[:, at] = part.astype(NARROW)
            mixed_sum[0:1, at] = column_sum(part)
    moves[4].wait()
    part = matmul_turned(mixed_low[...], attn_w[...])
    hat, r = whiten(stream[...])
    sums[G_ONE : G_ONE + 1, :] = column_sum(part * hat)
    sums[S_ONE : S_ONE + 1, :] = column_sum(part)
    return value + whiten_back(part * table[first : first + 1, :], hat, r)


def backward_shapes(length, rows):
    shapes = [((length, D), NARROW), ((length, MLP), NARROW), ((length, D), NARROW), ((length, 3 * D), NARROW)]
    shapes += [((rows, D), WIDE), ((1, MLP), WIDE), ((1, 3 * D), WIDE)]
    return [jax.ShapeDtypeStruct(s, t) for s, t in shapes]


def backward_scratch(length, weights):
    return [pltpu.VMEM(s, NARROW) for s in weights] + [
        pltpu.VMEM((length, MLP), WIDE), pltpu.VMEM((length, D), NARROW), DMA((len(weights) + 1,))
    ]


MORE = 6


def decode_back_kernel(returned, route, flow_out, before, leaving, keep_column, table, mixed, totals, middle, *refs):
    slope_src, attn_src, proj_src, one_src, two_src, dec_src = refs[:6]
    outs, (token_grad, before_grad, decoded_low, leaving_grad) = refs[6:13], refs[13:17]
    attn_w, proj_w, one_w, two_w, dec_w, slope, attended_grad, sem = refs[17:]
    moves = start_all(
        (two_src, slope_src, one_src, proj_src, attn_src, dec_src), (two_w, slope, one_w, proj_w, attn_w, dec_w), sem
    )
    slots = returned.shape[0]
    picks = lax.broadcasted_iota(jnp.int32, (slots, slots), 1) == route[...]
    picks = jnp.where(picks, 1.0, 0.0).astype(NARROW)
    grad = matmul(picks, returned[...])
    token_grad[...] = grad
    sums = outs[4]
    hat, r = whiten(flow_out[BUF:, :])
    sums[MORE : MORE + 1, :] = column_sum(grad * hat)
    sums[MORE + 1 : MORE + 2, :] = column_sum(grad)
    before_grad[:BUF, :] = jnp.zeros((BUF, D), WIDE)
    before_grad[BUF:, :] = whiten_back(grad * table[DEC_G : DEC_G + 1, :], hat, r)
    value = backward_block(
        before_grad[...], DEC_ROWS, before, None, table, mixed, totals, middle, outs,
        (attn_w, proj_w, one_w, two_w), slope, attended_grad, moves,
    )
    before_grad[...] = value
    kept = jnp.where(keep_column[...] > 0.0, value, 0.0)
    sums[MORE + 2 : MORE + 3, :] = column_sum(kept)
    sums[MORE + 3 : MORE + 4, :] = column_sum(value - kept)
    decoded_low[...] = kept.astype(NARROW)
    moves[5].wait()
    part = matmul_turned(decoded_low[...], dec_w[...])
    hat, r = whiten(leaving[...])
    sums[MORE + 4 : MORE + 5, :] = column_sum(part * hat)
    sums[MORE + 5 : MORE + 6, :] = column_sum(part)
    leaving_grad[...] = whiten_back(part * table[ENC_G : ENC_G + 1, :], hat, r)


def decode_back(returned, route, flow_out, before, leaving, keep_column, table, stored, dec, mid):
    length = BUF + SEQ
    weights = BLOCK_WEIGHTS + ((D, D),)
    normed, mixed, totals, attended, middle, second, slope, active = stored
    found = pl.pallas_call(
        decode_back_kernel,
        out_shape=backward_shapes(length, 16)
        + [jax.ShapeDtypeStruct((n, D), t) for n, t in ((SEQ, WIDE), (length, WIDE), (length, NARROW), (length, WIDE))],
        in_specs=[VMEM] * 10 + [HBM] * 6,
        out_specs=[VMEM] * 11,
        scratch_shapes=backward_scratch(length, weights),
        compiler_params=BIG,
        cost_estimate=block_cost(length, weights),
    )(
        returned, route[:, None], flow_out, before, leaving, keep_column, table, mixed, totals, middle,
        slope, dec.attn_weight, dec.proj_weight, dec.fc_one_weight, dec.fc_two_weight, mid.dec_weight,
    )
    return found[:7], found[7:]


def encode_back_kernel(leaving_grad, latents, stream, keep_row, table, mixed, totals, middle, *refs):
    slope_src, attn_src, proj_src, one_src, two_src = refs[:5]
    outs, (stream_grad, embed_grad) = refs[5:12], refs[12:14]
    attn_w, proj_w, one_w, two_w, slope, attended_grad, sem = refs[14:]
    moves = start_all((two_src, slope_src, one_src, proj_src, attn_src), (two_w, slope, one_w, proj_w, attn_w), sem)
    value = backward_block(
        leaving_grad[...], ENC_ROWS, stream, keep_row, table, mixed, totals, middle, outs,
        (attn_w, proj_w, one_w, two_w), slope, attended_grad, moves,
    )
    stream_grad[...] = value
    sums = outs[4]
    sums[MORE : MORE + 1, :] = column_sum(stream_grad[:BUF, :])
    tokens = stream_grad[BUF:, :]
    sums[MORE + 1 : MORE + 2, :] = column_sum(tokens)
    embed_grad[...] = lax.dot_general(latents[...], tokens.astype(NARROW), (((0,), (0,)), ((), ())), preferred_element_type=WIDE)


def encode_back(leaving_grad, latents, stream, keep_row, table, stored, enc):
    length = BUF + SEQ
    normed, mixed, totals, attended, middle, second, slope, active = stored
    found = pl.pallas_call(
        encode_back_kernel,
        out_shape=backward_shapes(length, 8)
        + [jax.ShapeDtypeStruct((n, D), WIDE) for n in (length, TOK_CH)],
        in_specs=[VMEM] * 8 + [HBM] * 5,
        out_specs=[VMEM] * 9,
        scratch_shapes=backward_scratch(length, BLOCK_WEIGHTS),
        compiler_params=BIG,
        cost_estimate=block_cost(length, BLOCK_WEIGHTS),
    )(
        leaving_grad, latents, stream, keep_row, table, mixed, totals, middle,
        slope, enc.attn_weight, enc.proj_weight, enc.fc_one_weight, enc.fc_two_weight,
    )
    return found[:7], found[7:]


class Vector:
    def __init__(self, array, *parts):
        self.array, self.parts = array, parts


def block_grads(stored, found):
    normed, mixed, totals, attended, middle, second, slope, active = stored
    out_low, inner_low, middle_low, mixed_low, sums, one_sum, mixed_sum = found

    def row(k):
        return Vector(sums, (k, 0, D))

    return dict(
        norm_one_gain=row(G_ONE), norm_one_shift=row(S_ONE), attn_weight=(normed, mixed_low),
        attn_bias=Vector(mixed_sum, (0, 0, D), (0, 2 * D, D)), proj_weight=(attended, middle_low), proj_bias=row(PROJ_B),
        norm_two_gain=row(G_TWO), norm_two_shift=row(S_TWO), fc_one_weight=(second, inner_low),
        fc_one_bias=Vector(one_sum, (0, 0, MLP)), fc_two_weight=(active, out_low), fc_two_bias=row(TWO_B),
    )


SUMS = 9


def eighths(value):
    found = value[:8]
    for k in range(8, value.shape[0], 8):
        found = found + value[k : k + 8]
    return found


def sigmoid(value):
    return 0.5 + 0.5 * jnp.tanh(0.5 * value)


def silu_and_slope(value):
    s = sigmoid(value)
    silu = value * s
    return silu, s + silu * (1.0 - s)


def turned_matmul(left, right):
    return lax.dot_general(left, right, (((0,), (0,)), ((), ())), preferred_element_type=WIDE)


def head_kernel(
    divisor, arrived, features, levels, noise, input_w, final_w, wide_b, ada_b, final_b,
    cond_src, time_src, ada_src, inner_src, outer_src,
    signal, mod_low, modulated, inner_low, active, outer_low, joined_low, cond_low, cond_back, wide_sums, final_grad, input_grad, last,
    cond, joined, hidden, mod, hat, inner, outer, top, total, sums, cond_w, time_w, ada_w, inner_w, outer_w, weight_sem,
):
    step = pl.program_id(0)
    sources, held = (cond_src, time_src, ada_src, inner_src, outer_src), (cond_w, time_w, ada_w, inner_w, outer_w)
    moves = [pltpu.make_async_copy(s, t, weight_sem.at[i]) for i, (s, t) in enumerate(zip(sources, held))]

    def need(*which):
        @pl.when(step == 0)
        def _():
            for i in which:
                moves[i].wait()

    def bias(k):
        return wide_b[k : k + 1, :]

    def add_sum(k, value):
        sums[k * 8 : (k + 1) * 8, :] = sums[k * 8 : (k + 1) * 8, :] + eighths(value)

    @pl.when(step == 0)
    def _():
        for move in moves:
            move.start()
        for ref in (sums, total, final_grad, input_grad, last):
            ref[...] = jnp.zeros_like(ref)
        moves[0].wait()
        moves[1].wait()
        cond[...] = matmul(arrived[:, :D], cond_w[...]) + bias(0)

    clean = arrived[:, D : D + TOK_CH].astype(WIDE)
    marks = arrived[:, D + TOK_CH : D + TOK_CH + 1].astype(WIDE)
    noisy = (levels[:, 0:1] * clean + levels[:, 1:2] * noise[...]).astype(NARROW)
    value, slope = silu_and_slope(matmul(features[...], time_w[...]) + bias(1) + cond[...])
    joined[...] = slope
    signal[...] = value.astype(NARROW)
    h = matmul(noisy, input_w[...]) + bias(2)
    hidden[...] = h
    value, first_r = whiten(h)
    hat[...] = value
    need(2, 3, 4)
    mod[...] = matmul(signal[...], ada_w[...])
    normed = hat[...] * bias(3) + bias(4)
    scale = 1.0 + (mod[:, HW : 2 * HW] + ada_b[0:1, HW : 2 * HW])
    modulated[...] = (normed * scale + (mod[:, :HW] + ada_b[0:1, :HW])).astype(NARROW)
    mod[:, HW : 2 * HW] = scale
    value, slope = silu_and_slope(matmul(modulated[...], inner_w[...]) + bias(5))
    inner[...] = slope
    active[...] = value.astype(NARROW)
    out = matmul(active[...], outer_w[...]) + bias(6)
    outer[...] = out
    gate = mod[:, 2 * HW :] + ada_b[0:1, 2 * HW :]
    mod[:, 2 * HW :] = gate
    value, r = whiten(hidden[...] + gate * out)
    top[...] = value
    final = value.astype(NARROW)
    error = matmul(final, final_w[...]) + final_b[0:1, :] - noise[...]
    pred_grad = 2.0 * error * marks / divisor[0]
    pred_low = pred_grad.astype(NARROW)
    last[0:1, :TOK_CH] = last[0:1, :TOK_CH] + column_sum(pred_grad)
    last[1:2, 0:1] = last[1:2, 0:1] + column_sum(jnp.sum(error * error, -1, keepdims=True) * marks)
    final_grad[...] = final_grad[...] + turned_matmul(final, pred_low)
    g = whiten_back(matmul_turned(pred_low, final_w[...]), top[...], r)
    hidden[...] = g
    gate_grad = g * outer[...]
    mod_low[:, 2 * HW :] = gate_grad.astype(NARROW)
    add_sum(0, gate_grad)
    out_grad = g * mod[:, 2 * HW :]
    outer_low[...] = out_grad.astype(NARROW)
    add_sum(1, out_grad)
    g = matmul_turned(outer_low[...], outer_w[...]) * inner[...]
    inner_low[...] = g.astype(NARROW)
    add_sum(2, g)
    g = matmul_turned(inner_low[...], inner_w[...])
    value = hat[...]
    mod_low[:, :HW] = g.astype(NARROW)
    add_sum(3, g)
    scale_grad = g * (value * bias(3) + bias(4))
    mod_low[:, HW : 2 * HW] = scale_grad.astype(NARROW)
    add_sum(4, scale_grad)
    g = g * mod[:, HW : 2 * HW]
    add_sum(5, g)
    add_sum(6, g * value)
    g = hidden[...] + whiten_back(g * bias(3), value, first_r)
    add_sum(7, g)
    input_grad[...] = input_grad[...] + turned_matmul(noisy, g.astype(NARROW))
    g = matmul_turned(mod_low[...], ada_w[...]) * joined[...]
    joined_low[...] = g.astype(NARROW)
    add_sum(8, g)
    total[...] = total[...] + g

    @pl.when(step == pl.num_programs(0) - 1)
    def _():
        found = total[...].astype(NARROW)
        cond_low[...] = found
        cond_back[...] = matmul_turned(found, cond_w[...]).astype(NARROW)
        for k in range(SUMS):
            wide_sums[k : k + 1, :] = column_sum(sums[k * 8 : (k + 1) * 8, :])


def head_pass(p, arrived, steps, noise, divisor):
    slots = arrived.shape[0]
    times = steps.astype(WIDE)
    features = time_features(times).astype(NARROW).reshape(-1, FREQ)
    level = alpha_level(times).reshape(-1, 1)
    levels = jnp.concatenate([jnp.sqrt(level), jnp.sqrt(1.0 - level)], 1)
    flat_noise = noise.reshape(-1, TOK_CH)
    wide_b = jnp.stack(
        [p.cond_bias, p.time_bias, p.input_bias, p.head_gain, p.head_shift, p.inner_bias, p.outer_bias, p.outer_bias]
    ).astype(WIDE)
    total = COPIES * slots

    def tiled(width):
        return pl.BlockSpec((slots, width), lambda i: (i, 0))

    def whole(x):
        return pl.BlockSpec(x, lambda i: (0, 0), pipeline_mode=pl.Buffered(1))

    weights = (p.cond_weight, p.time_weight, p.ada_weight, p.inner_weight, p.outer_weight)
    small = (p.input_weight, p.final_weight, wide_b, p.ada_bias.astype(WIDE)[None], p.final_bias.astype(WIDE)[None])
    kept = [((total, w), NARROW, tiled(w)) for w in (HW, 3 * HW, HW, HW, HW, HW, HW)]
    once = (((slots, HW), NARROW), ((slots, D), NARROW), ((16, HW), WIDE), ((HW, TOK_CH), WIDE), ((TOK_CH, HW), WIDE), ((8, LANES), WIDE))
    kept += [(s, t, whole(s)) for s, t in once]
    flops = 4 * total * (FREQ * HW // 2 + 5 * HW * HW) + 4 * slots * D * HW
    found = pl.pallas_call(
        head_kernel,
        grid=(COPIES,),
        out_shape=[jax.ShapeDtypeStruct(s, t) for s, t, _ in kept],
        in_specs=[pl.BlockSpec(memory_space=pltpu.SMEM), whole(arrived.shape), tiled(FREQ), tiled(2), tiled(TOK_CH)]
        + [whole(x.shape) for x in small] + [HBM] * len(weights),
        out_specs=[spec for _, _, spec in kept],
        scratch_shapes=[pltpu.VMEM((slots, w), WIDE) for w in (HW, HW, HW, 3 * HW, HW, HW, HW, HW, HW)]
        + [pltpu.VMEM((SUMS * 8, HW), WIDE)] + [pltpu.VMEM(x.shape, NARROW) for x in weights] + [DMA((len(weights),))],
        compiler_params=BIG,
        cost_estimate=pl.CostEstimate(flops=flops, bytes_accessed=26 * total * HW, transcendentals=3 * total * HW),
    )(divisor[None], arrived, features, levels, flat_noise, *small, *weights)
    signal, mod_low, modulated, inner_low, active, outer_low, joined_low, cond_low, cond_back, sums, final_grad, input_grad, last = found

    def row(k):
        return Vector(sums, (k, 0, HW))

    grads = dict(
        final_weight=final_grad, final_bias=Vector(last, (0, 0, LANES)),
        outer_weight=(active, outer_low), outer_bias=row(1), inner_weight=(modulated, inner_low), inner_bias=row(2),
        head_gain=row(6), head_shift=row(5), ada_weight=(signal, mod_low),
        ada_bias=Vector(sums, (3, 0, HW), (4, 0, HW), (0, 0, HW)), time_weight=(features, joined_low), time_bias=row(8),
        cond_weight=(arrived, cond_low), cond_bias=row(8), input_weight=input_grad, input_bias=row(7),
    )
    return last[1, 0], grads, cond_back


def time_features(times):
    half = FREQ // 2
    freqs = jnp.exp(-math.log(10000.0) * jnp.arange(half, dtype=WIDE) / half)
    angles = times[..., None] * freqs
    return jnp.concatenate([jnp.cos(angles), jnp.sin(angles)], -1)


def alpha_level(times):
    start = math.cos(0.008 / 1.008 * math.pi / 2) ** 2
    return jnp.cos(((times + 1.0) / STEPS_T + 0.008) / 1.008 * math.pi / 2) ** 2 / start


def exchange(payload, parts):
    shape = payload.shape
    moved = lax.all_to_all(payload.reshape(parts, -1, shape[-1]), "dp", split_axis=0, concat_axis=0, tiled=True)
    return moved.reshape(shape)


def body(latents, route, labels, timesteps, noise, image_weight, weights, momentum, average):
    ranks_dp, ranks_rep = lax.axis_size("dp"), lax.axis_size("rep")
    ranks = ranks_dp * ranks_rep
    meshed = (ranks_dp, ranks_rep) == (8, 4)
    rows = route.shape[0]
    images = labels.shape[0]
    assert images == 1 and rows == SEQ
    size = weights.shape[0] // LANES
    padded = -(-(size + 1) // 48) * 48
    masked = route < rows
    own = jnp.sum(masked.astype(WIDE))
    low = weights.reshape(size, LANES).astype(NARROW)
    block = jnp.concatenate([low, jnp.full((padded - size, LANES), own).astype(NARROW)], 0)
    gathered = spread(block) if meshed else lax.all_gather(block, BOTH, axis=0)
    base, enc, mid, dec, head = groups = [types.SimpleNamespace() for _ in GROUPS]
    unpack(gathered, size, groups)
    count = jnp.sum(gathered[:, size, 0].astype(WIDE))
    keep = jnp.concatenate([jnp.ones((BUF,), WIDE), 1.0 - masked.astype(WIDE)])
    keep_row, keep_column = keep[None], keep[:, None]
    at = next(e.start for e in ENTRIES if e.sparse) + labels[0] * (D // LANES) + jnp.arange(D // LANES, dtype=jnp.int32)
    classes = gathered[at // size, at % size].reshape(D)
    table, attn_b, fc_b = block_vectors(base, enc, mid, dec, head, classes)
    enc_stored, (stream, encoded, leaving, before) = encode(
        latents, keep_row, keep_column, table, attn_b[0], fc_b[0], base, enc, mid
    )
    token_weight = jnp.broadcast_to(image_weight.astype(NARROW)[:, None], (rows, 1))
    extra = jnp.concatenate([latents, token_weight, jnp.zeros((rows, LANES - TOK_CH - 1), NARROW)], 1)
    dec_stored, flow_out, payload = decode(before, route, extra, table, attn_b[1], fc_b[1], dec, head)
    arrived = exchange(payload, ranks_dp)
    divisor = TOK_CH * COPIES * count
    loss_part, head_grads, cond_back = head_pass(head, arrived, timesteps, noise, divisor)
    returned = exchange(cond_back, ranks_dp)
    height = -(-((ranks - 1) * size + padded) // 8) * 8
    full = fold({(4, name): value for name, value in head_grads.items()}, labels, height)
    dec_found, (token_grad, before_grad, decoded_low, leaving_grad) = decode_back(
        returned, route, flow_out, before, leaving, keep_column, table, dec_stored, dec, mid
    )
    enc_found, (stream_grad, embed_grad) = encode_back(leaving_grad, latents, stream, keep_row, table, enc_stored, enc)

    def row(found, k):
        return Vector(found[4], (MORE + k, 0, D))

    head_grads = dict(diffusion_pos=token_grad, dec_gain=row(dec_found, 0), dec_shift=row(dec_found, 1))
    mid_grads = dict(
        enc_gain=row(dec_found, 4), enc_shift=row(dec_found, 5), dec_weight=(encoded, decoded_low), dec_bias=row(dec_found, 2),
        mask_token=row(dec_found, 3), decoder_pos=before_grad,
    )
    base_grads = dict(encoder_pos=stream_grad, class_table=row(enc_found, 0), embed_weight=embed_grad, embed_bias=row(enc_found, 1))
    grads = {}
    parts = (base_grads, block_grads(enc_stored, enc_found), mid_grads, block_grads(dec_stored, dec_found), head_grads)
    for group, found in enumerate(parts):
        grads.update({(group, name): value for name, value in found.items()})
    full = fold(grads, labels, height, full)
    if meshed:
        lane = lax.broadcasted_iota(jnp.int32, (8, LANES), 1)
        mark = jnp.where(lane == lax.axis_index("dp") * ranks_rep + lax.axis_index("rep"), loss_part, 0.0)
        owned = collect(full, mark, size, padded)
        loss = jnp.sum(owned[padded - 8, :ranks]) / divisor
        owned = owned[:size]
    else:
        loss = lax.psum(loss_part, BOTH) / divisor
        owned = lax.psum_scatter(full[: ranks * size].reshape(ranks, size, LANES), BOTH, scatter_dimension=0, tiled=False)
    owned = owned.reshape(-1)
    rate = 0.05 * math.sqrt(images * ranks * SEQ)
    new_momentum = 0.9 * momentum + owned
    new_weights = weights - rate * (owned + 0.9 * new_momentum)
    new_average = 0.75 * average + 0.25 * new_weights
    return new_weights, new_momentum, new_average, loss


def solution(mesh):
    flat = P(BOTH)
    placed = (P(BOTH, None), flat, flat, P(None, BOTH), P(None, BOTH, None), flat, flat, flat, flat)
    return jax.shard_map(body, mesh=mesh, in_specs=placed, out_specs=(flat, flat, flat, P()), check_vma=False)
```

```python
import functools
import heapq
import math
import types

import jax
import jax.numpy as jnp
from jax import lax
from jax.experimental import pallas as pl
from jax.experimental.pallas import tpu as pltpu
from jax.sharding import PartitionSpec as P

D = 768
HEADS = 12
HEAD_DIM = 64
MLP = 3072
HW = 1024
TOK_CH = 16
FREQ = 256
CLASSES = 1000
BUF = 64
SEQ = 256
COPIES = 4
STEPS_T = 1000
LANES = 128
WIDE = jnp.float32
NARROW = jnp.bfloat16
NORM_EPS = 1e-06
MESH = pl.DeviceIdType.MESH
ANY = pl.BlockSpec(memory_space=pl.ANY)
HBM = pl.BlockSpec(memory_space=pltpu.HBM)
VMEM = pl.BlockSpec(memory_space=pltpu.VMEM)
DMA = pltpu.SemaphoreType.DMA
BOTH = ("dp", "rep")


def block_shapes():
    return dict(
        norm_one_gain=(D,), norm_one_shift=(D,), attn_weight=(D, 3 * D), attn_bias=(2 * D,),
        proj_weight=(D, D), proj_bias=(D,), norm_two_gain=(D,), norm_two_shift=(D,),
        fc_one_weight=(D, MLP), fc_one_bias=(MLP,), fc_two_weight=(MLP, D), fc_two_bias=(D,),
    )


ENC, DEC = 1, 3
GROUPS = (
    dict(embed_weight=(TOK_CH, D), embed_bias=(D,), class_table=(CLASSES, D), encoder_pos=(BUF + SEQ, D)),
    block_shapes(),
    dict(enc_gain=(D,), enc_shift=(D,), dec_weight=(D, D), dec_bias=(D,), mask_token=(D,), decoder_pos=(BUF + SEQ, D)),
    block_shapes(),
    dict(
        dec_gain=(D,), dec_shift=(D,), diffusion_pos=(SEQ, D), input_weight=(TOK_CH, HW), input_bias=(HW,),
        time_weight=(FREQ, HW), time_bias=(HW,), cond_weight=(D, HW), cond_bias=(HW,), head_gain=(HW,),
        head_shift=(HW,), ada_weight=(HW, 3 * HW), ada_bias=(3 * HW,), inner_weight=(HW, HW), inner_bias=(HW,),
        outer_weight=(HW, HW), outer_bias=(HW,), final_weight=(HW, TOK_CH), final_bias=(TOK_CH,),
    ),
)


class Entry:
    def __init__(self, group, name, shape, start):
        self.group, self.name, self.shape, self.start = group, name, shape, start
        self.rows = -(-math.prod(shape) // LANES)
        self.matrix = len(shape) == 2 and shape[1] % LANES == 0
        self.across = shape[1] // LANES if self.matrix else 1
        self.sparse = name == GROUP_SPARSE


GROUP_SPARSE = next(name for name, shape in GROUPS[0].items() if shape[0] == CLASSES)


def entries():
    found, start = [], 0
    for group, shapes in enumerate(GROUPS):
        for name, shape in shapes.items():
            found.append(Entry(group, name, shape, start))
            start += found[-1].rows
    return found


ENTRIES = entries()
USED = ENTRIES[-1].start + ENTRIES[-1].rows


STACKS = ((D, D), (HW, HW))
PLACES = [types.SimpleNamespace() for _ in GROUPS]
STACK_OF = {}
STACK_ROWS = []
for number, (width, tallest) in enumerate(STACKS):
    top = 0
    for e in ENTRIES:
        if e.matrix and not e.sparse and e.shape[1] == width and e.shape[0] <= tallest:
            setattr(PLACES[e.group], e.name, (top, e.shape[0]))
            STACK_OF[e] = number, top
            top += e.shape[0]
    STACK_ROWS.append(top)


def placed(stack, place):
    return stack.at[pl.ds(*place)]


def block_height(entry, limit):
    best = 0
    for height in range(8, entry.shape[0] + 1, 8):
        if entry.shape[0] % height == 0 and height * entry.across <= limit:
            best = height
    return best


class Slots:
    def __init__(self, number):
        self.number, self.base, self.last = number, 0, {}

    def at(self, b):
        return (self.base + b) % self.number

    def claim(self, b, put):
        for k in range(self.number):
            before = self.last.get((self.base + k) % self.number)
            if before is not None:

                @pl.when(b == k)
                def _(before=before):
                    before().wait()

        @pl.when(b >= self.number)
        def _():
            put(b - self.number).wait()

    def close(self, blocks, put):
        base = self.base
        for b in range(max(0, blocks - self.number), blocks):
            self.last[(base + b) % self.number] = functools.partial(put, b)
        self.base = base + blocks

    def drain(self):
        for before in self.last.values():
            before().wait()


SLOTS = 8
OUT = 3


def unfold_kernel(rows, padded, items, g_ref, *refs):
    count = len(items)
    total = len(STACKS) + sum(e not in STACK_OF for e, _ in items)
    stacks, alone = refs[: len(STACKS)], iter(refs[len(STACKS) : total])
    outs = [(stacks[STACK_OF[e][0]], STACK_OF[e][1]) if e in STACK_OF else (next(alone), 0) for e, _ in items]
    first, second, wide, first_sem, second_sem, out_sem = refs[total : total + 6]
    kinds = sorted({(h, e.across) for e, h in items})
    stages = dict(zip(kinds, refs[total + 6 :]))
    turns = {kind: Slots(OUT) for kind in kinds}
    bases = [0]
    for entry, height in items:
        bases.append(bases[-1] + entry.shape[0] // height)

    def spot(t, b):
        entry, height = items[t]
        span = height * entry.across
        start = entry.start + b * span
        dev = start // rows
        row = start - dev * rows
        low = jnp.minimum(row // 8 * 8, padded - span - 8)
        return dev, row, low, row + span > rows

    def copies(t, b):
        entry, height = items[t]
        window = height * entry.across + 8
        dev, row, low, more = spot(t, b)
        slot = (bases[t] + b) % SLOTS
        one = pltpu.make_async_copy(
            g_ref.at[dev, pl.ds(pl.multiple_of(low, 8), window)], first.at[slot, pl.ds(0, window)], first_sem.at[slot]
        )
        two = pltpu.make_async_copy(
            g_ref.at[jnp.minimum(dev + 1, g_ref.shape[0] - 1), pl.ds(0, window)],
            second.at[slot, pl.ds(0, window)], second_sem.at[slot],
        )
        return one, two, more

    def fetch(t, b):
        one, two, more = copies(t, b)
        one.start()

        @pl.when(more)
        def _():
            two.start()

    def fetch_number(g):
        if g < bases[-1]:
            t = next(t for t in range(count) if g < bases[t + 1])
            fetch(t, g - bases[t])

    ahead = SLOTS - 1
    for g in range(ahead):
        fetch_number(g)
    for t, (entry, height) in enumerate(items):
        kind = (height, entry.across)
        stage, turn = stages[kind], turns[kind]
        window = height * entry.across + 8
        blocks = entry.shape[0] // height

        def put(b, t=t, stage=stage, height=height, place=turn.base, kind=kind):
            slot = (place + b) % OUT
            into, top = outs[t]
            return pltpu.make_async_copy(
                stage.at[slot], into.at[pl.ds(pl.multiple_of(top + b * height, 8), height)], out_sem.at[kinds.index(kind), slot]
            )

        def body(b, carry, t=t, entry=entry, height=height, window=window, blocks=blocks, stage=stage, turn=turn, put=put):
            @pl.when(b + ahead < blocks)
            def _():
                fetch(t, b + ahead)

            for k in range(max(0, ahead - blocks), ahead):

                @pl.when(b == blocks - ahead + k)
                def _(k=k):
                    fetch_number(bases[t + 1] + k)

            dev, row, low, _ = spot(t, b)
            slot = (bases[t] + b) % SLOTS
            one, two, more = copies(t, b)
            one.wait()
            wide[pl.ds(0, window), :] = first[slot, pl.ds(0, window), :].astype(WIDE)

            @pl.when(more)
            def _():
                two.wait()
                wide[pl.ds(rows - low, window), :] = second[slot, pl.ds(0, window), :].astype(WIDE)

            turn.claim(b, put)
            off = row - low
            place = turn.at(b)
            for j in range(entry.across):
                stage[place, :, j * LANES : (j + 1) * LANES] = wide[pl.ds(off + j, height, stride=entry.across), :].astype(NARROW)
            put(b).start()
            return carry

        lax.fori_loop(0, blocks, body, 0)
        turn.close(blocks, put)
    for turn in turns.values():
        turn.drain()


def unfold(gathered, rows):
    padded = gathered.shape[1]
    items = [(e, block_height(e, min(2304, rows - 16))) for e in ENTRIES if e.matrix and not e.sparse]
    tall = max(e.across * h for e, h in items) + 8
    kinds = sorted({(h, e.across) for e, h in items})
    total = sum(math.prod(e.shape) for e, _ in items)
    alone = [e for e, _ in items if e not in STACK_OF]
    shapes = [(n, width) for n, (width, _) in zip(STACK_ROWS, STACKS)] + [e.shape for e in alone]
    outs = pl.pallas_call(
        functools.partial(unfold_kernel, rows, padded, items),
        out_shape=[jax.ShapeDtypeStruct(s, NARROW) for s in shapes],
        in_specs=[ANY],
        out_specs=[ANY] * len(shapes),
        scratch_shapes=[
            pltpu.VMEM((SLOTS, tall, LANES), NARROW), pltpu.VMEM((SLOTS, tall, LANES), NARROW),
            pltpu.VMEM((2 * tall, LANES), WIDE), DMA((SLOTS,)), DMA((SLOTS,)), DMA((len(kinds), OUT)),
        ]
        + [pltpu.VMEM((OUT, h, n * LANES), NARROW) for h, n in kinds],
        compiler_params=pltpu.CompilerParams(vmem_limit_bytes=48 * 1000 * 1000),
        cost_estimate=pl.CostEstimate(flops=total, bytes_accessed=4 * total, transcendentals=0),
    )(gathered)
    return outs[: len(STACKS)], {(e.group, e.name): out for e, out in zip(alone, outs[len(STACKS) :])}


def rows_at(gathered, rows, start, number):
    pieces = []
    while number > 0:
        dev, row = divmod(start, rows)
        take = min(number, rows - row)
        pieces.append(gathered[dev, row : row + take])
        start, number = start + take, number - take
    return pieces[0] if len(pieces) == 1 else jnp.concatenate(pieces, 0)


def unpack(gathered, rows, groups):
    stacks, matrices = unfold(gathered, rows)
    for e in ENTRIES:
        if e.sparse or e in STACK_OF:
            continue
        if e.matrix:
            value = matrices[(e.group, e.name)]
        else:
            value = rows_at(gathered, rows, e.start, e.rows).reshape(-1)[: math.prod(e.shape)].reshape(e.shape)
        setattr(groups[e.group], e.name, value)
    return stacks


DEPTH = 3
TALL = 256
CHUNK = 512
NEXT = 3


def product_height(entry):
    return min(TALL, entry.shape[0])


def fold_kernel(products, items, plain, vectors, lone_place, zero, count, going_on, label, *refs):
    refs = list(refs)

    def take(number):
        found, refs[:number] = refs[:number], []
        return found

    small = take(count)
    pairs = take(2 * len(products))
    given = take(len(items))
    rest = take(len(plain))
    take(int(going_on))
    (full,) = take(1)
    pair_sem, given_sem, plain_sem, out_sem, vector_sem = take(5)
    held = take(2 * len(products))
    loads = take(len(items))
    stage, lines = take(2)
    gets = [pltpu.make_async_copy(given[i], loads[i], given_sem.at[i]) for i in range(len(items))]
    fills = []
    for i, entry in enumerate(products):
        for k in (2 * i, 2 * i + 1):
            source = pairs[k]
            if source.shape != held[k].shape:
                source = source.at[:, pl.ds(0, held[k].shape[1])]
            fills.append(pltpu.make_async_copy(source, held[k], pair_sem.at[k]))
    for move in gets + fills[: 2 * NEXT]:
        move.start()
    moves = []
    for i, (start, number) in enumerate(plain):
        move = pltpu.make_async_copy(rest[i].at[pl.ds(0, number)], full.at[pl.ds(start, number)], plain_sem.at[i])
        move.start()
        moves.append(move)
    at = 0
    for i, (entry, which, parts) in enumerate(vectors):
        begin = at
        for k, column, width in parts:
            for j in range(0, width, LANES):
                lines[at : at + 1, :] = small[which][k : k + 1, column + j : column + j + LANES]
                at += 1
        move = pltpu.make_async_copy(lines.at[pl.ds(begin, at - begin)], full.at[pl.ds(entry.start, at - begin)], vector_sem.at[i])
        move.start()
        moves.append(move)
        at = -(-at // 8) * 8
    if zero:
        lines[at : at + zero, :] = jnp.zeros((zero, LANES), WIDE)
        move = pltpu.make_async_copy(lines.at[pl.ds(at, zero)], full.at[pl.ds(USED, zero)], vector_sem.at[len(vectors)])
        move.start()
        moves.append(move)
    turn = Slots(DEPTH)

    def each(entry, height, make):
        span = height * entry.across
        blocks = entry.shape[0] // height

        def put(b, base=turn.base):
            slot = (base + b) % DEPTH
            return pltpu.make_async_copy(
                stage.at[slot, pl.ds(0, span)], full.at[pl.ds(entry.start + b * span, span)], out_sem.at[slot]
            )

        def step(b, carry):
            turn.claim(b, put)
            make(b, turn.at(b))
            put(b).start()
            return carry

        lax.fori_loop(0, blocks, step, 0)
        turn.close(blocks, put)

    if lone_place:
        sparse = next(e for e in ENTRIES if e.sparse)
        height = block_height(sparse, 1200)
        row, row_at = small[lone_place[0]], lone_place[1]

        def lone(b, slot):
            here = lax.broadcasted_iota(jnp.int32, (height, LANES), 0) + b * height == label[0]
            for j in range(sparse.across):
                value = jnp.broadcast_to(row[row_at : row_at + 1, j * LANES : (j + 1) * LANES], (height, LANES))
                stage[slot, pl.ds(j, height, stride=sparse.across), :] = jnp.where(here, value, 0.0)

        each(sparse, height, lone)
    for t, entry in enumerate(items):
        gets[t].wait()

        def make(b, slot, t=t, entry=entry):
            for j in range(entry.across):
                stage[slot, pl.ds(j, entry.shape[0], stride=entry.across), :] = loads[t][:, j * LANES : (j + 1) * LANES]

        each(entry, entry.shape[0], make)
    for t, entry in enumerate(products):
        left, right = held[2 * t], held[2 * t + 1]
        for move in fills[2 * (t + NEXT) : 2 * (t + NEXT) + 2]:
            move.start()
        fills[2 * t].wait()
        fills[2 * t + 1].wait()
        height = product_height(entry)
        chunk = math.gcd(CHUNK, entry.shape[1])

        def make(b, slot, left=left, right=right, entry=entry, height=height, chunk=chunk):
            turned = left[:, pl.ds(pl.multiple_of(b * height, LANES), height)].T
            for k in range(entry.shape[1] // chunk):
                found = jnp.dot(turned, right[:, k * chunk : (k + 1) * chunk], preferred_element_type=WIDE)
                for j in range(chunk // LANES):
                    at = pl.ds(k * (chunk // LANES) + j, height, stride=entry.across)
                    stage[slot, at, :] = found[:, j * LANES : (j + 1) * LANES]

        each(entry, height, make)
    turn.drain()
    for move in moves:
        move.wait()


def fold(grads, label, height_total, full=None):
    wanted = [e for e in ENTRIES if (e.group, e.name) in grads]
    found = {e: grads[(e.group, e.name)] for e in wanted}
    products = [e for e in wanted if isinstance(found[e], tuple)]
    items = [e for e in wanted if e.matrix and not isinstance(found[e], (tuple, Vector))]
    small, vectors, plain, values, lone_place = [], [], [], [], None
    for e in wanted:
        if isinstance(found[e], Vector):
            place = next((i for i, x in enumerate(small) if x is found[e].array), len(small))
            small[place : place + 1] = [found[e].array]
            if e.sparse:
                lone_place = (place, found[e].parts[0][0])
            else:
                vectors.append((e, place, found[e].parts))
        elif not e.matrix and e not in products:
            plain.append((e.start, e.rows))
            values.append(found[e].reshape(e.rows, LANES))
    zero = height_total - USED if full is None else 0
    before = [] if full is None else [full]
    lines = sum(-(-e.rows // 8) * 8 for e, _, _ in vectors) + -(-zero // 8) * 8
    operands = [x for e in products for x in found[e]]
    holds = [(x.shape[0], n) for e in products for x, n in zip(found[e], e.shape)]
    tall = max([e.rows for e in items] + [e.across * product_height(e) for e in products])
    total = sum(e.rows for e in wanted) * LANES
    taken = 1 + len(small) + len(operands) + len(items) + len(plain)
    flops = sum(2 * math.prod(e.shape) * operands[2 * i].shape[0] for i, e in enumerate(products))
    return pl.pallas_call(
        functools.partial(fold_kernel, products, items, plain, vectors, lone_place, zero, len(small), bool(before)),
        out_shape=jax.ShapeDtypeStruct((height_total, LANES), WIDE),
        in_specs=[pl.BlockSpec(memory_space=pltpu.SMEM)] + [VMEM] * len(small) + [ANY] * (len(operands) + len(items) + len(plain) + len(before)),
        out_specs=ANY,
        input_output_aliases={taken: 0} if before else {},
        scratch_shapes=[DMA((len(operands),)), DMA((len(items),)), DMA((max(len(plain), 1),)), DMA((DEPTH,)), DMA((len(vectors) + 1,))]
        + [pltpu.VMEM(s, NARROW) for s in holds]
        + [pltpu.VMEM(e.shape, WIDE) for e in items]
        + [pltpu.VMEM((DEPTH, tall, LANES), WIDE), pltpu.VMEM((lines, LANES), WIDE)],
        compiler_params=pltpu.CompilerParams(vmem_limit_bytes=62 * 1000 * 1000),
        cost_estimate=pl.CostEstimate(flops=flops, bytes_accessed=4 * total, transcendentals=0),
    )(label, *small, *operands, *[found[e] for e in items], *values, *before)


X, Y, Z = 0, 1, 2
TREES = ((Z, X, Y), (Z, Y, X), (X, Z, Y), (X, Z, Y), (Y, Z, X), (Y, Z, X))
SHARES = len(TREES)
FAR = 3


def onward(order, arrived, way, p):
    z, x, y = p
    found = []
    if arrived >= 0 and order[arrived] == Z and 0 <= z + way <= FAR:
        found.append(((z + way, x, y), arrived, way))
    for j in range(arrived + 1, 3):
        if order[j] == X:
            found.append(((z, 1 - x, y), j, 0))
        elif order[j] == Y:
            found.append(((z, x, 1 - y), j, 0))
        else:
            found += [((z + s, x, y), j, s) for s in (1, -1) if 0 <= z + s <= FAR]
    return found


@functools.cache
def flow(lag=0.4):
    chips = [(z, x, y) for z in range(FAR + 1) for x in range(2) for y in range(2)]
    events, queues, busy, come, sent = [], {}, set(), {}, []
    number = iter(range(10**9))
    for u in range(SHARES):
        for p in chips:
            heapq.heappush(events, (0.0, next(number), 0, (p, p, u, -1, 0)))

    def pump(link, t):
        if link in busy or not queues.get(link):
            return
        what = heapq.heappop(queues[link])[2]
        busy.add(link)
        sent.append((t, link, what[1], what[2]))
        heapq.heappush(events, (t + 1.0, next(number), 1, (link, what)))

    while events:
        t, _, kind, what = heapq.heappop(events)
        if kind == 1:
            link, piece = what
            busy.discard(link)
            heapq.heappush(events, (t + lag, next(number), 0, piece))
            pump(link, t)
            continue
        p, q, u, k, way = what
        come[(u, p, q)] = t
        for to, k2, way2 in onward(TREES[u], k, way, p):
            left = len(onward(TREES[u], k2, way2, to))
            heapq.heappush(queues.setdefault((p, to), []), ((-left, t), next(number), (to, q, u, k2, way2)))
            pump((p, to), t)
    return come, sent


def spread_order():
    keyed = {}
    for (u, p, q), t in flow()[0].items():
        keyed.setdefault((u, q[0] - p[0], (q[1] - p[1]) % 2, (q[2] - p[2]) % 2), []).append(t)
    return sorted(keyed, key=lambda k: (sum(keyed[k]) / len(keyed[k]), k))


def last_hop(u, dz, dx, dy):
    apart = [k for k in range(3) if (dx, dy, dz)[TREES[u][k]] != 0]
    return apart[-1] if apart else -1


def hops(u, dz, dx, dy):
    order, arrived = TREES[u], last_hop(u, dz, dx, dy)
    found = []
    if arrived >= 0 and order[arrived] == Z:
        found.append((1, 0, 0) if dz < 0 else (-1, 0, 0))
    for k in range(arrived + 1, 3):
        found += [[(0, 1, 0)], [(0, 0, 1)], [(1, 0, 0), (-1, 0, 0)]][order[k]]
    return found


def only(condition, action):
    if condition is None:
        action()
    else:
        pl.when(condition)(action)


def spread_kernel(flat, route, out, wide, own, load_sem, keep_sem, send_sem, link_sem, core_send, core_sem):
    dp, rep = lax.axis_index("dp"), lax.axis_index("rep")
    z, x, y, c = dp // 2, dp % 2, rep // 2, rep % 2
    size, padded = flat.shape[0], own.shape[0]
    unit = padded // SHARES
    sibling = (dp, y * 2 + 1 - c)
    loads = []
    for u in range(SHARES):
        part = pl.ds(u * unit, min(unit, size - u * unit))
        loads.append(pltpu.make_async_copy(flat.at[part], wide.at[part], load_sem.at[u]))
        loads[u].start()

    def device(dz, dx, dy):
        return ((z + dz) * 2 + (x + dx) % 2, (y + dy) % 2 * 2 + c)

    def exists(dz):
        return None if dz == 0 else (z + dz >= 0 if dz < 0 else z + dz <= FAR)

    barrier = pltpu.get_barrier_semaphore()
    near = ((0, 1, 0), (0, 0, 1), (1, 0, 0), (-1, 0, 0))
    for hop in near:
        only(exists(hop[0]), lambda: pl.semaphore_signal(barrier, inc=1, device_id=device(*hop), device_id_type=MESH))
    pl.semaphore_signal(barrier, inc=1, device_id=sibling, device_id_type=MESH)
    inner = z * (FAR - z)
    only(inner == 0, lambda: pl.semaphore_wait(barrier, len(near)))
    only(inner > 0, lambda: pl.semaphore_wait(barrier, len(near) + 1))
    masked = jnp.sum(jnp.where(route[...] < SEQ, 1.0, 0.0))
    keeps, ends, number = [], [], 0
    for u, dz, dx, dy in spread_order():
        part = pl.ds(u * unit, unit)
        q = ((z + dz) * 2 + (x + dx) % 2) * 2 + (y + dy) % 2
        mine = dz == 0 and dx == 0 and dy == 0
        i = u * 16 + q

        def copy(to, send, come, part=part, q=q, mine=mine):
            here = out.at[q * 2 + c, part]
            return pltpu.make_async_remote_copy(
                own.at[part] if mine else here, here, send, come, device_id=to, device_id_type=MESH
            )

        goes = [(hop, number + k) for k, hop in enumerate(hops(u, dz, dx, dy))]
        number += len(goes)

        def run(i=i, copy=copy, goes=goes, mine=mine):
            if not mine:
                copy(sibling, send_sem.at[0], link_sem.at[i]).wait_recv()
            for hop, n in goes:
                only(exists(hop[0]), lambda: copy(device(*hop), send_sem.at[n], link_sem.at[i]).start())
            copy(sibling, core_send.at[i], core_sem.at[i]).start()

        def finish(i=i, copy=copy, goes=goes):
            for hop, n in goes:
                only(exists(hop[0]), lambda: copy(device(*hop), send_sem.at[n], link_sem.at[i]).wait_send())
            copy(sibling, core_send.at[i], core_sem.at[i]).wait()

        if mine:
            loads[u].wait()
            if u == SHARES - 1:
                wide[size:padded, :] = jnp.broadcast_to(masked, (padded - size, LANES))
            own[part, :] = wide[part, :].astype(NARROW)
            keeps.append(pltpu.make_async_copy(own.at[part], out.at[dp * 4 + rep, part], keep_sem.at[u]))
            keeps[-1].start()
        there = None if dz == 0 else jnp.logical_and(z + dz >= 0, z + dz <= FAR)
        only(there, run)
        ends.append((there, finish))
    for there, finish in ends:
        only(there, finish)
    for keep in keeps:
        keep.wait()


def spread(flat, route, padded):
    pieces = SHARES * 16
    sends = sum(len(hops(*key)) for key in spread_order())
    return pl.pallas_call(
        spread_kernel,
        out_shape=jax.ShapeDtypeStruct((32, padded, LANES), NARROW),
        in_specs=[ANY, VMEM],
        out_specs=ANY,
        scratch_shapes=[
            pltpu.VMEM((padded, LANES), WIDE), pltpu.VMEM((padded, LANES), NARROW), DMA((SHARES,)), DMA((SHARES,)),
            DMA((sends,)), DMA((pieces,)), DMA((pieces,)), DMA((pieces,)),
        ],
        compiler_params=pltpu.CompilerParams(collective_id=0, has_side_effects=True),
    )(flat, route.reshape(-1, LANES))


class Chip:
    def __init__(self, low):
        dp, rep = lax.axis_index("dp"), lax.axis_index("rep")
        self.low = low
        self.z, self.x, self.y, self.c = dp // 2, dp % 2, rep // 2, rep % 2
        self.way = 1 - 2 * (self.z // 2)

    def device(self, q, other=0):
        z = self.z + self.way * (q[0] - self.low)
        return z * 2 + (self.x + q[1]) % 2, (self.y + q[2]) % 2 * 2 + (self.c + other) % 2

    def block(self, q, other=0):
        dp, rep = self.device(q, other)
        return dp * 4 + rep

    def greet(self):
        low = self.low
        near = [(low, 1, 0), (low, 0, 1), (low + 1, 0, 0)] + ([(low - 1, 0, 0)] if low else [])
        barrier = pltpu.get_barrier_semaphore()
        for q in near:
            pl.semaphore_signal(barrier, inc=1, device_id=self.device(q), device_id_type=MESH)
        pl.semaphore_signal(barrier, inc=1, device_id=self.device((low, 0, 0), 1), device_id_type=MESH)
        pl.semaphore_wait(barrier, len(near) + 1)


def seen_from(p, r):
    low, way = min(p[0], FAR - p[0]), 1 if p[0] < 2 else -1
    return low + way * (r[0] - p[0]), (r[1] - p[1]) % 2, (r[2] - p[2]) % 2


@functools.cache
def sum_programs():
    come, sent = flow()
    last = max(come.values())
    found = []
    for z in (0, 1):
        p = (z, 0, 0)
        kids, parent, when = {}, {}, {}
        for t, link, q, u in sent:
            if link[0] == p:
                kids.setdefault((u, q), []).append(link[1])
                if q == p:
                    when[(u, p)] = max(when.get((u, p), 0.0), last - t)
            if link[1] == p:
                parent[(u, q)] = link[0]
                when[(u, q)] = last - t - 1.0
        tasks = sorted(when, key=lambda k: (when[k], k))
        found.append([(u, q, sorted(kids.get((u, q), [])), parent.get((u, q))) for u, q in tasks])
    return found


@functools.cache
def landing():
    return [{key: i for i, key in enumerate((u, q, k) for u, q, kids, _ in tasks for k in kids)} for tasks in sum_programs()]


RING = 12
SIDE = 4
EARLY = 12
STEP = 40


def add_rows(into, terms):
    def body(i, carry):
        at = pl.ds(pl.multiple_of(i * STEP, 8), STEP)
        total = into[at, :]
        for term in terms:
            total = total + term[at, :]
        into[at, :] = total
        return carry

    lax.fori_loop(0, into.shape[0] // STEP, body, 0)


def collect_at(low, size, full, mark, out, aside, store, ring, side, ring_sem, side_sem, send_sem, link_sem, core_send, core_sem, out_sem, marks, mark_sem):
    chip = Chip(low)
    me = (low, 0, 0)
    tasks, spots = sum_programs()[low], landing()
    count, unit = len(tasks), ring.shape[1]
    chip.greet()

    def part(i, other=0):
        return full.at[pl.ds(chip.block(tasks[i][1], other) * size + tasks[i][0] * unit, unit)]

    def across(i):
        return pltpu.make_async_remote_copy(
            part(i, 1), aside.at[i], core_send.at[i], core_sem.at[i], device_id=chip.device(me, 1), device_id_type=MESH
        )

    def ours(i):
        return pltpu.make_async_copy(part(i), ring.at[i % RING], ring_sem.at[i % RING])

    def theirs(i):
        return pltpu.make_async_copy(aside.at[i], side.at[i % SIDE], side_sem.at[i % SIDE])

    def along(i, spot, to):
        return pltpu.make_async_remote_copy(
            ring.at[i % RING], store.at[spot], send_sem.at[i], link_sem.at[spot], device_id=chip.device(to), device_id_type=MESH
        )

    tail = pl.ds(unit - 8, 8)
    ours_too = pltpu.make_async_copy(mark, marks.at[0], mark_sem.at[0])
    theirs_too = pltpu.make_async_remote_copy(
        mark, marks.at[1], mark_sem.at[1], mark_sem.at[2], device_id=chip.device(me, 1), device_id_type=MESH
    )
    ours_too.start()
    theirs_too.start()
    leaving = {}

    def fetch(i):
        if i - RING in leaving:
            leaving.pop(i - RING)()
        ours(i).start()
        across(i).wait_recv()
        theirs(i).start()

    for i in range(EARLY):
        across(i).start()
    for i in range(SIDE - 1):
        fetch(i)
    ours_too.wait()
    theirs_too.wait()
    for i, (u, q, kids, to) in enumerate(tasks):
        if i + EARLY < count:
            across(i + EARLY).start()
        if i + SIDE - 1 < count:
            fetch(i + SIDE - 1)
        ours(i).wait()
        theirs(i).wait()
        if u == SHARES - 1:
            ring[i % RING, tail, :] = marks[0] + marks[1]
            side[i % SIDE, tail, :] = jnp.zeros((8, LANES), WIDE)
        terms = [side.at[i % SIDE]]
        for kid in kids:
            spot = spots[low][(u, q, kid)]
            along(i, spot, kid).wait_recv()
            terms.append(store.at[spot])
        add_rows(ring.at[i % RING], terms)
        if to is None:
            move = pltpu.make_async_copy(ring.at[i % RING], out.at[pl.ds(u * unit, unit)], out_sem.at[u])
            move.start()
            leaving[i] = move.wait
        else:
            move = along(i, spots[min(to[0], FAR - to[0])][(u, seen_from(to, q), seen_from(to, me))], to)
            move.start()
            leaving[i] = move.wait_send
    for i in list(leaving):
        leaving.pop(i)()
    for i in range(count):
        across(i).wait_send()


def collect_kernel(size, *refs):
    z = lax.axis_index("dp") // 2
    inner = z * (FAR - z)

    @pl.when(inner == 0)
    def _():
        collect_at(0, size, *refs)

    @pl.when(inner > 0)
    def _():
        collect_at(1, size, *refs)


def collect(full, mark, size, rows):
    slots = max(len(spots) for spots in landing())
    count, unit = len(sum_programs()[0]), rows // SHARES
    return pl.pallas_call(
        functools.partial(collect_kernel, size),
        out_shape=(jax.ShapeDtypeStruct((rows, LANES), WIDE), jax.ShapeDtypeStruct((count, unit, LANES), WIDE)),
        in_specs=[ANY, ANY],
        out_specs=(ANY, ANY),
        scratch_shapes=[
            pltpu.VMEM((slots, unit, LANES), WIDE), pltpu.VMEM((RING, unit, LANES), WIDE), pltpu.VMEM((SIDE, unit, LANES), WIDE),
            DMA((RING,)), DMA((SIDE,)), DMA((count,)), DMA((slots,)), DMA((count,)), DMA((count,)), DMA((SHARES,)),
            pltpu.VMEM((2, 8, LANES), WIDE), DMA((3,)),
        ],
        compiler_params=pltpu.CompilerParams(collective_id=1, has_side_effects=True, vmem_limit_bytes=62 * 1000 * 1000),
    )(full, mark)[0]


HALF_ROOT = math.sqrt(0.5)
PDF = 1.0 / math.sqrt(2.0 * math.pi)
SCALE = HEAD_DIM ** (-0.5)
PART = 512
BIG = pltpu.CompilerParams(vmem_limit_bytes=66 * 1000 * 1000)
BLOCK_WEIGHTS = ((D, 3 * D), (D, D), (D, MLP), (MLP, D))
EMBED_B, ENC_G, ENC_S, DEC_B, MASK_T, DEC_G, DEC_S, CLASS, ENC_ROWS, DEC_ROWS, ALL_ROWS = 0, 1, 2, 3, 4, 5, 6, 7, 8, 14, 24


def matmul(left, right):
    return jnp.dot(left, right, preferred_element_type=WIDE)


def matmul_turned(left, right):
    return lax.dot_general(left, right, (((1,), (1,)), ((), ())), preferred_element_type=WIDE)


def column_sum(value):
    return jnp.sum(value, 0, keepdims=True)


def whiten(value):
    centered = value - jnp.mean(value, -1, keepdims=True)
    r = lax.rsqrt(jnp.mean(centered * centered, -1, keepdims=True) + NORM_EPS)
    return centered * r, r


def whiten_back(grad, hat, r):
    return r * (grad - jnp.mean(grad, -1, keepdims=True) - hat * jnp.mean(grad * hat, -1, keepdims=True))


def side_masks(length):
    lane = lax.broadcasted_iota(jnp.int32, (length, LANES), 1)
    return lane < HEAD_DIM, lane >= HEAD_DIM


def one_side(value, side):
    return jnp.where(side, value, jnp.zeros_like(value))


def start_all(sources, targets, sem):
    moves = [pltpu.make_async_copy(s, t, sem.at[i]) for i, (s, t) in enumerate(zip(sources, targets))]
    for move in moves:
        move.start()
    return moves


def block_vectors(base, enc, mid, dec, head, classes):
    rows = [base.embed_bias, mid.enc_gain, mid.enc_shift, mid.dec_bias, mid.mask_token, head.dec_gain, head.dec_shift, classes]
    for p in (enc, dec):
        rows += [p.norm_one_gain, p.norm_one_shift, p.norm_two_gain, p.norm_two_shift, p.proj_bias, p.fc_two_bias]
    rows += rows[: ALL_ROWS - len(rows)]
    gap = jnp.zeros((D,), NARROW)
    attn_b = [jnp.concatenate([p.attn_bias[:D], gap, p.attn_bias[D:]]).astype(WIDE)[None] for p in (enc, dec)]
    return jnp.stack(rows).astype(WIDE), attn_b, [p.fc_one_bias.astype(WIDE)[None] for p in (enc, dec)]


def forward_block(value, first, keep, table, attn_b, fc_b, outs, weights, moves):
    normed, mixed, totals, attended, middle, second, slope, active = outs
    attn_w, proj_w, one_w, two_w = weights
    hat, _ = whiten(value)
    normed[...] = (hat * table[first : first + 1, :] + table[first + 1 : first + 2, :]).astype(NARROW)
    moves[0].wait()
    for k in range(3):
        at = slice(k * D, (k + 1) * D)
        mixed[:, at] = (matmul(normed[...], attn_w[:, at]) + attn_b[0:1, at]).astype(NARROW)
    sides = side_masks(value.shape[0])
    for pair in range(HEADS // 2):
        q, k, v = (mixed[:, part * D + pair * LANES : part * D + (pair + 1) * LANES] for part in range(3))
        found = None
        for i, side in enumerate(sides):
            scores = matmul_turned(one_side(q, side), k) * SCALE
            if keep is not None:
                scores = jnp.where(keep[0:1, :] > 0.0, scores, -1e30)
            top = jnp.max(scores, -1, keepdims=True)
            powers = jnp.exp(scores - top)
            total = jnp.sum(powers, -1, keepdims=True)
            totals[:, 2 * pair + i : 2 * pair + i + 1] = top + jnp.log(total)
            probs = (powers * (1.0 / total)).astype(NARROW)
            part = matmul(probs, one_side(v, side))
            found = part if found is None else found + part
        attended[:, pair * LANES : (pair + 1) * LANES] = found.astype(NARROW)
    moves[1].wait()
    value = value + matmul(attended[...], proj_w[...]) + table[first + 4 : first + 5, :]
    middle[...] = value
    hat, _ = whiten(value)
    second[...] = (hat * table[first + 2 : first + 3, :] + table[first + 3 : first + 4, :]).astype(NARROW)
    moves[2].wait()
    for k in range(MLP // PART):
        at = slice(k * PART, (k + 1) * PART)
        value = matmul(second[...], one_w[:, at]) + fc_b[0:1, at]
        share = 0.5 + 0.5 * lax.erf(value * HALF_ROOT)
        active[:, at] = (value * share).astype(NARROW)
        slope[:, at] = share + value * (PDF * jnp.exp(-0.5 * value * value))
    moves[3].wait()
    return middle[...] + matmul(active[...], two_w[...]) + table[first + 5 : first + 6, :]


def forward_shapes(length):
    widths = [(D, NARROW), (3 * D, NARROW), (LANES, WIDE), (D, NARROW), (D, WIDE), (D, NARROW), (MLP, WIDE), (MLP, NARROW)]
    return [jax.ShapeDtypeStruct((length, w), t) for w, t in widths]


def encode_kernel(latents, keep_row, keep_column, table, attn_b, fc_b, stack, *refs):
    (attn_src, one_src, two_src), outs, (stream, encoded, leaving, before) = refs[:3], refs[3:11], refs[11:15]
    held, (embed_w, enc_pos, dec_pos), sem = refs[15:20], refs[20:23], refs[23]
    base, enc, mid = PLACES[:3]
    early = [placed(stack, place) for place in (base.embed_weight, base.encoder_pos, mid.decoder_pos)]
    sources = [attn_src, placed(stack, enc.proj_weight), one_src, two_src, placed(stack, mid.dec_weight)]
    moves = start_all(early + sources, (embed_w, enc_pos, dec_pos) + tuple(held), sem)
    for move in moves[:3]:
        move.wait()
    moves = moves[3:]
    pos = enc_pos[...].astype(WIDE)
    stream[:BUF, :] = table[CLASS : CLASS + 1, :] + pos[:BUF]
    stream[BUF:, :] = matmul(latents[...], embed_w[...]) + table[EMBED_B : EMBED_B + 1, :] + pos[BUF:]
    value = forward_block(stream[...], ENC_ROWS, keep_row, table, attn_b, fc_b, outs, held[:4], moves)
    leaving[...] = value
    hat, _ = whiten(value)
    encoded[...] = (hat * table[ENC_G : ENC_G + 1, :] + table[ENC_S : ENC_S + 1, :]).astype(NARROW)
    moves[4].wait()
    value = matmul(encoded[...], held[4][...]) + table[DEC_B : DEC_B + 1, :]
    value = jnp.where(keep_column[...] > 0.0, value, table[MASK_T : MASK_T + 1, :])
    before[...] = value + dec_pos[...].astype(WIDE)


def block_cost(length, weights):
    work = sum(math.prod(s) for s in weights)
    return pl.CostEstimate(flops=2 * length * work, bytes_accessed=2 * work + 36 * length * D, transcendentals=4 * length * MLP)


def encode(latents, keep_row, keep_column, table, attn_b, fc_b, stack, enc):
    length = BUF + SEQ
    weights = BLOCK_WEIGHTS + ((D, D),)
    found = pl.pallas_call(
        encode_kernel,
        out_shape=forward_shapes(length)
        + [jax.ShapeDtypeStruct((length, D), t) for t in (WIDE, NARROW, WIDE, WIDE)],
        in_specs=[VMEM] * 6 + [HBM] * 4,
        out_specs=[VMEM] * 12,
        scratch_shapes=[pltpu.VMEM(s, NARROW) for s in weights + ((TOK_CH, D), (length, D), (length, D))] + [DMA((8,))],
        compiler_params=BIG,
        cost_estimate=block_cost(length, weights),
    )(
        latents, keep_row, keep_column, table, attn_b, fc_b, stack, enc.attn_weight, enc.fc_one_weight, enc.fc_two_weight,
    )
    return found[:8], found[8:]


def decode_kernel(before, route, extra, table, attn_b, fc_b, stack, *refs):
    (attn_src, one_src, two_src), outs, (flow_out, payload) = refs[:3], refs[3:11], refs[11:13]
    held, diff_pos, sem = refs[13:17], refs[17], refs[18]
    sources = [attn_src, placed(stack, PLACES[DEC].proj_weight), one_src, two_src, placed(stack, PLACES[-1].diffusion_pos)]
    moves = start_all(sources, tuple(held) + (diff_pos,), sem)
    value = forward_block(before[...], DEC_ROWS, None, table, attn_b, fc_b, outs, held, moves)
    flow_out[...] = value
    hat, _ = whiten(flow_out[BUF:, :])
    moves[4].wait()
    value = hat * table[DEC_G : DEC_G + 1, :] + table[DEC_S : DEC_S + 1, :]
    conditions = (value + diff_pos[...].astype(WIDE)).astype(NARROW)
    slots = payload.shape[0]
    picks = lax.broadcasted_iota(jnp.int32, (slots, slots), 0) == route[...]
    picks = jnp.where(picks, 1.0, 0.0).astype(NARROW)
    payload[:, :D] = matmul(picks, conditions).astype(NARROW)
    payload[:, D:] = matmul(picks, extra[...]).astype(NARROW)


def decode(before, route, extra, table, attn_b, fc_b, stack, dec):
    length = BUF + SEQ
    found = pl.pallas_call(
        decode_kernel,
        out_shape=forward_shapes(length)
        + [jax.ShapeDtypeStruct((length, D), WIDE), jax.ShapeDtypeStruct((SEQ, D + LANES), NARROW)],
        in_specs=[VMEM] * 6 + [HBM] * 4,
        out_specs=[VMEM] * 10,
        scratch_shapes=[pltpu.VMEM(s, NARROW) for s in BLOCK_WEIGHTS + ((SEQ, D),)] + [DMA((5,))],
        compiler_params=BIG,
        cost_estimate=block_cost(length, BLOCK_WEIGHTS),
    )(
        before, route[None], extra, table, attn_b, fc_b, stack, dec.attn_weight, dec.fc_one_weight, dec.fc_two_weight,
    )
    return found[:8], found[8], found[9]


TWO_B, G_TWO, S_TWO, PROJ_B, G_ONE, S_ONE = 0, 1, 2, 3, 4, 5


def backward_block(value, first, stream, keep, table, mixed, totals, middle, outs, weights, slope, attended_grad, moves):
    out_low, inner_low, middle_low, mixed_low, sums, one_sum, mixed_sum = outs
    attn_w, proj_w, one_w, two_w = weights
    low = value.astype(NARROW)
    out_low[...] = low
    sums[TWO_B : TWO_B + 1, :] = column_sum(value)
    moves[0].wait()
    moves[1].wait()
    for k in range(MLP // PART):
        at = slice(k * PART, (k + 1) * PART)
        part = matmul_turned(low, two_w[at, :]) * slope[:, at]
        inner_low[:, at] = part.astype(NARROW)
        one_sum[0:1, at] = column_sum(part)
    moves[2].wait()
    part = matmul_turned(inner_low[...], one_w[...])
    hat, r = whiten(middle[...])
    sums[G_TWO : G_TWO + 1, :] = column_sum(part * hat)
    sums[S_TWO : S_TWO + 1, :] = column_sum(part)
    value = value + whiten_back(part * table[first + 2 : first + 3, :], hat, r)
    sums[PROJ_B : PROJ_B + 1, :] = column_sum(value)
    middle_low[...] = value.astype(NARROW)
    moves[3].wait()
    attended_grad[...] = matmul_turned(middle_low[...], proj_w[...]).astype(NARROW)
    sides = side_masks(value.shape[0])
    for pair in range(HEADS // 2):
        here = [slice(part * D + pair * LANES, part * D + (pair + 1) * LANES) for part in range(3)]
        q, k, v = (mixed[:, at] for at in here)
        g = attended_grad[:, here[0]]
        grads = [None, None, None]
        for i, side in enumerate(sides):
            q_side, k_side, g_side = one_side(q, side), one_side(k, side), one_side(g, side)
            scores = matmul_turned(q_side, k) * SCALE
            if keep is not None:
                scores = jnp.where(keep[0:1, :] > 0.0, scores, -1e30)
            probs = jnp.exp(scores - totals[:, 2 * pair + i : 2 * pair + i + 1])
            prob_grad = matmul_turned(g_side, v)
            score_grad = (probs * (prob_grad - jnp.sum(probs * prob_grad, -1, keepdims=True))).astype(NARROW)
            parts = (
                matmul(score_grad, k_side) * SCALE, matmul(score_grad.T, q_side) * SCALE, matmul(probs.astype(NARROW).T, g_side)
            )
            grads = [part if old is None else old + part for old, part in zip(grads, parts)]
        for at, part in zip(here, grads):
            mixed_low[:, at] = part.astype(NARROW)
            mixed_sum[0:1, at] = column_sum(part)
    moves[4].wait()
    part = matmul_turned(mixed_low[...], attn_w[...])
    hat, r = whiten(stream[...])
    sums[G_ONE : G_ONE + 1, :] = column_sum(part * hat)
    sums[S_ONE : S_ONE + 1, :] = column_sum(part)
    return value + whiten_back(part * table[first : first + 1, :], hat, r)


def backward_shapes(length, rows):
    shapes = [((length, D), NARROW), ((length, MLP), NARROW), ((length, D), NARROW), ((length, 3 * D), NARROW)]
    shapes += [((rows, D), WIDE), ((1, MLP), WIDE), ((1, 3 * D), WIDE)]
    return [jax.ShapeDtypeStruct(s, t) for s, t in shapes]


def backward_scratch(length, weights):
    return [pltpu.VMEM(s, NARROW) for s in weights] + [
        pltpu.VMEM((length, MLP), WIDE), pltpu.VMEM((length, D), NARROW), DMA((len(weights) + 1,))
    ]


MORE = 6


def decode_back_kernel(returned, route, flow_out, before, leaving, keep_column, table, mixed, totals, middle, *refs):
    slope_src, attn_src, one_src, two_src, stack = refs[:5]
    proj_src, dec_src = placed(stack, PLACES[DEC].proj_weight), placed(stack, PLACES[2].dec_weight)
    outs, (token_grad, before_grad, decoded_low, leaving_grad) = refs[5:12], refs[12:16]
    attn_w, proj_w, one_w, two_w, dec_w, slope, attended_grad, sem = refs[16:]
    moves = start_all(
        (two_src, slope_src, one_src, proj_src, attn_src, dec_src), (two_w, slope, one_w, proj_w, attn_w, dec_w), sem
    )
    slots = returned.shape[0]
    picks = lax.broadcasted_iota(jnp.int32, (slots, slots), 1) == route[...]
    picks = jnp.where(picks, 1.0, 0.0).astype(NARROW)
    grad = matmul(picks, returned[...])
    token_grad[...] = grad
    sums = outs[4]
    hat, r = whiten(flow_out[BUF:, :])
    sums[MORE : MORE + 1, :] = column_sum(grad * hat)
    sums[MORE + 1 : MORE + 2, :] = column_sum(grad)
    before_grad[:BUF, :] = jnp.zeros((BUF, D), WIDE)
    before_grad[BUF:, :] = whiten_back(grad * table[DEC_G : DEC_G + 1, :], hat, r)
    value = backward_block(
        before_grad[...], DEC_ROWS, before, None, table, mixed, totals, middle, outs,
        (attn_w, proj_w, one_w, two_w), slope, attended_grad, moves,
    )
    before_grad[...] = value
    kept = jnp.where(keep_column[...] > 0.0, value, 0.0)
    sums[MORE + 2 : MORE + 3, :] = column_sum(kept)
    sums[MORE + 3 : MORE + 4, :] = column_sum(value - kept)
    decoded_low[...] = kept.astype(NARROW)
    moves[5].wait()
    part = matmul_turned(decoded_low[...], dec_w[...])
    hat, r = whiten(leaving[...])
    sums[MORE + 4 : MORE + 5, :] = column_sum(part * hat)
    sums[MORE + 5 : MORE + 6, :] = column_sum(part)
    leaving_grad[...] = whiten_back(part * table[ENC_G : ENC_G + 1, :], hat, r)


def decode_back(returned, route, flow_out, before, leaving, keep_column, table, stored, stack, dec):
    length = BUF + SEQ
    weights = BLOCK_WEIGHTS + ((D, D),)
    normed, mixed, totals, attended, middle, second, slope, active = stored
    found = pl.pallas_call(
        decode_back_kernel,
        out_shape=backward_shapes(length, 16)
        + [jax.ShapeDtypeStruct((n, D), t) for n, t in ((SEQ, WIDE), (length, WIDE), (length, NARROW), (length, WIDE))],
        in_specs=[VMEM] * 10 + [HBM] * 5,
        out_specs=[VMEM] * 11,
        scratch_shapes=backward_scratch(length, weights),
        compiler_params=BIG,
        cost_estimate=block_cost(length, weights),
    )(
        returned, route[:, None], flow_out, before, leaving, keep_column, table, mixed, totals, middle,
        slope, dec.attn_weight, dec.fc_one_weight, dec.fc_two_weight, stack,
    )
    return found[:7], found[7:]


def encode_back_kernel(leaving_grad, latents, stream, keep_row, table, mixed, totals, middle, *refs):
    slope_src, attn_src, one_src, two_src, stack = refs[:5]
    proj_src = placed(stack, PLACES[ENC].proj_weight)
    outs, (stream_grad, embed_grad) = refs[5:12], refs[12:14]
    attn_w, proj_w, one_w, two_w, slope, attended_grad, sem = refs[14:]
    moves = start_all((two_src, slope_src, one_src, proj_src, attn_src), (two_w, slope, one_w, proj_w, attn_w), sem)
    value = backward_block(
        leaving_grad[...], ENC_ROWS, stream, keep_row, table, mixed, totals, middle, outs,
        (attn_w, proj_w, one_w, two_w), slope, attended_grad, moves,
    )
    stream_grad[...] = value
    sums = outs[4]
    sums[MORE : MORE + 1, :] = column_sum(stream_grad[:BUF, :])
    tokens = stream_grad[BUF:, :]
    sums[MORE + 1 : MORE + 2, :] = column_sum(tokens)
    embed_grad[...] = lax.dot_general(latents[...], tokens.astype(NARROW), (((0,), (0,)), ((), ())), preferred_element_type=WIDE)


def encode_back(leaving_grad, latents, stream, keep_row, table, stored, stack, enc):
    length = BUF + SEQ
    normed, mixed, totals, attended, middle, second, slope, active = stored
    found = pl.pallas_call(
        encode_back_kernel,
        out_shape=backward_shapes(length, 8)
        + [jax.ShapeDtypeStruct((n, D), WIDE) for n in (length, TOK_CH)],
        in_specs=[VMEM] * 8 + [HBM] * 5,
        out_specs=[VMEM] * 9,
        scratch_shapes=backward_scratch(length, BLOCK_WEIGHTS),
        compiler_params=BIG,
        cost_estimate=block_cost(length, BLOCK_WEIGHTS),
    )(
        leaving_grad, latents, stream, keep_row, table, mixed, totals, middle,
        slope, enc.attn_weight, enc.fc_one_weight, enc.fc_two_weight, stack,
    )
    return found[:7], found[7:]


class Vector:
    def __init__(self, array, *parts):
        self.array, self.parts = array, parts


def block_grads(stored, found):
    normed, mixed, totals, attended, middle, second, slope, active = stored
    out_low, inner_low, middle_low, mixed_low, sums, one_sum, mixed_sum = found

    def row(k):
        return Vector(sums, (k, 0, D))

    return dict(
        norm_one_gain=row(G_ONE), norm_one_shift=row(S_ONE), attn_weight=(normed, mixed_low),
        attn_bias=Vector(mixed_sum, (0, 0, D), (0, 2 * D, D)), proj_weight=(attended, middle_low), proj_bias=row(PROJ_B),
        norm_two_gain=row(G_TWO), norm_two_shift=row(S_TWO), fc_one_weight=(second, inner_low),
        fc_one_bias=Vector(one_sum, (0, 0, MLP)), fc_two_weight=(active, out_low), fc_two_bias=row(TWO_B),
    )


SUMS = 9


def eighths(value):
    found = value[:8]
    for k in range(8, value.shape[0], 8):
        found = found + value[k : k + 8]
    return found


def sigmoid(value):
    return 0.5 + 0.5 * jnp.tanh(0.5 * value)


def silu_and_slope(value):
    s = sigmoid(value)
    silu = value * s
    return silu, s + silu * (1.0 - s)


def turned_matmul(left, right):
    return lax.dot_general(left, right, (((0,), (0,)), ((), ())), preferred_element_type=WIDE)


def head_kernel(
    divisor, arrived, features, levels, noise, final_w, wide_b, ada_b, final_b, ada_src, stack,
    signal, mod_low, modulated, inner_low, active, outer_low, joined_low, cond_low, cond_back, wide_sums, final_grad, input_grad, last,
    cond, joined, hidden, mod, hat, inner, outer, top, total, sums, cond_w, time_w, input_w, ada_w, inner_w, outer_w, weight_sem,
):
    step = pl.program_id(0)
    own = PLACES[-1]
    sources = [placed(stack, place) for place in (own.cond_weight, own.time_weight, own.input_weight)]
    sources += [ada_src, placed(stack, own.inner_weight), placed(stack, own.outer_weight)]
    held = (cond_w, time_w, input_w, ada_w, inner_w, outer_w)
    moves = [pltpu.make_async_copy(s, t, weight_sem.at[i]) for i, (s, t) in enumerate(zip(sources, held))]

    def need(*which):
        @pl.when(step == 0)
        def _():
            for i in which:
                moves[i].wait()

    def bias(k):
        return wide_b[k : k + 1, :]

    def add_sum(k, value):
        sums[k * 8 : (k + 1) * 8, :] = sums[k * 8 : (k + 1) * 8, :] + eighths(value)

    @pl.when(step == 0)
    def _():
        for move in moves:
            move.start()
        for ref in (sums, total, final_grad, input_grad, last):
            ref[...] = jnp.zeros_like(ref)
        for move in moves[:3]:
            move.wait()
        cond[...] = matmul(arrived[:, :D], cond_w[...]) + bias(0)

    clean = arrived[:, D : D + TOK_CH].astype(WIDE)
    marks = arrived[:, D + TOK_CH : D + TOK_CH + 1].astype(WIDE)
    noisy = (levels[:, 0:1] * clean + levels[:, 1:2] * noise[...]).astype(NARROW)
    value, slope = silu_and_slope(matmul(features[...], time_w[...]) + bias(1) + cond[...])
    joined[...] = slope
    signal[...] = value.astype(NARROW)
    h = matmul(noisy, input_w[...]) + bias(2)
    hidden[...] = h
    value, first_r = whiten(h)
    hat[...] = value
    need(3, 4, 5)
    mod[...] = matmul(signal[...], ada_w[...])
    normed = hat[...] * bias(3) + bias(4)
    scale = 1.0 + (mod[:, HW : 2 * HW] + ada_b[0:1, HW : 2 * HW])
    modulated[...] = (normed * scale + (mod[:, :HW] + ada_b[0:1, :HW])).astype(NARROW)
    mod[:, HW : 2 * HW] = scale
    value, slope = silu_and_slope(matmul(modulated[...], inner_w[...]) + bias(5))
    inner[...] = slope
    active[...] = value.astype(NARROW)
    out = matmul(active[...], outer_w[...]) + bias(6)
    outer[...] = out
    gate = mod[:, 2 * HW :] + ada_b[0:1, 2 * HW :]
    mod[:, 2 * HW :] = gate
    value, r = whiten(hidden[...] + gate * out)
    top[...] = value
    final = value.astype(NARROW)
    error = matmul(final, final_w[...]) + final_b[0:1, :] - noise[...]
    pred_grad = 2.0 * error * marks / divisor[0]
    pred_low = pred_grad.astype(NARROW)
    last[0:1, :TOK_CH] = last[0:1, :TOK_CH] + column_sum(pred_grad)
    last[1:2, 0:1] = last[1:2, 0:1] + column_sum(jnp.sum(error * error, -1, keepdims=True) * marks)
    final_grad[...] = final_grad[...] + turned_matmul(final, pred_low)
    g = whiten_back(matmul_turned(pred_low, final_w[...]), top[...], r)
    hidden[...] = g
    gate_grad = g * outer[...]
    mod_low[:, 2 * HW :] = gate_grad.astype(NARROW)
    add_sum(0, gate_grad)
    out_grad = g * mod[:, 2 * HW :]
    outer_low[...] = out_grad.astype(NARROW)
    add_sum(1, out_grad)
    g = matmul_turned(outer_low[...], outer_w[...]) * inner[...]
    inner_low[...] = g.astype(NARROW)
    add_sum(2, g)
    g = matmul_turned(inner_low[...], inner_w[...])
    value = hat[...]
    mod_low[:, :HW] = g.astype(NARROW)
    add_sum(3, g)
    scale_grad = g * (value * bias(3) + bias(4))
    mod_low[:, HW : 2 * HW] = scale_grad.astype(NARROW)
    add_sum(4, scale_grad)
    g = g * mod[:, HW : 2 * HW]
    add_sum(5, g)
    add_sum(6, g * value)
    g = hidden[...] + whiten_back(g * bias(3), value, first_r)
    add_sum(7, g)
    input_grad[...] = input_grad[...] + turned_matmul(noisy, g.astype(NARROW))
    g = matmul_turned(mod_low[...], ada_w[...]) * joined[...]
    joined_low[...] = g.astype(NARROW)
    add_sum(8, g)
    total[...] = total[...] + g

    @pl.when(step == pl.num_programs(0) - 1)
    def _():
        found = total[...].astype(NARROW)
        cond_low[...] = found
        cond_back[...] = matmul_turned(found, cond_w[...]).astype(NARROW)
        for k in range(SUMS):
            wide_sums[k : k + 1, :] = column_sum(sums[k * 8 : (k + 1) * 8, :])


def head_pass(p, stack, arrived, steps, noise, divisor):
    slots = arrived.shape[0]
    times = steps.astype(WIDE)
    features = time_features(times).astype(NARROW).reshape(-1, FREQ)
    level = alpha_level(times).reshape(-1, 1)
    levels = jnp.concatenate([jnp.sqrt(level), jnp.sqrt(1.0 - level)], 1)
    flat_noise = noise.reshape(-1, TOK_CH)
    wide_b = jnp.stack(
        [p.cond_bias, p.time_bias, p.input_bias, p.head_gain, p.head_shift, p.inner_bias, p.outer_bias, p.outer_bias]
    ).astype(WIDE)
    total = COPIES * slots

    def tiled(width):
        return pl.BlockSpec((slots, width), lambda i: (i, 0))

    def whole(x):
        return pl.BlockSpec(x, lambda i: (0, 0), pipeline_mode=pl.Buffered(1))

    heights = (D, FREQ, TOK_CH, None, HW, HW)
    weights = [(h, HW) if h else (HW, 3 * HW) for h in heights]
    small = (p.final_weight, wide_b, p.ada_bias.astype(WIDE)[None], p.final_bias.astype(WIDE)[None])
    kept = [((total, w), NARROW, tiled(w)) for w in (HW, 3 * HW, HW, HW, HW, HW, HW)]
    once = (((slots, HW), NARROW), ((slots, D), NARROW), ((16, HW), WIDE), ((HW, TOK_CH), WIDE), ((TOK_CH, HW), WIDE), ((8, LANES), WIDE))
    kept += [(s, t, whole(s)) for s, t in once]
    flops = 4 * total * (FREQ * HW // 2 + 5 * HW * HW) + 4 * slots * D * HW
    found = pl.pallas_call(
        head_kernel,
        grid=(COPIES,),
        out_shape=[jax.ShapeDtypeStruct(s, t) for s, t, _ in kept],
        in_specs=[pl.BlockSpec(memory_space=pltpu.SMEM), whole(arrived.shape), tiled(FREQ), tiled(2), tiled(TOK_CH)]
        + [whole(x.shape) for x in small] + [HBM] * 2,
        out_specs=[spec for _, _, spec in kept],
        scratch_shapes=[pltpu.VMEM((slots, w), WIDE) for w in (HW, HW, HW, 3 * HW, HW, HW, HW, HW, HW)]
        + [pltpu.VMEM((SUMS * 8, HW), WIDE)] + [pltpu.VMEM(s, NARROW) for s in weights] + [DMA((len(weights),))],
        compiler_params=BIG,
        cost_estimate=pl.CostEstimate(flops=flops, bytes_accessed=26 * total * HW, transcendentals=3 * total * HW),
    )(divisor[None], arrived, features, levels, flat_noise, *small, p.ada_weight, stack)
    signal, mod_low, modulated, inner_low, active, outer_low, joined_low, cond_low, cond_back, sums, final_grad, input_grad, last = found

    def row(k):
        return Vector(sums, (k, 0, HW))

    grads = dict(
        final_weight=final_grad, final_bias=Vector(last, (0, 0, LANES)),
        outer_weight=(active, outer_low), outer_bias=row(1), inner_weight=(modulated, inner_low), inner_bias=row(2),
        head_gain=row(6), head_shift=row(5), ada_weight=(signal, mod_low),
        ada_bias=Vector(sums, (3, 0, HW), (4, 0, HW), (0, 0, HW)), time_weight=(features, joined_low), time_bias=row(8),
        cond_weight=(arrived, cond_low), cond_bias=row(8), input_weight=input_grad, input_bias=row(7),
    )
    return last[1, 0], grads, cond_back


def time_features(times):
    half = FREQ // 2
    freqs = jnp.exp(-math.log(10000.0) * jnp.arange(half, dtype=WIDE) / half)
    angles = times[..., None] * freqs
    return jnp.concatenate([jnp.cos(angles), jnp.sin(angles)], -1)


def alpha_level(times):
    start = math.cos(0.008 / 1.008 * math.pi / 2) ** 2
    return jnp.cos(((times + 1.0) / STEPS_T + 0.008) / 1.008 * math.pi / 2) ** 2 / start


def exchange(payload, parts):
    shape = payload.shape
    moved = lax.all_to_all(payload.reshape(parts, -1, shape[-1]), "dp", split_axis=0, concat_axis=0, tiled=True)
    return moved.reshape(shape)


def body(latents, route, labels, timesteps, noise, image_weight, weights, momentum, average):
    ranks_dp, ranks_rep = lax.axis_size("dp"), lax.axis_size("rep")
    ranks = ranks_dp * ranks_rep
    meshed = (ranks_dp, ranks_rep) == (8, 4)
    rows = route.shape[0]
    images = labels.shape[0]
    assert images == 1 and rows == SEQ
    size = weights.shape[0] // LANES
    padded = -(-(size + 1) // 48) * 48
    masked = route < rows
    flat = weights.reshape(size, LANES)
    if meshed:
        gathered = spread(flat, route, padded)
    else:
        extra = jnp.full((padded - size, LANES), jnp.sum(masked.astype(WIDE)))
        gathered = lax.all_gather(jnp.concatenate([flat, extra], 0).astype(NARROW), BOTH, axis=0)
    base, enc, mid, dec, head = groups = [types.SimpleNamespace() for _ in GROUPS]
    stack, head_stack = unpack(gathered, size, groups)
    count = jnp.sum(gathered[:, size, 0].astype(WIDE))
    keep = jnp.concatenate([jnp.ones((BUF,), WIDE), 1.0 - masked.astype(WIDE)])
    keep_row, keep_column = keep[None], keep[:, None]
    at = next(e.start for e in ENTRIES if e.sparse) + labels[0] * (D // LANES) + jnp.arange(D // LANES, dtype=jnp.int32)
    classes = gathered[at // size, at % size].reshape(D)
    table, attn_b, fc_b = block_vectors(base, enc, mid, dec, head, classes)
    enc_stored, (stream, encoded, leaving, before) = encode(
        latents, keep_row, keep_column, table, attn_b[0], fc_b[0], stack, enc
    )
    token_weight = jnp.broadcast_to(image_weight.astype(NARROW)[:, None], (rows, 1))
    extra = jnp.concatenate([latents, token_weight, jnp.zeros((rows, LANES - TOK_CH - 1), NARROW)], 1)
    dec_stored, flow_out, payload = decode(before, route, extra, table, attn_b[1], fc_b[1], stack, dec)
    arrived = exchange(payload, ranks_dp)
    divisor = TOK_CH * COPIES * count
    loss_part, head_grads, cond_back = head_pass(head, head_stack, arrived, timesteps, noise, divisor)
    returned = exchange(cond_back, ranks_dp)
    height = -(-((ranks - 1) * size + padded) // 8) * 8
    full = fold({(4, name): value for name, value in head_grads.items()}, labels, height)
    dec_found, (token_grad, before_grad, decoded_low, leaving_grad) = decode_back(
        returned, route, flow_out, before, leaving, keep_column, table, dec_stored, stack, dec
    )
    enc_found, (stream_grad, embed_grad) = encode_back(leaving_grad, latents, stream, keep_row, table, enc_stored, stack, enc)

    def row(found, k):
        return Vector(found[4], (MORE + k, 0, D))

    head_grads = dict(diffusion_pos=token_grad, dec_gain=row(dec_found, 0), dec_shift=row(dec_found, 1))
    mid_grads = dict(
        enc_gain=row(dec_found, 4), enc_shift=row(dec_found, 5), dec_weight=(encoded, decoded_low), dec_bias=row(dec_found, 2),
        mask_token=row(dec_found, 3), decoder_pos=before_grad,
    )
    base_grads = dict(encoder_pos=stream_grad, class_table=row(enc_found, 0), embed_weight=embed_grad, embed_bias=row(enc_found, 1))
    grads = {}
    parts = (base_grads, block_grads(enc_stored, enc_found), mid_grads, block_grads(dec_stored, dec_found), head_grads)
    for group, found in enumerate(parts):
        grads.update({(group, name): value for name, value in found.items()})
    full = fold(grads, labels, height, full)
    if meshed:
        lane = lax.broadcasted_iota(jnp.int32, (8, LANES), 1)
        mark = jnp.where(lane == lax.axis_index("dp") * ranks_rep + lax.axis_index("rep"), loss_part, 0.0)
        owned = collect(full, mark, size, padded)
        loss = jnp.sum(owned[padded - 8, :ranks]) / divisor
        owned = owned[:size]
    else:
        loss = lax.psum(loss_part, BOTH) / divisor
        owned = lax.psum_scatter(full[: ranks * size].reshape(ranks, size, LANES), BOTH, scatter_dimension=0, tiled=False)
    owned = owned.reshape(-1)
    rate = 0.05 * math.sqrt(images * ranks * SEQ)
    new_momentum = 0.9 * momentum + owned
    new_weights = weights - rate * (owned + 0.9 * new_momentum)
    new_average = 0.75 * average + 0.25 * new_weights
    return new_weights, new_momentum, new_average, loss


def solution(mesh):
    flat = P(BOTH)
    placed = (P(BOTH, None), flat, flat, P(None, BOTH), P(None, BOTH, None), flat, flat, flat, flat)
    return jax.shard_map(body, mesh=mesh, in_specs=placed, out_specs=(flat, flat, flat, P()), check_vma=False)
```

```python
import functools
import heapq
import math
import types

import jax
import jax.numpy as jnp
from jax import lax
from jax.experimental import pallas as pl
from jax.experimental.pallas import tpu as pltpu
from jax.sharding import PartitionSpec as P

D = 768
HEADS = 12
HEAD_DIM = 64
MLP = 3072
HW = 1024
TOK_CH = 16
FREQ = 256
CLASSES = 1000
BUF = 64
SEQ = 256
COPIES = 4
STEPS_T = 1000
LANES = 128
WIDE = jnp.float32
NARROW = jnp.bfloat16
NORM_EPS = 1e-06
MESH = pl.DeviceIdType.MESH
ANY = pl.BlockSpec(memory_space=pl.ANY)
HBM = pl.BlockSpec(memory_space=pltpu.HBM)
VMEM = pl.BlockSpec(memory_space=pltpu.VMEM)
DMA = pltpu.SemaphoreType.DMA
BOTH = ("dp", "rep")


def block_shapes():
    return dict(
        norm_one_gain=(D,), norm_one_shift=(D,), attn_weight=(D, 3 * D), attn_bias=(2 * D,),
        proj_weight=(D, D), proj_bias=(D,), norm_two_gain=(D,), norm_two_shift=(D,),
        fc_one_weight=(D, MLP), fc_one_bias=(MLP,), fc_two_weight=(MLP, D), fc_two_bias=(D,),
    )


ENC, DEC = 1, 3
GROUPS = (
    dict(embed_weight=(TOK_CH, D), embed_bias=(D,), class_table=(CLASSES, D), encoder_pos=(BUF + SEQ, D)),
    block_shapes(),
    dict(enc_gain=(D,), enc_shift=(D,), dec_weight=(D, D), dec_bias=(D,), mask_token=(D,), decoder_pos=(BUF + SEQ, D)),
    block_shapes(),
    dict(
        dec_gain=(D,), dec_shift=(D,), diffusion_pos=(SEQ, D), input_weight=(TOK_CH, HW), input_bias=(HW,),
        time_weight=(FREQ, HW), time_bias=(HW,), cond_weight=(D, HW), cond_bias=(HW,), head_gain=(HW,),
        head_shift=(HW,), ada_weight=(HW, 3 * HW), ada_bias=(3 * HW,), inner_weight=(HW, HW), inner_bias=(HW,),
        outer_weight=(HW, HW), outer_bias=(HW,), final_weight=(HW, TOK_CH), final_bias=(TOK_CH,),
    ),
)


class Entry:
    def __init__(self, group, name, shape, start):
        self.group, self.name, self.shape, self.start = group, name, shape, start
        self.rows = -(-math.prod(shape) // LANES)
        self.matrix = len(shape) == 2 and shape[1] % LANES == 0
        self.across = shape[1] // LANES if self.matrix else 1
        self.sparse = name == GROUP_SPARSE


GROUP_SPARSE = next(name for name, shape in GROUPS[0].items() if shape[0] == CLASSES)


def entries():
    found, start = [], 0
    for group, shapes in enumerate(GROUPS):
        for name, shape in shapes.items():
            found.append(Entry(group, name, shape, start))
            start += found[-1].rows
    return found


ENTRIES = entries()
USED = ENTRIES[-1].start + ENTRIES[-1].rows


STACKS = ((D, D), (HW, HW))
PLACES = [types.SimpleNamespace() for _ in GROUPS]
STACK_OF = {}
STACK_ROWS = []
for number, (width, tallest) in enumerate(STACKS):
    top = 0
    for e in ENTRIES:
        if e.matrix and not e.sparse and e.shape[1] == width and e.shape[0] <= tallest:
            setattr(PLACES[e.group], e.name, (top, e.shape[0]))
            STACK_OF[e] = number, top
            top += e.shape[0]
    STACK_ROWS.append(top)


def placed(stack, place):
    return stack.at[pl.ds(*place)]


def block_height(entry, limit):
    best = 0
    for height in range(8, entry.shape[0] + 1, 8):
        if entry.shape[0] % height == 0 and height * entry.across <= limit:
            best = height
    return best


class Slots:
    def __init__(self, number):
        self.number, self.base, self.last = number, 0, {}

    def at(self, b):
        return (self.base + b) % self.number

    def claim(self, b, put):
        for k in range(self.number):
            before = self.last.get((self.base + k) % self.number)
            if before is not None:

                @pl.when(b == k)
                def _(before=before):
                    before().wait()

        @pl.when(b >= self.number)
        def _():
            put(b - self.number).wait()

    def close(self, blocks, put):
        base = self.base
        for b in range(max(0, blocks - self.number), blocks):
            self.last[(base + b) % self.number] = functools.partial(put, b)
        self.base = base + blocks

    def drain(self):
        for before in self.last.values():
            before().wait()


SLOTS = 8
OUT = 3


def unfold_kernel(rows, padded, items, g_ref, *refs):
    count = len(items)
    total = len(STACKS) + sum(e not in STACK_OF for e, _ in items)
    stacks, alone = refs[: len(STACKS)], iter(refs[len(STACKS) : total])
    outs = [(stacks[STACK_OF[e][0]], STACK_OF[e][1]) if e in STACK_OF else (next(alone), 0) for e, _ in items]
    first, second, wide, first_sem, second_sem, out_sem = refs[total : total + 6]
    kinds = sorted({(h, e.across) for e, h in items})
    stages = dict(zip(kinds, refs[total + 6 :]))
    turns = {kind: Slots(OUT) for kind in kinds}
    bases = [0]
    for entry, height in items:
        bases.append(bases[-1] + entry.shape[0] // height)

    def spot(t, b):
        entry, height = items[t]
        span = height * entry.across
        start = entry.start + b * span
        dev = start // rows
        row = start - dev * rows
        low = jnp.minimum(row // 8 * 8, padded - span - 8)
        return dev, row, low, row + span > rows

    def copies(t, b):
        entry, height = items[t]
        window = height * entry.across + 8
        dev, row, low, more = spot(t, b)
        slot = (bases[t] + b) % SLOTS
        one = pltpu.make_async_copy(
            g_ref.at[dev, pl.ds(pl.multiple_of(low, 8), window)], first.at[slot, pl.ds(0, window)], first_sem.at[slot]
        )
        two = pltpu.make_async_copy(
            g_ref.at[jnp.minimum(dev + 1, g_ref.shape[0] - 1), pl.ds(0, window)],
            second.at[slot, pl.ds(0, window)], second_sem.at[slot],
        )
        return one, two, more

    def fetch(t, b):
        one, two, more = copies(t, b)
        one.start()

        @pl.when(more)
        def _():
            two.start()

    def fetch_number(g):
        if g < bases[-1]:
            t = next(t for t in range(count) if g < bases[t + 1])
            fetch(t, g - bases[t])

    ahead = SLOTS - 1
    for g in range(ahead):
        fetch_number(g)
    for t, (entry, height) in enumerate(items):
        kind = (height, entry.across)
        stage, turn = stages[kind], turns[kind]
        window = height * entry.across + 8
        blocks = entry.shape[0] // height

        def put(b, t=t, stage=stage, height=height, place=turn.base, kind=kind):
            slot = (place + b) % OUT
            into, top = outs[t]
            return pltpu.make_async_copy(
                stage.at[slot], into.at[pl.ds(pl.multiple_of(top + b * height, 8), height)], out_sem.at[kinds.index(kind), slot]
            )

        def body(b, carry, t=t, entry=entry, height=height, window=window, blocks=blocks, stage=stage, turn=turn, put=put):
            @pl.when(b + ahead < blocks)
            def _():
                fetch(t, b + ahead)

            for k in range(max(0, ahead - blocks), ahead):

                @pl.when(b == blocks - ahead + k)
                def _(k=k):
                    fetch_number(bases[t + 1] + k)

            dev, row, low, _ = spot(t, b)
            slot = (bases[t] + b) % SLOTS
            one, two, more = copies(t, b)
            one.wait()
            wide[pl.ds(0, window), :] = first[slot, pl.ds(0, window), :].astype(WIDE)

            @pl.when(more)
            def _():
                two.wait()
                wide[pl.ds(rows - low, window), :] = second[slot, pl.ds(0, window), :].astype(WIDE)

            turn.claim(b, put)
            off = row - low
            place = turn.at(b)
            for j in range(entry.across):
                stage[place, :, j * LANES : (j + 1) * LANES] = wide[pl.ds(off + j, height, stride=entry.across), :].astype(NARROW)
            put(b).start()
            return carry

        lax.fori_loop(0, blocks, body, 0)
        turn.close(blocks, put)
    for turn in turns.values():
        turn.drain()


def unfold(gathered, rows):
    padded = gathered.shape[1]
    items = [(e, block_height(e, min(2304, rows - 16))) for e in ENTRIES if e.matrix and not e.sparse]
    tall = max(e.across * h for e, h in items) + 8
    kinds = sorted({(h, e.across) for e, h in items})
    total = sum(math.prod(e.shape) for e, _ in items)
    alone = [e for e, _ in items if e not in STACK_OF]
    shapes = [(n, width) for n, (width, _) in zip(STACK_ROWS, STACKS)] + [e.shape for e in alone]
    outs = pl.pallas_call(
        functools.partial(unfold_kernel, rows, padded, items),
        out_shape=[jax.ShapeDtypeStruct(s, NARROW) for s in shapes],
        in_specs=[ANY],
        out_specs=[ANY] * len(shapes),
        scratch_shapes=[
            pltpu.VMEM((SLOTS, tall, LANES), NARROW), pltpu.VMEM((SLOTS, tall, LANES), NARROW),
            pltpu.VMEM((2 * tall, LANES), WIDE), DMA((SLOTS,)), DMA((SLOTS,)), DMA((len(kinds), OUT)),
        ]
        + [pltpu.VMEM((OUT, h, n * LANES), NARROW) for h, n in kinds],
        compiler_params=pltpu.CompilerParams(vmem_limit_bytes=48 * 1000 * 1000),
        cost_estimate=pl.CostEstimate(flops=total, bytes_accessed=4 * total, transcendentals=0),
    )(gathered)
    return outs[: len(STACKS)], {(e.group, e.name): out for e, out in zip(alone, outs[len(STACKS) :])}


def rows_at(gathered, rows, start, number):
    pieces = []
    while number > 0:
        dev, row = divmod(start, rows)
        take = min(number, rows - row)
        pieces.append(gathered[dev, row : row + take])
        start, number = start + take, number - take
    return pieces[0] if len(pieces) == 1 else jnp.concatenate(pieces, 0)


def unpack(gathered, rows, groups):
    stacks, matrices = unfold(gathered, rows)
    for e in ENTRIES:
        if e.sparse or e in STACK_OF:
            continue
        if e.matrix:
            value = matrices[(e.group, e.name)]
        else:
            value = rows_at(gathered, rows, e.start, e.rows).reshape(-1)[: math.prod(e.shape)].reshape(e.shape)
        setattr(groups[e.group], e.name, value)
    return stacks


DEPTH = 3
TALL = 256
CHUNK = 512
NEXT = 3


def product_height(entry):
    return min(TALL, entry.shape[0])


def fold_kernel(products, items, plain, vectors, lone_place, zero, count, going_on, label, *refs):
    refs = list(refs)

    def take(number):
        found, refs[:number] = refs[:number], []
        return found

    small = take(count)
    pairs = take(2 * len(products))
    given = take(len(items))
    rest = take(len(plain))
    take(int(going_on))
    (full,) = take(1)
    pair_sem, given_sem, plain_sem, out_sem, vector_sem = take(5)
    held = take(2 * len(products))
    loads = take(len(items))
    stage, lines = take(2)
    gets = [pltpu.make_async_copy(given[i], loads[i], given_sem.at[i]) for i in range(len(items))]
    fills = []
    for i, entry in enumerate(products):
        for k in (2 * i, 2 * i + 1):
            source = pairs[k]
            if source.shape != held[k].shape:
                source = source.at[:, pl.ds(0, held[k].shape[1])]
            fills.append(pltpu.make_async_copy(source, held[k], pair_sem.at[k]))
    for move in gets + fills[: 2 * NEXT]:
        move.start()
    moves = []
    for i, (start, number) in enumerate(plain):
        move = pltpu.make_async_copy(rest[i].at[pl.ds(0, number)], full.at[pl.ds(start, number)], plain_sem.at[i])
        move.start()
        moves.append(move)
    at = 0
    for i, (entry, which, parts) in enumerate(vectors):
        begin = at
        for k, column, width in parts:
            for j in range(0, width, LANES):
                lines[at : at + 1, :] = small[which][k : k + 1, column + j : column + j + LANES]
                at += 1
        move = pltpu.make_async_copy(lines.at[pl.ds(begin, at - begin)], full.at[pl.ds(entry.start, at - begin)], vector_sem.at[i])
        move.start()
        moves.append(move)
        at = -(-at // 8) * 8
    if zero:
        lines[at : at + zero, :] = jnp.zeros((zero, LANES), WIDE)
        move = pltpu.make_async_copy(lines.at[pl.ds(at, zero)], full.at[pl.ds(USED, zero)], vector_sem.at[len(vectors)])
        move.start()
        moves.append(move)
    turn = Slots(DEPTH)

    def each(entry, height, make):
        span = height * entry.across
        blocks = entry.shape[0] // height

        def put(b, base=turn.base):
            slot = (base + b) % DEPTH
            return pltpu.make_async_copy(
                stage.at[slot, pl.ds(0, span)], full.at[pl.ds(entry.start + b * span, span)], out_sem.at[slot]
            )

        def step(b, carry):
            turn.claim(b, put)
            make(b, turn.at(b))
            put(b).start()
            return carry

        lax.fori_loop(0, blocks, step, 0)
        turn.close(blocks, put)

    if lone_place:
        sparse = next(e for e in ENTRIES if e.sparse)
        height = block_height(sparse, 1200)
        row, row_at = small[lone_place[0]], lone_place[1]

        def lone(b, slot):
            here = lax.broadcasted_iota(jnp.int32, (height, LANES), 0) + b * height == label[0]
            for j in range(sparse.across):
                value = jnp.broadcast_to(row[row_at : row_at + 1, j * LANES : (j + 1) * LANES], (height, LANES))
                stage[slot, pl.ds(j, height, stride=sparse.across), :] = jnp.where(here, value, 0.0)

        each(sparse, height, lone)
    for t, entry in enumerate(items):
        gets[t].wait()

        def make(b, slot, t=t, entry=entry):
            for j in range(entry.across):
                stage[slot, pl.ds(j, entry.shape[0], stride=entry.across), :] = loads[t][:, j * LANES : (j + 1) * LANES]

        each(entry, entry.shape[0], make)
    for t, entry in enumerate(products):
        left, right = held[2 * t], held[2 * t + 1]
        for move in fills[2 * (t + NEXT) : 2 * (t + NEXT) + 2]:
            move.start()
        fills[2 * t].wait()
        fills[2 * t + 1].wait()
        height = product_height(entry)
        chunk = math.gcd(CHUNK, entry.shape[1])

        def make(b, slot, left=left, right=right, entry=entry, height=height, chunk=chunk):
            turned = left[:, pl.ds(pl.multiple_of(b * height, LANES), height)].T
            for k in range(entry.shape[1] // chunk):
                found = jnp.dot(turned, right[:, k * chunk : (k + 1) * chunk], preferred_element_type=WIDE)
                for j in range(chunk // LANES):
                    at = pl.ds(k * (chunk // LANES) + j, height, stride=entry.across)
                    stage[slot, at, :] = found[:, j * LANES : (j + 1) * LANES]

        each(entry, height, make)
    turn.drain()
    for move in moves:
        move.wait()


def fold(grads, label, height_total, full=None):
    wanted = [e for e in ENTRIES if (e.group, e.name) in grads]
    found = {e: grads[(e.group, e.name)] for e in wanted}
    products = [e for e in wanted if isinstance(found[e], tuple)]
    items = [e for e in wanted if e.matrix and not isinstance(found[e], (tuple, Vector))]
    small, vectors, plain, values, lone_place = [], [], [], [], None
    for e in wanted:
        if isinstance(found[e], Vector):
            place = next((i for i, x in enumerate(small) if x is found[e].array), len(small))
            small[place : place + 1] = [found[e].array]
            if e.sparse:
                lone_place = (place, found[e].parts[0][0])
            else:
                vectors.append((e, place, found[e].parts))
        elif not e.matrix and e not in products:
            plain.append((e.start, e.rows))
            values.append(found[e].reshape(e.rows, LANES))
    zero = height_total - USED if full is None else 0
    before = [] if full is None else [full]
    lines = sum(-(-e.rows // 8) * 8 for e, _, _ in vectors) + -(-zero // 8) * 8
    operands = [x for e in products for x in found[e]]
    holds = [(x.shape[0], n) for e in products for x, n in zip(found[e], e.shape)]
    tall = max([e.rows for e in items] + [e.across * product_height(e) for e in products])
    total = sum(e.rows for e in wanted) * LANES
    taken = 1 + len(small) + len(operands) + len(items) + len(plain)
    flops = sum(2 * math.prod(e.shape) * operands[2 * i].shape[0] for i, e in enumerate(products))
    return pl.pallas_call(
        functools.partial(fold_kernel, products, items, plain, vectors, lone_place, zero, len(small), bool(before)),
        out_shape=jax.ShapeDtypeStruct((height_total, LANES), WIDE),
        in_specs=[pl.BlockSpec(memory_space=pltpu.SMEM)] + [VMEM] * len(small) + [ANY] * (len(operands) + len(items) + len(plain) + len(before)),
        out_specs=ANY,
        input_output_aliases={taken: 0} if before else {},
        scratch_shapes=[DMA((len(operands),)), DMA((len(items),)), DMA((max(len(plain), 1),)), DMA((DEPTH,)), DMA((len(vectors) + 1,))]
        + [pltpu.VMEM(s, NARROW) for s in holds]
        + [pltpu.VMEM(e.shape, WIDE) for e in items]
        + [pltpu.VMEM((DEPTH, tall, LANES), WIDE), pltpu.VMEM((lines, LANES), WIDE)],
        compiler_params=pltpu.CompilerParams(vmem_limit_bytes=62 * 1000 * 1000),
        cost_estimate=pl.CostEstimate(flops=flops, bytes_accessed=4 * total, transcendentals=0),
    )(label, *small, *operands, *[found[e] for e in items], *values, *before)


X, Y, Z = 0, 1, 2
TREES = ((Z, X, Y), (Z, Y, X), (X, Z, Y), (X, Z, Y), (Y, Z, X), (Y, Z, X))
SHARES = len(TREES)
FAR = 3


def onward(order, arrived, way, p):
    z, x, y = p
    found = []
    if arrived >= 0 and order[arrived] == Z and 0 <= z + way <= FAR:
        found.append(((z + way, x, y), arrived, way))
    for j in range(arrived + 1, 3):
        if order[j] == X:
            found.append(((z, 1 - x, y), j, 0))
        elif order[j] == Y:
            found.append(((z, x, 1 - y), j, 0))
        else:
            found += [((z + s, x, y), j, s) for s in (1, -1) if 0 <= z + s <= FAR]
    return found


@functools.cache
def flow(lag=0.4):
    chips = [(z, x, y) for z in range(FAR + 1) for x in range(2) for y in range(2)]
    events, queues, busy, come, sent = [], {}, set(), {}, []
    number = iter(range(10**9))
    for u in range(SHARES):
        for p in chips:
            heapq.heappush(events, (0.0, next(number), 0, (p, p, u, -1, 0)))

    def pump(link, t):
        if link in busy or not queues.get(link):
            return
        what = heapq.heappop(queues[link])[2]
        busy.add(link)
        sent.append((t, link, what[1], what[2]))
        heapq.heappush(events, (t + 1.0, next(number), 1, (link, what)))

    while events:
        t, _, kind, what = heapq.heappop(events)
        if kind == 1:
            link, piece = what
            busy.discard(link)
            heapq.heappush(events, (t + lag, next(number), 0, piece))
            pump(link, t)
            continue
        p, q, u, k, way = what
        come[(u, p, q)] = t
        for to, k2, way2 in onward(TREES[u], k, way, p):
            left = len(onward(TREES[u], k2, way2, to))
            heapq.heappush(queues.setdefault((p, to), []), ((-left, t), next(number), (to, q, u, k2, way2)))
            pump((p, to), t)
    return come, sent


def spread_order():
    keyed = {}
    for (u, p, q), t in flow()[0].items():
        keyed.setdefault((u, q[0] - p[0], (q[1] - p[1]) % 2, (q[2] - p[2]) % 2), []).append(t)
    return sorted(keyed, key=lambda k: (sum(keyed[k]) / len(keyed[k]), k))


def last_hop(u, dz, dx, dy):
    apart = [k for k in range(3) if (dx, dy, dz)[TREES[u][k]] != 0]
    return apart[-1] if apart else -1


def hops(u, dz, dx, dy):
    order, arrived = TREES[u], last_hop(u, dz, dx, dy)
    found = []
    if arrived >= 0 and order[arrived] == Z:
        found.append((1, 0, 0) if dz < 0 else (-1, 0, 0))
    for k in range(arrived + 1, 3):
        found += [[(0, 1, 0)], [(0, 0, 1)], [(1, 0, 0), (-1, 0, 0)]][order[k]]
    return found


def only(condition, action):
    if condition is None:
        action()
    else:
        pl.when(condition)(action)


def spread_kernel(flat, route, out, wide, own, load_sem, keep_sem, send_sem, link_sem, core_send, core_sem):
    dp, rep = lax.axis_index("dp"), lax.axis_index("rep")
    z, x, y, c = dp // 2, dp % 2, rep // 2, rep % 2
    size, padded = flat.shape[0], own.shape[0]
    unit = padded // SHARES
    sibling = (dp, y * 2 + 1 - c)
    loads = []
    for u in range(SHARES):
        part = pl.ds(u * unit, min(unit, size - u * unit))
        loads.append(pltpu.make_async_copy(flat.at[part], wide.at[part], load_sem.at[u]))
        loads[u].start()

    def device(dz, dx, dy):
        return ((z + dz) * 2 + (x + dx) % 2, (y + dy) % 2 * 2 + c)

    def exists(dz):
        return None if dz == 0 else (z + dz >= 0 if dz < 0 else z + dz <= FAR)

    barrier = pltpu.get_barrier_semaphore()
    near = ((0, 1, 0), (0, 0, 1), (1, 0, 0), (-1, 0, 0))
    for hop in near:
        only(exists(hop[0]), lambda: pl.semaphore_signal(barrier, inc=1, device_id=device(*hop), device_id_type=MESH))
    pl.semaphore_signal(barrier, inc=1, device_id=sibling, device_id_type=MESH)
    inner = z * (FAR - z)
    only(inner == 0, lambda: pl.semaphore_wait(barrier, len(near)))
    only(inner > 0, lambda: pl.semaphore_wait(barrier, len(near) + 1))
    masked = jnp.sum(jnp.where(route[...] < SEQ, 1.0, 0.0))
    keeps, ends, number = [], [], 0
    for u, dz, dx, dy in spread_order():
        part = pl.ds(u * unit, unit)
        q = ((z + dz) * 2 + (x + dx) % 2) * 2 + (y + dy) % 2
        mine = dz == 0 and dx == 0 and dy == 0
        i = u * 16 + q

        def copy(to, send, come, part=part, q=q, mine=mine):
            here = out.at[q * 2 + c, part]
            return pltpu.make_async_remote_copy(
                own.at[part] if mine else here, here, send, come, device_id=to, device_id_type=MESH
            )

        goes = [(hop, number + k) for k, hop in enumerate(hops(u, dz, dx, dy))]
        number += len(goes)

        def run(i=i, copy=copy, goes=goes, mine=mine):
            if not mine:
                copy(sibling, send_sem.at[0], link_sem.at[i]).wait_recv()
            for hop, n in goes:
                only(exists(hop[0]), lambda: copy(device(*hop), send_sem.at[n], link_sem.at[i]).start())
            copy(sibling, core_send.at[i], core_sem.at[i]).start()

        def finish(i=i, copy=copy, goes=goes):
            for hop, n in goes:
                only(exists(hop[0]), lambda: copy(device(*hop), send_sem.at[n], link_sem.at[i]).wait_send())
            copy(sibling, core_send.at[i], core_sem.at[i]).wait()

        if mine:
            loads[u].wait()
            if u == SHARES - 1:
                wide[size:padded, :] = jnp.broadcast_to(masked, (padded - size, LANES))
            own[part, :] = wide[part, :].astype(NARROW)
            keeps.append(pltpu.make_async_copy(own.at[part], out.at[dp * 4 + rep, part], keep_sem.at[u]))
            keeps[-1].start()
        there = None if dz == 0 else jnp.logical_and(z + dz >= 0, z + dz <= FAR)
        only(there, run)
        ends.append((there, finish))
    for there, finish in ends:
        only(there, finish)
    for keep in keeps:
        keep.wait()


def spread(flat, route, padded):
    pieces = SHARES * 16
    sends = sum(len(hops(*key)) for key in spread_order())
    return pl.pallas_call(
        spread_kernel,
        out_shape=jax.ShapeDtypeStruct((32, padded, LANES), NARROW),
        in_specs=[ANY, VMEM],
        out_specs=ANY,
        scratch_shapes=[
            pltpu.VMEM((padded, LANES), WIDE), pltpu.VMEM((padded, LANES), NARROW), DMA((SHARES,)), DMA((SHARES,)),
            DMA((sends,)), DMA((pieces,)), DMA((pieces,)), DMA((pieces,)),
        ],
        compiler_params=pltpu.CompilerParams(collective_id=0, has_side_effects=True),
    )(flat, route.reshape(-1, LANES))


class Chip:
    def __init__(self, low):
        dp, rep = lax.axis_index("dp"), lax.axis_index("rep")
        self.low = low
        self.z, self.x, self.y, self.c = dp // 2, dp % 2, rep // 2, rep % 2
        self.way = 1 - 2 * (self.z // 2)

    def device(self, q, other=0):
        z = self.z + self.way * (q[0] - self.low)
        return z * 2 + (self.x + q[1]) % 2, (self.y + q[2]) % 2 * 2 + (self.c + other) % 2

    def block(self, q, other=0):
        dp, rep = self.device(q, other)
        return dp * 4 + rep

    def greet(self):
        low = self.low
        near = [(low, 1, 0), (low, 0, 1), (low + 1, 0, 0)] + ([(low - 1, 0, 0)] if low else [])
        barrier = pltpu.get_barrier_semaphore()
        for q in near:
            pl.semaphore_signal(barrier, inc=1, device_id=self.device(q), device_id_type=MESH)
        pl.semaphore_signal(barrier, inc=1, device_id=self.device((low, 0, 0), 1), device_id_type=MESH)
        pl.semaphore_wait(barrier, len(near) + 1)


def seen_from(p, r):
    low, way = min(p[0], FAR - p[0]), 1 if p[0] < 2 else -1
    return low + way * (r[0] - p[0]), (r[1] - p[1]) % 2, (r[2] - p[2]) % 2


@functools.cache
def sum_programs():
    come, sent = flow()
    last = max(come.values())
    found = []
    for z in (0, 1):
        p = (z, 0, 0)
        kids, parent, when = {}, {}, {}
        for t, link, q, u in sent:
            if link[0] == p:
                kids.setdefault((u, q), []).append(link[1])
                if q == p:
                    when[(u, p)] = max(when.get((u, p), 0.0), last - t)
            if link[1] == p:
                parent[(u, q)] = link[0]
                when[(u, q)] = last - t - 1.0
        tasks = sorted(when, key=lambda k: (when[k], k))
        found.append([(u, q, sorted(kids.get((u, q), [])), parent.get((u, q))) for u, q in tasks])
    return found


@functools.cache
def landing():
    return [{key: i for i, key in enumerate((u, q, k) for u, q, kids, _ in tasks for k in kids)} for tasks in sum_programs()]


RING = 12
SIDE = 4
EARLY = 12
STEP = 40


def add_rows(into, terms):
    def body(i, carry):
        at = pl.ds(pl.multiple_of(i * STEP, 8), STEP)
        total = into[at, :]
        for term in terms:
            total = total + term[at, :]
        into[at, :] = total
        return carry

    lax.fori_loop(0, into.shape[0] // STEP, body, 0)


def collect_at(low, size, full, mark, out, aside, store, ring, side, ring_sem, side_sem, send_sem, link_sem, core_send, core_sem, out_sem, marks, mark_sem):
    chip = Chip(low)
    me = (low, 0, 0)
    tasks, spots = sum_programs()[low], landing()
    count, unit = len(tasks), ring.shape[1]
    chip.greet()

    def part(i, other=0):
        return full.at[pl.ds(chip.block(tasks[i][1], other) * size + tasks[i][0] * unit, unit)]

    def across(i):
        return pltpu.make_async_remote_copy(
            part(i, 1), aside.at[i], core_send.at[i], core_sem.at[i], device_id=chip.device(me, 1), device_id_type=MESH
        )

    def ours(i):
        return pltpu.make_async_copy(part(i), ring.at[i % RING], ring_sem.at[i % RING])

    def theirs(i):
        return pltpu.make_async_copy(aside.at[i], side.at[i % SIDE], side_sem.at[i % SIDE])

    def along(i, spot, to):
        return pltpu.make_async_remote_copy(
            ring.at[i % RING], store.at[spot], send_sem.at[i], link_sem.at[spot], device_id=chip.device(to), device_id_type=MESH
        )

    tail = pl.ds(unit - 8, 8)
    ours_too = pltpu.make_async_copy(mark, marks.at[0], mark_sem.at[0])
    theirs_too = pltpu.make_async_remote_copy(
        mark, marks.at[1], mark_sem.at[1], mark_sem.at[2], device_id=chip.device(me, 1), device_id_type=MESH
    )
    ours_too.start()
    theirs_too.start()
    leaving = {}

    def fetch(i):
        if i - RING in leaving:
            leaving.pop(i - RING)()
        ours(i).start()
        across(i).wait_recv()
        theirs(i).start()

    for i in range(EARLY):
        across(i).start()
    for i in range(SIDE - 1):
        fetch(i)
    ours_too.wait()
    theirs_too.wait()
    for i, (u, q, kids, to) in enumerate(tasks):
        if i + EARLY < count:
            across(i + EARLY).start()
        if i + SIDE - 1 < count:
            fetch(i + SIDE - 1)
        ours(i).wait()
        theirs(i).wait()
        if u == SHARES - 1:
            ring[i % RING, tail, :] = marks[0] + marks[1]
            side[i % SIDE, tail, :] = jnp.zeros((8, LANES), WIDE)
        terms = [side.at[i % SIDE]]
        for kid in kids:
            spot = spots[low][(u, q, kid)]
            along(i, spot, kid).wait_recv()
            terms.append(store.at[spot])
        add_rows(ring.at[i % RING], terms)
        if to is None:
            move = pltpu.make_async_copy(ring.at[i % RING], out.at[pl.ds(u * unit, unit)], out_sem.at[u])
            move.start()
            leaving[i] = move.wait
        else:
            move = along(i, spots[min(to[0], FAR - to[0])][(u, seen_from(to, q), seen_from(to, me))], to)
            move.start()
            leaving[i] = move.wait_send
    for i in list(leaving):
        leaving.pop(i)()
    for i in range(count):
        across(i).wait_send()


def collect_kernel(size, *refs):
    z = lax.axis_index("dp") // 2
    inner = z * (FAR - z)

    @pl.when(inner == 0)
    def _():
        collect_at(0, size, *refs)

    @pl.when(inner > 0)
    def _():
        collect_at(1, size, *refs)


def collect(full, mark, size, rows):
    slots = max(len(spots) for spots in landing())
    count, unit = len(sum_programs()[0]), rows // SHARES
    return pl.pallas_call(
        functools.partial(collect_kernel, size),
        out_shape=(jax.ShapeDtypeStruct((rows, LANES), WIDE), jax.ShapeDtypeStruct((count, unit, LANES), WIDE)),
        in_specs=[ANY, ANY],
        out_specs=(ANY, ANY),
        scratch_shapes=[
            pltpu.VMEM((slots, unit, LANES), WIDE), pltpu.VMEM((RING, unit, LANES), WIDE), pltpu.VMEM((SIDE, unit, LANES), WIDE),
            DMA((RING,)), DMA((SIDE,)), DMA((count,)), DMA((slots,)), DMA((count,)), DMA((count,)), DMA((SHARES,)),
            pltpu.VMEM((2, 8, LANES), WIDE), DMA((3,)),
        ],
        compiler_params=pltpu.CompilerParams(collective_id=1, has_side_effects=True, vmem_limit_bytes=62 * 1000 * 1000),
    )(full, mark)[0]


HALF_ROOT = math.sqrt(0.5)
PDF = 1.0 / math.sqrt(2.0 * math.pi)
SCALE = HEAD_DIM ** (-0.5)
PART = 512
BIG = pltpu.CompilerParams(vmem_limit_bytes=66 * 1000 * 1000)
BLOCK_WEIGHTS = ((D, 3 * D), (D, D), (D, MLP), (MLP, D))
EMBED_B, ENC_G, ENC_S, DEC_B, MASK_T, DEC_G, DEC_S, CLASS, ENC_ROWS, DEC_ROWS, ALL_ROWS = 0, 1, 2, 3, 4, 5, 6, 7, 8, 14, 24


def matmul(left, right):
    return jnp.dot(left, right, preferred_element_type=WIDE)


def matmul_turned(left, right):
    return lax.dot_general(left, right, (((1,), (1,)), ((), ())), preferred_element_type=WIDE)


def column_sum(value):
    return jnp.sum(value, 0, keepdims=True)


def whiten(value):
    centered = value - jnp.mean(value, -1, keepdims=True)
    r = lax.rsqrt(jnp.mean(centered * centered, -1, keepdims=True) + NORM_EPS)
    return centered * r, r


def whiten_back(grad, hat, r):
    return r * (grad - jnp.mean(grad, -1, keepdims=True) - hat * jnp.mean(grad * hat, -1, keepdims=True))


def side_masks(length):
    lane = lax.broadcasted_iota(jnp.int32, (length, LANES), 1)
    return lane < HEAD_DIM, lane >= HEAD_DIM


def one_side(value, side):
    return jnp.where(side, value, jnp.zeros_like(value))


def start_all(sources, targets, sem):
    moves = [pltpu.make_async_copy(s, t, sem.at[i]) for i, (s, t) in enumerate(zip(sources, targets))]
    for move in moves:
        move.start()
    return moves


def block_vectors(base, enc, mid, dec, head, classes):
    rows = [base.embed_bias, mid.enc_gain, mid.enc_shift, mid.dec_bias, mid.mask_token, head.dec_gain, head.dec_shift, classes]
    for p in (enc, dec):
        rows += [p.norm_one_gain, p.norm_one_shift, p.norm_two_gain, p.norm_two_shift, p.proj_bias, p.fc_two_bias]
    rows += rows[: ALL_ROWS - len(rows)]
    gap = jnp.zeros((D,), NARROW)
    attn_b = [jnp.concatenate([p.attn_bias[:D], gap, p.attn_bias[D:]]).astype(WIDE)[None] for p in (enc, dec)]
    return jnp.stack(rows).astype(WIDE), attn_b, [p.fc_one_bias.astype(WIDE)[None] for p in (enc, dec)]


class Here:
    def wait(self):
        pass


def forward_block(value, first, keep, table, attn_b, fc_b, outs, weights, moves):
    normed, mixed, totals, attended, middle, second, slope, active = outs
    attn_w, proj_w, one_w, two_w = weights
    hat, _ = whiten(value)
    normed[...] = (hat * table[first : first + 1, :] + table[first + 1 : first + 2, :]).astype(NARROW)
    moves[0].wait()
    for k in range(3):
        at = slice(k * D, (k + 1) * D)
        mixed[:, at] = (matmul(normed[...], attn_w[:, at]) + attn_b[0:1, at]).astype(NARROW)
    sides = side_masks(value.shape[0])
    for pair in range(HEADS // 2):
        q, k, v = (mixed[:, part * D + pair * LANES : part * D + (pair + 1) * LANES] for part in range(3))
        found = None
        for i, side in enumerate(sides):
            scores = matmul_turned(one_side(q, side), k) * SCALE
            if keep is not None:
                scores = jnp.where(keep[0:1, :] > 0.0, scores, -1e30)
            top = jnp.max(scores, -1, keepdims=True)
            powers = jnp.exp(scores - top)
            total = jnp.sum(powers, -1, keepdims=True)
            totals[:, 2 * pair + i : 2 * pair + i + 1] = top + jnp.log(total)
            probs = (powers * (1.0 / total)).astype(NARROW)
            part = matmul(probs, one_side(v, side))
            found = part if found is None else found + part
        attended[:, pair * LANES : (pair + 1) * LANES] = found.astype(NARROW)
    moves[1].wait()
    value = value + matmul(attended[...], proj_w[...]) + table[first + 4 : first + 5, :]
    middle[...] = value
    hat, _ = whiten(value)
    second[...] = (hat * table[first + 2 : first + 3, :] + table[first + 3 : first + 4, :]).astype(NARROW)
    moves[2].wait()
    for k in range(MLP // PART):
        at = slice(k * PART, (k + 1) * PART)
        value = matmul(second[...], one_w[:, at]) + fc_b[0:1, at]
        share = 0.5 + 0.5 * lax.erf(value * HALF_ROOT)
        active[:, at] = (value * share).astype(NARROW)
        slope[:, at] = share + value * (PDF * jnp.exp(-0.5 * value * value))
    moves[3].wait()
    return middle[...] + matmul(active[...], two_w[...]) + table[first + 5 : first + 6, :]


def forward_shapes(length):
    widths = [(D, NARROW), (3 * D, NARROW), (LANES, WIDE), (D, NARROW), (D, WIDE), (D, NARROW), (MLP, WIDE), (MLP, NARROW)]
    return [jax.ShapeDtypeStruct((length, w), t) for w, t in widths]


def encode_kernel(latents, keep_row, keep_column, table, attn_b, fc_b, stack, *refs):
    (attn_src, one_src, two_src), outs, (stream, encoded, leaving, before) = refs[:3], refs[3:11], refs[11:15]
    attn_w, one_w, two_w, sem = refs[15:]
    base, enc, mid = PLACES[:3]
    embed_w, enc_pos, dec_pos = (placed(stack, place) for place in (base.embed_weight, base.encoder_pos, mid.decoder_pos))
    held = attn_w, placed(stack, enc.proj_weight), one_w, two_w, placed(stack, mid.dec_weight)
    moves = start_all((attn_src, one_src, two_src), (attn_w, one_w, two_w), sem)
    moves.insert(1, Here())
    pos = enc_pos[...].astype(WIDE)
    stream[:BUF, :] = table[CLASS : CLASS + 1, :] + pos[:BUF]
    stream[BUF:, :] = matmul(latents[...], embed_w[...]) + table[EMBED_B : EMBED_B + 1, :] + pos[BUF:]
    value = forward_block(stream[...], ENC_ROWS, keep_row, table, attn_b, fc_b, outs, held[:4], moves)
    leaving[...] = value
    hat, _ = whiten(value)
    encoded[...] = (hat * table[ENC_G : ENC_G + 1, :] + table[ENC_S : ENC_S + 1, :]).astype(NARROW)
    value = matmul(encoded[...], held[4][...]) + table[DEC_B : DEC_B + 1, :]
    value = jnp.where(keep_column[...] > 0.0, value, table[MASK_T : MASK_T + 1, :])
    before[...] = value + dec_pos[...].astype(WIDE)


def block_cost(length, weights):
    work = sum(math.prod(s) for s in weights)
    return pl.CostEstimate(flops=2 * length * work, bytes_accessed=2 * work + 36 * length * D, transcendentals=4 * length * MLP)


def encode(latents, keep_row, keep_column, table, attn_b, fc_b, stack, enc):
    length = BUF + SEQ
    weights = BLOCK_WEIGHTS + ((D, D),)
    found = pl.pallas_call(
        encode_kernel,
        out_shape=forward_shapes(length)
        + [jax.ShapeDtypeStruct((length, D), t) for t in (WIDE, NARROW, WIDE, WIDE)],
        in_specs=[VMEM] * 7 + [HBM] * 3,
        out_specs=[VMEM] * 12,
        scratch_shapes=[pltpu.VMEM(s, NARROW) for s in BLOCK_WEIGHTS if s != (D, D)] + [DMA((3,))],
        compiler_params=BIG,
        cost_estimate=block_cost(length, weights),
    )(
        latents, keep_row, keep_column, table, attn_b, fc_b, stack, enc.attn_weight, enc.fc_one_weight, enc.fc_two_weight,
    )
    return found[:8], found[8:]


def decode_kernel(before, route, extra, table, attn_b, fc_b, stack, *refs):
    (attn_src, one_src, two_src), outs, (flow_out, payload) = refs[:3], refs[3:11], refs[11:13]
    attn_w, one_w, two_w, sem = refs[13:]
    held = attn_w, placed(stack, PLACES[DEC].proj_weight), one_w, two_w
    diff_pos = placed(stack, PLACES[-1].diffusion_pos)
    moves = start_all((attn_src, one_src, two_src), (attn_w, one_w, two_w), sem)
    moves.insert(1, Here())
    value = forward_block(before[...], DEC_ROWS, None, table, attn_b, fc_b, outs, held, moves)
    flow_out[...] = value
    hat, _ = whiten(flow_out[BUF:, :])
    value = hat * table[DEC_G : DEC_G + 1, :] + table[DEC_S : DEC_S + 1, :]
    conditions = (value + diff_pos[...].astype(WIDE)).astype(NARROW)
    slots = payload.shape[0]
    picks = lax.broadcasted_iota(jnp.int32, (slots, slots), 0) == route[...]
    picks = jnp.where(picks, 1.0, 0.0).astype(NARROW)
    payload[:, :D] = matmul(picks, conditions).astype(NARROW)
    payload[:, D:] = matmul(picks, extra[...]).astype(NARROW)


def decode(before, route, extra, table, attn_b, fc_b, stack, dec):
    length = BUF + SEQ
    found = pl.pallas_call(
        decode_kernel,
        out_shape=forward_shapes(length)
        + [jax.ShapeDtypeStruct((length, D), WIDE), jax.ShapeDtypeStruct((SEQ, D + LANES), NARROW)],
        in_specs=[VMEM] * 7 + [HBM] * 3,
        out_specs=[VMEM] * 10,
        scratch_shapes=[pltpu.VMEM(s, NARROW) for s in BLOCK_WEIGHTS if s != (D, D)] + [DMA((3,))],
        compiler_params=BIG,
        cost_estimate=block_cost(length, BLOCK_WEIGHTS),
    )(
        before, route[None], extra, table, attn_b, fc_b, stack, dec.attn_weight, dec.fc_one_weight, dec.fc_two_weight,
    )
    return found[:8], found[8], found[9]


TWO_B, G_TWO, S_TWO, PROJ_B, G_ONE, S_ONE = 0, 1, 2, 3, 4, 5


def backward_block(value, first, stream, keep, table, mixed, totals, middle, outs, weights, slope, attended_grad, moves):
    out_low, inner_low, middle_low, mixed_low, sums, one_sum, mixed_sum = outs
    attn_w, proj_w, one_w, two_w = weights
    low = value.astype(NARROW)
    out_low[...] = low
    sums[TWO_B : TWO_B + 1, :] = column_sum(value)
    moves[0].wait()
    moves[1].wait()
    for k in range(MLP // PART):
        at = slice(k * PART, (k + 1) * PART)
        part = matmul_turned(low, two_w[at, :]) * slope[:, at]
        inner_low[:, at] = part.astype(NARROW)
        one_sum[0:1, at] = column_sum(part)
    moves[2].wait()
    part = matmul_turned(inner_low[...], one_w[...])
    hat, r = whiten(middle[...])
    sums[G_TWO : G_TWO + 1, :] = column_sum(part * hat)
    sums[S_TWO : S_TWO + 1, :] = column_sum(part)
    value = value + whiten_back(part * table[first + 2 : first + 3, :], hat, r)
    sums[PROJ_B : PROJ_B + 1, :] = column_sum(value)
    middle_low[...] = value.astype(NARROW)
    moves[3].wait()
    attended_grad[...] = matmul_turned(middle_low[...], proj_w[...]).astype(NARROW)
    sides = side_masks(value.shape[0])
    for pair in range(HEADS // 2):
        here = [slice(part * D + pair * LANES, part * D + (pair + 1) * LANES) for part in range(3)]
        q, k, v = (mixed[:, at] for at in here)
        g = attended_grad[:, here[0]]
        grads = [None, None, None]
        for i, side in enumerate(sides):
            q_side, k_side, g_side = one_side(q, side), one_side(k, side), one_side(g, side)
            scores = matmul_turned(q_side, k) * SCALE
            if keep is not None:
                scores = jnp.where(keep[0:1, :] > 0.0, scores, -1e30)
            probs = jnp.exp(scores - totals[:, 2 * pair + i : 2 * pair + i + 1])
            prob_grad = matmul_turned(g_side, v)
            score_grad = (probs * (prob_grad - jnp.sum(probs * prob_grad, -1, keepdims=True))).astype(NARROW)
            parts = (
                matmul(score_grad, k_side) * SCALE, matmul(score_grad.T, q_side) * SCALE, matmul(probs.astype(NARROW).T, g_side)
            )
            grads = [part if old is None else old + part for old, part in zip(grads, parts)]
        for at, part in zip(here, grads):
            mixed_low[:, at] = part.astype(NARROW)
            mixed_sum[0:1, at] = column_sum(part)
    moves[4].wait()
    part = matmul_turned(mixed_low[...], attn_w[...])
    hat, r = whiten(stream[...])
    sums[G_ONE : G_ONE + 1, :] = column_sum(part * hat)
    sums[S_ONE : S_ONE + 1, :] = column_sum(part)
    return value + whiten_back(part * table[first : first + 1, :], hat, r)


def backward_shapes(length, rows):
    shapes = [((length, D), NARROW), ((length, MLP), NARROW), ((length, D), NARROW), ((length, 3 * D), NARROW)]
    shapes += [((rows, D), WIDE), ((1, MLP), WIDE), ((1, 3 * D), WIDE)]
    return [jax.ShapeDtypeStruct(s, t) for s, t in shapes]


def backward_scratch(length, weights):
    return [pltpu.VMEM(s, NARROW) for s in weights] + [
        pltpu.VMEM((length, MLP), WIDE), pltpu.VMEM((length, D), NARROW), DMA((len(weights) + 1,))
    ]


MORE = 6


def decode_back_kernel(returned, route, flow_out, before, leaving, keep_column, table, mixed, totals, middle, *refs):
    slope_src, attn_src, one_src, two_src, stack = refs[:5]
    proj_src, dec_src = placed(stack, PLACES[DEC].proj_weight), placed(stack, PLACES[2].dec_weight)
    outs, (token_grad, before_grad, decoded_low, leaving_grad) = refs[5:12], refs[12:16]
    attn_w, proj_w, one_w, two_w, dec_w, slope, attended_grad, sem = refs[16:]
    moves = start_all(
        (two_src, slope_src, one_src, proj_src, attn_src, dec_src), (two_w, slope, one_w, proj_w, attn_w, dec_w), sem
    )
    slots = returned.shape[0]
    picks = lax.broadcasted_iota(jnp.int32, (slots, slots), 1) == route[...]
    picks = jnp.where(picks, 1.0, 0.0).astype(NARROW)
    grad = matmul(picks, returned[...])
    token_grad[...] = grad
    sums = outs[4]
    hat, r = whiten(flow_out[BUF:, :])
    sums[MORE : MORE + 1, :] = column_sum(grad * hat)
    sums[MORE + 1 : MORE + 2, :] = column_sum(grad)
    before_grad[:BUF, :] = jnp.zeros((BUF, D), WIDE)
    before_grad[BUF:, :] = whiten_back(grad * table[DEC_G : DEC_G + 1, :], hat, r)
    value = backward_block(
        before_grad[...], DEC_ROWS, before, None, table, mixed, totals, middle, outs,
        (attn_w, proj_w, one_w, two_w), slope, attended_grad, moves,
    )
    before_grad[...] = value
    kept = jnp.where(keep_column[...] > 0.0, value, 0.0)
    sums[MORE + 2 : MORE + 3, :] = column_sum(kept)
    sums[MORE + 3 : MORE + 4, :] = column_sum(value - kept)
    decoded_low[...] = kept.astype(NARROW)
    moves[5].wait()
    part = matmul_turned(decoded_low[...], dec_w[...])
    hat, r = whiten(leaving[...])
    sums[MORE + 4 : MORE + 5, :] = column_sum(part * hat)
    sums[MORE + 5 : MORE + 6, :] = column_sum(part)
    leaving_grad[...] = whiten_back(part * table[ENC_G : ENC_G + 1, :], hat, r)


def decode_back(returned, route, flow_out, before, leaving, keep_column, table, stored, stack, dec):
    length = BUF + SEQ
    weights = BLOCK_WEIGHTS + ((D, D),)
    normed, mixed, totals, attended, middle, second, slope, active = stored
    found = pl.pallas_call(
        decode_back_kernel,
        out_shape=backward_shapes(length, 16)
        + [jax.ShapeDtypeStruct((n, D), t) for n, t in ((SEQ, WIDE), (length, WIDE), (length, NARROW), (length, WIDE))],
        in_specs=[VMEM] * 10 + [HBM] * 5,
        out_specs=[VMEM] * 11,
        scratch_shapes=backward_scratch(length, weights),
        compiler_params=BIG,
        cost_estimate=block_cost(length, weights),
    )(
        returned, route[:, None], flow_out, before, leaving, keep_column, table, mixed, totals, middle,
        slope, dec.attn_weight, dec.fc_one_weight, dec.fc_two_weight, stack,
    )
    return found[:7], found[7:]


def encode_back_kernel(leaving_grad, latents, stream, keep_row, table, mixed, totals, middle, *refs):
    slope_src, attn_src, one_src, two_src, stack = refs[:5]
    proj_src = placed(stack, PLACES[ENC].proj_weight)
    outs, (stream_grad, embed_grad) = refs[5:12], refs[12:14]
    attn_w, proj_w, one_w, two_w, slope, attended_grad, sem = refs[14:]
    moves = start_all((two_src, slope_src, one_src, proj_src, attn_src), (two_w, slope, one_w, proj_w, attn_w), sem)
    value = backward_block(
        leaving_grad[...], ENC_ROWS, stream, keep_row, table, mixed, totals, middle, outs,
        (attn_w, proj_w, one_w, two_w), slope, attended_grad, moves,
    )
    stream_grad[...] = value
    sums = outs[4]
    sums[MORE : MORE + 1, :] = column_sum(stream_grad[:BUF, :])
    tokens = stream_grad[BUF:, :]
    sums[MORE + 1 : MORE + 2, :] = column_sum(tokens)
    embed_grad[...] = lax.dot_general(latents[...], tokens.astype(NARROW), (((0,), (0,)), ((), ())), preferred_element_type=WIDE)


def encode_back(leaving_grad, latents, stream, keep_row, table, stored, stack, enc):
    length = BUF + SEQ
    normed, mixed, totals, attended, middle, second, slope, active = stored
    found = pl.pallas_call(
        encode_back_kernel,
        out_shape=backward_shapes(length, 8)
        + [jax.ShapeDtypeStruct((n, D), WIDE) for n in (length, TOK_CH)],
        in_specs=[VMEM] * 8 + [HBM] * 5,
        out_specs=[VMEM] * 9,
        scratch_shapes=backward_scratch(length, BLOCK_WEIGHTS),
        compiler_params=BIG,
        cost_estimate=block_cost(length, BLOCK_WEIGHTS),
    )(
        leaving_grad, latents, stream, keep_row, table, mixed, totals, middle,
        slope, enc.attn_weight, enc.fc_one_weight, enc.fc_two_weight, stack,
    )
    return found[:7], found[7:]


class Vector:
    def __init__(self, array, *parts):
        self.array, self.parts = array, parts


def block_grads(stored, found):
    normed, mixed, totals, attended, middle, second, slope, active = stored
    out_low, inner_low, middle_low, mixed_low, sums, one_sum, mixed_sum = found

    def row(k):
        return Vector(sums, (k, 0, D))

    return dict(
        norm_one_gain=row(G_ONE), norm_one_shift=row(S_ONE), attn_weight=(normed, mixed_low),
        attn_bias=Vector(mixed_sum, (0, 0, D), (0, 2 * D, D)), proj_weight=(attended, middle_low), proj_bias=row(PROJ_B),
        norm_two_gain=row(G_TWO), norm_two_shift=row(S_TWO), fc_one_weight=(second, inner_low),
        fc_one_bias=Vector(one_sum, (0, 0, MLP)), fc_two_weight=(active, out_low), fc_two_bias=row(TWO_B),
    )


SUMS = 9


def eighths(value):
    found = value[:8]
    for k in range(8, value.shape[0], 8):
        found = found + value[k : k + 8]
    return found


def sigmoid(value):
    return 0.5 + 0.5 * jnp.tanh(0.5 * value)


def silu_and_slope(value):
    s = sigmoid(value)
    silu = value * s
    return silu, s + silu * (1.0 - s)


def turned_matmul(left, right):
    return lax.dot_general(left, right, (((0,), (0,)), ((), ())), preferred_element_type=WIDE)


def head_kernel(
    divisor, arrived, features, levels, noise, final_w, wide_b, ada_b, final_b, ada_src, stack,
    signal, mod_low, modulated, inner_low, active, outer_low, joined_low, cond_low, cond_back, wide_sums, final_grad, input_grad, last,
    cond, joined, hidden, mod, hat, inner, outer, top, total, sums, cond_w, time_w, input_w, ada_w, inner_w, outer_w, weight_sem,
):
    step = pl.program_id(0)
    own = PLACES[-1]
    sources = [placed(stack, place) for place in (own.cond_weight, own.time_weight, own.input_weight)]
    sources += [ada_src, placed(stack, own.inner_weight), placed(stack, own.outer_weight)]
    held = (cond_w, time_w, input_w, ada_w, inner_w, outer_w)
    moves = [pltpu.make_async_copy(s, t, weight_sem.at[i]) for i, (s, t) in enumerate(zip(sources, held))]

    def need(*which):
        @pl.when(step == 0)
        def _():
            for i in which:
                moves[i].wait()

    def bias(k):
        return wide_b[k : k + 1, :]

    def add_sum(k, value):
        sums[k * 8 : (k + 1) * 8, :] = sums[k * 8 : (k + 1) * 8, :] + eighths(value)

    @pl.when(step == 0)
    def _():
        for move in moves:
            move.start()
        for ref in (sums, total, final_grad, input_grad, last):
            ref[...] = jnp.zeros_like(ref)
        for move in moves[:3]:
            move.wait()
        cond[...] = matmul(arrived[:, :D], cond_w[...]) + bias(0)

    clean = arrived[:, D : D + TOK_CH].astype(WIDE)
    marks = arrived[:, D + TOK_CH : D + TOK_CH + 1].astype(WIDE)
    noisy = (levels[:, 0:1] * clean + levels[:, 1:2] * noise[...]).astype(NARROW)
    value, slope = silu_and_slope(matmul(features[...], time_w[...]) + bias(1) + cond[...])
    joined[...] = slope
    signal[...] = value.astype(NARROW)
    h = matmul(noisy, input_w[...]) + bias(2)
    hidden[...] = h
    value, first_r = whiten(h)
    hat[...] = value
    need(3, 4, 5)
    mod[...] = matmul(signal[...], ada_w[...])
    normed = hat[...] * bias(3) + bias(4)
    scale = 1.0 + (mod[:, HW : 2 * HW] + ada_b[0:1, HW : 2 * HW])
    modulated[...] = (normed * scale + (mod[:, :HW] + ada_b[0:1, :HW])).astype(NARROW)
    mod[:, HW : 2 * HW] = scale
    value, slope = silu_and_slope(matmul(modulated[...], inner_w[...]) + bias(5))
    inner[...] = slope
    active[...] = value.astype(NARROW)
    out = matmul(active[...], outer_w[...]) + bias(6)
    outer[...] = out
    gate = mod[:, 2 * HW :] + ada_b[0:1, 2 * HW :]
    mod[:, 2 * HW :] = gate
    value, r = whiten(hidden[...] + gate * out)
    top[...] = value
    final = value.astype(NARROW)
    error = matmul(final, final_w[...]) + final_b[0:1, :] - noise[...]
    pred_grad = 2.0 * error * marks / divisor[0]
    pred_low = pred_grad.astype(NARROW)
    last[0:1, :TOK_CH] = last[0:1, :TOK_CH] + column_sum(pred_grad)
    last[1:2, 0:1] = last[1:2, 0:1] + column_sum(jnp.sum(error * error, -1, keepdims=True) * marks)
    final_grad[...] = final_grad[...] + turned_matmul(final, pred_low)
    g = whiten_back(matmul_turned(pred_low, final_w[...]), top[...], r)
    hidden[...] = g
    gate_grad = g * outer[...]
    mod_low[:, 2 * HW :] = gate_grad.astype(NARROW)
    add_sum(0, gate_grad)
    out_grad = g * mod[:, 2 * HW :]
    outer_low[...] = out_grad.astype(NARROW)
    add_sum(1, out_grad)
    g = matmul_turned(outer_low[...], outer_w[...]) * inner[...]
    inner_low[...] = g.astype(NARROW)
    add_sum(2, g)
    g = matmul_turned(inner_low[...], inner_w[...])
    value = hat[...]
    mod_low[:, :HW] = g.astype(NARROW)
    add_sum(3, g)
    scale_grad = g * (value * bias(3) + bias(4))
    mod_low[:, HW : 2 * HW] = scale_grad.astype(NARROW)
    add_sum(4, scale_grad)
    g = g * mod[:, HW : 2 * HW]
    add_sum(5, g)
    add_sum(6, g * value)
    g = hidden[...] + whiten_back(g * bias(3), value, first_r)
    add_sum(7, g)
    input_grad[...] = input_grad[...] + turned_matmul(noisy, g.astype(NARROW))
    g = matmul_turned(mod_low[...], ada_w[...]) * joined[...]
    joined_low[...] = g.astype(NARROW)
    add_sum(8, g)
    total[...] = total[...] + g

    @pl.when(step == pl.num_programs(0) - 1)
    def _():
        found = total[...].astype(NARROW)
        cond_low[...] = found
        cond_back[...] = matmul_turned(found, cond_w[...]).astype(NARROW)
        last[1:2, :] = jnp.broadcast_to(last[1:2, 0:1], (1, LANES))
        for k in range(SUMS):
            wide_sums[k : k + 1, :] = column_sum(sums[k * 8 : (k + 1) * 8, :])


def head_pass(p, stack, arrived, steps, noise, divisor):
    slots = arrived.shape[0]
    times = steps.astype(WIDE)
    features = time_features(times).astype(NARROW).reshape(-1, FREQ)
    level = alpha_level(times).reshape(-1, 1)
    levels = jnp.concatenate([jnp.sqrt(level), jnp.sqrt(1.0 - level)], 1)
    flat_noise = noise.reshape(-1, TOK_CH)
    wide_b = jnp.stack(
        [p.cond_bias, p.time_bias, p.input_bias, p.head_gain, p.head_shift, p.inner_bias, p.outer_bias, p.outer_bias]
    ).astype(WIDE)
    total = COPIES * slots

    def tiled(width):
        return pl.BlockSpec((slots, width), lambda i: (i, 0))

    def whole(x):
        return pl.BlockSpec(x, lambda i: (0, 0), pipeline_mode=pl.Buffered(1))

    heights = (D, FREQ, TOK_CH, None, HW, HW)
    weights = [(h, HW) if h else (HW, 3 * HW) for h in heights]
    small = (p.final_weight, wide_b, p.ada_bias.astype(WIDE)[None], p.final_bias.astype(WIDE)[None])
    kept = [((total, w), NARROW, tiled(w)) for w in (HW, 3 * HW, HW, HW, HW, HW, HW)]
    once = (((slots, HW), NARROW), ((slots, D), NARROW), ((16, HW), WIDE), ((HW, TOK_CH), WIDE), ((TOK_CH, HW), WIDE), ((8, LANES), WIDE))
    kept += [(s, t, whole(s)) for s, t in once]
    flops = 4 * total * (FREQ * HW // 2 + 5 * HW * HW) + 4 * slots * D * HW
    found = pl.pallas_call(
        head_kernel,
        grid=(COPIES,),
        out_shape=[jax.ShapeDtypeStruct(s, t) for s, t, _ in kept],
        in_specs=[pl.BlockSpec(memory_space=pltpu.SMEM), whole(arrived.shape), tiled(FREQ), tiled(2), tiled(TOK_CH)]
        + [whole(x.shape) for x in small] + [HBM] * 2,
        out_specs=[spec for _, _, spec in kept],
        scratch_shapes=[pltpu.VMEM((slots, w), WIDE) for w in (HW, HW, HW, 3 * HW, HW, HW, HW, HW, HW)]
        + [pltpu.VMEM((SUMS * 8, HW), WIDE)] + [pltpu.VMEM(s, NARROW) for s in weights] + [DMA((len(weights),))],
        compiler_params=BIG,
        cost_estimate=pl.CostEstimate(flops=flops, bytes_accessed=26 * total * HW, transcendentals=3 * total * HW),
    )(divisor[None], arrived, features, levels, flat_noise, *small, p.ada_weight, stack)
    signal, mod_low, modulated, inner_low, active, outer_low, joined_low, cond_low, cond_back, sums, final_grad, input_grad, last = found

    def row(k):
        return Vector(sums, (k, 0, HW))

    grads = dict(
        final_weight=final_grad, final_bias=Vector(last, (0, 0, LANES)),
        outer_weight=(active, outer_low), outer_bias=row(1), inner_weight=(modulated, inner_low), inner_bias=row(2),
        head_gain=row(6), head_shift=row(5), ada_weight=(signal, mod_low),
        ada_bias=Vector(sums, (3, 0, HW), (4, 0, HW), (0, 0, HW)), time_weight=(features, joined_low), time_bias=row(8),
        cond_weight=(arrived, cond_low), cond_bias=row(8), input_weight=input_grad, input_bias=row(7),
    )
    return last[1:2], grads, cond_back


def time_features(times):
    half = FREQ // 2
    freqs = jnp.exp(-math.log(10000.0) * jnp.arange(half, dtype=WIDE) / half)
    angles = times[..., None] * freqs
    return jnp.concatenate([jnp.cos(angles), jnp.sin(angles)], -1)


def alpha_level(times):
    start = math.cos(0.008 / 1.008 * math.pi / 2) ** 2
    return jnp.cos(((times + 1.0) / STEPS_T + 0.008) / 1.008 * math.pi / 2) ** 2 / start


def exchange(payload, parts):
    shape = payload.shape
    moved = lax.all_to_all(payload.reshape(parts, -1, shape[-1]), "dp", split_axis=0, concat_axis=0, tiled=True)
    return moved.reshape(shape)


def body(latents, route, labels, timesteps, noise, image_weight, weights, momentum, average):
    ranks_dp, ranks_rep = lax.axis_size("dp"), lax.axis_size("rep")
    ranks = ranks_dp * ranks_rep
    meshed = (ranks_dp, ranks_rep) == (8, 4)
    rows = route.shape[0]
    images = labels.shape[0]
    assert images == 1 and rows == SEQ
    size = weights.shape[0] // LANES
    padded = -(-(size + 1) // 48) * 48
    masked = route < rows
    flat = weights.reshape(size, LANES)
    if meshed:
        gathered = spread(flat, route, padded)
    else:
        extra = jnp.full((padded - size, LANES), jnp.sum(masked.astype(WIDE)))
        gathered = lax.all_gather(jnp.concatenate([flat, extra], 0).astype(NARROW), BOTH, axis=0)
    base, enc, mid, dec, head = groups = [types.SimpleNamespace() for _ in GROUPS]
    stack, head_stack = unpack(gathered, size, groups)
    count = jnp.sum(gathered[:, size, 0].astype(WIDE))
    keep = jnp.concatenate([jnp.ones((BUF,), WIDE), 1.0 - masked.astype(WIDE)])
    keep_row, keep_column = keep[None], keep[:, None]
    at = next(e.start for e in ENTRIES if e.sparse) + labels[0] * (D // LANES) + jnp.arange(D // LANES, dtype=jnp.int32)
    classes = gathered[at // size, at % size].reshape(D)
    table, attn_b, fc_b = block_vectors(base, enc, mid, dec, head, classes)
    enc_stored, (stream, encoded, leaving, before) = encode(
        latents, keep_row, keep_column, table, attn_b[0], fc_b[0], stack, enc
    )
    token_weight = jnp.broadcast_to(image_weight.astype(NARROW)[:, None], (rows, 1))
    extra = jnp.concatenate([latents, token_weight, jnp.zeros((rows, LANES - TOK_CH - 1), NARROW)], 1)
    dec_stored, flow_out, payload = decode(before, route, extra, table, attn_b[1], fc_b[1], stack, dec)
    arrived = exchange(payload, ranks_dp)
    divisor = TOK_CH * COPIES * count
    loss_part, head_grads, cond_back = head_pass(head, head_stack, arrived, timesteps, noise, divisor)
    returned = exchange(cond_back, ranks_dp)
    height = -(-((ranks - 1) * size + padded) // 8) * 8
    full = fold({(4, name): value for name, value in head_grads.items()}, labels, height)
    dec_found, (token_grad, before_grad, decoded_low, leaving_grad) = decode_back(
        returned, route, flow_out, before, leaving, keep_column, table, dec_stored, stack, dec
    )
    enc_found, (stream_grad, embed_grad) = encode_back(leaving_grad, latents, stream, keep_row, table, enc_stored, stack, enc)

    def row(found, k):
        return Vector(found[4], (MORE + k, 0, D))

    head_grads = dict(diffusion_pos=token_grad, dec_gain=row(dec_found, 0), dec_shift=row(dec_found, 1))
    mid_grads = dict(
        enc_gain=row(dec_found, 4), enc_shift=row(dec_found, 5), dec_weight=(encoded, decoded_low), dec_bias=row(dec_found, 2),
        mask_token=row(dec_found, 3), decoder_pos=before_grad,
    )
    base_grads = dict(encoder_pos=stream_grad, class_table=row(enc_found, 0), embed_weight=embed_grad, embed_bias=row(enc_found, 1))
    grads = {}
    parts = (base_grads, block_grads(enc_stored, enc_found), mid_grads, block_grads(dec_stored, dec_found), head_grads)
    for group, found in enumerate(parts):
        grads.update({(group, name): value for name, value in found.items()})
    full = fold(grads, labels, height, full)
    if meshed:
        lane = lax.broadcasted_iota(jnp.int32, (8, LANES), 1)
        mark = jnp.where(lane == lax.axis_index("dp") * ranks_rep + lax.axis_index("rep"), loss_part, 0.0)
        owned = collect(full, mark, size, padded)
        loss = jnp.sum(owned[padded - 8, :ranks]) / divisor
        owned = owned[:size]
    else:
        loss = lax.psum(loss_part[0, 0], BOTH) / divisor
        owned = lax.psum_scatter(full[: ranks * size].reshape(ranks, size, LANES), BOTH, scatter_dimension=0, tiled=False)
    owned = owned.reshape(-1)
    rate = 0.05 * math.sqrt(images * ranks * SEQ)
    new_momentum = 0.9 * momentum + owned
    new_weights = weights - rate * (owned + 0.9 * new_momentum)
    new_average = 0.75 * average + 0.25 * new_weights
    return new_weights, new_momentum, new_average, loss


def solution(mesh):
    flat = P(BOTH)
    placed = (P(BOTH, None), flat, flat, P(None, BOTH), P(None, BOTH, None), flat, flat, flat, flat)
    return jax.shard_map(body, mesh=mesh, in_specs=placed, out_specs=(flat, flat, flat, P()), check_vma=False)
```

```python
import functools
import heapq
import math
import types

import jax
import jax.numpy as jnp
from jax import lax
from jax.experimental import pallas as pl
from jax.experimental.pallas import tpu as pltpu
from jax.sharding import PartitionSpec as P

D = 768
HEADS = 12
HEAD_DIM = 64
MLP = 3072
HW = 1024
TOK_CH = 16
FREQ = 256
CLASSES = 1000
BUF = 64
SEQ = 256
COPIES = 4
STEPS_T = 1000
LANES = 128
WIDE = jnp.float32
NARROW = jnp.bfloat16
NORM_EPS = 1e-06
MESH = pl.DeviceIdType.MESH
ANY = pl.BlockSpec(memory_space=pl.ANY)
HBM = pl.BlockSpec(memory_space=pltpu.HBM)
VMEM = pl.BlockSpec(memory_space=pltpu.VMEM)
DMA = pltpu.SemaphoreType.DMA
BOTH = ("dp", "rep")


def block_shapes():
    return dict(
        norm_one_gain=(D,), norm_one_shift=(D,), attn_weight=(D, 3 * D), attn_bias=(2 * D,),
        proj_weight=(D, D), proj_bias=(D,), norm_two_gain=(D,), norm_two_shift=(D,),
        fc_one_weight=(D, MLP), fc_one_bias=(MLP,), fc_two_weight=(MLP, D), fc_two_bias=(D,),
    )


ENC, DEC = 1, 3
GROUPS = (
    dict(embed_weight=(TOK_CH, D), embed_bias=(D,), class_table=(CLASSES, D), encoder_pos=(BUF + SEQ, D)),
    block_shapes(),
    dict(enc_gain=(D,), enc_shift=(D,), dec_weight=(D, D), dec_bias=(D,), mask_token=(D,), decoder_pos=(BUF + SEQ, D)),
    block_shapes(),
    dict(
        dec_gain=(D,), dec_shift=(D,), diffusion_pos=(SEQ, D), input_weight=(TOK_CH, HW), input_bias=(HW,),
        time_weight=(FREQ, HW), time_bias=(HW,), cond_weight=(D, HW), cond_bias=(HW,), head_gain=(HW,),
        head_shift=(HW,), ada_weight=(HW, 3 * HW), ada_bias=(3 * HW,), inner_weight=(HW, HW), inner_bias=(HW,),
        outer_weight=(HW, HW), outer_bias=(HW,), final_weight=(HW, TOK_CH), final_bias=(TOK_CH,),
    ),
)


class Entry:
    def __init__(self, group, name, shape, start):
        self.group, self.name, self.shape, self.start = group, name, shape, start
        self.rows = -(-math.prod(shape) // LANES)
        self.matrix = len(shape) == 2 and shape[1] % LANES == 0
        self.across = shape[1] // LANES if self.matrix else 1
        self.sparse = name == GROUP_SPARSE


GROUP_SPARSE = next(name for name, shape in GROUPS[0].items() if shape[0] == CLASSES)


def entries():
    found, start = [], 0
    for group, shapes in enumerate(GROUPS):
        for name, shape in shapes.items():
            found.append(Entry(group, name, shape, start))
            start += found[-1].rows
    return found


ENTRIES = entries()
USED = ENTRIES[-1].start + ENTRIES[-1].rows


STACKS = ((D, D), (HW, HW))
PLACES = [types.SimpleNamespace() for _ in GROUPS]
STACK_OF = {}
STACK_ROWS = []
for number, (width, tallest) in enumerate(STACKS):
    top = 0
    for e in ENTRIES:
        if e.matrix and not e.sparse and e.shape[1] == width and e.shape[0] <= tallest:
            setattr(PLACES[e.group], e.name, (top, e.shape[0]))
            STACK_OF[e] = number, top
            top += e.shape[0]
    STACK_ROWS.append(top)


def placed(stack, place):
    return stack.at[pl.ds(*place)]


def block_height(entry, limit):
    best = 0
    for height in range(8, entry.shape[0] + 1, 8):
        if entry.shape[0] % height == 0 and height * entry.across <= limit:
            best = height
    return best


class Slots:
    def __init__(self, number):
        self.number, self.base, self.last = number, 0, {}

    def at(self, b):
        return (self.base + b) % self.number

    def claim(self, b, put):
        for k in range(self.number):
            before = self.last.get((self.base + k) % self.number)
            if before is not None:

                @pl.when(b == k)
                def _(before=before):
                    before().wait()

        @pl.when(b >= self.number)
        def _():
            put(b - self.number).wait()

    def close(self, blocks, put):
        base = self.base
        for b in range(max(0, blocks - self.number), blocks):
            self.last[(base + b) % self.number] = functools.partial(put, b)
        self.base = base + blocks

    def drain(self):
        for before in self.last.values():
            before().wait()


SLOTS = 8
OUT = 3


def unfold_kernel(rows, padded, items, g_ref, *refs):
    count = len(items)
    total = len(STACKS) + sum(e not in STACK_OF for e, _ in items)
    stacks, alone = refs[: len(STACKS)], iter(refs[len(STACKS) : total])
    outs = [(stacks[STACK_OF[e][0]], STACK_OF[e][1]) if e in STACK_OF else (next(alone), 0) for e, _ in items]
    first, second, wide, first_sem, second_sem, out_sem = refs[total : total + 6]
    kinds = sorted({(h, e.across) for e, h in items})
    stages = dict(zip(kinds, refs[total + 6 :]))
    turns = {kind: Slots(OUT) for kind in kinds}
    bases = [0]
    for entry, height in items:
        bases.append(bases[-1] + entry.shape[0] // height)

    def spot(t, b):
        entry, height = items[t]
        span = height * entry.across
        start = entry.start + b * span
        dev = start // rows
        row = start - dev * rows
        low = jnp.minimum(row // 8 * 8, padded - span - 8)
        return dev, row, low, row + span > rows

    def copies(t, b):
        entry, height = items[t]
        window = height * entry.across + 8
        dev, row, low, more = spot(t, b)
        slot = (bases[t] + b) % SLOTS
        one = pltpu.make_async_copy(
            g_ref.at[dev, pl.ds(pl.multiple_of(low, 8), window)], first.at[slot, pl.ds(0, window)], first_sem.at[slot]
        )
        two = pltpu.make_async_copy(
            g_ref.at[jnp.minimum(dev + 1, g_ref.shape[0] - 1), pl.ds(0, window)],
            second.at[slot, pl.ds(0, window)], second_sem.at[slot],
        )
        return one, two, more

    def fetch(t, b):
        one, two, more = copies(t, b)
        one.start()

        @pl.when(more)
        def _():
            two.start()

    def fetch_number(g):
        if g < bases[-1]:
            t = next(t for t in range(count) if g < bases[t + 1])
            fetch(t, g - bases[t])

    ahead = SLOTS - 1
    for g in range(ahead):
        fetch_number(g)
    for t, (entry, height) in enumerate(items):
        kind = (height, entry.across)
        stage, turn = stages[kind], turns[kind]
        window = height * entry.across + 8
        blocks = entry.shape[0] // height

        def put(b, t=t, stage=stage, height=height, place=turn.base, kind=kind):
            slot = (place + b) % OUT
            into, top = outs[t]
            return pltpu.make_async_copy(
                stage.at[slot], into.at[pl.ds(pl.multiple_of(top + b * height, 8), height)], out_sem.at[kinds.index(kind), slot]
            )

        def body(b, carry, t=t, entry=entry, height=height, window=window, blocks=blocks, stage=stage, turn=turn, put=put):
            @pl.when(b + ahead < blocks)
            def _():
                fetch(t, b + ahead)

            for k in range(max(0, ahead - blocks), ahead):

                @pl.when(b == blocks - ahead + k)
                def _(k=k):
                    fetch_number(bases[t + 1] + k)

            dev, row, low, _ = spot(t, b)
            slot = (bases[t] + b) % SLOTS
            one, two, more = copies(t, b)
            one.wait()
            wide[pl.ds(0, window), :] = first[slot, pl.ds(0, window), :].astype(WIDE)

            @pl.when(more)
            def _():
                two.wait()
                wide[pl.ds(rows - low, window), :] = second[slot, pl.ds(0, window), :].astype(WIDE)

            turn.claim(b, put)
            off = row - low
            place = turn.at(b)
            for j in range(entry.across):
                stage[place, :, j * LANES : (j + 1) * LANES] = wide[pl.ds(off + j, height, stride=entry.across), :].astype(NARROW)
            put(b).start()
            return carry

        lax.fori_loop(0, blocks, body, 0)
        turn.close(blocks, put)
    for turn in turns.values():
        turn.drain()


def unfold(gathered, rows):
    padded = gathered.shape[1]
    items = [(e, block_height(e, min(2304, rows - 16))) for e in ENTRIES if e.matrix and not e.sparse]
    tall = max(e.across * h for e, h in items) + 8
    kinds = sorted({(h, e.across) for e, h in items})
    total = sum(math.prod(e.shape) for e, _ in items)
    alone = [e for e, _ in items if e not in STACK_OF]
    shapes = [(n, width) for n, (width, _) in zip(STACK_ROWS, STACKS)] + [e.shape for e in alone]
    outs = pl.pallas_call(
        functools.partial(unfold_kernel, rows, padded, items),
        out_shape=[jax.ShapeDtypeStruct(s, NARROW) for s in shapes],
        in_specs=[ANY],
        out_specs=[ANY] * len(shapes),
        scratch_shapes=[
            pltpu.VMEM((SLOTS, tall, LANES), NARROW), pltpu.VMEM((SLOTS, tall, LANES), NARROW),
            pltpu.VMEM((2 * tall, LANES), WIDE), DMA((SLOTS,)), DMA((SLOTS,)), DMA((len(kinds), OUT)),
        ]
        + [pltpu.VMEM((OUT, h, n * LANES), NARROW) for h, n in kinds],
        compiler_params=pltpu.CompilerParams(vmem_limit_bytes=48 * 1000 * 1000),
        cost_estimate=pl.CostEstimate(flops=total, bytes_accessed=4 * total, transcendentals=0),
    )(gathered)
    return outs[: len(STACKS)], {(e.group, e.name): out for e, out in zip(alone, outs[len(STACKS) :])}


def rows_at(gathered, rows, start, number):
    pieces = []
    while number > 0:
        dev, row = divmod(start, rows)
        take = min(number, rows - row)
        pieces.append(gathered[dev, row : row + take])
        start, number = start + take, number - take
    return pieces[0] if len(pieces) == 1 else jnp.concatenate(pieces, 0)


def unpack(gathered, rows, groups):
    stacks, matrices = unfold(gathered, rows)
    for e in ENTRIES:
        if e.sparse or e in STACK_OF:
            continue
        if e.matrix:
            value = matrices[(e.group, e.name)]
        else:
            value = rows_at(gathered, rows, e.start, e.rows).reshape(-1)[: math.prod(e.shape)].reshape(e.shape)
        setattr(groups[e.group], e.name, value)
    return stacks


DEPTH = 5
TALL = 256
CHUNK = 512
NEXT = 3


def product_height(entry):
    return min(TALL, entry.shape[0])


def fold_kernel(products, items, plain, vectors, lone_place, zero, count, going_on, label, *refs):
    refs = list(refs)

    def take(number):
        found, refs[:number] = refs[:number], []
        return found

    small = take(count)
    pairs = take(2 * len(products))
    given = take(len(items))
    rest = take(len(plain))
    take(int(going_on))
    (full,) = take(1)
    pair_sem, given_sem, plain_sem, out_sem, vector_sem = take(5)
    held = take(2 * len(products))
    loads = take(len(items))
    stage, lines = take(2)
    gets = [pltpu.make_async_copy(given[i], loads[i], given_sem.at[i]) for i in range(len(items))]
    fills = []
    for i, entry in enumerate(products):
        for k in (2 * i, 2 * i + 1):
            source = pairs[k]
            if source.shape != held[k].shape:
                source = source.at[:, pl.ds(0, held[k].shape[1])]
            fills.append(pltpu.make_async_copy(source, held[k], pair_sem.at[k]))
    for move in gets + fills[: 2 * NEXT]:
        move.start()
    moves = []
    for i, (start, number) in enumerate(plain):
        move = pltpu.make_async_copy(rest[i].at[pl.ds(0, number)], full.at[pl.ds(start, number)], plain_sem.at[i])
        move.start()
        moves.append(move)
    at = 0
    for i, (entry, which, parts) in enumerate(vectors):
        begin = at
        for k, column, width in parts:
            for j in range(0, width, LANES):
                lines[at : at + 1, :] = small[which][k : k + 1, column + j : column + j + LANES]
                at += 1
        move = pltpu.make_async_copy(lines.at[pl.ds(begin, at - begin)], full.at[pl.ds(entry.start, at - begin)], vector_sem.at[i])
        move.start()
        moves.append(move)
        at = -(-at // 8) * 8
    if zero:
        lines[at : at + zero, :] = jnp.zeros((zero, LANES), WIDE)
        move = pltpu.make_async_copy(lines.at[pl.ds(at, zero)], full.at[pl.ds(USED, zero)], vector_sem.at[len(vectors)])
        move.start()
        moves.append(move)
    turn = Slots(DEPTH)

    def each(entry, height, make):
        span = height * entry.across
        blocks = entry.shape[0] // height

        def put(b, base=turn.base):
            slot = (base + b) % DEPTH
            return pltpu.make_async_copy(
                stage.at[slot, pl.ds(0, span)], full.at[pl.ds(entry.start + b * span, span)], out_sem.at[slot]
            )

        def step(b, carry):
            turn.claim(b, put)
            make(b, turn.at(b))
            put(b).start()
            return carry

        lax.fori_loop(0, blocks, step, 0)
        turn.close(blocks, put)

    if lone_place:
        sparse = next(e for e in ENTRIES if e.sparse)
        height = block_height(sparse, 1200)
        row, row_at = small[lone_place[0]], lone_place[1]

        def lone(b, slot):
            here = lax.broadcasted_iota(jnp.int32, (height, LANES), 0) + b * height == label[0]
            for j in range(sparse.across):
                value = jnp.broadcast_to(row[row_at : row_at + 1, j * LANES : (j + 1) * LANES], (height, LANES))
                stage[slot, pl.ds(j, height, stride=sparse.across), :] = jnp.where(here, value, 0.0)

        each(sparse, height, lone)
    for t, entry in enumerate(items):
        gets[t].wait()

        def make(b, slot, t=t, entry=entry):
            for j in range(entry.across):
                stage[slot, pl.ds(j, entry.shape[0], stride=entry.across), :] = loads[t][:, j * LANES : (j + 1) * LANES]

        each(entry, entry.shape[0], make)
    for t, entry in enumerate(products):
        left, right = held[2 * t], held[2 * t + 1]
        for move in fills[2 * (t + NEXT) : 2 * (t + NEXT) + 2]:
            move.start()
        fills[2 * t].wait()
        fills[2 * t + 1].wait()
        height = product_height(entry)
        chunk = math.gcd(CHUNK, entry.shape[1])

        def make(b, slot, left=left, right=right, entry=entry, height=height, chunk=chunk):
            turned = left[:, pl.ds(pl.multiple_of(b * height, LANES), height)].T
            for k in range(entry.shape[1] // chunk):
                found = jnp.dot(turned, right[:, k * chunk : (k + 1) * chunk], preferred_element_type=WIDE)
                for j in range(chunk // LANES):
                    at = pl.ds(k * (chunk // LANES) + j, height, stride=entry.across)
                    stage[slot, at, :] = found[:, j * LANES : (j + 1) * LANES]

        each(entry, height, make)
    turn.drain()
    for move in moves:
        move.wait()


def fold(grads, label, height_total, full=None):
    wanted = [e for e in ENTRIES if (e.group, e.name) in grads]
    found = {e: grads[(e.group, e.name)] for e in wanted}
    products = [e for e in wanted if isinstance(found[e], tuple)]
    items = [e for e in wanted if e.matrix and not isinstance(found[e], (tuple, Vector))]
    small, vectors, plain, values, lone_place = [], [], [], [], None
    for e in wanted:
        if isinstance(found[e], Vector):
            place = next((i for i, x in enumerate(small) if x is found[e].array), len(small))
            small[place : place + 1] = [found[e].array]
            if e.sparse:
                lone_place = (place, found[e].parts[0][0])
            else:
                vectors.append((e, place, found[e].parts))
        elif not e.matrix and e not in products:
            plain.append((e.start, e.rows))
            values.append(found[e].reshape(e.rows, LANES))
    zero = height_total - USED if full is None else 0
    before = [] if full is None else [full]
    lines = sum(-(-e.rows // 8) * 8 for e, _, _ in vectors) + -(-zero // 8) * 8
    operands = [x for e in products for x in found[e]]
    holds = [(x.shape[0], n) for e in products for x, n in zip(found[e], e.shape)]
    tall = max([e.rows for e in items] + [e.across * product_height(e) for e in products])
    total = sum(e.rows for e in wanted) * LANES
    taken = 1 + len(small) + len(operands) + len(items) + len(plain)
    flops = sum(2 * math.prod(e.shape) * operands[2 * i].shape[0] for i, e in enumerate(products))
    return pl.pallas_call(
        functools.partial(fold_kernel, products, items, plain, vectors, lone_place, zero, len(small), bool(before)),
        out_shape=jax.ShapeDtypeStruct((height_total, LANES), WIDE),
        in_specs=[pl.BlockSpec(memory_space=pltpu.SMEM)] + [VMEM] * len(small) + [ANY] * (len(operands) + len(items) + len(plain) + len(before)),
        out_specs=ANY,
        input_output_aliases={taken: 0} if before else {},
        scratch_shapes=[DMA((len(operands),)), DMA((len(items),)), DMA((max(len(plain), 1),)), DMA((DEPTH,)), DMA((len(vectors) + 1,))]
        + [pltpu.VMEM(s, NARROW) for s in holds]
        + [pltpu.VMEM(e.shape, WIDE) for e in items]
        + [pltpu.VMEM((DEPTH, tall, LANES), WIDE), pltpu.VMEM((lines, LANES), WIDE)],
        compiler_params=pltpu.CompilerParams(vmem_limit_bytes=62 * 1000 * 1000),
        cost_estimate=pl.CostEstimate(flops=flops, bytes_accessed=4 * total, transcendentals=0),
    )(label, *small, *operands, *[found[e] for e in items], *values, *before)


X, Y, Z = 0, 1, 2
TREES = ((Z, X, Y), (Z, Y, X), (X, Z, Y), (X, Z, Y), (Y, Z, X), (Y, Z, X))
SHARES = len(TREES)
FAR = 3


def onward(order, arrived, way, p):
    z, x, y = p
    found = []
    if arrived >= 0 and order[arrived] == Z and 0 <= z + way <= FAR:
        found.append(((z + way, x, y), arrived, way))
    for j in range(arrived + 1, 3):
        if order[j] == X:
            found.append(((z, 1 - x, y), j, 0))
        elif order[j] == Y:
            found.append(((z, x, 1 - y), j, 0))
        else:
            found += [((z + s, x, y), j, s) for s in (1, -1) if 0 <= z + s <= FAR]
    return found


@functools.cache
def flow(lag=0.4):
    chips = [(z, x, y) for z in range(FAR + 1) for x in range(2) for y in range(2)]
    events, queues, busy, come, sent = [], {}, set(), {}, []
    number = iter(range(10**9))
    for u in range(SHARES):
        for p in chips:
            heapq.heappush(events, (0.0, next(number), 0, (p, p, u, -1, 0)))

    def pump(link, t):
        if link in busy or not queues.get(link):
            return
        what = heapq.heappop(queues[link])[2]
        busy.add(link)
        sent.append((t, link, what[1], what[2]))
        heapq.heappush(events, (t + 1.0, next(number), 1, (link, what)))

    while events:
        t, _, kind, what = heapq.heappop(events)
        if kind == 1:
            link, piece = what
            busy.discard(link)
            heapq.heappush(events, (t + lag, next(number), 0, piece))
            pump(link, t)
            continue
        p, q, u, k, way = what
        come[(u, p, q)] = t
        for to, k2, way2 in onward(TREES[u], k, way, p):
            left = len(onward(TREES[u], k2, way2, to))
            heapq.heappush(queues.setdefault((p, to), []), ((-left, t), next(number), (to, q, u, k2, way2)))
            pump((p, to), t)
    return come, sent


def spread_order():
    keyed = {}
    for (u, p, q), t in flow()[0].items():
        keyed.setdefault((u, q[0] - p[0], (q[1] - p[1]) % 2, (q[2] - p[2]) % 2), []).append(t)
    return sorted(keyed, key=lambda k: (sum(keyed[k]) / len(keyed[k]), k))


def last_hop(u, dz, dx, dy):
    apart = [k for k in range(3) if (dx, dy, dz)[TREES[u][k]] != 0]
    return apart[-1] if apart else -1


def hops(u, dz, dx, dy):
    order, arrived = TREES[u], last_hop(u, dz, dx, dy)
    found = []
    if arrived >= 0 and order[arrived] == Z:
        found.append((1, 0, 0) if dz < 0 else (-1, 0, 0))
    for k in range(arrived + 1, 3):
        found += [[(0, 1, 0)], [(0, 0, 1)], [(1, 0, 0), (-1, 0, 0)]][order[k]]
    return found


def only(condition, action):
    if condition is None:
        action()
    else:
        pl.when(condition)(action)


def spread_kernel(flat, route, out, wide, own, load_sem, keep_sem, send_sem, link_sem, core_send, core_sem):
    dp, rep = lax.axis_index("dp"), lax.axis_index("rep")
    z, x, y, c = dp // 2, dp % 2, rep // 2, rep % 2
    size, padded = flat.shape[0], own.shape[0]
    unit = padded // SHARES
    sibling = (dp, y * 2 + 1 - c)
    loads = []
    for u in range(SHARES):
        part = pl.ds(u * unit, min(unit, size - u * unit))
        loads.append(pltpu.make_async_copy(flat.at[part], wide.at[part], load_sem.at[u]))
        loads[u].start()

    def device(dz, dx, dy):
        return ((z + dz) * 2 + (x + dx) % 2, (y + dy) % 2 * 2 + c)

    def exists(dz):
        return None if dz == 0 else (z + dz >= 0 if dz < 0 else z + dz <= FAR)

    barrier = pltpu.get_barrier_semaphore()
    near = ((0, 1, 0), (0, 0, 1), (1, 0, 0), (-1, 0, 0))
    for hop in near:
        only(exists(hop[0]), lambda: pl.semaphore_signal(barrier, inc=1, device_id=device(*hop), device_id_type=MESH))
    pl.semaphore_signal(barrier, inc=1, device_id=sibling, device_id_type=MESH)
    inner = z * (FAR - z)
    only(inner == 0, lambda: pl.semaphore_wait(barrier, len(near)))
    only(inner > 0, lambda: pl.semaphore_wait(barrier, len(near) + 1))
    masked = jnp.sum(jnp.where(route[...] < SEQ, 1.0, 0.0))
    keeps, ends, number = [], [], 0
    for u, dz, dx, dy in spread_order():
        part = pl.ds(u * unit, unit)
        q = ((z + dz) * 2 + (x + dx) % 2) * 2 + (y + dy) % 2
        mine = dz == 0 and dx == 0 and dy == 0
        i = u * 16 + q

        def copy(to, send, come, part=part, q=q, mine=mine):
            here = out.at[q * 2 + c, part]
            return pltpu.make_async_remote_copy(
                own.at[part] if mine else here, here, send, come, device_id=to, device_id_type=MESH
            )

        goes = [(hop, number + k) for k, hop in enumerate(hops(u, dz, dx, dy))]
        number += len(goes)

        def run(i=i, copy=copy, goes=goes, mine=mine):
            if not mine:
                copy(sibling, send_sem.at[0], link_sem.at[i]).wait_recv()
            for hop, n in goes:
                only(exists(hop[0]), lambda: copy(device(*hop), send_sem.at[n], link_sem.at[i]).start())
            copy(sibling, core_send.at[i], core_sem.at[i]).start()

        def finish(i=i, copy=copy, goes=goes):
            for hop, n in goes:
                only(exists(hop[0]), lambda: copy(device(*hop), send_sem.at[n], link_sem.at[i]).wait_send())
            copy(sibling, core_send.at[i], core_sem.at[i]).wait()

        if mine:
            loads[u].wait()
            if u == SHARES - 1:
                wide[size:padded, :] = jnp.broadcast_to(masked, (padded - size, LANES))
            own[part, :] = wide[part, :].astype(NARROW)
            keeps.append(pltpu.make_async_copy(own.at[part], out.at[dp * 4 + rep, part], keep_sem.at[u]))
            keeps[-1].start()
        there = None if dz == 0 else jnp.logical_and(z + dz >= 0, z + dz <= FAR)
        only(there, run)
        ends.append((there, finish))
    for there, finish in ends:
        only(there, finish)
    for keep in keeps:
        keep.wait()


def spread(flat, route, padded):
    pieces = SHARES * 16
    sends = sum(len(hops(*key)) for key in spread_order())
    return pl.pallas_call(
        spread_kernel,
        out_shape=jax.ShapeDtypeStruct((32, padded, LANES), NARROW),
        in_specs=[ANY, VMEM],
        out_specs=ANY,
        scratch_shapes=[
            pltpu.VMEM((padded, LANES), WIDE), pltpu.VMEM((padded, LANES), NARROW), DMA((SHARES,)), DMA((SHARES,)),
            DMA((sends,)), DMA((pieces,)), DMA((pieces,)), DMA((pieces,)),
        ],
        compiler_params=pltpu.CompilerParams(collective_id=0, has_side_effects=True),
    )(flat, route.reshape(-1, LANES))


class Chip:
    def __init__(self, low):
        dp, rep = lax.axis_index("dp"), lax.axis_index("rep")
        self.low = low
        self.z, self.x, self.y, self.c = dp // 2, dp % 2, rep // 2, rep % 2
        self.way = 1 - 2 * (self.z // 2)

    def device(self, q, other=0):
        z = self.z + self.way * (q[0] - self.low)
        return z * 2 + (self.x + q[1]) % 2, (self.y + q[2]) % 2 * 2 + (self.c + other) % 2

    def block(self, q, other=0):
        dp, rep = self.device(q, other)
        return dp * 4 + rep

    def greet(self):
        low = self.low
        near = [(low, 1, 0), (low, 0, 1), (low + 1, 0, 0)] + ([(low - 1, 0, 0)] if low else [])
        barrier = pltpu.get_barrier_semaphore()
        for q in near:
            pl.semaphore_signal(barrier, inc=1, device_id=self.device(q), device_id_type=MESH)
        pl.semaphore_signal(barrier, inc=1, device_id=self.device((low, 0, 0), 1), device_id_type=MESH)
        pl.semaphore_wait(barrier, len(near) + 1)


def seen_from(p, r):
    low, way = min(p[0], FAR - p[0]), 1 if p[0] < 2 else -1
    return low + way * (r[0] - p[0]), (r[1] - p[1]) % 2, (r[2] - p[2]) % 2


@functools.cache
def sum_programs():
    come, sent = flow()
    last = max(come.values())
    found = []
    for z in (0, 1):
        p = (z, 0, 0)
        kids, parent, when = {}, {}, {}
        for t, link, q, u in sent:
            if link[0] == p:
                kids.setdefault((u, q), []).append(link[1])
                if q == p:
                    when[(u, p)] = max(when.get((u, p), 0.0), last - t)
            if link[1] == p:
                parent[(u, q)] = link[0]
                when[(u, q)] = last - t - 1.0
        tasks = sorted(when, key=lambda k: (when[k], k))
        found.append([(u, q, sorted(kids.get((u, q), [])), parent.get((u, q))) for u, q in tasks])
    return found


@functools.cache
def landing():
    return [{key: i for i, key in enumerate((u, q, k) for u, q, kids, _ in tasks for k in kids)} for tasks in sum_programs()]


RING = 12
SIDE = 4
EARLY = 12
STEP = 40


def add_rows(into, terms):
    def body(i, carry):
        at = pl.ds(pl.multiple_of(i * STEP, 8), STEP)
        total = into[at, :]
        for term in terms:
            total = total + term[at, :]
        into[at, :] = total
        return carry

    lax.fori_loop(0, into.shape[0] // STEP, body, 0)


def collect_at(low, size, full, mark, out, aside, store, ring, side, ring_sem, side_sem, send_sem, link_sem, core_send, core_sem, out_sem, marks, mark_sem):
    chip = Chip(low)
    me = (low, 0, 0)
    tasks, spots = sum_programs()[low], landing()
    count, unit = len(tasks), ring.shape[1]
    chip.greet()

    def part(i, other=0):
        return full.at[pl.ds(chip.block(tasks[i][1], other) * size + tasks[i][0] * unit, unit)]

    def across(i):
        return pltpu.make_async_remote_copy(
            part(i, 1), aside.at[i], core_send.at[i], core_sem.at[i], device_id=chip.device(me, 1), device_id_type=MESH
        )

    def ours(i):
        return pltpu.make_async_copy(part(i), ring.at[i % RING], ring_sem.at[i % RING])

    def theirs(i):
        return pltpu.make_async_copy(aside.at[i], side.at[i % SIDE], side_sem.at[i % SIDE])

    def along(i, spot, to):
        return pltpu.make_async_remote_copy(
            ring.at[i % RING], store.at[spot], send_sem.at[i], link_sem.at[spot], device_id=chip.device(to), device_id_type=MESH
        )

    tail = pl.ds(unit - 8, 8)
    ours_too = pltpu.make_async_copy(mark, marks.at[0], mark_sem.at[0])
    theirs_too = pltpu.make_async_remote_copy(
        mark, marks.at[1], mark_sem.at[1], mark_sem.at[2], device_id=chip.device(me, 1), device_id_type=MESH
    )
    ours_too.start()
    theirs_too.start()
    leaving = {}

    def fetch(i):
        if i - RING in leaving:
            leaving.pop(i - RING)()
        ours(i).start()
        across(i).wait_recv()
        theirs(i).start()

    for i in range(EARLY):
        across(i).start()
    for i in range(SIDE - 1):
        fetch(i)
    ours_too.wait()
    theirs_too.wait()
    for i, (u, q, kids, to) in enumerate(tasks):
        if i + EARLY < count:
            across(i + EARLY).start()
        if i + SIDE - 1 < count:
            fetch(i + SIDE - 1)
        ours(i).wait()
        theirs(i).wait()
        if u == SHARES - 1:
            ring[i % RING, tail, :] = marks[0] + marks[1]
            side[i % SIDE, tail, :] = jnp.zeros((8, LANES), WIDE)
        terms = [side.at[i % SIDE]]
        for kid in kids:
            spot = spots[low][(u, q, kid)]
            along(i, spot, kid).wait_recv()
            terms.append(store.at[spot])
        add_rows(ring.at[i % RING], terms)
        if to is None:
            move = pltpu.make_async_copy(ring.at[i % RING], out.at[pl.ds(u * unit, unit)], out_sem.at[u])
            move.start()
            leaving[i] = move.wait
        else:
            move = along(i, spots[min(to[0], FAR - to[0])][(u, seen_from(to, q), seen_from(to, me))], to)
            move.start()
            leaving[i] = move.wait_send
    for i in list(leaving):
        leaving.pop(i)()
    for i in range(count):
        across(i).wait_send()


def collect_kernel(size, *refs):
    z = lax.axis_index("dp") // 2
    inner = z * (FAR - z)

    @pl.when(inner == 0)
    def _():
        collect_at(0, size, *refs)

    @pl.when(inner > 0)
    def _():
        collect_at(1, size, *refs)


def collect(full, mark, size, rows):
    slots = max(len(spots) for spots in landing())
    count, unit = len(sum_programs()[0]), rows // SHARES
    return pl.pallas_call(
        functools.partial(collect_kernel, size),
        out_shape=(jax.ShapeDtypeStruct((rows, LANES), WIDE), jax.ShapeDtypeStruct((count, unit, LANES), WIDE)),
        in_specs=[ANY, ANY],
        out_specs=(ANY, ANY),
        scratch_shapes=[
            pltpu.VMEM((slots, unit, LANES), WIDE), pltpu.VMEM((RING, unit, LANES), WIDE), pltpu.VMEM((SIDE, unit, LANES), WIDE),
            DMA((RING,)), DMA((SIDE,)), DMA((count,)), DMA((slots,)), DMA((count,)), DMA((count,)), DMA((SHARES,)),
            pltpu.VMEM((2, 8, LANES), WIDE), DMA((3,)),
        ],
        compiler_params=pltpu.CompilerParams(collective_id=1, has_side_effects=True, vmem_limit_bytes=62 * 1000 * 1000),
    )(full, mark)[0]


HALF_ROOT = math.sqrt(0.5)
PDF = 1.0 / math.sqrt(2.0 * math.pi)
SCALE = HEAD_DIM ** (-0.5)
PART = 512
BIG = pltpu.CompilerParams(vmem_limit_bytes=66 * 1000 * 1000)
BLOCK_WEIGHTS = ((D, 3 * D), (D, D), (D, MLP), (MLP, D))
EMBED_B, ENC_G, ENC_S, DEC_B, MASK_T, DEC_G, DEC_S, CLASS, ENC_ROWS, DEC_ROWS, ALL_ROWS = 0, 1, 2, 3, 4, 5, 6, 7, 8, 14, 24


def matmul(left, right):
    return jnp.dot(left, right, preferred_element_type=WIDE)


def matmul_turned(left, right):
    return lax.dot_general(left, right, (((1,), (1,)), ((), ())), preferred_element_type=WIDE)


def column_sum(value):
    return jnp.sum(value, 0, keepdims=True)


def whiten(value):
    centered = value - jnp.mean(value, -1, keepdims=True)
    r = lax.rsqrt(jnp.mean(centered * centered, -1, keepdims=True) + NORM_EPS)
    return centered * r, r


def whiten_back(grad, hat, r):
    return r * (grad - jnp.mean(grad, -1, keepdims=True) - hat * jnp.mean(grad * hat, -1, keepdims=True))


def side_masks(length):
    lane = lax.broadcasted_iota(jnp.int32, (length, LANES), 1)
    return lane < HEAD_DIM, lane >= HEAD_DIM


def one_side(value, side):
    return jnp.where(side, value, jnp.zeros_like(value))


def start_all(sources, targets, sem):
    moves = [pltpu.make_async_copy(s, t, sem.at[i]) for i, (s, t) in enumerate(zip(sources, targets))]
    for move in moves:
        move.start()
    return moves


def block_vectors(base, enc, mid, dec, head, classes):
    rows = [base.embed_bias, mid.enc_gain, mid.enc_shift, mid.dec_bias, mid.mask_token, head.dec_gain, head.dec_shift, classes]
    for p in (enc, dec):
        rows += [p.norm_one_gain, p.norm_one_shift, p.norm_two_gain, p.norm_two_shift, p.proj_bias, p.fc_two_bias]
    rows += rows[: ALL_ROWS - len(rows)]
    gap = jnp.zeros((D,), NARROW)
    attn_b = [jnp.concatenate([p.attn_bias[:D], gap, p.attn_bias[D:]]).astype(WIDE)[None] for p in (enc, dec)]
    return jnp.stack(rows).astype(WIDE), attn_b, [p.fc_one_bias.astype(WIDE)[None] for p in (enc, dec)]


class Here:
    def wait(self):
        pass


def forward_block(value, first, keep, table, attn_b, fc_b, outs, weights, moves):
    normed, mixed, totals, attended, middle, second, slope, active = outs
    attn_w, proj_w, one_w, two_w = weights
    hat, _ = whiten(value)
    normed[...] = (hat * table[first : first + 1, :] + table[first + 1 : first + 2, :]).astype(NARROW)
    moves[0].wait()
    for k in range(3):
        at = slice(k * D, (k + 1) * D)
        mixed[:, at] = (matmul(normed[...], attn_w[:, at]) + attn_b[0:1, at]).astype(NARROW)
    sides = side_masks(value.shape[0])
    for pair in range(HEADS // 2):
        q, k, v = (mixed[:, part * D + pair * LANES : part * D + (pair + 1) * LANES] for part in range(3))
        found = None
        for i, side in enumerate(sides):
            scores = matmul_turned(one_side(q, side), k) * SCALE
            if keep is not None:
                scores = jnp.where(keep[0:1, :] > 0.0, scores, -1e30)
            top = jnp.max(scores, -1, keepdims=True)
            powers = jnp.exp(scores - top)
            total = jnp.sum(powers, -1, keepdims=True)
            totals[:, 2 * pair + i : 2 * pair + i + 1] = top + jnp.log(total)
            probs = (powers * (1.0 / total)).astype(NARROW)
            part = matmul(probs, one_side(v, side))
            found = part if found is None else found + part
        attended[:, pair * LANES : (pair + 1) * LANES] = found.astype(NARROW)
    moves[1].wait()
    value = value + matmul(attended[...], proj_w[...]) + table[first + 4 : first + 5, :]
    middle[...] = value
    hat, _ = whiten(value)
    second[...] = (hat * table[first + 2 : first + 3, :] + table[first + 3 : first + 4, :]).astype(NARROW)
    moves[2].wait()
    for k in range(MLP // PART):
        at = slice(k * PART, (k + 1) * PART)
        value = matmul(second[...], one_w[:, at]) + fc_b[0:1, at]
        share = 0.5 + 0.5 * lax.erf(value * HALF_ROOT)
        active[:, at] = (value * share).astype(NARROW)
        slope[:, at] = share + value * (PDF * jnp.exp(-0.5 * value * value))
    moves[3].wait()
    return middle[...] + matmul(active[...], two_w[...]) + table[first + 5 : first + 6, :]


def forward_shapes(length):
    widths = [(D, NARROW), (3 * D, NARROW), (LANES, WIDE), (D, NARROW), (D, WIDE), (D, NARROW), (MLP, WIDE), (MLP, NARROW)]
    return [jax.ShapeDtypeStruct((length, w), t) for w, t in widths]


def encode_kernel(latents, keep_row, keep_column, table, attn_b, fc_b, stack, *refs):
    (attn_src, one_src, two_src), outs, (stream, encoded, leaving, before) = refs[:3], refs[3:11], refs[11:15]
    attn_w, one_w, two_w, sem = refs[15:]
    base, enc, mid = PLACES[:3]
    embed_w, enc_pos, dec_pos = (placed(stack, place) for place in (base.embed_weight, base.encoder_pos, mid.decoder_pos))
    held = attn_w, placed(stack, enc.proj_weight), one_w, two_w, placed(stack, mid.dec_weight)
    moves = start_all((attn_src, one_src, two_src), (attn_w, one_w, two_w), sem)
    moves.insert(1, Here())
    pos = enc_pos[...].astype(WIDE)
    stream[:BUF, :] = table[CLASS : CLASS + 1, :] + pos[:BUF]
    stream[BUF:, :] = matmul(latents[...], embed_w[...]) + table[EMBED_B : EMBED_B + 1, :] + pos[BUF:]
    value = forward_block(stream[...], ENC_ROWS, keep_row, table, attn_b, fc_b, outs, held[:4], moves)
    leaving[...] = value
    hat, _ = whiten(value)
    encoded[...] = (hat * table[ENC_G : ENC_G + 1, :] + table[ENC_S : ENC_S + 1, :]).astype(NARROW)
    value = matmul(encoded[...], held[4][...]) + table[DEC_B : DEC_B + 1, :]
    value = jnp.where(keep_column[...] > 0.0, value, table[MASK_T : MASK_T + 1, :])
    before[...] = value + dec_pos[...].astype(WIDE)


def block_cost(length, weights):
    work = sum(math.prod(s) for s in weights)
    return pl.CostEstimate(flops=2 * length * work, bytes_accessed=2 * work + 36 * length * D, transcendentals=4 * length * MLP)


def encode(latents, keep_row, keep_column, table, attn_b, fc_b, stack, enc):
    length = BUF + SEQ
    weights = BLOCK_WEIGHTS + ((D, D),)
    found = pl.pallas_call(
        encode_kernel,
        out_shape=forward_shapes(length)
        + [jax.ShapeDtypeStruct((length, D), t) for t in (WIDE, NARROW, WIDE, WIDE)],
        in_specs=[VMEM] * 7 + [HBM] * 3,
        out_specs=[VMEM] * 12,
        scratch_shapes=[pltpu.VMEM(s, NARROW) for s in BLOCK_WEIGHTS if s != (D, D)] + [DMA((3,))],
        compiler_params=BIG,
        cost_estimate=block_cost(length, weights),
    )(
        latents, keep_row, keep_column, table, attn_b, fc_b, stack, enc.attn_weight, enc.fc_one_weight, enc.fc_two_weight,
    )
    return found[:8], found[8:]


def decode_kernel(before, route, extra, table, attn_b, fc_b, stack, *refs):
    (attn_src, one_src, two_src), outs, (flow_out, payload) = refs[:3], refs[3:11], refs[11:13]
    attn_w, one_w, two_w, sem = refs[13:]
    held = attn_w, placed(stack, PLACES[DEC].proj_weight), one_w, two_w
    diff_pos = placed(stack, PLACES[-1].diffusion_pos)
    moves = start_all((attn_src, one_src, two_src), (attn_w, one_w, two_w), sem)
    moves.insert(1, Here())
    value = forward_block(before[...], DEC_ROWS, None, table, attn_b, fc_b, outs, held, moves)
    flow_out[...] = value
    hat, _ = whiten(flow_out[BUF:, :])
    value = hat * table[DEC_G : DEC_G + 1, :] + table[DEC_S : DEC_S + 1, :]
    conditions = (value + diff_pos[...].astype(WIDE)).astype(NARROW)
    slots = payload.shape[0]
    picks = lax.broadcasted_iota(jnp.int32, (slots, slots), 0) == route[...]
    picks = jnp.where(picks, 1.0, 0.0).astype(NARROW)
    payload[:, :D] = matmul(picks, conditions).astype(NARROW)
    payload[:, D:] = matmul(picks, extra[...]).astype(NARROW)


def decode(before, route, extra, table, attn_b, fc_b, stack, dec):
    length = BUF + SEQ
    found = pl.pallas_call(
        decode_kernel,
        out_shape=forward_shapes(length)
        + [jax.ShapeDtypeStruct((length, D), WIDE), jax.ShapeDtypeStruct((SEQ, D + LANES), NARROW)],
        in_specs=[VMEM] * 7 + [HBM] * 3,
        out_specs=[VMEM] * 10,
        scratch_shapes=[pltpu.VMEM(s, NARROW) for s in BLOCK_WEIGHTS if s != (D, D)] + [DMA((3,))],
        compiler_params=BIG,
        cost_estimate=block_cost(length, BLOCK_WEIGHTS),
    )(
        before, route[None], extra, table, attn_b, fc_b, stack, dec.attn_weight, dec.fc_one_weight, dec.fc_two_weight,
    )
    return found[:8], found[8], found[9]


TWO_B, G_TWO, S_TWO, PROJ_B, G_ONE, S_ONE = 0, 1, 2, 3, 4, 5


def backward_block(value, first, stream, keep, table, mixed, totals, middle, outs, weights, slope, attended_grad, moves):
    out_low, inner_low, middle_low, mixed_low, sums, one_sum, mixed_sum = outs
    attn_w, proj_w, one_w, two_w = weights
    low = value.astype(NARROW)
    out_low[...] = low
    sums[TWO_B : TWO_B + 1, :] = column_sum(value)
    moves[0].wait()
    moves[1].wait()
    for k in range(MLP // PART):
        at = slice(k * PART, (k + 1) * PART)
        part = matmul_turned(low, two_w[at, :]) * slope[:, at]
        inner_low[:, at] = part.astype(NARROW)
        one_sum[0:1, at] = column_sum(part)
    moves[2].wait()
    part = matmul_turned(inner_low[...], one_w[...])
    hat, r = whiten(middle[...])
    sums[G_TWO : G_TWO + 1, :] = column_sum(part * hat)
    sums[S_TWO : S_TWO + 1, :] = column_sum(part)
    value = value + whiten_back(part * table[first + 2 : first + 3, :], hat, r)
    sums[PROJ_B : PROJ_B + 1, :] = column_sum(value)
    middle_low[...] = value.astype(NARROW)
    moves[3].wait()
    attended_grad[...] = matmul_turned(middle_low[...], proj_w[...]).astype(NARROW)
    sides = side_masks(value.shape[0])
    for pair in range(HEADS // 2):
        here = [slice(part * D + pair * LANES, part * D + (pair + 1) * LANES) for part in range(3)]
        q, k, v = (mixed[:, at] for at in here)
        g = attended_grad[:, here[0]]
        grads = [None, None, None]
        for i, side in enumerate(sides):
            q_side, k_side, g_side = one_side(q, side), one_side(k, side), one_side(g, side)
            scores = matmul_turned(q_side, k) * SCALE
            if keep is not None:
                scores = jnp.where(keep[0:1, :] > 0.0, scores, -1e30)
            probs = jnp.exp(scores - totals[:, 2 * pair + i : 2 * pair + i + 1])
            prob_grad = matmul_turned(g_side, v)
            score_grad = (probs * (prob_grad - jnp.sum(probs * prob_grad, -1, keepdims=True))).astype(NARROW)
            parts = (
                matmul(score_grad, k_side) * SCALE, matmul(score_grad.T, q_side) * SCALE, matmul(probs.astype(NARROW).T, g_side)
            )
            grads = [part if old is None else old + part for old, part in zip(grads, parts)]
        for at, part in zip(here, grads):
            mixed_low[:, at] = part.astype(NARROW)
            mixed_sum[0:1, at] = column_sum(part)
    moves[4].wait()
    part = matmul_turned(mixed_low[...], attn_w[...])
    hat, r = whiten(stream[...])
    sums[G_ONE : G_ONE + 1, :] = column_sum(part * hat)
    sums[S_ONE : S_ONE + 1, :] = column_sum(part)
    return value + whiten_back(part * table[first : first + 1, :], hat, r)


def backward_shapes(length, rows):
    shapes = [((length, D), NARROW), ((length, MLP), NARROW), ((length, D), NARROW), ((length, 3 * D), NARROW)]
    shapes += [((rows, D), WIDE), ((1, MLP), WIDE), ((1, 3 * D), WIDE)]
    return [jax.ShapeDtypeStruct(s, t) for s, t in shapes]


def backward_scratch(length, weights):
    return [pltpu.VMEM(s, NARROW) for s in weights] + [
        pltpu.VMEM((length, MLP), WIDE), pltpu.VMEM((length, D), NARROW), DMA((len(weights) + 1,))
    ]


MORE = 6


def decode_back_kernel(returned, route, flow_out, before, leaving, keep_column, table, mixed, totals, middle, *refs):
    slope_src, attn_src, one_src, two_src, stack = refs[:5]
    proj_src, dec_src = placed(stack, PLACES[DEC].proj_weight), placed(stack, PLACES[2].dec_weight)
    outs, (token_grad, before_grad, decoded_low, leaving_grad) = refs[5:12], refs[12:16]
    attn_w, proj_w, one_w, two_w, dec_w, slope, attended_grad, sem = refs[16:]
    moves = start_all(
        (two_src, slope_src, one_src, proj_src, attn_src, dec_src), (two_w, slope, one_w, proj_w, attn_w, dec_w), sem
    )
    slots = returned.shape[0]
    picks = lax.broadcasted_iota(jnp.int32, (slots, slots), 1) == route[...]
    picks = jnp.where(picks, 1.0, 0.0).astype(NARROW)
    grad = matmul(picks, returned[...])
    token_grad[...] = grad
    sums = outs[4]
    hat, r = whiten(flow_out[BUF:, :])
    sums[MORE : MORE + 1, :] = column_sum(grad * hat)
    sums[MORE + 1 : MORE + 2, :] = column_sum(grad)
    before_grad[:BUF, :] = jnp.zeros((BUF, D), WIDE)
    before_grad[BUF:, :] = whiten_back(grad * table[DEC_G : DEC_G + 1, :], hat, r)
    value = backward_block(
        before_grad[...], DEC_ROWS, before, None, table, mixed, totals, middle, outs,
        (attn_w, proj_w, one_w, two_w), slope, attended_grad, moves,
    )
    before_grad[...] = value
    kept = jnp.where(keep_column[...] > 0.0, value, 0.0)
    sums[MORE + 2 : MORE + 3, :] = column_sum(kept)
    sums[MORE + 3 : MORE + 4, :] = column_sum(value - kept)
    decoded_low[...] = kept.astype(NARROW)
    moves[5].wait()
    part = matmul_turned(decoded_low[...], dec_w[...])
    hat, r = whiten(leaving[...])
    sums[MORE + 4 : MORE + 5, :] = column_sum(part * hat)
    sums[MORE + 5 : MORE + 6, :] = column_sum(part)
    leaving_grad[...] = whiten_back(part * table[ENC_G : ENC_G + 1, :], hat, r)


def decode_back(returned, route, flow_out, before, leaving, keep_column, table, stored, stack, dec):
    length = BUF + SEQ
    weights = BLOCK_WEIGHTS + ((D, D),)
    normed, mixed, totals, attended, middle, second, slope, active = stored
    found = pl.pallas_call(
        decode_back_kernel,
        out_shape=backward_shapes(length, 16)
        + [jax.ShapeDtypeStruct((n, D), t) for n, t in ((SEQ, WIDE), (length, WIDE), (length, NARROW), (length, WIDE))],
        in_specs=[VMEM] * 10 + [HBM] * 5,
        out_specs=[VMEM] * 11,
        scratch_shapes=backward_scratch(length, weights),
        compiler_params=BIG,
        cost_estimate=block_cost(length, weights),
    )(
        returned, route[:, None], flow_out, before, leaving, keep_column, table, mixed, totals, middle,
        slope, dec.attn_weight, dec.fc_one_weight, dec.fc_two_weight, stack,
    )
    return found[:7], found[7:]


def encode_back_kernel(leaving_grad, latents, stream, keep_row, table, mixed, totals, middle, *refs):
    slope_src, attn_src, one_src, two_src, stack = refs[:5]
    proj_src = placed(stack, PLACES[ENC].proj_weight)
    outs, (stream_grad, embed_grad) = refs[5:12], refs[12:14]
    attn_w, proj_w, one_w, two_w, slope, attended_grad, sem = refs[14:]
    moves = start_all((two_src, slope_src, one_src, proj_src, attn_src), (two_w, slope, one_w, proj_w, attn_w), sem)
    value = backward_block(
        leaving_grad[...], ENC_ROWS, stream, keep_row, table, mixed, totals, middle, outs,
        (attn_w, proj_w, one_w, two_w), slope, attended_grad, moves,
    )
    stream_grad[...] = value
    sums = outs[4]
    sums[MORE : MORE + 1, :] = column_sum(stream_grad[:BUF, :])
    tokens = stream_grad[BUF:, :]
    sums[MORE + 1 : MORE + 2, :] = column_sum(tokens)
    embed_grad[...] = lax.dot_general(latents[...], tokens.astype(NARROW), (((0,), (0,)), ((), ())), preferred_element_type=WIDE)


def encode_back(leaving_grad, latents, stream, keep_row, table, stored, stack, enc):
    length = BUF + SEQ
    normed, mixed, totals, attended, middle, second, slope, active = stored
    found = pl.pallas_call(
        encode_back_kernel,
        out_shape=backward_shapes(length, 8)
        + [jax.ShapeDtypeStruct((n, D), WIDE) for n in (length, TOK_CH)],
        in_specs=[VMEM] * 8 + [HBM] * 5,
        out_specs=[VMEM] * 9,
        scratch_shapes=backward_scratch(length, BLOCK_WEIGHTS),
        compiler_params=BIG,
        cost_estimate=block_cost(length, BLOCK_WEIGHTS),
    )(
        leaving_grad, latents, stream, keep_row, table, mixed, totals, middle,
        slope, enc.attn_weight, enc.fc_one_weight, enc.fc_two_weight, stack,
    )
    return found[:7], found[7:]


class Vector:
    def __init__(self, array, *parts):
        self.array, self.parts = array, parts


def block_grads(stored, found):
    normed, mixed, totals, attended, middle, second, slope, active = stored
    out_low, inner_low, middle_low, mixed_low, sums, one_sum, mixed_sum = found

    def row(k):
        return Vector(sums, (k, 0, D))

    return dict(
        norm_one_gain=row(G_ONE), norm_one_shift=row(S_ONE), attn_weight=(normed, mixed_low),
        attn_bias=Vector(mixed_sum, (0, 0, D), (0, 2 * D, D)), proj_weight=(attended, middle_low), proj_bias=row(PROJ_B),
        norm_two_gain=row(G_TWO), norm_two_shift=row(S_TWO), fc_one_weight=(second, inner_low),
        fc_one_bias=Vector(one_sum, (0, 0, MLP)), fc_two_weight=(active, out_low), fc_two_bias=row(TWO_B),
    )


SUMS = 9


def eighths(value):
    found = value[:8]
    for k in range(8, value.shape[0], 8):
        found = found + value[k : k + 8]
    return found


def sigmoid(value):
    return 0.5 + 0.5 * jnp.tanh(0.5 * value)


def silu_and_slope(value):
    s = sigmoid(value)
    silu = value * s
    return silu, s + silu * (1.0 - s)


def turned_matmul(left, right):
    return lax.dot_general(left, right, (((0,), (0,)), ((), ())), preferred_element_type=WIDE)


def head_kernel(
    divisor, arrived, features, levels, noise, final_w, wide_b, ada_b, final_b, ada_src, stack,
    signal, mod_low, modulated, inner_low, active, outer_low, joined_low, cond_low, cond_back, wide_sums, final_grad, input_grad, last,
    cond, joined, hidden, mod, hat, inner, outer, top, total, sums, cond_w, time_w, input_w, ada_w, inner_w, outer_w, weight_sem,
):
    step = pl.program_id(0)
    own = PLACES[-1]
    sources = [placed(stack, place) for place in (own.cond_weight, own.time_weight, own.input_weight)]
    sources += [ada_src, placed(stack, own.inner_weight), placed(stack, own.outer_weight)]
    held = (cond_w, time_w, input_w, ada_w, inner_w, outer_w)
    moves = [pltpu.make_async_copy(s, t, weight_sem.at[i]) for i, (s, t) in enumerate(zip(sources, held))]

    def need(*which):
        @pl.when(step == 0)
        def _():
            for i in which:
                moves[i].wait()

    def bias(k):
        return wide_b[k : k + 1, :]

    def add_sum(k, value):
        sums[k * 8 : (k + 1) * 8, :] = sums[k * 8 : (k + 1) * 8, :] + eighths(value)

    @pl.when(step == 0)
    def _():
        for move in moves:
            move.start()
        for ref in (sums, total, final_grad, input_grad, last):
            ref[...] = jnp.zeros_like(ref)
        for move in moves[:3]:
            move.wait()
        cond[...] = matmul(arrived[:, :D], cond_w[...]) + bias(0)

    clean = arrived[:, D : D + TOK_CH].astype(WIDE)
    marks = arrived[:, D + TOK_CH : D + TOK_CH + 1].astype(WIDE)
    noisy = (levels[:, 0:1] * clean + levels[:, 1:2] * noise[...]).astype(NARROW)
    value, slope = silu_and_slope(matmul(features[...], time_w[...]) + bias(1) + cond[...])
    joined[...] = slope
    signal[...] = value.astype(NARROW)
    h = matmul(noisy, input_w[...]) + bias(2)
    hidden[...] = h
    value, first_r = whiten(h)
    hat[...] = value
    need(3, 4, 5)
    mod[...] = matmul(signal[...], ada_w[...])
    normed = hat[...] * bias(3) + bias(4)
    scale = 1.0 + (mod[:, HW : 2 * HW] + ada_b[0:1, HW : 2 * HW])
    modulated[...] = (normed * scale + (mod[:, :HW] + ada_b[0:1, :HW])).astype(NARROW)
    mod[:, HW : 2 * HW] = scale
    value, slope = silu_and_slope(matmul(modulated[...], inner_w[...]) + bias(5))
    inner[...] = slope
    active[...] = value.astype(NARROW)
    out = matmul(active[...], outer_w[...]) + bias(6)
    outer[...] = out
    gate = mod[:, 2 * HW :] + ada_b[0:1, 2 * HW :]
    mod[:, 2 * HW :] = gate
    value, r = whiten(hidden[...] + gate * out)
    top[...] = value
    final = value.astype(NARROW)
    error = matmul(final, final_w[...]) + final_b[0:1, :] - noise[...]
    pred_grad = 2.0 * error * marks / divisor[0]
    pred_low = pred_grad.astype(NARROW)
    last[0:1, :TOK_CH] = last[0:1, :TOK_CH] + column_sum(pred_grad)
    last[1:2, 0:1] = last[1:2, 0:1] + column_sum(jnp.sum(error * error, -1, keepdims=True) * marks)
    final_grad[...] = final_grad[...] + turned_matmul(final, pred_low)
    g = whiten_back(matmul_turned(pred_low, final_w[...]), top[...], r)
    hidden[...] = g
    gate_grad = g * outer[...]
    mod_low[:, 2 * HW :] = gate_grad.astype(NARROW)
    add_sum(0, gate_grad)
    out_grad = g * mod[:, 2 * HW :]
    outer_low[...] = out_grad.astype(NARROW)
    add_sum(1, out_grad)
    g = matmul_turned(outer_low[...], outer_w[...]) * inner[...]
    inner_low[...] = g.astype(NARROW)
    add_sum(2, g)
    g = matmul_turned(inner_low[...], inner_w[...])
    value = hat[...]
    mod_low[:, :HW] = g.astype(NARROW)
    add_sum(3, g)
    scale_grad = g * (value * bias(3) + bias(4))
    mod_low[:, HW : 2 * HW] = scale_grad.astype(NARROW)
    add_sum(4, scale_grad)
    g = g * mod[:, HW : 2 * HW]
    add_sum(5, g)
    add_sum(6, g * value)
    g = hidden[...] + whiten_back(g * bias(3), value, first_r)
    add_sum(7, g)
    input_grad[...] = input_grad[...] + turned_matmul(noisy, g.astype(NARROW))
    g = matmul_turned(mod_low[...], ada_w[...]) * joined[...]
    joined_low[...] = g.astype(NARROW)
    add_sum(8, g)
    total[...] = total[...] + g

    @pl.when(step == pl.num_programs(0) - 1)
    def _():
        found = total[...].astype(NARROW)
        cond_low[...] = found
        cond_back[...] = matmul_turned(found, cond_w[...]).astype(NARROW)
        last[1:2, :] = jnp.broadcast_to(last[1:2, 0:1], (1, LANES))
        for k in range(SUMS):
            wide_sums[k : k + 1, :] = column_sum(sums[k * 8 : (k + 1) * 8, :])


def head_pass(p, stack, arrived, steps, noise, divisor):
    slots = arrived.shape[0]
    times = steps.astype(WIDE)
    features = time_features(times).astype(NARROW).reshape(-1, FREQ)
    level = alpha_level(times).reshape(-1, 1)
    levels = jnp.concatenate([jnp.sqrt(level), jnp.sqrt(1.0 - level)], 1)
    flat_noise = noise.reshape(-1, TOK_CH)
    wide_b = jnp.stack(
        [p.cond_bias, p.time_bias, p.input_bias, p.head_gain, p.head_shift, p.inner_bias, p.outer_bias, p.outer_bias]
    ).astype(WIDE)
    total = COPIES * slots

    def tiled(width):
        return pl.BlockSpec((slots, width), lambda i: (i, 0))

    def whole(x):
        return pl.BlockSpec(x, lambda i: (0, 0), pipeline_mode=pl.Buffered(1))

    heights = (D, FREQ, TOK_CH, None, HW, HW)
    weights = [(h, HW) if h else (HW, 3 * HW) for h in heights]
    small = (p.final_weight, wide_b, p.ada_bias.astype(WIDE)[None], p.final_bias.astype(WIDE)[None])
    kept = [((total, w), NARROW, tiled(w)) for w in (HW, 3 * HW, HW, HW, HW, HW, HW)]
    once = (((slots, HW), NARROW), ((slots, D), NARROW), ((16, HW), WIDE), ((HW, TOK_CH), WIDE), ((TOK_CH, HW), WIDE), ((8, LANES), WIDE))
    kept += [(s, t, whole(s)) for s, t in once]
    flops = 4 * total * (FREQ * HW // 2 + 5 * HW * HW) + 4 * slots * D * HW
    found = pl.pallas_call(
        head_kernel,
        grid=(COPIES,),
        out_shape=[jax.ShapeDtypeStruct(s, t) for s, t, _ in kept],
        in_specs=[pl.BlockSpec(memory_space=pltpu.SMEM), whole(arrived.shape), tiled(FREQ), tiled(2), tiled(TOK_CH)]
        + [whole(x.shape) for x in small] + [HBM] * 2,
        out_specs=[spec for _, _, spec in kept],
        scratch_shapes=[pltpu.VMEM((slots, w), WIDE) for w in (HW, HW, HW, 3 * HW, HW, HW, HW, HW, HW)]
        + [pltpu.VMEM((SUMS * 8, HW), WIDE)] + [pltpu.VMEM(s, NARROW) for s in weights] + [DMA((len(weights),))],
        compiler_params=BIG,
        cost_estimate=pl.CostEstimate(flops=flops, bytes_accessed=26 * total * HW, transcendentals=3 * total * HW),
    )(divisor[None], arrived, features, levels, flat_noise, *small, p.ada_weight, stack)
    signal, mod_low, modulated, inner_low, active, outer_low, joined_low, cond_low, cond_back, sums, final_grad, input_grad, last = found

    def row(k):
        return Vector(sums, (k, 0, HW))

    grads = dict(
        final_weight=final_grad, final_bias=Vector(last, (0, 0, LANES)),
        outer_weight=(active, outer_low), outer_bias=row(1), inner_weight=(modulated, inner_low), inner_bias=row(2),
        head_gain=row(6), head_shift=row(5), ada_weight=(signal, mod_low),
        ada_bias=Vector(sums, (3, 0, HW), (4, 0, HW), (0, 0, HW)), time_weight=(features, joined_low), time_bias=row(8),
        cond_weight=(arrived, cond_low), cond_bias=row(8), input_weight=input_grad, input_bias=row(7),
    )
    return last[1:2], grads, cond_back


def time_features(times):
    half = FREQ // 2
    freqs = jnp.exp(-math.log(10000.0) * jnp.arange(half, dtype=WIDE) / half)
    angles = times[..., None] * freqs
    return jnp.concatenate([jnp.cos(angles), jnp.sin(angles)], -1)


def alpha_level(times):
    start = math.cos(0.008 / 1.008 * math.pi / 2) ** 2
    return jnp.cos(((times + 1.0) / STEPS_T + 0.008) / 1.008 * math.pi / 2) ** 2 / start


def exchange(payload, parts):
    shape = payload.shape
    moved = lax.all_to_all(payload.reshape(parts, -1, shape[-1]), "dp", split_axis=0, concat_axis=0, tiled=True)
    return moved.reshape(shape)


def body(latents, route, labels, timesteps, noise, image_weight, weights, momentum, average):
    ranks_dp, ranks_rep = lax.axis_size("dp"), lax.axis_size("rep")
    ranks = ranks_dp * ranks_rep
    meshed = (ranks_dp, ranks_rep) == (8, 4)
    rows = route.shape[0]
    images = labels.shape[0]
    assert images == 1 and rows == SEQ
    size = weights.shape[0] // LANES
    padded = -(-(size + 1) // 48) * 48
    masked = route < rows
    flat = weights.reshape(size, LANES)
    if meshed:
        gathered = spread(flat, route, padded)
    else:
        extra = jnp.full((padded - size, LANES), jnp.sum(masked.astype(WIDE)))
        gathered = lax.all_gather(jnp.concatenate([flat, extra], 0).astype(NARROW), BOTH, axis=0)
    base, enc, mid, dec, head = groups = [types.SimpleNamespace() for _ in GROUPS]
    stack, head_stack = unpack(gathered, size, groups)
    count = jnp.sum(gathered[:, size, 0].astype(WIDE))
    keep = jnp.concatenate([jnp.ones((BUF,), WIDE), 1.0 - masked.astype(WIDE)])
    keep_row, keep_column = keep[None], keep[:, None]
    at = next(e.start for e in ENTRIES if e.sparse) + labels[0] * (D // LANES) + jnp.arange(D // LANES, dtype=jnp.int32)
    classes = gathered[at // size, at % size].reshape(D)
    table, attn_b, fc_b = block_vectors(base, enc, mid, dec, head, classes)
    enc_stored, (stream, encoded, leaving, before) = encode(
        latents, keep_row, keep_column, table, attn_b[0], fc_b[0], stack, enc
    )
    token_weight = jnp.broadcast_to(image_weight.astype(NARROW)[:, None], (rows, 1))
    extra = jnp.concatenate([latents, token_weight, jnp.zeros((rows, LANES - TOK_CH - 1), NARROW)], 1)
    dec_stored, flow_out, payload = decode(before, route, extra, table, attn_b[1], fc_b[1], stack, dec)
    arrived = exchange(payload, ranks_dp)
    divisor = TOK_CH * COPIES * count
    loss_part, head_grads, cond_back = head_pass(head, head_stack, arrived, timesteps, noise, divisor)
    returned = exchange(cond_back, ranks_dp)
    height = -(-((ranks - 1) * size + padded) // 8) * 8
    full = fold({(4, name): value for name, value in head_grads.items()}, labels, height)
    dec_found, (token_grad, before_grad, decoded_low, leaving_grad) = decode_back(
        returned, route, flow_out, before, leaving, keep_column, table, dec_stored, stack, dec
    )
    enc_found, (stream_grad, embed_grad) = encode_back(leaving_grad, latents, stream, keep_row, table, enc_stored, stack, enc)

    def row(found, k):
        return Vector(found[4], (MORE + k, 0, D))

    head_grads = dict(diffusion_pos=token_grad, dec_gain=row(dec_found, 0), dec_shift=row(dec_found, 1))
    mid_grads = dict(
        enc_gain=row(dec_found, 4), enc_shift=row(dec_found, 5), dec_weight=(encoded, decoded_low), dec_bias=row(dec_found, 2),
        mask_token=row(dec_found, 3), decoder_pos=before_grad,
    )
    base_grads = dict(encoder_pos=stream_grad, class_table=row(enc_found, 0), embed_weight=embed_grad, embed_bias=row(enc_found, 1))
    grads = {}
    parts = (base_grads, block_grads(enc_stored, enc_found), mid_grads, block_grads(dec_stored, dec_found), head_grads)
    for group, found in enumerate(parts):
        grads.update({(group, name): value for name, value in found.items()})
    full = fold(grads, labels, height, full)
    if meshed:
        lane = lax.broadcasted_iota(jnp.int32, (8, LANES), 1)
        mark = jnp.where(lane == lax.axis_index("dp") * ranks_rep + lax.axis_index("rep"), loss_part, 0.0)
        owned = collect(full, mark, size, padded)
        loss = jnp.sum(owned[padded - 8, :ranks]) / divisor
        owned = owned[:size]
    else:
        loss = lax.psum(loss_part[0, 0], BOTH) / divisor
        owned = lax.psum_scatter(full[: ranks * size].reshape(ranks, size, LANES), BOTH, scatter_dimension=0, tiled=False)
    owned = owned.reshape(-1)
    rate = 0.05 * math.sqrt(images * ranks * SEQ)
    new_momentum = 0.9 * momentum + owned
    new_weights = weights - rate * (owned + 0.9 * new_momentum)
    new_average = 0.75 * average + 0.25 * new_weights
    return new_weights, new_momentum, new_average, loss


def solution(mesh):
    flat = P(BOTH)
    placed = (P(BOTH, None), flat, flat, P(None, BOTH), P(None, BOTH, None), flat, flat, flat, flat)
    return jax.shard_map(body, mesh=mesh, in_specs=placed, out_specs=(flat, flat, flat, P()), check_vma=False)
```
